32 devices in a mesh: dp: 4 (over x, core), gate: 8 (over z, y).
Axes of the slice: x: 2, y: 2, z: 4, core: 2. Of those that a mesh axis runs over, the one named last changes fastest.
Arguments:
- frames: bfloat16 [20, 16, 16384], P(None, None, 'dp'), may hold values from -6 to 6
- regions: int32 [16384], P('dp'), may hold values from 0 to 7, as said below
- valid: int32 [15, 16384], P(None, 'dp'), may hold values from 0 to 1, as said below
- step_count: int32 [4], replicated, may hold values from 1 to 20
- conv_w: float32 [2, 4, 128, 1296], P(None, None, 'gate'), may hold values from -0.15625 to 0.15625
- cell_params: float32 [2, 7, 128], P(None, None, 'gate'), may hold values from -3 to 3
- head_w: float32 [16, 128], replicated, may hold values from -0.5 to 0.5
- head_b: float32 [16], replicated, may hold values from -2 to 2
- conv_mom: float32 [2, 4, 128, 1296], P(None, None, 'gate'), may hold values from -0.0009765625 to 0.0009765625
- cell_mom: float32 [2, 7, 128], P(None, None, 'gate'), may hold values from -0.005859375 to 0.005859375
- head_mom: float32 [16, 128], replicated, may hold values from -0.005859375 to 0.005859375
- bias_mom: float32 [16], replicated, may hold values from -0.01171875 to 0.01171875
- conv_avg: float32 [2, 4, 128, 1296], P(None, None, 'gate'), may hold values from -0.15625 to 0.15625
- cell_avg: float32 [2, 7, 128], P(None, None, 'gate'), may hold values from -3 to 3
- head_avg: float32 [16, 128], replicated, may hold values from -0.5 to 0.5
- bias_avg: float32 [16], replicated, may hold values from -2 to 2
Outputs:
- loss: float32 [], replicated
- conv_mom_new: float32 [2, 4, 128, 1296], P(None, None, 'gate')
- conv_avg_new: float32 [2, 4, 128, 1296], P(None, None, 'gate')
- conv_new: float32 [2, 4, 128, 1296], P(None, None, 'gate')
- conv_low: bfloat16 [2, 4, 128, 1296], P(None, None, 'gate')
- cell_mom_new: float32 [2, 7, 128], P(None, None, 'gate')
- cell_avg_new: float32 [2, 7, 128], P(None, None, 'gate')
- cell_new: float32 [2, 7, 128], P(None, None, 'gate')
- cell_low: bfloat16 [2, 7, 128], P(None, None, 'gate')
- head_mom_new: float32 [16, 128], replicated
- head_avg_new: float32 [16, 128], replicated
- head_new: float32 [16, 128], replicated
- head_low: bfloat16 [16, 128], replicated
- bias_mom_new: float32 [16], replicated
- bias_avg_new: float32 [16], replicated
- bias_new: float32 [16], replicated
- bias_low: bfloat16 [16], replicated
The draws below stay inside these ranges and needn't reach their ends.
Inputs may be any that keep to these rules, and one draw needn't show every extreme that they name: `regions`: each device's canvas of 32 x 128 pixels is cut into four column bands, each cut into an upper and a lower rectangle; pixel ids are 2 x band + (1 if lower); every id 0 to 7 occurs on every canvas, and the first and last row and column of a canvas always differ in id. `valid`: on canvas b of the 4 canvases each value is 1 with probability (20 + (75 * b) // max(3, 1)) / 100, independently.
All inputs are finite; a program needn't handle non-finite values.
Results may differ from the reference program's by a relative error of at most 0.0059.
Values may be sent and summed in bfloat16 or wider, within the bound.
No kernel may reach another device: no remote copies, remote signals or barrier semaphores. Data moves between devices by JAX's collectives and lax.ppermute only.
A program may use at most 256 MiB of HBM per device.

```python
import jax
import jax.numpy as jnp
from jax import lax

CIN = 16
HID = 128
EIN = 5
EOUT = 15
ROWS = 32
COLS = 128
PIX = 16384


def draw_regions(key, part):
    canvases = PIX // (ROWS * COLS)
    keys = jax.random.split(key, canvases)

    def one_canvas(canvas_key):
        first_key, second_key = jax.random.split(canvas_key)
        cuts = jnp.sort(jax.random.permutation(first_key, COLS - 1)[:3] + 1)
        row_cuts = jax.random.randint(second_key, (4,), 1, ROWS)
        column = jnp.arange(COLS)
        band = jnp.sum((column[:, None] >= cuts[None, :]).astype(jnp.int32), axis=1)
        row_index = jnp.arange(ROWS)
        lower = (row_index[:, None] >= row_cuts[band][None, :]).astype(jnp.int32)
        return (band[None, :] * 2 + lower).reshape(-1)
    return jax.vmap(one_canvas)(keys).reshape(-1).astype(jnp.int32)


def draw_valid(key, part):
    canvases = PIX // (ROWS * COLS)
    canvas_of = jnp.arange(PIX, dtype=jnp.int32) // (ROWS * COLS)
    threshold = 20 + 75 * canvas_of // max(canvases - 1, 1)
    rolls = jax.random.randint(jax.random.fold_in(key, 7), (EOUT, PIX), 0, 100)
    return (rolls < threshold[None, :]).astype(jnp.int32)


def plant(result, own_key, low, high):
    longest = result.shape.index(max(result.shape))
    spots = []
    for shift in (0, 1):
        where = [jax.random.randint(jax.random.fold_in(own_key, axis), (), 0, length) for axis, length in enumerate(result.shape)]
        where[longest] = (where[longest] + shift) % result.shape[longest]
        spots.append(tuple(where))
    return result.at[spots[0]].set(low).at[spots[1]].set(high)


def levels(rng, shape, shards, low, top_value):
    loudness = 1.0
    for axis_at, blocks in shards:
        steps = jax.random.uniform(jax.random.fold_in(jax.random.fold_in(rng, 6), axis_at), (blocks,), jnp.float32, low / len(shards), top_value / len(shards))
        loudness = loudness * jnp.repeat(jnp.exp(steps), shape[axis_at] // blocks).reshape((-1,) + (1,) * (len(shape) - 1 - axis_at))
    return loudness


def centred(key, shape, scale, limit, cuts=(), held_as=jnp.bfloat16):
    array = scale * jax.random.normal(key, shape, jnp.float32)
    if cuts:
        array = array * levels(key, shape, cuts, -0.22, 0.18)
    return jnp.clip(array, -limit, limit).astype(held_as)


def setup_inputs(seed: int = 0) -> dict:
    key_of = jax.random.split(jax.random.key(seed), 17)
    frames = centred(key_of[0], (EIN + EOUT, CIN, PIX), 1.0, 6.0, ((2, 4),))
    regions = draw_regions(jax.random.fold_in(key_of[16], 71), 0)
    valid = draw_valid(jax.random.fold_in(key_of[16], 71), 0)
    step_count = plant(jax.random.randint(key_of[3], (4,), 1, 21), jax.random.fold_in(key_of[3], 1), 1, 20).astype(jnp.int32)
    conv_w = centred(key_of[4], (2, 4, HID, 9 * (CIN + HID)), (9 * (CIN + HID)) ** -0.5, 0.15625, ((2, 8),), jnp.float32)
    cell_params = centred(key_of[5], (2, 7, HID), 0.5, 3.0, ((2, 8),), jnp.float32)
    head_w = centred(key_of[6], (CIN, HID), HID ** -0.5, 0.5, (), jnp.float32)
    head_b = centred(key_of[7], (CIN,), 0.3, 2.0, (), jnp.float32)
    conv_mom = centred(key_of[8], (2, 4, HID, 9 * (CIN + HID)), (0.5 / (CIN * (EOUT * PIX) ** 0.5)), 0.0009765625, ((2, 8),), jnp.float32)
    cell_mom = centred(key_of[9], (2, 7, HID), (3.0 / (CIN * (EOUT * PIX) ** 0.5)), 0.005859375, ((2, 8),), jnp.float32)
    head_mom = centred(key_of[10], (CIN, HID), (3.0 / (CIN * (EOUT * PIX) ** 0.5)), 0.005859375, (), jnp.float32)
    bias_mom = centred(key_of[11], (CIN,), (6.0 / (CIN * (EOUT * PIX) ** 0.5)), 0.01171875, (), jnp.float32)
    conv_avg = centred(key_of[12], (2, 4, HID, 9 * (CIN + HID)), (9 * (CIN + HID)) ** -0.5, 0.15625, ((2, 8),), jnp.float32)
    cell_avg = centred(key_of[13], (2, 7, HID), 0.5, 3.0, ((2, 8),), jnp.float32)
    head_avg = centred(key_of[14], (CIN, HID), HID ** -0.5, 0.5, (), jnp.float32)
    bias_avg = centred(key_of[15], (CIN,), 0.3, 2.0, (), jnp.float32)
    return dict(frames=frames, regions=regions, valid=valid, step_count=step_count, conv_w=conv_w, cell_params=cell_params, head_w=head_w, head_b=head_b, conv_mom=conv_mom, cell_mom=cell_mom, head_mom=head_mom, bias_mom=bias_mom, conv_avg=conv_avg, cell_avg=cell_avg, head_avg=head_avg, bias_avg=bias_avg)


MU = 0.9
RATE_SCALE = 0.05

@jax.custom_vjp
def low(v):
    return lax.optimization_barrier(v.astype(jnp.bfloat16)).astype(jnp.float32)

@jax.custom_vjp
def low_back(v):
    return v

def low_keep(v):
    return (low(v), None)

def low_pass(kept, grad):
    return (grad,)

def back_keep(v):
    return (v, None)

def back_low(kept, grad):
    return (low(grad),)
low.defvjp(low_keep, low_pass)
low_back.defvjp(back_keep, back_low)

def tap_offsets():
    return [dr * COLS + dc for dr in (-1, 0, 1) for dc in (-1, 0, 1)]

def shifted(field, off):
    blocks = field.reshape(field.shape[0], PIX // (ROWS * COLS), ROWS * COLS)
    return jnp.roll(blocks, -off, axis=2).reshape(field.shape)

def conv(weights, inp, masks):
    flat = weights.reshape(4 * HID, 9, CIN + HID)
    total = jnp.zeros((4 * HID, PIX), jnp.float32)
    for tap, off in enumerate(tap_offsets()):
        total = total + jnp.dot(flat[:, tap, :], shifted(inp, off) * masks[tap], precision=lax.Precision.HIGHEST)
    return total

def run_layer(weights, params, masks, hidden, cell, inputs, head):

    def step(carry, xs):
        hidden, cell_prev = carry
        inp = jnp.concatenate([xs[0], hidden], 0)
        pre = low_back(conv(weights, inp, masks)).reshape(4, HID, PIX) + params[:4, :, None]
        in_gate = jax.nn.sigmoid(pre[0] + params[4][:, None] * cell_prev)
        forget = jax.nn.sigmoid(pre[1] + params[5][:, None] * cell_prev)
        update = jnp.tanh(pre[3])
        cell_new = forget * cell_prev + in_gate * update
        out_gate = jax.nn.sigmoid(pre[2] + params[6][:, None] * cell_new)
        hidden_new = low(out_gate * jnp.tanh(cell_new))
        if head is None:
            return ((hidden_new, cell_new), jnp.zeros((), jnp.float32))
        head_lowered, head_bias, count = head
        guess = low_back(jnp.dot(head_lowered, hidden_new, precision=lax.Precision.HIGHEST) + head_bias[:, None])
        error = guess - xs[1]
        return ((hidden_new, cell_new), jnp.sum(xs[2][None, :] * error * error) / count)
    return lax.scan(jax.checkpoint(step), (hidden, cell), inputs)

def reference(frames, regions, valid, step_count, conv_w, cell_params, head_w, head_b, conv_mom, cell_mom, head_mom, bias_mom, conv_avg, cell_avg, head_avg, bias_avg):
    frame_data = frames.astype(jnp.float32)
    masks = [(shifted(regions[None], off)[0] == regions).astype(jnp.float32) for off in tap_offsets()]
    live = valid.astype(jnp.float32)
    count = CIN * jnp.sum(live)

    def loss_fn(conv_w, cell_params, head_w, head_b):
        weights = low(conv_w)
        head_lowered = low(head_w)
        hidden = jnp.zeros((HID, PIX), jnp.float32)
        cell = jnp.zeros((HID, PIX), jnp.float32)
        (hidden, cell), unused = run_layer(weights[0], cell_params[0], masks, hidden, cell, (frame_data[:EIN],), None)
        inputs = (frame_data[EIN - 1:EIN + EOUT - 1], frame_data[EIN:], live)
        carry, terms = run_layer(weights[1], cell_params[1], masks, hidden, cell, inputs, (head_lowered, head_b, count))
        return jnp.sum(terms)
    loss, pullback = jax.vjp(loss_fn, conv_w, cell_params, head_w, head_b)
    grads = pullback(jnp.ones((), jnp.float32))
    rate = RATE_SCALE * CIN * jnp.sqrt(jnp.float32(EOUT * PIX))
    outs = [loss]
    for index, (param, grad, mom, avg) in enumerate(zip((conv_w, cell_params, head_w, head_b), grads, (conv_mom, cell_mom, head_mom, bias_mom), (conv_avg, cell_avg, head_avg, bias_avg))):
        steps_done = step_count[index].astype(jnp.float32)
        mom_new = MU * mom + grad
        param_new = param - rate * (grad + MU * mom_new)
        avg_new = avg + (param_new - avg) / (steps_done + 1.0)
        outs += [mom_new, avg_new, param_new, param_new.astype(jnp.bfloat16)]
    return tuple(outs)
```

```python
import functools

import jax
import jax.numpy as jnp
from jax import lax
from jax.experimental import pallas as pl
from jax.experimental.pallas import tpu as pltpu
from jax.sharding import PartitionSpec as P

EIN = 5
EOUT = 15
COLS = 128

MU = 0.9
RATE_SCALE = 0.05
F32 = jnp.float32
BF16 = jnp.bfloat16
VMEM_LIMIT = 60 * 1024 * 1024


def ring_order(groups):
    wide = groups // 4
    if wide <= 1:
        return list(range(groups))
    order = [(z, 0) for z in range(4)]
    for z in range(3, -1, -1):
        ys = range(1, wide) if z % 2 else range(wide - 1, 0, -1)
        order += [(z, y) for y in ys]
    return [z * wide + y for z, y in order]


def split_steps(steps, most):
    calls = -(-steps // most)
    base, extra = divmod(steps, calls)
    return [base + (1 if i < extra else 0) for i in range(calls)]


def nesterov(param, grad, mom, avg, steps_done, rate):
    mom_new = MU * mom + grad
    param_new = param - rate * (grad + MU * mom_new)
    avg_new = avg + (param_new - avg) / (steps_done + 1.0)
    return [mom_new, avg_new, param_new, param_new.astype(BF16)]


def logistic(v):
    return 0.5 * jnp.tanh(0.5 * v) + 0.5


def dot_nt(a, b):
    return lax.dot_general(a, b, (((1,), (1,)), ((), ())), preferred_element_type=F32)


def dot_tn(a, b):
    return lax.dot_general(a, b, (((0,), (0,)), ((), ())), preferred_element_type=F32)


def cut(total, pieces):
    base, extra = divmod(total, pieces)
    spans, at = [], 0
    for i in range(pieces):
        size = base + (1 if i < extra else 0)
        spans.append((at, size))
        at += size
    return spans


class Geometry:
    def __init__(self, groups, pixels):
        self.rows = pixels // COLS
        self.own = COLS // groups
        self.halo = min(5, self.own // 2)
        self.calls = [(0, n) for n in split_steps(EIN, self.halo)] + [(1, n) for n in split_steps(EOUT, self.halo)]
        self.front = self.own + 4 * self.halo
        self.back = self.own + 2 * self.halo
        self.union = self.front + (len(self.calls) - 1) * self.halo


def make_variants(geo, hn, hb, mrm, mrp, base):
    rows = geo.rows
    for c0, cw in cut(geo.front, 4):
        r0, m = c0 * rows, cw * rows
        h = hn[r0 : r0 + m, :]
        up = pltpu.roll(h, 1, 0)
        down = pltpu.roll(h, m - 1, 0)
        g0 = base * rows + r0
        hb[0, r0 : r0 + m, :] = up.astype(BF16) * mrm[g0 : g0 + m, :]
        hb[1, r0 : r0 + m, :] = h.astype(BF16)
        hb[2, r0 : r0 + m, :] = down.astype(BF16) * mrp[g0 : g0 + m, :]


def forward_kernel(geo, layer, base, steps, first, *refs):
    refs = list(refs)
    if not first:
        near, far = refs[:2]
        refs = refs[2:]
    xcol, wh, wx, params, mrm, mrp, mcm, mcp = refs[:8]
    gates_out, cprev_out, hvar_out, hnew_out, xown_out, state_out = refs[8:14]
    hb, hn, cb, xs = refs[14:]
    rows, halo, own, front, back = geo.rows, geo.halo, geo.own, geo.front, geo.back
    step = pl.program_id(0)

    @pl.when(step == 0)
    def _():
        if first:
            hn[...] = jnp.zeros_like(hn)
            cb[...] = jnp.zeros_like(cb)
        else:
            nb = back * rows
            hn[:nb, :] = near[:, :128].astype(F32)
            hn[nb:, :] = far[:, :128].astype(F32)
            cb[:nb, :] = near[:, 128:].astype(F32)
            cb[nb:, :] = far[:, 128:].astype(F32)
        make_variants(geo, hn, hb, mrm, mrp, base)

    s0, sn = (2 * halo - 1) * rows, (own + 2) * rows
    for v in range(3):
        hvar_out[0, v, :, :] = hb[v, s0 : s0 + sn, :]
    cprev_out[0, :, :] = cb[halo * rows : (halo + back) * rows, :].astype(BF16)
    xs[...] = xcol[0].T
    xown_out[0, :, :] = xs[2 * halo * rows : (2 * halo + own) * rows, :]

    for c0, cw in cut(front - 2, 4):
        r0, m = (c0 + 1) * rows, cw * rows
        g0 = base * rows + r0
        parts = []
        for dr in range(3):
            left = hb[dr, r0 - rows : r0 - rows + m, :] * mcm[g0 : g0 + m, :]
            mid = hb[dr, r0 : r0 + m, :]
            right = hb[dr, r0 + rows : r0 + rows + m, :] * mcp[g0 : g0 + m, :]
            parts += [left, mid, right]
        z = dot_nt(jnp.concatenate(parts, 1), wh[...]) + dot_nt(xs[r0 : r0 + m, :], wx[...])
        c = cb[r0 : r0 + m, :]
        gi = logistic(z[:, 0:128] + params[0:1, :] + params[4:5, :] * c)
        gf = logistic(z[:, 128:256] + params[1:2, :] + params[5:6, :] * c)
        gg = jnp.tanh(z[:, 384:512] + params[3:4, :])
        cn = gf * c + gi * gg
        go = logistic(z[:, 256:384] + params[2:3, :] + params[6:7, :] * cn)
        h = go * jnp.tanh(cn)
        cb[r0 : r0 + m, :] = cn
        hn[r0 : r0 + m, :] = h.astype(BF16).astype(F32)
        lo, hi = max(c0 + 1, halo), min(c0 + 1 + cw, halo + back)
        a, b = (lo - c0 - 1) * rows, (hi - c0 - 1) * rows
        o = (lo - halo) * rows
        n = b - a
        if n > 0:
            gates_out[0, o : o + n, 0:128] = gi[a:b].astype(BF16)
            gates_out[0, o : o + n, 128:256] = gf[a:b].astype(BF16)
            gates_out[0, o : o + n, 256:384] = go[a:b].astype(BF16)
            gates_out[0, o : o + n, 384:512] = gg[a:b].astype(BF16)
            hnew_out[0, o : o + n, :] = h[a:b].astype(BF16)

    make_variants(geo, hn, hb, mrm, mrp, base)

    @pl.when(step == steps - 1)
    def _():
        a, b = halo * rows, (halo + back) * rows
        state_out[:, :128] = hn[a:b, :].astype(BF16)
        state_out[:, 128:] = cb[a:b, :].astype(BF16)


def whole(shape):
    return pl.BlockSpec(shape, lambda *_: (0,) * len(shape))


def forward_call(geo, layer, base, start, steps, state, xcol, wh, wx, params, masks):
    rows, own, front, back = geo.rows, geo.own, geo.front, geo.back
    chans9 = xcol.shape[1]
    by_step = lambda *dims: pl.BlockSpec((1,) + dims, lambda t: (t,) + (0,) * len(dims))
    operands = list(state) + [xcol, wh, wx, params] + list(masks)
    in_specs = [whole(s.shape) for s in state]
    in_specs += [by_step(chans9, front * rows)]
    in_specs += [whole(v.shape) for v in operands[len(state) + 1 :]]
    shapes = [
        (steps, back * rows, 512),
        (steps, back * rows, 128),
        (steps, 3, (own + 2) * rows, 128),
        (steps, back * rows, 128),
        (steps, own * rows, chans9),
    ]
    outs = [jax.ShapeDtypeStruct(s, BF16) for s in shapes] + [jax.ShapeDtypeStruct((back * rows, 256), BF16)]
    out_specs = [by_step(*s[1:]) for s in shapes] + [whole((back * rows, 256))]
    px = front * rows
    return pl.pallas_call(
        functools.partial(forward_kernel, geo, layer, base, steps, not state),
        grid=(steps,),
        in_specs=in_specs,
        out_specs=out_specs,
        out_shape=outs,
        scratch_shapes=[
            pltpu.VMEM((3, px, 128), BF16),
            pltpu.VMEM((px, 128), F32),
            pltpu.VMEM((px, 128), F32),
            pltpu.VMEM((px, chans9), BF16),
        ],
        compiler_params=pltpu.CompilerParams(vmem_limit_bytes=VMEM_LIMIT),
        cost_estimate=pl.CostEstimate(
            flops=steps * px * 512 * 1296 * 2, bytes_accessed=8 << 20, transcendentals=steps * px * 640
        ),
        name=f"forward_{base}",
    )(*operands)


def backward_kernel(geo, layer, base, steps, first, last, *refs):
    refs = list(refs)
    if not first:
        local, far = refs[:2]
        refs = refs[2:]
    gates, cprev, wb, params, mrm, mrp, mcm, mcp = refs[:8]
    refs = refs[8:]
    if layer == 1:
        hnew, target, live, head, head_b = refs[:5]
        refs = refs[5:]
    dz_out, sums_out, head_out, carry_out, send_out = refs[:5]
    dh, dc, dzb = refs[5:]
    rows, halo, own, back = geo.rows, geo.halo, geo.own, geo.back
    o0, on = halo * rows, own * rows
    step = pl.program_id(0)

    @pl.when(step == 0)
    def _():
        sums_out[...] = jnp.zeros_like(sums_out)
        head_out[...] = jnp.zeros_like(head_out)
        dzb[...] = jnp.zeros_like(dzb)
        if first:
            dh[...] = jnp.zeros_like(dh)
            dc[...] = jnp.zeros_like(dc)
        else:
            nf = 2 * halo * rows
            dh[:nf, :] = far[:, :128].astype(F32)
            dc[:nf, :] = far[:, 128:].astype(F32)
            dh[nf:, :] = local[:, :128]
            dc[nf:, :] = local[:, 128:]

    if layer == 1:
        guess = dot_nt(head[...], hnew[0]) + head_b[...]
        err = guess - target[0].astype(F32)
        dy = live[0] * err
        low = dy.astype(BF16)
        head_out[:, 0:128] += jnp.dot(low[:, o0 : o0 + on], hnew[0, o0 : o0 + on, :], preferred_element_type=F32)
        own_dy = low[:, o0 : o0 + on].astype(F32)
        head_out[:, 128:129] += jnp.sum(own_dy, 1, keepdims=True)
        head_out[:, 129:130] += jnp.sum((dy * err)[:, o0 : o0 + on], 1, keepdims=True)
        dh[...] += dot_tn(low, head[...])

    for c0, cw in cut(back, 4):
        r0, m = c0 * rows, cw * rows
        span = slice(r0, r0 + m)
        gi = gates[0, span, 0:128].astype(F32)
        gf = gates[0, span, 128:256].astype(F32)
        go = gates[0, span, 256:384].astype(F32)
        gg = gates[0, span, 384:512].astype(F32)
        c = cprev[0, span, :].astype(F32)
        cn = gf * c + gi * gg
        tc = jnp.tanh(cn)
        g = dh[span, :]
        d_o = g * tc * go * (1.0 - go)
        d_c = dc[span, :] + g * go * (1.0 - tc * tc) + d_o * params[6:7, :]
        d_i = d_c * gg * gi * (1.0 - gi)
        d_f = d_c * c * gf * (1.0 - gf)
        d_g = d_c * gi * (1.0 - gg * gg)
        dc[span, :] = d_c * gf + d_i * params[4:5, :] + d_f * params[5:6, :]
        p0 = rows + r0
        for n, d in enumerate((d_i, d_f, d_o, d_g)):
            dzb[p0 : p0 + m, n * 128 : (n + 1) * 128] = d.astype(BF16)
        a = max(r0, o0) - r0
        b = min(r0 + m, o0 + on) - r0
        if b > a:
            for n, d in enumerate((d_i, d_f, d_o, d_g, d_i * c, d_f * c, d_o * cn)):
                part = d[a:b].reshape((b - a) // 8, 8, 128)
                sums_out[n * 8 : (n + 1) * 8, :] += jnp.sum(part, 0)

    dz_out[0, :, :] = dzb[rows + o0 : rows + o0 + on, :]

    @pl.when(step < (steps - 1 if last else steps))
    def _():
        for c0, cw in cut(back, 4):
            r0, m = c0 * rows, cw * rows
            total = None
            g0 = (base + halo) * rows + r0
            for dr in range(3):
                parts = []
                for dc_i in range(3):
                    src = r0 - (dc_i - 1) * rows
                    v = dzb[rows + src : rows + src + m, :]
                    gm = g0 - (dc_i - 1) * rows
                    if dc_i == 0:
                        keep = mcm[gm : gm + m, :]
                    elif dc_i == 2:
                        keep = mcp[gm : gm + m, :]
                    if dc_i != 1:
                        v = v * jnp.concatenate([keep] * 4, 1)
                    parts.append(v)
                acc = jnp.dot(jnp.concatenate(parts, 1), wb[dr], preferred_element_type=F32)
                if dr == 0:
                    acc = acc * mrm[g0 : g0 + m, :].astype(F32)
                    acc = pltpu.roll(acc, m - 1, 0)
                elif dr == 2:
                    acc = acc * mrp[g0 : g0 + m, :].astype(F32)
                    acc = pltpu.roll(acc, 1, 0)
                total = acc if total is None else total + acc
            dh[r0 : r0 + m, :] = total

    @pl.when(step == steps - 1)
    def _():
        carry_out[:, :128] = dh[o0 : o0 + on, :]
        carry_out[:, 128:] = dc[o0 : o0 + on, :]
        ns = 2 * halo * rows
        s0 = o0 + on - ns
        send_out[:, :128] = dh[s0 : s0 + ns, :].astype(BF16)
        send_out[:, 128:] = dc[s0 : s0 + ns, :].astype(BF16)


def backward_call(geo, layer, base, steps, last, state, saved, wb, params, masks, extra):
    rows, own, back, halo = geo.rows, geo.own, geo.back, geo.halo
    by_step = lambda *dims: pl.BlockSpec((1,) + dims, lambda t: (steps - 1 - t,) + (0,) * len(dims))
    operands = list(state) + [saved["gates"], saved["cprev"], wb, params] + list(masks)
    in_specs = [whole(s.shape) for s in state]
    in_specs += [by_step(back * rows, 512), by_step(back * rows, 128)]
    in_specs += [whole(v.shape) for v in operands[len(state) + 2 :]]
    if layer == 1:
        target, live, head, head_b = extra
        operands += [saved["hnew"], target, live, head, head_b]
        in_specs += [
            by_step(back * rows, 128),
            by_step(target.shape[1], back * rows),
            by_step(1, back * rows),
            whole(head.shape),
            whole(head_b.shape),
        ]
    outs = [
        jax.ShapeDtypeStruct((steps, own * rows, 512), BF16),
        jax.ShapeDtypeStruct((56, 128), F32),
        jax.ShapeDtypeStruct((16, 256), F32),
        jax.ShapeDtypeStruct((own * rows, 256), F32),
        jax.ShapeDtypeStruct((2 * halo * rows, 256), BF16),
    ]
    out_specs = [by_step(own * rows, 512)] + [whole(o.shape) for o in outs[1:]]
    px = back * rows
    return pl.pallas_call(
        functools.partial(backward_kernel, geo, layer, base, steps, not state, last),
        grid=(steps,),
        in_specs=in_specs,
        out_specs=out_specs,
        out_shape=outs,
        scratch_shapes=[
            pltpu.VMEM((px, 128), F32),
            pltpu.VMEM((px, 128), F32),
            pltpu.VMEM((px + 2 * rows, 512), BF16),
        ],
        compiler_params=pltpu.CompilerParams(vmem_limit_bytes=VMEM_LIMIT),
        cost_estimate=pl.CostEstimate(
            flops=steps * px * 512 * 1536 * 2, bytes_accessed=8 << 20, transcendentals=steps * px * 128
        ),
        name=f"backward_{base}",
    )(*operands)


def weight_kernel(geo, base, steps, add, *refs):
    if add:
        acc, dz, hvar, xown, mcm, mcp, out, rhs = refs
    else:
        dz, hvar, xown, mcm, mcp, out, rhs = refs
    rows, own, halo = geo.rows, geo.own, geo.halo
    on = own * rows
    g0 = (base + 2 * halo) * rows
    wide = hvar.shape[-1]
    taps = [(dr, dc) for dr in range(3) for dc in range(3)]
    for n in range(0, 10, 2):
        for k in range(2):
            for j in range(steps):
                at = slice(j * on, (j + 1) * on)
                if n + k < 9:
                    dr, dc = taps[n + k]
                    v = hvar[j, dr, dc * rows : dc * rows + on, :]
                    if dc == 0:
                        v = v * mcm[g0 : g0 + on, :]
                    elif dc == 2:
                        v = v * mcp[g0 : g0 + on, :]
                    rhs[at, k * wide : (k + 1) * wide] = v
                else:
                    rhs[at, wide : wide + xown.shape[-1]] = xown[j]
        width = 2 * wide if n + 1 < 9 else wide + xown.shape[-1]
        lo = n * wide
        g = dot_tn(dz[...], rhs[:, :width])
        if add:
            g = g + acc[:, lo : lo + width]
        out[:, lo : lo + width] = g


def weight_call(geo, base, steps, acc, dz, hvar, xown, mcm, mcp):
    on = geo.own * geo.rows
    dz = dz.reshape(steps * on, 512)
    chans9 = xown.shape[-1]
    operands = ([] if acc is None else [acc]) + [dz, hvar, xown, mcm, mcp]
    return pl.pallas_call(
        functools.partial(weight_kernel, geo, base, steps, acc is not None),
        out_shape=jax.ShapeDtypeStruct((512, 1152 + chans9), F32),
        scratch_shapes=[pltpu.VMEM((steps * on, 384), BF16)],
        compiler_params=pltpu.CompilerParams(vmem_limit_bytes=VMEM_LIMIT),
        cost_estimate=pl.CostEstimate(
            flops=steps * on * 512 * 1296 * 2, bytes_accessed=16 << 20, transcendentals=0
        ),
        name=f"weights_{base}",
    )(*operands)


def swap_pairs(size, bit):
    return [(i, i ^ bit) for i in range(size)]


def butterfly_bits(size):
    bits, bit = [], 1
    while bit < size:
        bits.append(bit)
        bit *= 2
    return bits


def gather_dp(piece, ranks):
    me = lax.axis_index("dp")
    for bit in butterfly_bits(ranks)[1:] + [1]:
        other = lax.ppermute(piece, "dp", swap_pairs(ranks, bit))
        high = (me & bit) != 0
        pair = jnp.stack([jnp.where(high, other, piece), jnp.where(high, piece, other)])
        if bit == 1:
            piece = jnp.swapaxes(pair, 0, 1).reshape((-1,) + piece.shape[1:])
        else:
            piece = pair.reshape((-1,) + piece.shape[1:])
    return piece


def scatter_sum_dp(whole_sum, ranks, small):
    me = lax.axis_index("dp")
    value = whole_sum
    bits = butterfly_bits(ranks)
    for n, bit in enumerate([1] + bits[:0:-1]):
        if bit == 1:
            halves = value.reshape((ranks // 2, 2) + value.shape[1:])
            low, high = halves[:, 0], halves[:, 1]
        else:
            half = value.shape[0] // 2
            low, high = value[:half], value[half:]
        mine_high = (me & bit) != 0
        send = jnp.where(mine_high, low, high).astype(BF16)
        keep = jnp.where(mine_high, high, low)
        pairs = swap_pairs(ranks, bit)
        value = keep + lax.ppermute(send, "dp", pairs).astype(F32)
        hi = small.astype(BF16)
        lo = (small - hi.astype(F32)).astype(BF16)
        got = lax.ppermute(jnp.stack([hi, lo]), "dp", pairs).astype(F32)
        small = small + (got[0] + got[1])
    return value[0], small


def on_device(
    frames,
    regions,
    valid,
    step_count,
    conv_w,
    cell_params,
    head_w,
    head_b,
    conv_mom,
    cell_mom,
    head_mom,
    bias_mom,
    conv_avg,
    cell_avg,
    head_avg,
    bias_avg,
):
    share = conv_w.shape[2]
    chans = frames.shape[1]
    pixels = frames.shape[2]
    wide = head_w.shape[1]
    groups = lax.axis_size("gate")
    ranks = lax.axis_size("dp")
    geo = Geometry(groups, pixels)
    rows, own, halo, front, back, union = geo.rows, geo.own, geo.halo, geo.front, geo.back, geo.union
    gate_at = lax.axis_index("gate")
    dp_at = lax.axis_index("dp")

    order = ring_order(groups)
    place = [order.index(g) for g in range(groups)]
    spot = jnp.asarray(place, jnp.int32)[gate_at]
    from_right = [(order[(i + 1) % groups], order[i]) for i in range(groups)]
    from_left = [(order[i], order[(i + 1) % groups]) for i in range(groups)]

    taps = conv_w.reshape(2, 4 * share, 9, chans + wide).astype(BF16)
    packed = jnp.concatenate(
        [taps[..., chans:].reshape(2, 4 * share, 9 * wide), taps[..., :chans].reshape(2, 4 * share, 9 * chans)], -1
    )
    slab = 4 * share // ranks
    packed_w = packed.shape[-1]
    mine = lax.dynamic_slice_in_dim(packed.reshape(2, ranks, slab, packed_w), dp_at, 1, 1)[:, 0]
    everyone = lax.all_to_all(
        jnp.broadcast_to(mine[None], (groups, 2, slab, packed_w)), "gate", 0, 0, tiled=True
    )
    gathered = gather_dp(everyone[None], ranks)
    full = gathered.transpose(2, 1, 0, 3, 4).reshape(2, groups, 4, share, packed_w)
    full = full.transpose(0, 2, 1, 3, 4).reshape(2, 4 * wide, packed_w)
    cell_all = lax.all_gather(cell_params, "gate", axis=2, tiled=True)

    def window(field, dtype):
        lead = field.shape[:-1]
        grid = jnp.swapaxes(field.astype(dtype).reshape(lead + (rows, COLS)), -1, -2)
        flat = grid.reshape(lead + (pixels,))
        start = jnp.mod(spot * own - 2 * halo - 1, COLS) * rows
        twice = jnp.concatenate([flat, flat], -1)
        return lax.dynamic_slice_in_dim(twice, start, (union + 2) * rows, len(lead))

    px = union * rows
    ids = window(regions, jnp.int32)
    pad_ids = jnp.pad(ids, (1, 1), constant_values=-1)
    offsets = [dc * rows + dr for dr in (-1, 0, 1) for dc in (-1, 0, 1)]

    def shifted(v, off):
        return lax.slice_in_dim(v, 1 + rows + off, 1 + rows + off + px, axis=v.ndim - 1)

    here = shifted(pad_ids, 0)
    keeps = [shifted(pad_ids, off) == here for off in offsets]
    spread = lambda m: jnp.broadcast_to(m[:, None], (px, 128)).astype(BF16)
    column_ids = here - here % 2
    pad_cols = pad_ids - pad_ids % 2
    masks = (
        spread(keeps[1]),
        spread(keeps[7]),
        spread(shifted(pad_cols, -rows) == column_ids),
        spread(shifted(pad_cols, rows) == column_ids),
    )
    seen = window(frames, BF16)
    pad_seen = jnp.pad(seen, ((0, 0), (0, 0), (1, 1)))
    xcol = jnp.concatenate(
        [jnp.where(keep, shifted(pad_seen, off), jnp.zeros((), BF16)) for keep, off in zip(keeps, offsets)], 1
    )
    centre = shifted(pad_seen, 0)
    live = shifted(jnp.pad(window(valid, F32), ((0, 0), (1, 1))), 0)[:, None, :]

    head_low = head_w.astype(BF16)
    head_bias = head_b[:, None]
    wh = [full[l, :, : 9 * wide] for l in range(2)]
    wx = [full[l, :, 9 * wide :] for l in range(2)]
    wb = [
        wh[l].reshape(4 * wide, 3, 3, wide).transpose(1, 2, 0, 3).reshape(3, 3 * 4 * wide, wide) for l in range(2)
    ]

    state = ()
    kept = []
    t = 0
    for n, (layer, steps) in enumerate(geo.calls):
        base = n * halo
        first_frame = t if layer == 0 else t - 1
        xin = xcol[first_frame : first_frame + steps, :, base * rows : (base + front) * rows]
        got = forward_call(geo, layer, base, t, steps, state, xin, wh[layer], wx[layer], cell_all[layer], masks)
        kept.append(dict(gates=got[0], cprev=got[1], hvar=got[2], hnew=got[3], xown=got[4], t=t))
        out = got[5]
        t += steps
        if n + 1 < len(geo.calls):
            far = lax.ppermute(out[2 * halo * rows : 4 * halo * rows], "gate", from_right)
            state = (out, far)

    state = ()
    grads = [None, None]
    cell_sums = [jnp.zeros((56, 128), F32) for _ in range(2)]
    head_sums = jnp.zeros((16, 256), F32)
    for n in range(len(geo.calls) - 1, -1, -1):
        layer, steps = geo.calls[n]
        base = n * halo
        saved = kept[n]
        extra = None
        if layer == 1:
            t = saved["t"]
            a, b = (base + halo) * rows, (base + halo + back) * rows
            extra = (centre[t : t + steps, :, a:b], live[t - EIN : t - EIN + steps, :, a:b], head_low, head_bias)
        got = backward_call(
            geo, layer, base, steps, n == 0, state, saved, wb[layer], cell_all[layer], masks, extra
        )
        if n > 0:
            far = lax.ppermute(got[4], "gate", from_left)
            state = (got[3], far)
        grads[layer] = weight_call(
            geo, base, steps, grads[layer], got[0], saved["hvar"], saved["xown"], masks[2], masks[3]
        )
        cell_sums[layer] = cell_sums[layer] + got[1]
        if layer == 1:
            head_sums = head_sums + got[2]

    cells = jnp.stack(cell_sums).reshape(2, 7, 8, wide).sum(2)
    mine_live = lax.dynamic_slice_in_dim(valid.reshape(EOUT, rows, COLS), spot * own, own, 2)
    counted = jnp.sum(mine_live).astype(F32)
    loss_sum = jnp.sum(head_sums[:, 129])
    shared_small = jnp.concatenate(
        [head_sums[:, :128].reshape(-1), head_sums[:, 128], loss_sum[None], counted[None]]
    )
    small = jnp.concatenate([cells.reshape(-1), shared_small])
    big = jnp.stack(grads).reshape(2, 4, groups, share, packed_w).transpose(2, 1, 3, 0, 4)
    big = big.reshape(groups, ranks, slab, 2, packed_w).transpose(1, 0, 2, 3, 4)
    part, small = scatter_sum_dp(big, ranks, small)
    ncell = 14 * wide
    for_gate = small[:ncell].reshape(14, groups, share).transpose(1, 0, 2).reshape(groups, 14 * share)
    to_gate = jnp.concatenate(
        [for_gate, jnp.broadcast_to(small[None, ncell:], (groups, small.shape[0] - ncell))], 1
    )
    hi = to_gate.astype(BF16)
    lo = (to_gate - hi.astype(F32)).astype(BF16)
    width = slab * 2 * packed_w
    message = jnp.concatenate([part.reshape(groups, width).astype(BF16), hi, lo], 1)
    got = lax.all_to_all(message, "gate", 0, 0, tiled=True).astype(F32)
    got = jnp.sum(got.reshape(groups, -1), 0)
    nsmall = to_gate.shape[1]
    small_sum = got[width : width + nsmall] + got[width + nsmall :]
    piece = got[:width].reshape(1, slab, 2, packed_w)
    rows_all = gather_dp(piece, ranks).reshape(4 * share, 2, packed_w).transpose(1, 0, 2)
    count = chans * small_sum[-1]
    scale = 2.0 / count
    rows_all = rows_all * scale
    grad_conv = jnp.concatenate(
        [
            rows_all[..., 9 * wide :].reshape(2, 4 * share, 9, chans),
            rows_all[..., : 9 * wide].reshape(2, 4 * share, 9, wide),
        ],
        -1,
    ).reshape(conv_w.shape)
    grad_cell = small_sum[: 14 * share].reshape(2, 7, share) * scale
    rest = small_sum[14 * share :]
    grad_head = rest[: chans * wide].reshape(chans, wide) * scale
    grad_bias = rest[chans * wide : chans * wide + chans] * scale
    loss = rest[chans * wide + chans] / count

    rate = RATE_SCALE * chans * jnp.sqrt(jnp.float32(EOUT * pixels * ranks))
    counts_done = step_count.astype(F32)
    outs = [loss]
    outs += nesterov(conv_w, grad_conv, conv_mom, conv_avg, counts_done[0], rate)
    outs += nesterov(cell_params, grad_cell, cell_mom, cell_avg, counts_done[1], rate)
    outs += nesterov(head_w, grad_head, head_mom, head_avg, counts_done[2], rate)
    outs += nesterov(head_b, grad_bias, bias_mom, bias_avg, counts_done[3], rate)
    return tuple(outs)


def solution(mesh):
    in_specs = (
        P(None, None, "dp"),
        P("dp"),
        P(None, "dp"),
        P(),
        P(None, None, "gate", None),
        P(None, None, "gate"),
        P(),
        P(),
        P(None, None, "gate", None),
        P(None, None, "gate"),
        P(),
        P(),
        P(None, None, "gate", None),
        P(None, None, "gate"),
        P(),
        P(),
    )
    out_specs = (
        P(),
        P(None, None, "gate", None),
        P(None, None, "gate", None),
        P(None, None, "gate", None),
        P(None, None, "gate", None),
        P(None, None, "gate"),
        P(None, None, "gate"),
        P(None, None, "gate"),
        P(None, None, "gate"),
        P(),
        P(),
        P(),
        P(),
        P(),
        P(),
        P(),
        P(),
    )
    return jax.shard_map(
        on_device, mesh=mesh, in_specs=in_specs, out_specs=out_specs, check_vma=False
    )
```

```python
import functools

import jax
import jax.numpy as jnp
from jax import lax
from jax.experimental import pallas as pl
from jax.experimental.pallas import tpu as pltpu
from jax.sharding import PartitionSpec as P

EIN = 5
EOUT = 15
COLS = 128

MU = 0.9
RATE_SCALE = 0.05
F32 = jnp.float32
BF16 = jnp.bfloat16
VMEM_LIMIT = 60 * 1024 * 1024


def ring_order(groups):
    wide = groups // 4
    if wide <= 1:
        return list(range(groups))
    order = [(z, 0) for z in range(4)]
    for z in range(3, -1, -1):
        ys = range(1, wide) if z % 2 else range(wide - 1, 0, -1)
        order += [(z, y) for y in ys]
    return [z * wide + y for z, y in order]


def split_steps(steps, most):
    calls = -(-steps // most)
    base, extra = divmod(steps, calls)
    return [base + (1 if i < extra else 0) for i in range(calls)]


def nesterov(param, grad, mom, avg, steps_done, rate):
    mom_new = MU * mom + grad
    param_new = param - rate * (grad + MU * mom_new)
    avg_new = avg + (param_new - avg) / (steps_done + 1.0)
    return [mom_new, avg_new, param_new, param_new.astype(BF16)]


def logistic(v):
    return 0.5 * jnp.tanh(0.5 * v) + 0.5


def dot_nt(a, b):
    return lax.dot_general(a, b, (((1,), (1,)), ((), ())), preferred_element_type=F32)


def dot_tn(a, b):
    return lax.dot_general(a, b, (((0,), (0,)), ((), ())), preferred_element_type=F32)


def cut(total, pieces):
    base, extra = divmod(total, pieces)
    spans, at = [], 0
    for i in range(pieces):
        size = base + (1 if i < extra else 0)
        spans.append((at, size))
        at += size
    return spans


def cut_by_four(total, pieces):
    spans, at = [], 0
    for i in range(pieces):
        left = pieces - i
        size = total - at if left == 1 else (total - at) // left // 4 * 4
        if size:
            spans.append((at, size))
        at += size
    return spans


class Geometry:
    def __init__(self, groups, pixels):
        self.rows = pixels // COLS
        self.own = COLS // groups
        self.halo = min(5, self.own // 2)
        self.calls = [(0, n) for n in split_steps(EIN, self.halo)] + [(1, n) for n in split_steps(EOUT, self.halo)]
        self.front = self.own + 4 * self.halo
        self.back = self.own + 2 * self.halo
        self.union = self.front + (len(self.calls) - 1) * self.halo
        self.window = -(-(self.union + 2) * self.rows // 256) * 256


TAPS = [(dr, dc) for dr in (-1, 0, 1) for dc in (-1, 0, 1)]
CELL_COLS = 16


def window_kernel(geo, start, frames, valid, regions, win, meta, mrm, mrp, mcm, mcp, count, lhs, pick):
    rows, own, halo, union, width = geo.rows, geo.own, geo.halo, geo.union, geo.window
    nf = frames.shape[0]
    nv = valid.shape[0]
    lhs[:nf, :] = frames[...]
    lhs[nf : nf + nv, :] = valid[...].astype(F32).astype(BF16)
    lhs[nf + nv : nf + nv + 1, :] = regions[...].astype(F32).astype(BF16)
    per = 256 // rows
    source = lax.broadcasted_iota(jnp.int32, (COLS, 256), 0)
    lane = lax.broadcasted_iota(jnp.int32, (COLS, 256), 1)
    lane_row = lax.broadcasted_iota(jnp.int32, (1, 256), 1) % rows

    def one(n, carry):
        column = (start[0] + n * per + lane // rows) % COLS
        hit = (source == column).astype(F32).astype(BF16)
        for r in range(rows):
            keep = (lane_row == r).astype(F32).astype(BF16)
            pick[r * COLS : (r + 1) * COLS, :] = hit * keep
        got = jnp.dot(lhs[...], pick[...], preferred_element_type=F32)
        at = pl.multiple_of(n * 256, 256)
        win[:, pl.ds(at, 256)] = got[:nf].astype(BF16)
        meta[:, pl.ds(at, 256)] = got[nf:]
        return carry

    lax.fori_loop(0, width // 256, one, 0)
    px = union * rows
    ids = meta[nv : nv + 1, :]
    bands = jnp.floor(ids * 0.5)
    here = ids[:, rows : rows + px]
    band_here = bands[:, rows : rows + px]
    picked = [
        ids[:, rows - 1 : rows - 1 + px] == here,
        ids[:, rows + 1 : rows + 1 + px] == here,
        bands[:, :px] == band_here,
        bands[:, 2 * rows : 2 * rows + px] == band_here,
    ]
    row_at = lax.broadcasted_iota(jnp.int32, (8, px), 0)
    stack = jnp.zeros((8, px), F32)
    for k, m in enumerate(picked):
        stack = jnp.where(row_at == k, jnp.broadcast_to(m.astype(F32), (8, px)), stack)
    stack = stack.astype(BF16)
    sel = lax.broadcasted_iota(jnp.int32, (8, 128), 0)
    for k, out in enumerate((mrm, mrp, mcm, mcp)):
        out[...] = dot_tn(stack, (sel == k).astype(F32).astype(BF16)).astype(BF16)
    a = (2 * halo + 1) * rows
    count[...] = jnp.broadcast_to(jnp.sum(meta[:nv, a : a + own * rows]), count.shape)


def window_call(geo, start, frames, valid, regions):
    nf, nv = frames.shape[0], valid.shape[0]
    pixels = frames.shape[1]
    px = geo.union * geo.rows
    smem = pl.BlockSpec(memory_space=pltpu.SMEM)
    vmem = pl.BlockSpec(memory_space=pltpu.VMEM)
    total = nf + nv + 1
    return pl.pallas_call(
        functools.partial(window_kernel, geo),
        in_specs=[smem, vmem, vmem, vmem],
        out_specs=[vmem] * 7,
        out_shape=[
            jax.ShapeDtypeStruct((nf, geo.window), BF16),
            jax.ShapeDtypeStruct((nv + 1, geo.window), F32),
        ]
        + [jax.ShapeDtypeStruct((px, 128), BF16)] * 4
        + [jax.ShapeDtypeStruct((8, 128), F32)],
        scratch_shapes=[pltpu.VMEM((total, pixels), BF16), pltpu.VMEM((pixels, 256), BF16)],
        compiler_params=pltpu.CompilerParams(vmem_limit_bytes=VMEM_LIMIT),
        cost_estimate=pl.CostEstimate(
            flops=2 * total * pixels * geo.window, bytes_accessed=10 << 20, transcendentals=0
        ),
        name="window",
    )(start, frames, valid, regions)


def peephole_rows(chans9, wx):
    col = lax.broadcasted_iota(jnp.int32, (8, wx.shape[1]), 1)
    sel = ((col >= chans9 + 3) & (col < chans9 + 6)).astype(F32).astype(BF16)
    got = dot_nt(sel, wx[...])
    return [got[0:1, k * 128 : (k + 1) * 128] for k in range(3)]


def make_variants(geo, hn, hb, mrm, mrp, base):
    rows = geo.rows
    for c0, cw in cut(geo.front, 4):
        r0, m = c0 * rows, cw * rows
        h = hn[r0 : r0 + m, :]
        up = pltpu.roll(h, 1, 0)
        down = pltpu.roll(h, m - 1, 0)
        g0 = base * rows + r0
        hb[0, r0 : r0 + m, :] = up.astype(BF16) * mrm[g0 : g0 + m, :]
        hb[1, r0 : r0 + m, :] = h.astype(BF16)
        hb[2, r0 : r0 + m, :] = down.astype(BF16) * mrp[g0 : g0 + m, :]


def forward_kernel(geo, layer, base, steps, first, *refs):
    refs = list(refs)
    if not first:
        near, far = refs[:2]
        refs = refs[2:]
    win, meta, wh, wx, mrm, mrp, mcm, mcp = refs[:8]
    gates_out, cprev_out, hvar_out, hnew_out, xown_out, state_out = refs[8:14]
    hb, hn, cb, xs, keeps, peeps = refs[14:]
    rows, halo, own, front, back = geo.rows, geo.halo, geo.own, geo.front, geo.back
    chans = win.shape[0]
    chans9 = 9 * chans
    lanes = (front - 2) * rows
    x0 = (base + 2) * rows
    step = pl.program_id(0)

    @pl.when(step == 0)
    def _():
        if first:
            hn[...] = jnp.zeros_like(hn)
            cb[...] = jnp.zeros_like(cb)
        else:
            nb = back * rows
            hn[:nb, :] = near[:, :128].astype(F32)
            hn[nb:, :] = far[:, :128].astype(F32)
            cb[:nb, :] = near[:, 128:].astype(F32)
            cb[nb:, :] = far[:, 128:].astype(F32)
        make_variants(geo, hn, hb, mrm, mrp, base)
        ids = meta[meta.shape[0] - 1 :, :]
        here = ids[:, x0 : x0 + lanes]
        for tap, (dr, dc) in enumerate(TAPS):
            off = x0 + dc * rows + dr
            same = (ids[:, off : off + lanes] == here).astype(F32)
            keeps[tap * chans : (tap + 1) * chans, :] = jnp.broadcast_to(same, (chans, lanes)).astype(BF16)
        ones = lax.broadcasted_iota(jnp.int32, (CELL_COLS, lanes), 0) < 3
        xs[chans9:, :] = ones.astype(F32).astype(BF16)
        for k, row in enumerate(peephole_rows(chans9, wx)):
            peeps[k : k + 1, :] = row

    s0, sn = (2 * halo - 1) * rows, (own + 2) * rows
    for v in range(3):
        hvar_out[0, v, :, :] = hb[v, s0 : s0 + sn, :]
    cprev_out[0, :, :] = cb[halo * rows : (halo + back) * rows, :].astype(BF16)
    for tap, (dr, dc) in enumerate(TAPS):
        off = x0 + dc * rows + dr
        part = slice(tap * chans, (tap + 1) * chans)
        xs[part, :] = win[:, off : off + lanes] * keeps[part, :]
    q0 = (2 * halo - 1) * rows
    xown_out[0, :, :] = xs[:, q0 : q0 + own * rows]

    for c0, cw in cut_by_four(front - 2, 4):
        r0, m = (c0 + 1) * rows, cw * rows
        g0 = base * rows + r0
        parts = []
        for dr in range(3):
            left = hb[dr, r0 - rows : r0 - rows + m, :] * mcm[g0 : g0 + m, :]
            mid = hb[dr, r0 : r0 + m, :]
            right = hb[dr, r0 + rows : r0 + rows + m, :] * mcp[g0 : g0 + m, :]
            parts += [left, mid, right]
        z = dot_nt(jnp.concatenate(parts, 1), wh[...]) + lax.dot_general(
            xs[:, r0 - rows : r0 - rows + m], wx[...], (((0,), (1,)), ((), ())), preferred_element_type=F32
        )
        c = cb[r0 : r0 + m, :]
        gi = logistic(z[:, 0:128] + peeps[0:1, :] * c)
        gf = logistic(z[:, 128:256] + peeps[1:2, :] * c)
        gg = jnp.tanh(z[:, 384:512])
        cn = gf * c + gi * gg
        go = logistic(z[:, 256:384] + peeps[2:3, :] * cn)
        h = go * jnp.tanh(cn)
        cb[r0 : r0 + m, :] = cn
        hn[r0 : r0 + m, :] = h.astype(BF16).astype(F32)
        lo, hi = max(c0 + 1, halo), min(c0 + 1 + cw, halo + back)
        a, b = (lo - c0 - 1) * rows, (hi - c0 - 1) * rows
        o = (lo - halo) * rows
        n = b - a
        if n > 0:
            gates_out[0, o : o + n, 0:128] = gi[a:b].astype(BF16)
            gates_out[0, o : o + n, 128:256] = gf[a:b].astype(BF16)
            gates_out[0, o : o + n, 256:384] = go[a:b].astype(BF16)
            gates_out[0, o : o + n, 384:512] = gg[a:b].astype(BF16)
            hnew_out[0, o : o + n, :] = h[a:b].astype(BF16)

    make_variants(geo, hn, hb, mrm, mrp, base)

    @pl.when(step == steps - 1)
    def _():
        a, b = halo * rows, (halo + back) * rows
        state_out[:, :128] = hn[a:b, :].astype(BF16)
        state_out[:, 128:] = cb[a:b, :].astype(BF16)


def whole(shape):
    return pl.BlockSpec(shape, lambda *_: (0,) * len(shape))


def forward_call(geo, layer, base, first_frame, steps, state, win, meta, wh, wx, masks):
    rows, own, front, back = geo.rows, geo.own, geo.front, geo.back
    chans = win.shape[0] // (EIN + EOUT)
    depth = wx.shape[1]
    by_step = lambda *dims: pl.BlockSpec((1,) + dims, lambda t: (t,) + (0,) * len(dims))
    operands = list(state) + [win, meta, wh, wx] + list(masks)
    in_specs = [whole(s.shape) for s in state]
    in_specs += [pl.BlockSpec((chans, win.shape[1]), lambda t: (first_frame + t, 0))]
    in_specs += [whole(v.shape) for v in operands[len(state) + 1 :]]
    shapes = [
        (steps, back * rows, 512),
        (steps, back * rows, 128),
        (steps, 3, (own + 2) * rows, 128),
        (steps, back * rows, 128),
        (steps, depth, own * rows),
    ]
    outs = [jax.ShapeDtypeStruct(s, BF16) for s in shapes] + [jax.ShapeDtypeStruct((back * rows, 256), BF16)]
    out_specs = [by_step(*s[1:]) for s in shapes] + [whole((back * rows, 256))]
    px = front * rows
    return pl.pallas_call(
        functools.partial(forward_kernel, geo, layer, base, steps, not state),
        grid=(steps,),
        in_specs=in_specs,
        out_specs=out_specs,
        out_shape=outs,
        scratch_shapes=[
            pltpu.VMEM((3, px, 128), BF16),
            pltpu.VMEM((px, 128), F32),
            pltpu.VMEM((px, 128), F32),
            pltpu.VMEM((depth, px - 2 * rows), BF16),
            pltpu.VMEM((9 * chans, px - 2 * rows), BF16),
            pltpu.VMEM((8, 128), F32),
        ],
        compiler_params=pltpu.CompilerParams(vmem_limit_bytes=VMEM_LIMIT),
        cost_estimate=pl.CostEstimate(
            flops=steps * px * 512 * 1296 * 2, bytes_accessed=8 << 20, transcendentals=steps * px * 640
        ),
        name=f"forward_{base}",
    )(*operands)


def backward_kernel(geo, layer, base, steps, first_live, first, last, *refs):
    refs = list(refs)
    if not first:
        local, far = refs[:2]
        refs = refs[2:]
    gates, cprev, wb, wx, mrm, mrp, mcm, mcp = refs[:8]
    refs = refs[8:]
    if layer == 1:
        hnew, target, meta, head, head_b = refs[:5]
        refs = refs[5:]
    dz_out, sums_out, head_out, carry_out, send_out = refs[:5]
    dh, dc, dzb, peeps = refs[5:]
    rows, halo, own, back = geo.rows, geo.halo, geo.own, geo.back
    o0, on = halo * rows, own * rows
    step = pl.program_id(0)

    @pl.when(step == 0)
    def _():
        sums_out[...] = jnp.zeros_like(sums_out)
        head_out[...] = jnp.zeros_like(head_out)
        dzb[...] = jnp.zeros_like(dzb)
        for k, row in enumerate(peephole_rows(wx.shape[1] - CELL_COLS, wx)):
            peeps[k : k + 1, :] = row
        if first:
            dh[...] = jnp.zeros_like(dh)
            dc[...] = jnp.zeros_like(dc)
        else:
            nf = 2 * halo * rows
            dh[:nf, :] = far[:, :128].astype(F32)
            dc[:nf, :] = far[:, 128:].astype(F32)
            dh[nf:, :] = local[:, :128]
            dc[nf:, :] = local[:, 128:]

    if layer == 1:
        guess = dot_nt(head[...], hnew[0]) + head_b[...]
        a0 = (base + halo + 1) * rows
        err = guess - target[:, a0 : a0 + back * rows].astype(F32)
        dy = meta[pl.ds(first_live + steps - 1 - step, 1), a0 : a0 + back * rows] * err
        low = dy.astype(BF16)
        head_out[:, 0:128] += jnp.dot(low[:, o0 : o0 + on], hnew[0, o0 : o0 + on, :], preferred_element_type=F32)
        own_dy = low[:, o0 : o0 + on].astype(F32)
        head_out[:, 128:129] += jnp.sum(own_dy, 1, keepdims=True)
        head_out[:, 129:130] += jnp.sum((dy * err)[:, o0 : o0 + on], 1, keepdims=True)
        dh[...] += dot_tn(low, head[...])

    for c0, cw in cut(back, 4):
        r0, m = c0 * rows, cw * rows
        span = slice(r0, r0 + m)
        gi = gates[0, span, 0:128].astype(F32)
        gf = gates[0, span, 128:256].astype(F32)
        go = gates[0, span, 256:384].astype(F32)
        gg = gates[0, span, 384:512].astype(F32)
        c = cprev[0, span, :].astype(F32)
        cn = gf * c + gi * gg
        tc = jnp.tanh(cn)
        g = dh[span, :]
        d_o = g * tc * go * (1.0 - go)
        d_c = dc[span, :] + g * go * (1.0 - tc * tc) + d_o * peeps[2:3, :]
        d_i = d_c * gg * gi * (1.0 - gi)
        d_f = d_c * c * gf * (1.0 - gf)
        d_g = d_c * gi * (1.0 - gg * gg)
        dc[span, :] = d_c * gf + d_i * peeps[0:1, :] + d_f * peeps[1:2, :]
        p0 = rows + r0
        for n, d in enumerate((d_i, d_f, d_o, d_g)):
            dzb[p0 : p0 + m, n * 128 : (n + 1) * 128] = d.astype(BF16)
        a = max(r0, o0) - r0
        b = min(r0 + m, o0 + on) - r0
        if b > a:
            for n, d in enumerate((d_i, d_f, d_o, d_g, d_i * c, d_f * c, d_o * cn)):
                part = d[a:b].reshape((b - a) // 8, 8, 128)
                sums_out[n * 8 : (n + 1) * 8, :] += jnp.sum(part, 0)

    dz_out[0, :, :] = dzb[rows + o0 : rows + o0 + on, :]

    @pl.when(step < (steps - 1 if last else steps))
    def _():
        for c0, cw in cut(back, 4):
            r0, m = c0 * rows, cw * rows
            total = None
            g0 = (base + halo) * rows + r0
            for dr in range(3):
                parts = []
                for dc_i in range(3):
                    src = r0 - (dc_i - 1) * rows
                    v = dzb[rows + src : rows + src + m, :]
                    gm = g0 - (dc_i - 1) * rows
                    if dc_i == 0:
                        keep = mcm[gm : gm + m, :]
                    elif dc_i == 2:
                        keep = mcp[gm : gm + m, :]
                    if dc_i != 1:
                        v = v * jnp.concatenate([keep] * 4, 1)
                    parts.append(v)
                acc = jnp.dot(jnp.concatenate(parts, 1), wb[dr], preferred_element_type=F32)
                if dr == 0:
                    acc = acc * mrm[g0 : g0 + m, :].astype(F32)
                    acc = pltpu.roll(acc, m - 1, 0)
                elif dr == 2:
                    acc = acc * mrp[g0 : g0 + m, :].astype(F32)
                    acc = pltpu.roll(acc, 1, 0)
                total = acc if total is None else total + acc
            dh[r0 : r0 + m, :] = total

    @pl.when(step == steps - 1)
    def _():
        carry_out[:, :128] = dh[o0 : o0 + on, :]
        carry_out[:, 128:] = dc[o0 : o0 + on, :]
        ns = 2 * halo * rows
        s0 = o0 + on - ns
        send_out[:, :128] = dh[s0 : s0 + ns, :].astype(BF16)
        send_out[:, 128:] = dc[s0 : s0 + ns, :].astype(BF16)


def backward_call(geo, layer, base, steps, last, state, saved, wb, wx, masks, extra):
    rows, own, back, halo = geo.rows, geo.own, geo.back, geo.halo
    by_step = lambda *dims: pl.BlockSpec((1,) + dims, lambda t: (steps - 1 - t,) + (0,) * len(dims))
    first_live = saved["t"] - EIN
    operands = list(state) + [saved["gates"], saved["cprev"], wb, wx] + list(masks)
    in_specs = [whole(s.shape) for s in state]
    in_specs += [by_step(back * rows, 512), by_step(back * rows, 128)]
    in_specs += [whole(v.shape) for v in operands[len(state) + 2 :]]
    if layer == 1:
        win, meta, head, head_b = extra
        operands += [saved["hnew"], win, meta, head, head_b]
        t0 = saved["t"]
        in_specs += [
            by_step(back * rows, 128),
            pl.BlockSpec((head.shape[0], win.shape[1]), lambda t: (t0 + steps - 1 - t, 0)),
            whole(meta.shape),
            whole(head.shape),
            whole(head_b.shape),
        ]
    outs = [
        jax.ShapeDtypeStruct((steps, own * rows, 512), BF16),
        jax.ShapeDtypeStruct((56, 128), F32),
        jax.ShapeDtypeStruct((16, 256), F32),
        jax.ShapeDtypeStruct((own * rows, 256), F32),
        jax.ShapeDtypeStruct((2 * halo * rows, 256), BF16),
    ]
    out_specs = [by_step(own * rows, 512)] + [whole(o.shape) for o in outs[1:]]
    px = back * rows
    return pl.pallas_call(
        functools.partial(backward_kernel, geo, layer, base, steps, first_live, not state, last),
        grid=(steps,),
        in_specs=in_specs,
        out_specs=out_specs,
        out_shape=outs,
        scratch_shapes=[
            pltpu.VMEM((px, 128), F32),
            pltpu.VMEM((px, 128), F32),
            pltpu.VMEM((px + 2 * rows, 512), BF16),
            pltpu.VMEM((8, 128), F32),
        ],
        compiler_params=pltpu.CompilerParams(vmem_limit_bytes=VMEM_LIMIT),
        cost_estimate=pl.CostEstimate(
            flops=steps * px * 512 * 1536 * 2, bytes_accessed=8 << 20, transcendentals=steps * px * 128
        ),
        name=f"backward_{base}",
    )(*operands)


def weight_kernel(geo, base, steps, add, *refs):
    if add:
        acc, dz, hvar, xown, mcm, mcp, out, rhs = refs
    else:
        dz, hvar, xown, mcm, mcp, out, rhs = refs
    rows, own, halo = geo.rows, geo.own, geo.halo
    on = own * rows
    g0 = (base + 2 * halo) * rows
    wide = hvar.shape[-1]
    taps = [(dr, dc) for dr in range(3) for dc in range(3)]
    chans9 = xown.shape[1] - CELL_COLS
    inputs = None
    for j in range(steps):
        part = jnp.dot(xown[j], dz[j * on : (j + 1) * on, :], preferred_element_type=F32)
        inputs = part if inputs is None else inputs + part
    inputs = inputs.T[:, :chans9]
    if add:
        inputs = inputs + acc[:, 9 * wide :]
    out[:, 9 * wide :] = inputs
    for n in range(0, 9, 2):
        for k in range(min(2, 9 - n)):
            for j in range(steps):
                at = slice(j * on, (j + 1) * on)
                dr, dc = taps[n + k]
                v = hvar[j, dr, dc * rows : dc * rows + on, :]
                if dc == 0:
                    v = v * mcm[g0 : g0 + on, :]
                elif dc == 2:
                    v = v * mcp[g0 : g0 + on, :]
                rhs[at, k * wide : (k + 1) * wide] = v
        width = min(2, 9 - n) * wide
        lo = n * wide
        g = dot_tn(dz[...], rhs[:, :width])
        if add:
            g = g + acc[:, lo : lo + width]
        out[:, lo : lo + width] = g


def weight_call(geo, base, steps, acc, dz, hvar, xown, mcm, mcp):
    on = geo.own * geo.rows
    dz = dz.reshape(steps * on, 512)
    chans9 = xown.shape[1] - CELL_COLS
    operands = ([] if acc is None else [acc]) + [dz, hvar, xown, mcm, mcp]
    return pl.pallas_call(
        functools.partial(weight_kernel, geo, base, steps, acc is not None),
        out_shape=jax.ShapeDtypeStruct((512, 1152 + chans9), F32),
        scratch_shapes=[pltpu.VMEM((steps * on, 256), BF16)],
        compiler_params=pltpu.CompilerParams(vmem_limit_bytes=VMEM_LIMIT),
        cost_estimate=pl.CostEstimate(
            flops=steps * on * 512 * 1296 * 2, bytes_accessed=16 << 20, transcendentals=0
        ),
        name=f"weights_{base}",
    )(*operands)


def swap_pairs(size, bit):
    return [(i, i ^ bit) for i in range(size)]


def butterfly_bits(size):
    bits, bit = [], 1
    while bit < size:
        bits.append(bit)
        bit *= 2
    return bits


def gather_dp(piece, ranks):
    me = lax.axis_index("dp")
    for bit in butterfly_bits(ranks)[1:] + [1]:
        other = lax.ppermute(piece, "dp", swap_pairs(ranks, bit))
        high = (me & bit) != 0
        pair = jnp.stack([jnp.where(high, other, piece), jnp.where(high, piece, other)])
        if bit == 1:
            piece = jnp.swapaxes(pair, 0, 1).reshape((-1,) + piece.shape[1:])
        else:
            piece = pair.reshape((-1,) + piece.shape[1:])
    return piece


def scatter_sum_dp(whole_sum, ranks, small):
    me = lax.axis_index("dp")
    value = whole_sum
    bits = butterfly_bits(ranks)
    for n, bit in enumerate([1] + bits[:0:-1]):
        if bit == 1:
            halves = value.reshape((ranks // 2, 2) + value.shape[1:])
            low, high = halves[:, 0], halves[:, 1]
        else:
            half = value.shape[0] // 2
            low, high = value[:half], value[half:]
        mine_high = (me & bit) != 0
        send = jnp.where(mine_high, low, high).astype(BF16)
        keep = jnp.where(mine_high, high, low)
        pairs = swap_pairs(ranks, bit)
        value = keep + lax.ppermute(send, "dp", pairs).astype(F32)
        hi = small.astype(BF16)
        lo = (small - hi.astype(F32)).astype(BF16)
        got = lax.ppermute(jnp.stack([hi, lo]), "dp", pairs).astype(F32)
        small = small + (got[0] + got[1])
    return value[0], small


def on_device(
    frames,
    regions,
    valid,
    step_count,
    conv_w,
    cell_params,
    head_w,
    head_b,
    conv_mom,
    cell_mom,
    head_mom,
    bias_mom,
    conv_avg,
    cell_avg,
    head_avg,
    bias_avg,
):
    share = conv_w.shape[2]
    chans = frames.shape[1]
    pixels = frames.shape[2]
    wide = head_w.shape[1]
    groups = lax.axis_size("gate")
    ranks = lax.axis_size("dp")
    geo = Geometry(groups, pixels)
    rows, own, halo, front, back, union = geo.rows, geo.own, geo.halo, geo.front, geo.back, geo.union
    gate_at = lax.axis_index("gate")
    dp_at = lax.axis_index("dp")

    order = ring_order(groups)
    place = [order.index(g) for g in range(groups)]
    spot = jnp.asarray(place, jnp.int32)[gate_at]
    from_right = [(order[(i + 1) % groups], order[i]) for i in range(groups)]
    from_left = [(order[i], order[(i + 1) % groups]) for i in range(groups)]

    taps = conv_w.reshape(2, 4 * share, 9, chans + wide).astype(BF16)
    parts = [
        taps[..., chans:].reshape(2, 4 * share, 9 * wide),
        taps[..., :chans].reshape(2, 4 * share, 9 * chans),
    ]
    cells = jnp.stack([cell_params[:, :4], jnp.pad(cell_params[:, 4:], ((0, 0), (0, 1), (0, 0)))], -1)
    cell_hi = cells.astype(BF16)
    cells = cells - cell_hi.astype(F32)
    cell_mid = cells.astype(BF16)
    cell_lo = (cells - cell_mid.astype(F32)).astype(BF16)
    cell_parts = jnp.stack([cell_hi, cell_mid, cell_lo], -1).reshape(2, 4 * share, 6)
    parts.append(jnp.pad(cell_parts, ((0, 0), (0, 0), (0, CELL_COLS - 6))))
    packed = jnp.concatenate(parts, -1)
    slab = 4 * share // ranks
    packed_w = 9 * (wide + chans)
    sent_w = packed.shape[-1]
    mine = lax.dynamic_slice_in_dim(packed.reshape(2, ranks, slab, sent_w), dp_at, 1, 1)[:, 0]
    everyone = lax.all_to_all(
        jnp.broadcast_to(mine[None], (groups, 2, slab, sent_w)), "gate", 0, 0, tiled=True
    )
    gathered = gather_dp(everyone[None], ranks)
    full = gathered.transpose(2, 1, 0, 3, 4).reshape(2, groups, 4, share, sent_w)
    full = full.transpose(0, 2, 1, 3, 4).reshape(2, 4 * wide, sent_w)

    start = jnp.mod(spot * own - 2 * halo - 1, COLS).astype(jnp.int32).reshape(1)
    win, meta, mrm, mrp, mcm, mcp, counted = window_call(
        geo, start, frames.reshape(-1, pixels), valid, regions.reshape(1, pixels)
    )
    masks = (mrm, mrp, mcm, mcp)

    head_low = head_w.astype(BF16)
    head_bias = head_b[:, None]
    wh = [full[l, :, : 9 * wide] for l in range(2)]
    wx = [full[l, :, 9 * wide :] for l in range(2)]
    wb = [
        wh[l].reshape(4 * wide, 3, 3, wide).transpose(1, 2, 0, 3).reshape(3, 3 * 4 * wide, wide) for l in range(2)
    ]

    state = ()
    kept = []
    t = 0
    for n, (layer, steps) in enumerate(geo.calls):
        base = n * halo
        first_frame = t if layer == 0 else t - 1
        got = forward_call(geo, layer, base, first_frame, steps, state, win, meta, wh[layer], wx[layer], masks)
        kept.append(dict(gates=got[0], cprev=got[1], hvar=got[2], hnew=got[3], xown=got[4], t=t))
        out = got[5]
        t += steps
        if n + 1 < len(geo.calls):
            far = lax.ppermute(out[2 * halo * rows : 4 * halo * rows], "gate", from_right)
            state = (out, far)

    state = ()
    grads = [None, None]
    cell_sums = [jnp.zeros((56, 128), F32) for _ in range(2)]
    head_sums = jnp.zeros((16, 256), F32)
    for n in range(len(geo.calls) - 1, -1, -1):
        layer, steps = geo.calls[n]
        base = n * halo
        saved = kept[n]
        extra = None
        if layer == 1:
            extra = (win, meta, head_low, head_bias)
        got = backward_call(
            geo, layer, base, steps, n == 0, state, saved, wb[layer], wx[layer], masks, extra
        )
        if n > 0:
            far = lax.ppermute(got[4], "gate", from_left)
            state = (got[3], far)
        grads[layer] = weight_call(
            geo, base, steps, grads[layer], got[0], saved["hvar"], saved["xown"], masks[2], masks[3]
        )
        cell_sums[layer] = cell_sums[layer] + got[1]
        if layer == 1:
            head_sums = head_sums + got[2]

    cells = jnp.stack(cell_sums).reshape(2, 7, 8, wide).sum(2)
    loss_sum = jnp.sum(head_sums[:, 129])
    shared_small = jnp.concatenate(
        [head_sums[:, :128].reshape(-1), head_sums[:, 128], loss_sum[None], counted[0, :1]]
    )
    small = jnp.concatenate([cells.reshape(-1), shared_small])
    big = jnp.stack(grads).reshape(2, 4, groups, share, packed_w).transpose(2, 1, 3, 0, 4)
    big = big.reshape(groups, ranks, slab, 2, packed_w).transpose(1, 0, 2, 3, 4)
    part, small = scatter_sum_dp(big, ranks, small)
    ncell = 14 * wide
    for_gate = small[:ncell].reshape(14, groups, share).transpose(1, 0, 2).reshape(groups, 14 * share)
    to_gate = jnp.concatenate(
        [for_gate, jnp.broadcast_to(small[None, ncell:], (groups, small.shape[0] - ncell))], 1
    )
    hi = to_gate.astype(BF16)
    lo = (to_gate - hi.astype(F32)).astype(BF16)
    width = slab * 2 * packed_w
    message = jnp.concatenate([part.reshape(groups, width).astype(BF16), hi, lo], 1)
    got = lax.all_to_all(message, "gate", 0, 0, tiled=True).astype(F32)
    got = jnp.sum(got.reshape(groups, -1), 0)
    nsmall = to_gate.shape[1]
    small_sum = got[width : width + nsmall] + got[width + nsmall :]
    piece = got[:width].reshape(1, slab, 2, packed_w)
    rows_all = gather_dp(piece, ranks).reshape(4 * share, 2, packed_w).transpose(1, 0, 2)
    count = chans * small_sum[-1]
    scale = 2.0 / count
    rows_all = rows_all * scale
    grad_conv = jnp.concatenate(
        [
            rows_all[..., 9 * wide :].reshape(2, 4 * share, 9, chans),
            rows_all[..., : 9 * wide].reshape(2, 4 * share, 9, wide),
        ],
        -1,
    ).reshape(conv_w.shape)
    grad_cell = small_sum[: 14 * share].reshape(2, 7, share) * scale
    rest = small_sum[14 * share :]
    grad_head = rest[: chans * wide].reshape(chans, wide) * scale
    grad_bias = rest[chans * wide : chans * wide + chans] * scale
    loss = rest[chans * wide + chans] / count

    rate = RATE_SCALE * chans * jnp.sqrt(jnp.float32(EOUT * pixels * ranks))
    counts_done = step_count.astype(F32)
    outs = [loss]
    outs += nesterov(conv_w, grad_conv, conv_mom, conv_avg, counts_done[0], rate)
    outs += nesterov(cell_params, grad_cell, cell_mom, cell_avg, counts_done[1], rate)
    outs += nesterov(head_w, grad_head, head_mom, head_avg, counts_done[2], rate)
    outs += nesterov(head_b, grad_bias, bias_mom, bias_avg, counts_done[3], rate)
    return tuple(outs)


def solution(mesh):
    in_specs = (
        P(None, None, "dp"),
        P("dp"),
        P(None, "dp"),
        P(),
        P(None, None, "gate", None),
        P(None, None, "gate"),
        P(),
        P(),
        P(None, None, "gate", None),
        P(None, None, "gate"),
        P(),
        P(),
        P(None, None, "gate", None),
        P(None, None, "gate"),
        P(),
        P(),
    )
    out_specs = (
        P(),
        P(None, None, "gate", None),
        P(None, None, "gate", None),
        P(None, None, "gate", None),
        P(None, None, "gate", None),
        P(None, None, "gate"),
        P(None, None, "gate"),
        P(None, None, "gate"),
        P(None, None, "gate"),
        P(),
        P(),
        P(),
        P(),
        P(),
        P(),
        P(),
        P(),
    )
    return jax.shard_map(
        on_device, mesh=mesh, in_specs=in_specs, out_specs=out_specs, check_vma=False
    )
```

```python
import functools

import jax
import jax.numpy as jnp
from jax import lax
from jax.experimental import pallas as pl
from jax.experimental.pallas import tpu as pltpu
from jax.sharding import PartitionSpec as P

EIN = 5
EOUT = 15
COLS = 128

MU = 0.9
RATE_SCALE = 0.05
F32 = jnp.float32
BF16 = jnp.bfloat16
VMEM_LIMIT = 60 * 1024 * 1024


def ring_order(groups):
    wide = groups // 4
    if wide <= 1:
        return list(range(groups))
    order = [(z, 0) for z in range(4)]
    for z in range(3, -1, -1):
        ys = range(1, wide) if z % 2 else range(wide - 1, 0, -1)
        order += [(z, y) for y in ys]
    return [z * wide + y for z, y in order]


def split_steps(steps, most):
    calls = -(-steps // most)
    base, extra = divmod(steps, calls)
    return [base + (1 if i < extra else 0) for i in range(calls)]


def nesterov(param, grad, mom, avg, steps_done, rate):
    mom_new = MU * mom + grad
    param_new = param - rate * (grad + MU * mom_new)
    avg_new = avg + (param_new - avg) / (steps_done + 1.0)
    return [mom_new, avg_new, param_new, param_new.astype(BF16)]


def logistic(v):
    return 0.5 * jnp.tanh(0.5 * v) + 0.5


def dot_nt(a, b):
    return lax.dot_general(a, b, (((1,), (1,)), ((), ())), preferred_element_type=F32)


def dot_tn(a, b):
    return lax.dot_general(a, b, (((0,), (0,)), ((), ())), preferred_element_type=F32)


def cut(total, pieces):
    base, extra = divmod(total, pieces)
    spans, at = [], 0
    for i in range(pieces):
        size = base + (1 if i < extra else 0)
        spans.append((at, size))
        at += size
    return spans


def cut_by_four(total, pieces):
    spans, at = [], 0
    for i in range(pieces):
        left = pieces - i
        size = total - at if left == 1 else (total - at) // left // 4 * 4
        if size:
            spans.append((at, size))
        at += size
    return spans


class Geometry:
    def __init__(self, groups, pixels):
        self.rows = pixels // COLS
        self.own = COLS // groups
        self.halo = min(5, self.own // 2)
        self.calls = [(0, n) for n in split_steps(EIN, self.halo)] + [(1, n) for n in split_steps(EOUT, self.halo)]
        self.front = self.own + 4 * self.halo
        self.back = self.own + 2 * self.halo
        self.union = self.front + (len(self.calls) - 1) * self.halo
        self.window = -(-(self.union + 2) * self.rows // 256) * 256


TAPS = [(dr, dc) for dr in (-1, 0, 1) for dc in (-1, 0, 1)]
CELL_COLS = 16


def window_kernel(geo, start, frames, valid, regions, win, meta, mrm, mrp, mcm, mcp, count, lhs, pick):
    rows, own, halo, union, width = geo.rows, geo.own, geo.halo, geo.union, geo.window
    nf = frames.shape[0]
    nv = valid.shape[0]
    lhs[:nf, :] = frames[...]
    lhs[nf : nf + nv, :] = valid[...].astype(F32).astype(BF16)
    lhs[nf + nv : nf + nv + 1, :] = regions[...].astype(F32).astype(BF16)
    per = 256 // rows
    source = lax.broadcasted_iota(jnp.int32, (COLS, 256), 0)
    lane = lax.broadcasted_iota(jnp.int32, (COLS, 256), 1)
    lane_row = lax.broadcasted_iota(jnp.int32, (1, 256), 1) % rows

    def one(n, carry):
        column = (start[0] + n * per + lane // rows) % COLS
        hit = (source == column).astype(F32).astype(BF16)
        for r in range(rows):
            keep = (lane_row == r).astype(F32).astype(BF16)
            pick[r * COLS : (r + 1) * COLS, :] = hit * keep
        got = jnp.dot(lhs[...], pick[...], preferred_element_type=F32)
        at = pl.multiple_of(n * 256, 256)
        win[:, pl.ds(at, 256)] = got[:nf].astype(BF16)
        meta[:, pl.ds(at, 256)] = got[nf:]
        return carry

    lax.fori_loop(0, width // 256, one, 0)
    px = union * rows
    ids = meta[nv : nv + 1, :]
    bands = jnp.floor(ids * 0.5)
    here = ids[:, rows : rows + px]
    band_here = bands[:, rows : rows + px]
    picked = [
        ids[:, rows - 1 : rows - 1 + px] == here,
        ids[:, rows + 1 : rows + 1 + px] == here,
        bands[:, :px] == band_here,
        bands[:, 2 * rows : 2 * rows + px] == band_here,
    ]
    row_at = lax.broadcasted_iota(jnp.int32, (8, px), 0)
    stack = jnp.zeros((8, px), F32)
    for k, m in enumerate(picked):
        stack = jnp.where(row_at == k, jnp.broadcast_to(m.astype(F32), (8, px)), stack)
    stack = stack.astype(BF16)
    sel = lax.broadcasted_iota(jnp.int32, (8, 128), 0)
    for k, out in enumerate((mrm, mrp, mcm, mcp)):
        out[...] = dot_tn(stack, (sel == k).astype(F32).astype(BF16)).astype(BF16)
    a = (2 * halo + 1) * rows
    count[...] = jnp.broadcast_to(jnp.sum(meta[:nv, a : a + own * rows]), count.shape)


def window_call(geo, start, frames, valid, regions):
    nf, nv = frames.shape[0], valid.shape[0]
    pixels = frames.shape[1]
    px = geo.union * geo.rows
    smem = pl.BlockSpec(memory_space=pltpu.SMEM)
    vmem = pl.BlockSpec(memory_space=pltpu.VMEM)
    total = nf + nv + 1
    return pl.pallas_call(
        functools.partial(window_kernel, geo),
        in_specs=[smem, vmem, vmem, vmem],
        out_specs=[vmem] * 7,
        out_shape=[
            jax.ShapeDtypeStruct((nf, geo.window), BF16),
            jax.ShapeDtypeStruct((nv + 1, geo.window), F32),
        ]
        + [jax.ShapeDtypeStruct((px, 128), BF16)] * 4
        + [jax.ShapeDtypeStruct((8, 128), F32)],
        scratch_shapes=[pltpu.VMEM((total, pixels), BF16), pltpu.VMEM((pixels, 256), BF16)],
        compiler_params=pltpu.CompilerParams(vmem_limit_bytes=VMEM_LIMIT),
        cost_estimate=pl.CostEstimate(
            flops=2 * total * pixels * geo.window, bytes_accessed=10 << 20, transcendentals=0
        ),
        name="window",
    )(start, frames, valid, regions)


def pack_kernel(groups, rank, conv, cells, out0, out1):
    share, depth9 = conv.shape[2:]
    chans9 = out0.shape[-1] - CELL_COLS - 9 * 128
    chans = chans9 // 9
    depth = chans + 128
    row = lax.broadcasted_iota(jnp.int32, (7, CELL_COLS), 0)
    col = lax.broadcasted_iota(jnp.int32, (7, CELL_COLS), 1)
    half = (rank[0] & 1) * 2
    for l, at, gate, out in ((0, 0, rank[0], out0), (1, 0, half, out1), (1, share, half + 1, out1)):
        w = conv[l, gate].astype(BF16)
        parts = [w[:, k * depth + chans : (k + 1) * depth] for k in range(9)]
        parts += [w[:, k * depth : k * depth + chans] for k in range(9)]
        rest = cells[:, l, :]
        cols = jnp.zeros((share, CELL_COLS), F32)
        for k in range(3):
            low = rest.astype(BF16)
            rest = rest - low.astype(F32)
            sel = ((row == gate) & (col == k)) | ((row == gate + 4) & (col == 3 + k))
            cols = cols + dot_tn(low, sel.astype(F32).astype(BF16))
        parts.append(cols.astype(BF16))
        line = jnp.concatenate(parts, 1)
        for g in range(groups):
            out[g, at : at + share, :] = line


def pack_call(groups, rank, conv_w, cells, sent_w):
    share = conv_w.shape[2]
    return plain_call(
        functools.partial(pack_kernel, groups),
        "pack",
        [jax.ShapeDtypeStruct((groups, k * share, sent_w), BF16) for k in (1, 2)],
        rank,
        conv_w,
        cells,
        smem=1,
    )


def peephole_rows(wf):
    tail = wf[:, 9 * 128 :]
    depth = tail.shape[1]
    col = lax.broadcasted_iota(jnp.int32, (8, depth), 1)
    at = depth - CELL_COLS + 3
    sel = ((col >= at) & (col < at + 3)).astype(F32).astype(BF16)
    got = dot_nt(sel, tail)
    return [got[0:1, k * 128 : (k + 1) * 128] for k in range(3)]


def make_variants(geo, hn, hb, mrm, mrp, base):
    rows = geo.rows
    for c0, cw in cut(geo.front, 4):
        r0, m = c0 * rows, cw * rows
        h = hn[r0 : r0 + m, :]
        up = pltpu.roll(h, 1, 0)
        down = pltpu.roll(h, m - 1, 0)
        g0 = base * rows + r0
        hb[0, r0 : r0 + m, :] = up.astype(BF16) * mrm[g0 : g0 + m, :]
        hb[1, r0 : r0 + m, :] = h.astype(BF16)
        hb[2, r0 : r0 + m, :] = down.astype(BF16) * mrp[g0 : g0 + m, :]


def forward_kernel(geo, layer, base, steps, first, gather, *refs):
    refs = list(refs)
    if gather:
        rank, pieces, refs = refs[0], refs[1 : 1 + gather], refs[1 + gather :]
    if not first:
        near, far = refs[:2]
        refs = refs[2:]
    if gather:
        win, meta, mrm, mrp, mcm, mcp = refs[:6]
        wf = refs[13]
        refs = refs[6:13] + refs[14:]
    else:
        win, meta, wf, mrm, mrp, mcm, mcp = refs[:7]
        refs = refs[7:]
    gates_out, cprev_out, hvar_out, hnew_out, xown_out, state_out, send_out = refs[:7]
    hb, hn, cb, xs, keeps, peeps = refs[7:]
    rows, halo, own, front, back = geo.rows, geo.halo, geo.own, geo.front, geo.back
    chans = win.shape[0]
    chans9 = 9 * chans
    lanes = (front - 2) * rows
    x0 = (base + 2) * rows
    step = pl.program_id(0)

    @pl.when(step == 0)
    def _():
        if first:
            hn[...] = jnp.zeros_like(hn)
            cb[...] = jnp.zeros_like(cb)
        else:
            nb = back * rows
            hn[:nb, :] = near[:, :128].astype(F32)
            hn[nb:, :] = far[:, :128].astype(F32)
            cb[:nb, :] = near[:, 128:].astype(F32)
            cb[nb:, :] = far[:, 128:].astype(F32)
        make_variants(geo, hn, hb, mrm, mrp, base)
        if gather:
            for k, piece in enumerate(pieces):
                if gather == 4:
                    wf[pl.ds(pl.multiple_of((rank[0] ^ k) * 128, 128), 128), :] = piece[...]
                    continue
                peers, span = piece.shape[0], piece.shape[1] // 2
                half = pl.multiple_of(((rank[0] ^ k) & 1) * 256, 256)
                for g in range(peers):
                    for j in range(2):
                        at = pl.multiple_of(half + j * 128 + g * span, span)
                        wf[pl.ds(at, span), :] = piece[g, j * span : (j + 1) * span, :]
        ids = meta[meta.shape[0] - 1 :, :]
        here = ids[:, x0 : x0 + lanes]
        for tap, (dr, dc) in enumerate(TAPS):
            off = x0 + dc * rows + dr
            same = (ids[:, off : off + lanes] == here).astype(F32)
            keeps[tap * chans : (tap + 1) * chans, :] = jnp.broadcast_to(same, (chans, lanes)).astype(BF16)
        ones = lax.broadcasted_iota(jnp.int32, (CELL_COLS, lanes), 0) < 3
        xs[chans9:, :] = ones.astype(F32).astype(BF16)
        for k, row in enumerate(peephole_rows(wf)):
            peeps[k : k + 1, :] = row

    s0, sn = (2 * halo - 1) * rows, (own + 2) * rows
    for v in range(3):
        hvar_out[0, v, :, :] = hb[v, s0 : s0 + sn, :]
    cprev_out[0, :, :] = cb[halo * rows : (halo + back) * rows, :].astype(BF16)
    for tap, (dr, dc) in enumerate(TAPS):
        off = x0 + dc * rows + dr
        part = slice(tap * chans, (tap + 1) * chans)
        xs[part, :] = win[:, off : off + lanes] * keeps[part, :]
    q0 = (2 * halo - 1) * rows
    xown_out[0, :, :] = xs[:, q0 : q0 + own * rows]

    for c0, cw in cut_by_four(front - 2, 4):
        r0, m = (c0 + 1) * rows, cw * rows
        g0 = base * rows + r0
        parts = []
        for dr in range(3):
            left = hb[dr, r0 - rows : r0 - rows + m, :] * mcm[g0 : g0 + m, :]
            mid = hb[dr, r0 : r0 + m, :]
            right = hb[dr, r0 + rows : r0 + rows + m, :] * mcp[g0 : g0 + m, :]
            parts += [left, mid, right]
        z = dot_nt(jnp.concatenate(parts, 1), wf[:, : 9 * 128]) + lax.dot_general(
            xs[:, r0 - rows : r0 - rows + m], wf[:, 9 * 128 :], (((0,), (1,)), ((), ())), preferred_element_type=F32
        )
        c = cb[r0 : r0 + m, :]
        gi = logistic(z[:, 0:128] + peeps[0:1, :] * c)
        gf = logistic(z[:, 128:256] + peeps[1:2, :] * c)
        gg = jnp.tanh(z[:, 384:512])
        cn = gf * c + gi * gg
        go = logistic(z[:, 256:384] + peeps[2:3, :] * cn)
        h = go * jnp.tanh(cn)
        cb[r0 : r0 + m, :] = cn
        hn[r0 : r0 + m, :] = h.astype(BF16).astype(F32)
        lo, hi = max(c0 + 1, halo), min(c0 + 1 + cw, halo + back)
        a, b = (lo - c0 - 1) * rows, (hi - c0 - 1) * rows
        o = (lo - halo) * rows
        n = b - a
        if n > 0:
            gates_out[0, o : o + n, 0:128] = gi[a:b].astype(BF16)
            gates_out[0, o : o + n, 128:256] = gf[a:b].astype(BF16)
            gates_out[0, o : o + n, 256:384] = go[a:b].astype(BF16)
            gates_out[0, o : o + n, 384:512] = gg[a:b].astype(BF16)
            hnew_out[0, o : o + n, :] = h[a:b].astype(BF16)

    make_variants(geo, hn, hb, mrm, mrp, base)

    @pl.when(step == steps - 1)
    def _():
        a, b = halo * rows, (halo + back) * rows
        state_out[:, :128] = hn[a:b, :].astype(BF16)
        state_out[:, 128:] = cb[a:b, :].astype(BF16)
        a, b = 3 * halo * rows, 5 * halo * rows
        send_out[:, :128] = hn[a:b, :].astype(BF16)
        send_out[:, 128:] = cb[a:b, :].astype(BF16)


def whole(shape):
    return pl.BlockSpec(shape, lambda *_: (0,) * len(shape))


def forward_call(geo, layer, base, first_frame, steps, state, win, meta, weights, masks):
    rows, own, front, back = geo.rows, geo.own, geo.front, geo.back
    chans = win.shape[0] // (EIN + EOUT)
    gather = len(weights) - 1 if isinstance(weights, tuple) else 0
    sent_w = weights[1].shape[-1] if gather else weights.shape[1]
    depth = sent_w - 9 * 128
    by_step = lambda *dims: pl.BlockSpec((1,) + dims, lambda t: (t,) + (0,) * len(dims))
    lead = list(weights) if gather else []
    operands = lead + list(state) + [win, meta] + ([] if gather else [weights]) + list(masks)
    in_specs = [pl.BlockSpec(memory_space=pltpu.SMEM)] if gather else []
    in_specs += [whole(v.shape) for v in lead[1:]]
    in_specs += [whole(s.shape) for s in state]
    in_specs += [pl.BlockSpec((chans, win.shape[1]), lambda t: (first_frame + t, 0))]
    in_specs += [whole(v.shape) for v in operands[len(lead) + len(state) + 1 :]]
    shapes = [
        (steps, back * rows, 512),
        (steps, back * rows, 128),
        (steps, 3, (own + 2) * rows, 128),
        (steps, back * rows, 128),
        (steps, depth, own * rows),
    ]
    flat = [(back * rows, 256), (2 * geo.halo * rows, 256)] + ([(512, sent_w)] if gather else [])
    outs = [jax.ShapeDtypeStruct(s, BF16) for s in shapes + flat]
    out_specs = [by_step(*s[1:]) for s in shapes] + [whole(s) for s in flat]
    px = front * rows
    return pl.pallas_call(
        functools.partial(forward_kernel, geo, layer, base, steps, not state, gather),
        grid=(steps,),
        in_specs=in_specs,
        out_specs=out_specs,
        out_shape=outs,
        scratch_shapes=[
            pltpu.VMEM((3, px, 128), BF16),
            pltpu.VMEM((px, 128), F32),
            pltpu.VMEM((px, 128), F32),
            pltpu.VMEM((depth, px - 2 * rows), BF16),
            pltpu.VMEM((9 * chans, px - 2 * rows), BF16),
            pltpu.VMEM((8, 128), F32),
        ],
        compiler_params=pltpu.CompilerParams(vmem_limit_bytes=VMEM_LIMIT),
        cost_estimate=pl.CostEstimate(
            flops=steps * px * 512 * 1296 * 2, bytes_accessed=8 << 20, transcendentals=steps * px * 640
        ),
        name=f"forward_{base}",
    )(*operands)


def backward_kernel(geo, layer, base, steps, first_live, first, last, carried, *refs):
    refs = list(refs)
    if carried:
        sums_in, head_in = refs[:2]
        refs = refs[2:]
    if not first:
        local, far = refs[:2]
        refs = refs[2:]
    gates, cprev, wf, mrm, mrp, mcm, mcp = refs[:7]
    refs = refs[7:]
    if layer == 1:
        hnew, target, meta, head, head_b = refs[:5]
        refs = refs[5:]
    dz_out, sums_out, head_out, carry_out, send_out = refs[:5]
    dh, dc, dzb, peeps, wb = refs[5:]
    rows, halo, own, back = geo.rows, geo.halo, geo.own, geo.back
    o0, on = halo * rows, own * rows
    step = pl.program_id(0)

    @pl.when(step == 0)
    def _():
        sums_out[...] = sums_in[...] if carried else jnp.zeros_like(sums_out)
        head_out[...] = head_in[...] if carried else jnp.zeros_like(head_out)
        for tap in range(9):
            wb[tap // 3, tap % 3 * 512 : (tap % 3 + 1) * 512, :] = wf[:, tap * 128 : (tap + 1) * 128]
        dzb[...] = jnp.zeros_like(dzb)
        for k, row in enumerate(peephole_rows(wf)):
            peeps[k : k + 1, :] = row
        if first:
            dh[...] = jnp.zeros_like(dh)
            dc[...] = jnp.zeros_like(dc)
        else:
            nf = 2 * halo * rows
            dh[:nf, :] = far[:, :128].astype(F32)
            dc[:nf, :] = far[:, 128:].astype(F32)
            dh[nf:, :] = local[:, :128]
            dc[nf:, :] = local[:, 128:]

    if layer == 1:
        guess = dot_nt(head[...], hnew[0]) + head_b[...]
        a0 = (base + halo + 1) * rows
        err = guess - target[:, a0 : a0 + back * rows].astype(F32)
        dy = meta[pl.ds(first_live + steps - 1 - step, 1), a0 : a0 + back * rows] * err
        low = dy.astype(BF16)
        head_out[:, 0:128] += jnp.dot(low[:, o0 : o0 + on], hnew[0, o0 : o0 + on, :], preferred_element_type=F32)
        own_dy = low[:, o0 : o0 + on].astype(F32)
        head_out[:, 128:129] += jnp.sum(own_dy, 1, keepdims=True)
        head_out[:, 129:130] += jnp.sum((dy * err)[:, o0 : o0 + on], 1, keepdims=True)
        dh[...] += dot_tn(low, head[...])

    for c0, cw in cut(back, 4):
        r0, m = c0 * rows, cw * rows
        span = slice(r0, r0 + m)
        gi = gates[0, span, 0:128].astype(F32)
        gf = gates[0, span, 128:256].astype(F32)
        go = gates[0, span, 256:384].astype(F32)
        gg = gates[0, span, 384:512].astype(F32)
        c = cprev[0, span, :].astype(F32)
        cn = gf * c + gi * gg
        tc = jnp.tanh(cn)
        g = dh[span, :]
        d_o = g * tc * go * (1.0 - go)
        d_c = dc[span, :] + g * go * (1.0 - tc * tc) + d_o * peeps[2:3, :]
        d_i = d_c * gg * gi * (1.0 - gi)
        d_f = d_c * c * gf * (1.0 - gf)
        d_g = d_c * gi * (1.0 - gg * gg)
        dc[span, :] = d_c * gf + d_i * peeps[0:1, :] + d_f * peeps[1:2, :]
        p0 = rows + r0
        for n, d in enumerate((d_i, d_f, d_o, d_g)):
            dzb[p0 : p0 + m, n * 128 : (n + 1) * 128] = d.astype(BF16)
        a = max(r0, o0) - r0
        b = min(r0 + m, o0 + on) - r0
        if b > a:
            for n, d in enumerate((d_i, d_f, d_o, d_g, d_i * c, d_f * c, d_o * cn)):
                part = d[a:b].reshape((b - a) // 8, 8, 128)
                sums_out[n * 8 : (n + 1) * 8, :] += jnp.sum(part, 0)

    dz_out[0, :, :] = dzb[rows + o0 : rows + o0 + on, :]

    @pl.when(step < (steps - 1 if last else steps))
    def _():
        for c0, cw in cut(back, 4):
            r0, m = c0 * rows, cw * rows
            total = None
            g0 = (base + halo) * rows + r0
            for dr in range(3):
                parts = []
                for dc_i in range(3):
                    src = r0 - (dc_i - 1) * rows
                    v = dzb[rows + src : rows + src + m, :]
                    gm = g0 - (dc_i - 1) * rows
                    if dc_i == 0:
                        keep = mcm[gm : gm + m, :]
                    elif dc_i == 2:
                        keep = mcp[gm : gm + m, :]
                    if dc_i != 1:
                        v = v * jnp.concatenate([keep] * 4, 1)
                    parts.append(v)
                acc = jnp.dot(jnp.concatenate(parts, 1), wb[dr], preferred_element_type=F32)
                if dr == 0:
                    acc = acc * mrm[g0 : g0 + m, :].astype(F32)
                    acc = pltpu.roll(acc, m - 1, 0)
                elif dr == 2:
                    acc = acc * mrp[g0 : g0 + m, :].astype(F32)
                    acc = pltpu.roll(acc, 1, 0)
                total = acc if total is None else total + acc
            dh[r0 : r0 + m, :] = total

    @pl.when(step == steps - 1)
    def _():
        carry_out[:, :128] = dh[o0 : o0 + on, :]
        carry_out[:, 128:] = dc[o0 : o0 + on, :]
        ns = 2 * halo * rows
        s0 = o0 + on - ns
        send_out[:, :128] = dh[s0 : s0 + ns, :].astype(BF16)
        send_out[:, 128:] = dc[s0 : s0 + ns, :].astype(BF16)


def backward_call(geo, layer, base, steps, last, carried, state, saved, wf, masks, extra):
    rows, own, back, halo = geo.rows, geo.own, geo.back, geo.halo
    by_step = lambda *dims: pl.BlockSpec((1,) + dims, lambda t: (steps - 1 - t,) + (0,) * len(dims))
    first_live = saved["t"] - EIN
    lead = list(carried) + list(state)
    operands = lead + [saved["gates"], saved["cprev"], wf] + list(masks)
    in_specs = [whole(s.shape) for s in lead]
    in_specs += [by_step(back * rows, 512), by_step(back * rows, 128)]
    in_specs += [whole(v.shape) for v in operands[len(lead) + 2 :]]
    if layer == 1:
        win, meta, head, head_b = extra
        operands += [saved["hnew"], win, meta, head, head_b]
        t0 = saved["t"]
        in_specs += [
            by_step(back * rows, 128),
            pl.BlockSpec((head.shape[0], win.shape[1]), lambda t: (t0 + steps - 1 - t, 0)),
            whole(meta.shape),
            whole(head.shape),
            whole(head_b.shape),
        ]
    outs = [
        jax.ShapeDtypeStruct((steps, own * rows, 512), BF16),
        jax.ShapeDtypeStruct((56, 128), F32),
        jax.ShapeDtypeStruct((16, 256), F32),
        jax.ShapeDtypeStruct((own * rows, 256), F32),
        jax.ShapeDtypeStruct((2 * halo * rows, 256), BF16),
    ]
    out_specs = [by_step(own * rows, 512)] + [whole(o.shape) for o in outs[1:]]
    px = back * rows
    return pl.pallas_call(
        functools.partial(backward_kernel, geo, layer, base, steps, first_live, not state, last, bool(carried)),
        grid=(steps,),
        in_specs=in_specs,
        out_specs=out_specs,
        out_shape=outs,
        scratch_shapes=[
            pltpu.VMEM((px, 128), F32),
            pltpu.VMEM((px, 128), F32),
            pltpu.VMEM((px + 2 * rows, 512), BF16),
            pltpu.VMEM((8, 128), F32),
            pltpu.VMEM((3, 3 * 512, 128), BF16),
        ],
        compiler_params=pltpu.CompilerParams(vmem_limit_bytes=VMEM_LIMIT),
        cost_estimate=pl.CostEstimate(
            flops=steps * px * 512 * 1536 * 2, bytes_accessed=8 << 20, transcendentals=steps * px * 128
        ),
        name=f"backward_{base}",
    )(*operands)


def split_low(v):
    hi = v.astype(BF16)
    return jnp.concatenate([hi, (v - hi.astype(F32)).astype(BF16)], 1)


def joined(v):
    half = v.shape[-1] // 2
    return v[..., :half].astype(F32) + v[..., half:].astype(F32)


def weight_kernel(geo, base, steps, add, final, small, *refs):
    refs = list(refs)
    if final:
        rank, refs = refs[0], refs[1:]
    if add:
        acc, refs = refs[0], refs[1:]
    if small:
        sums0, sums1, head, count = refs[:4]
        refs = refs[4:]
    dz, hvar, xown, mcm, mcp = refs[:5]
    refs = refs[5:]
    rows, own, halo = geo.rows, geo.own, geo.halo
    on = own * rows
    g0 = (base + 2 * halo) * rows
    wide = hvar.shape[-1]
    taps = [(dr, dc) for dr in range(3) for dc in range(3)]
    rhs = refs[-1]
    if final:
        odd = (rank[0] & 1) == 1

    def put(lo, width, g):
        if add:
            g = g + acc[:, lo : lo + width]
        if not final:
            refs[0][:, lo : lo + width] = g
            return
        keep, send = refs[:2]
        for j in range(2):
            even_gate = g[2 * j * wide : (2 * j + 1) * wide]
            odd_gate = g[(2 * j + 1) * wide : (2 * j + 2) * wide]
            keep[j, :, lo : lo + width] = jnp.where(odd, odd_gate, even_gate)
            send[j * wide : (j + 1) * wide, lo : lo + width] = jnp.where(odd, even_gate, odd_gate).astype(BF16)

    chans9 = xown.shape[1] - CELL_COLS
    inputs = None
    for j in range(steps):
        part = jnp.dot(xown[j], dz[j * on : (j + 1) * on, :], preferred_element_type=F32)
        inputs = part if inputs is None else inputs + part
    put(9 * wide, chans9, inputs.T[:, :chans9])
    for n in range(0, 9, 2):
        for k in range(min(2, 9 - n)):
            for j in range(steps):
                at = slice(j * on, (j + 1) * on)
                dr, dc = taps[n + k]
                v = hvar[j, dr, dc * rows : dc * rows + on, :]
                if dc == 0:
                    v = v * mcm[g0 : g0 + on, :]
                elif dc == 2:
                    v = v * mcp[g0 : g0 + on, :]
                rhs[at, k * wide : (k + 1) * wide] = v
        width = min(2, 9 - n) * wide
        put(n * wide, width, dot_tn(dz[...], rhs[:, :width]))
    if final:
        refs[1][2 * wide :, :] = jnp.zeros((16, refs[1].shape[1]), BF16)
    if small:
        few = jnp.concatenate(
            [jnp.sum(v[...].reshape(7, 8, wide), 1) for v in (sums0, sums1)] + [jnp.zeros((2, wide), F32)], 0
        )
        col = lax.broadcasted_iota(jnp.int32, (16, wide), 1)
        extra = jnp.where(col == 2, jnp.broadcast_to(count[0:1, :], (16, wide)), head[:, wide:])
        few = jnp.concatenate([few, head[:, :wide], extra], 1)
        refs[2][...] = few
        refs[1][2 * wide :, : 6 * wide] = split_low(few)


def weight_call(geo, base, steps, acc, dz, hvar, xown, mcm, mcp, rank=None, small=()):
    on = geo.own * geo.rows
    dz = dz.reshape(steps * on, 512)
    chans9 = xown.shape[1] - CELL_COLS
    width = 1152 + chans9
    final = rank is not None
    operands = ([rank] if final else []) + ([] if acc is None else [acc]) + list(small) + [dz, hvar, xown, mcm, mcp]
    in_specs = [pl.BlockSpec(memory_space=pltpu.VMEM)] * len(operands)
    if final:
        in_specs[0] = pl.BlockSpec(memory_space=pltpu.SMEM)
        out_shape = [
            jax.ShapeDtypeStruct((2, 128, width), F32),
            jax.ShapeDtypeStruct((256 + 16, width), BF16),
        ]
        if small:
            out_shape.append(jax.ShapeDtypeStruct((16, 384), F32))
    else:
        out_shape = jax.ShapeDtypeStruct((512, width), F32)
    return pl.pallas_call(
        functools.partial(weight_kernel, geo, base, steps, acc is not None, final, bool(small)),
        in_specs=in_specs,
        out_shape=out_shape,
        scratch_shapes=[pltpu.VMEM((steps * on, 256), BF16)],
        compiler_params=pltpu.CompilerParams(vmem_limit_bytes=VMEM_LIMIT),
        cost_estimate=pl.CostEstimate(
            flops=steps * on * 512 * 1296 * 2, bytes_accessed=16 << 20, transcendentals=0
        ),
        name=f"weights_{base}",
    )(*operands)


SMALL_AT = 1408


def core_stage_kernel(rank, keep, got, *refs):
    wide = keep.shape[1]
    high = (rank[0] & 2) == 2
    small = len(refs) > 2
    if small:
        few, keep_out, send_out, few_out = refs
    else:
        keep_out, send_out = refs
    a = keep[0] + got[:wide, :].astype(F32)
    b = keep[1] + got[wide : 2 * wide, :].astype(F32)
    keep_out[...] = jnp.where(high, b, a)
    send_out[:wide, :] = jnp.where(high, a, b).astype(BF16)
    if small:
        total = few[...] + joined(got[2 * wide :, : 6 * wide])
        few_out[...] = total
        send_out[wide:, :] = jnp.zeros((16, send_out.shape[1]), BF16)
        send_out[wide:, : 6 * wide] = split_low(total)


def chip_stage_kernel(groups, keep, got, *refs):
    wide, width = keep.shape
    small = len(refs) > 1
    if small:
        few, out = refs
    else:
        (out,) = refs
    share = wide // groups
    total = (keep[...] + got[:wide, :].astype(F32)).astype(BF16)
    if small:
        sums = few[...] + joined(got[wide:, : 6 * wide])
        head = split_low(sums[:, wide : 2 * wide])
        extra = split_low(sums[:, 2 * wide : 2 * wide + 16])
        fill = jnp.zeros((16, SMALL_AT - width - 2 * share - 32), BF16)
    for g in range(groups):
        part = total[g * share : (g + 1) * share, :]
        if not small:
            out[g, :, :] = part
        else:
            cells = split_low(sums[:, g * share : (g + 1) * share])
            out[g, :, :] = jnp.concatenate([part, cells, extra, fill, head], 1)


def sum_stage_kernel(got, out):
    total = got[0].astype(F32)
    for g in range(1, got.shape[0]):
        total = total + got[g].astype(F32)
    out[...] = total


def finish_kernel(rate, chans, got, steps_done, *refs):
    (cell_refs, head_refs, bias_refs), refs = (refs[:3], refs[3:6], refs[6:9]), refs[9:]
    shard, scalars, loss, cell_outs, head_outs, bias_outs = refs[0], refs[1], refs[2], refs[3:7], refs[7:11], refs[11:]
    total = got[0].astype(F32)
    for g in range(1, got.shape[0]):
        total = total + got[g].astype(F32)
    width = shard.shape[1]
    share = total.shape[0]
    shard[...] = total[:, :width]
    cells = total[:, width : width + share] + total[:, width + share : width + 2 * share]
    at = width + 2 * share
    extra = total[:, at : at + 16] + total[:, at + 16 : at + 32]
    head = total[:, SMALL_AT : SMALL_AT + 128] + total[:, SMALL_AT + 128 :]
    count = chans * extra[0:1, 2:3]
    scale = 2.0 / count
    fresh = [1.0 / (jnp.full((1, 1), steps_done[k].astype(F32)) + 1.0) for k in range(4)]
    loss[...] = jnp.sum(extra[:, 1:2], 0, keepdims=True) / count
    lane = lax.broadcasted_iota(jnp.int32, (8, 128), 1)
    scalars[...] = jnp.where(lane == 0, scale, jnp.where(lane == 1, rate, fresh[0]))

    def update(refs, outs, at, grad, fresh):
        param, mom, avg = (v[at] for v in refs)
        grad = grad * scale
        m = MU * mom + grad
        p = param - rate * (grad + MU * m)
        outs[0][at] = m
        outs[1][at] = avg + (p - avg) * fresh
        outs[2][at] = p
        outs[3][at] = p.astype(BF16)

    for l in range(2):
        update(cell_refs, cell_outs, (slice(None), l, slice(None)), cells[l * 7 : (l + 1) * 7, :], fresh[1])
    update(head_refs, head_outs, (slice(None), slice(None)), head, fresh[2])
    row = lax.broadcasted_iota(jnp.int32, (16, 16), 0)
    col = lax.broadcasted_iota(jnp.int32, (16, 16), 1)
    bias = jnp.sum(jnp.where(row == col, jnp.broadcast_to(extra[:, 0:1], (16, 16)), 0.0), 0, keepdims=True)
    update(bias_refs, bias_outs, (slice(None), slice(None)), bias, fresh[3])


def plain_call(kernel, name, out_shape, *operands, smem=0, moved=4 << 20, smem_at=()):
    where = [pltpu.SMEM if i < smem or i in smem_at else pltpu.VMEM for i in range(len(operands))]
    specs = [pl.BlockSpec(memory_space=m) for m in where]
    return pl.pallas_call(
        kernel,
        in_specs=specs,
        out_shape=out_shape,
        compiler_params=pltpu.CompilerParams(vmem_limit_bytes=VMEM_LIMIT),
        cost_estimate=pl.CostEstimate(flops=1 << 20, bytes_accessed=moved, transcendentals=0),
        name=name,
    )(*operands)


def core_stage(name, rank, keep, got, small):
    wide, width = keep.shape[1:]
    more = 16 if small else 0
    shapes = [jax.ShapeDtypeStruct((wide, width), F32), jax.ShapeDtypeStruct((wide + more, width), BF16)]
    shapes += [jax.ShapeDtypeStruct(v.shape, F32) for v in small]
    return plain_call(core_stage_kernel, "core_stage_" + name, shapes, rank, keep, got, *small, smem=1)


def chip_stage(name, groups, keep, got, small):
    wide, width = keep.shape
    lanes = SMALL_AT + 256 if small else width
    shape = jax.ShapeDtypeStruct((groups, wide // groups, lanes), BF16)
    kernel = functools.partial(chip_stage_kernel, groups)
    return plain_call(kernel, "chip_stage_" + name, shape, keep, got, *small, moved=2 << 20)


def sum_stage(name, got):
    shape = jax.ShapeDtypeStruct(got.shape[1:], F32)
    return plain_call(sum_stage_kernel, "sum_stage_" + name, shape, got, moved=1 << 20)


def finish_stage(rate, chans, width, got, step_count, small_args):
    shapes = [
        jax.ShapeDtypeStruct((got.shape[1], width), F32),
        jax.ShapeDtypeStruct((8, 128), F32),
        jax.ShapeDtypeStruct((1, 1), F32),
    ]
    for v in small_args[::3]:
        shapes += [jax.ShapeDtypeStruct(v.shape, F32)] * 3 + [jax.ShapeDtypeStruct(v.shape, BF16)]
    kernel = functools.partial(finish_kernel, rate, chans)
    return plain_call(kernel, "finish", shapes, got, step_count, *small_args, moved=1 << 20, smem_at=(1,))


def update_kernel(rank, scalars, *refs):
    pieces = (refs[:4], refs[4:8])
    param, mom, avg, mom_out, avg_out, new_out, low_out, grad = refs[8:]
    layer = pl.program_id(0)
    chans = (grad.shape[-1] - 9 * 128) // 9
    scale, rate, fresh = (scalars[0:1, k : k + 1] for k in range(3))
    for l in range(2):

        @pl.when(layer == l)
        def _():
            for k, piece in enumerate(pieces[l]):
                v = piece[...]
                parts = []
                for tap in range(9):
                    parts.append(v[:, 9 * 128 + tap * chans : 9 * 128 + (tap + 1) * chans])
                    parts.append(v[:, tap * 128 : (tap + 1) * 128])
                grad[rank[0] ^ k] = jnp.concatenate(parts, 1) * scale

    g = grad[...]
    m = MU * mom[0] + g
    p = param[0] - rate * (g + MU * m)
    mom_out[0] = m
    new_out[0] = p
    low_out[0] = p.astype(BF16)
    avg_out[0] = avg[0] + (p - avg[0]) * fresh


def update_call(rank, scalars, pieces, param, mom, avg):
    layers, gates, share, width = param.shape
    block = pl.BlockSpec((1, gates, share, width), lambda l: (l, 0, 0, 0))
    smem = pl.BlockSpec(memory_space=pltpu.SMEM)
    shape = jax.ShapeDtypeStruct(param.shape, F32)
    return pl.pallas_call(
        update_kernel,
        grid=(layers,),
        in_specs=[smem, whole(scalars.shape)] + [whole(v.shape) for v in pieces] + [block] * 3,
        out_specs=[block] * 4,
        out_shape=[shape] * 3 + [jax.ShapeDtypeStruct(param.shape, BF16)],
        scratch_shapes=[pltpu.VMEM((gates, share, width), F32)],
        compiler_params=pltpu.CompilerParams(vmem_limit_bytes=VMEM_LIMIT),
        cost_estimate=pl.CostEstimate(flops=1 << 20, bytes_accessed=6 << 20, transcendentals=0),
        name="update",
    )(rank, scalars, *pieces, param, mom, avg)


def swap_pairs(size, bit):
    return [(i, i ^ bit) for i in range(size)]


def butterfly_bits(size):
    bits, bit = [], 1
    while bit < size:
        bits.append(bit)
        bit *= 2
    return bits


def gather_dp(piece, ranks):
    me = lax.axis_index("dp")
    for bit in butterfly_bits(ranks)[1:] + [1]:
        other = lax.ppermute(piece, "dp", swap_pairs(ranks, bit))
        high = (me & bit) != 0
        pair = jnp.stack([jnp.where(high, other, piece), jnp.where(high, piece, other)])
        if bit == 1:
            piece = jnp.swapaxes(pair, 0, 1).reshape((-1,) + piece.shape[1:])
        else:
            piece = pair.reshape((-1,) + piece.shape[1:])
    return piece


def scatter_sum_dp(whole_sum, ranks, small):
    me = lax.axis_index("dp")
    value = whole_sum
    bits = butterfly_bits(ranks)
    for n, bit in enumerate([1] + bits[:0:-1]):
        if bit == 1:
            halves = value.reshape((ranks // 2, 2) + value.shape[1:])
            low, high = halves[:, 0], halves[:, 1]
        else:
            half = value.shape[0] // 2
            low, high = value[:half], value[half:]
        mine_high = (me & bit) != 0
        send = jnp.where(mine_high, low, high).astype(BF16)
        keep = jnp.where(mine_high, high, low)
        pairs = swap_pairs(ranks, bit)
        value = keep + lax.ppermute(send, "dp", pairs).astype(F32)
        hi = lax.reduce_precision(small, 8, 7)
        got = lax.ppermute(jnp.stack([hi, small - hi]).astype(BF16), "dp", pairs).astype(F32)
        small = small + (got[0] + got[1])
    return value[0], small


def gathered_weights(conv_w, cell_params, dp_at, groups, ranks, chans):
    share = conv_w.shape[2]
    wide = share * groups
    taps = conv_w.reshape(2, 4 * share, 9, chans + wide).astype(BF16)
    parts = [
        taps[..., chans:].reshape(2, 4 * share, 9 * wide),
        taps[..., :chans].reshape(2, 4 * share, 9 * chans),
    ]
    cells = jnp.stack([cell_params[:, :4], jnp.pad(cell_params[:, 4:], ((0, 0), (0, 1), (0, 0)))], -1)
    cell_hi = lax.reduce_precision(cells, 8, 7)
    cell_mid = lax.reduce_precision(cells - cell_hi, 8, 7)
    cell_lo = cells - cell_hi - cell_mid
    cell_parts = jnp.stack([cell_hi, cell_mid, cell_lo], -1).astype(BF16).reshape(2, 4 * share, 6)
    parts.append(jnp.pad(cell_parts, ((0, 0), (0, 0), (0, CELL_COLS - 6))))
    packed = jnp.concatenate(parts, -1)
    slab = 4 * share // ranks
    sent_w = packed.shape[-1]
    mine = lax.dynamic_slice_in_dim(packed.reshape(2, ranks, slab, sent_w), dp_at, 1, 1)[:, 0]
    everyone = lax.all_to_all(
        jnp.broadcast_to(mine[None], (groups, 2, slab, sent_w)), "gate", 0, 0, tiled=True
    )
    gathered = gather_dp(everyone[None], ranks)
    full = gathered.transpose(2, 1, 0, 3, 4).reshape(2, groups, 4, share, sent_w)
    full = full.transpose(0, 2, 1, 3, 4).reshape(2, 4 * wide, sent_w)
    return [full[0], full[1]]


def on_device(
    frames,
    regions,
    valid,
    step_count,
    conv_w,
    cell_params,
    head_w,
    head_b,
    conv_mom,
    cell_mom,
    head_mom,
    bias_mom,
    conv_avg,
    cell_avg,
    head_avg,
    bias_avg,
):
    share = conv_w.shape[2]
    chans = frames.shape[1]
    pixels = frames.shape[2]
    wide = head_w.shape[1]
    groups = lax.axis_size("gate")
    ranks = lax.axis_size("dp")
    geo = Geometry(groups, pixels)
    rows, own, halo, front, back, union = geo.rows, geo.own, geo.halo, geo.front, geo.back, geo.union
    gate_at = lax.axis_index("gate")
    dp_at = lax.axis_index("dp")

    order = ring_order(groups)
    place = [order.index(g) for g in range(groups)]
    spot = jnp.asarray(place, jnp.int32)[gate_at]
    from_right = [(order[(i + 1) % groups], order[i]) for i in range(groups)]
    from_left = [(order[i], order[(i + 1) % groups]) for i in range(groups)]

    slab = 4 * share // ranks
    packed_w = 9 * (wide + chans)
    sent_w = packed_w + CELL_COLS
    direct = ranks == 4 and slab == share and share % 16 == 0
    rank = dp_at.astype(jnp.int32).reshape(1)

    start = jnp.mod(spot * own - 2 * halo - 1, COLS).astype(jnp.int32).reshape(1)
    win, meta, mrm, mrp, mcm, mcp, counted = window_call(
        geo, start, frames.reshape(-1, pixels), valid, regions.reshape(1, pixels)
    )
    masks = (mrm, mrp, mcm, mcp)

    head_low = head_w.astype(BF16)
    head_bias = head_b[:, None]
    if direct:
        by_core, by_chip = swap_pairs(ranks, 1), swap_pairs(ranks, 2)
        cells_first = jnp.swapaxes(cell_params, 0, 1)
        mine0, mine1 = pack_call(groups, rank, conv_w, cells_first, sent_w)
        mixed0 = lax.all_to_all(mine0, "gate", 0, 0, tiled=True).reshape(groups * share, sent_w)
        mixed0, win, mine1 = lax.optimization_barrier((mixed0, win, mine1))
        over_x = lax.ppermute(mixed0, "dp", by_chip)
        over_core = lax.ppermute(mixed0, "dp", by_core)
        weights = [(rank, mixed0, over_core, over_x, lax.ppermute(over_x, "dp", by_core))]
        mixed1 = lax.all_to_all(mine1, "gate", 0, 0, tiled=True)
        weights.append((rank, mixed1))
    else:
        weights = gathered_weights(conv_w, cell_params, dp_at, groups, ranks, chans)

    state = ()
    kept = []
    t = 0
    for n, (layer, steps) in enumerate(geo.calls):
        base = n * halo
        first_frame = t if layer == 0 else t - 1
        got = forward_call(geo, layer, base, first_frame, steps, state, win, meta, weights[layer], masks)
        if len(got) > 7:
            weights[layer] = got[7]
        if direct and n == 0:
            mixed1, sent = lax.optimization_barrier((weights[1][1], got[6]))
            weights[1] = (rank, mixed1, lax.ppermute(mixed1, "dp", swap_pairs(ranks, 1)))
            got = [*got[:6], sent, *got[7:]]
        kept.append(dict(gates=got[0], cprev=got[1], hvar=got[2], hnew=got[3], xown=got[4], t=t))
        out = got[5]
        t += steps
        if n + 1 < len(geo.calls):
            far = lax.ppermute(got[6], "gate", from_right)
            state = (out, far)

    state = ()
    grads = [None, None]
    cell_sums = [None, None]
    head_sums = None
    for n in range(len(geo.calls) - 1, -1, -1):
        layer, steps = geo.calls[n]
        base = n * halo
        saved = kept[n]
        extra = (win, meta, head_low, head_bias) if layer == 1 else None
        carried = () if cell_sums[layer] is None else (cell_sums[layer], head_sums)
        got = backward_call(
            geo, layer, base, steps, n == 0, carried, state, saved, weights[layer], masks, extra
        )
        if n > 0:
            far = lax.ppermute(got[4], "gate", from_left)
            state = (got[3], far)
        cell_sums[layer] = got[1]
        if layer == 1:
            head_sums = got[2]
        done = direct and (n == 0 or geo.calls[n - 1][0] != layer)
        dz = got[0]
        if done and layer == 0:
            keep1, send1, dz = lax.optimization_barrier((*core_stage("1", rank, grads[1][0], crossed1, ()), dz))
            crossed1 = lax.ppermute(send1, "dp", swap_pairs(ranks, 2))
        grads[layer] = weight_call(
            geo,
            base,
            steps,
            grads[layer],
            dz,
            saved["hvar"],
            saved["xown"],
            masks[2],
            masks[3],
            rank if done else None,
            (cell_sums[0], cell_sums[1], head_sums, counted) if done and layer == 0 else (),
        )
        if done and layer == 1:
            crossed1 = lax.ppermute(grads[1][1], "dp", swap_pairs(ranks, 1))
    if direct:
        pairs = swap_pairs(ranks, 1)
        across = swap_pairs(ranks, 2)
        keep0, send0, few = grads[0]
        send0, crossed1 = lax.optimization_barrier((send0, crossed1))
        crossed0 = lax.ppermute(send0, "dp", pairs)
        message1, crossed0 = lax.optimization_barrier((chip_stage("1", groups, keep1, crossed1, ()), crossed0))
        mixed1 = lax.all_to_all(message1, "gate", 0, 0, tiled=True)
        keep0, send0, few = core_stage("0", rank, keep0, crossed0, (few,))
        crossed0 = lax.ppermute(send0, "dp", across)
        shard1, crossed0 = lax.optimization_barrier((sum_stage("1", mixed1), crossed0))
        from_dp1 = [lax.ppermute(shard1, "dp", swap_pairs(ranks, k)) for k in (1, 2, 3)]
        message0 = chip_stage("0", groups, keep0, crossed0, (few,))
        mixed0 = lax.all_to_all(message0, "gate", 0, 0, tiled=True)
        *from_dp1, mixed0 = lax.optimization_barrier((*from_dp1, mixed0))
        total_pixels = EOUT * pixels * ranks
        flip = lambda v: jnp.swapaxes(v, 0, 1)
        small_args = [cells_first, flip(cell_mom), flip(cell_avg), head_w, head_mom, head_avg]
        small_args += [v[None] for v in (head_b, bias_mom, bias_avg)]
        rate = float(RATE_SCALE * chans * total_pixels**0.5)
        done = finish_stage(rate, chans, packed_w, mixed0, step_count, small_args)
        shard0, scalars, loss = done[:3]
        pieces = [shard0] + [lax.ppermute(shard0, "dp", swap_pairs(ranks, k)) for k in (1, 2, 3)]
        pieces += [shard1] + from_dp1
        outs = [loss[0, 0]]
        outs += update_call(rank, scalars, pieces, conv_w, conv_mom, conv_avg)
        outs += [flip(v) for v in done[3:7]] + list(done[7:11]) + [v[0] for v in done[11:15]]
        return tuple(outs)

    rate = RATE_SCALE * chans * jnp.sqrt(jnp.float32(EOUT * pixels * ranks))
    counts_done = step_count.astype(F32)
    cells = jnp.stack(cell_sums).reshape(2, 7, 8, wide).sum(2)
    loss_sum = jnp.sum(head_sums[:, 129])
    shared_small = jnp.concatenate(
        [head_sums[:, :128].reshape(-1), head_sums[:, 128], loss_sum[None], counted[0, :1]]
    )
    small = jnp.concatenate([cells.reshape(-1), shared_small])
    big = jnp.stack(grads).reshape(2, 4, groups, share, packed_w).transpose(2, 1, 3, 0, 4)
    big = big.reshape(groups, ranks, slab, 2, packed_w).transpose(1, 0, 2, 3, 4)
    part, small = scatter_sum_dp(big, ranks, small)
    ncell = 14 * wide
    for_gate = small[:ncell].reshape(14, groups, share).transpose(1, 0, 2).reshape(groups, 14 * share)
    to_gate = jnp.concatenate(
        [for_gate, jnp.broadcast_to(small[None, ncell:], (groups, small.shape[0] - ncell))], 1
    )
    hi = lax.reduce_precision(to_gate, 8, 7)
    lo = (to_gate - hi).astype(BF16)
    hi = hi.astype(BF16)
    width = slab * 2 * packed_w
    message = jnp.concatenate([part.reshape(groups, width).astype(BF16), hi, lo], 1)
    got = lax.all_to_all(message, "gate", 0, 0, tiled=True).astype(F32)
    got = jnp.sum(got.reshape(groups, -1), 0)
    nsmall = to_gate.shape[1]
    small_sum = got[width : width + nsmall] + got[width + nsmall :]
    piece = got[:width].reshape(1, slab, 2, packed_w)
    rows_all = gather_dp(piece, ranks).reshape(4 * share, 2, packed_w).transpose(1, 0, 2)
    count = chans * small_sum[-1]
    scale = 2.0 / count
    rows_all = rows_all * scale
    grad_conv = jnp.concatenate(
        [
            rows_all[..., 9 * wide :].reshape(2, 4 * share, 9, chans),
            rows_all[..., : 9 * wide].reshape(2, 4 * share, 9, wide),
        ],
        -1,
    ).reshape(conv_w.shape)
    grad_cell = small_sum[: 14 * share].reshape(2, 7, share) * scale
    rest = small_sum[14 * share :]
    grad_head = rest[: chans * wide].reshape(chans, wide) * scale
    grad_bias = rest[chans * wide : chans * wide + chans] * scale
    loss = rest[chans * wide + chans] / count

    outs = [loss]
    outs += nesterov(conv_w, grad_conv, conv_mom, conv_avg, counts_done[0], rate)
    outs += nesterov(cell_params, grad_cell, cell_mom, cell_avg, counts_done[1], rate)
    outs += nesterov(head_w, grad_head, head_mom, head_avg, counts_done[2], rate)
    outs += nesterov(head_b, grad_bias, bias_mom, bias_avg, counts_done[3], rate)
    return tuple(outs)


def solution(mesh):
    in_specs = (
        P(None, None, "dp"),
        P("dp"),
        P(None, "dp"),
        P(),
        P(None, None, "gate", None),
        P(None, None, "gate"),
        P(),
        P(),
        P(None, None, "gate", None),
        P(None, None, "gate"),
        P(),
        P(),
        P(None, None, "gate", None),
        P(None, None, "gate"),
        P(),
        P(),
    )
    out_specs = (
        P(),
        P(None, None, "gate", None),
        P(None, None, "gate", None),
        P(None, None, "gate", None),
        P(None, None, "gate", None),
        P(None, None, "gate"),
        P(None, None, "gate"),
        P(None, None, "gate"),
        P(None, None, "gate"),
        P(),
        P(),
        P(),
        P(),
        P(),
        P(),
        P(),
        P(),
    )
    return jax.shard_map(
        on_device, mesh=mesh, in_specs=in_specs, out_specs=out_specs, check_vma=False
    )
```

```python
import functools

import jax
import jax.numpy as jnp
from jax import lax
from jax.experimental import pallas as pl
from jax.experimental.pallas import tpu as pltpu
from jax.sharding import PartitionSpec as P

EIN = 5
EOUT = 15
COLS = 128

MU = 0.9
RATE_SCALE = 0.05
F32 = jnp.float32
BF16 = jnp.bfloat16
VMEM_LIMIT = 60 * 1024 * 1024


def ring_order(groups):
    wide = groups // 4
    if wide <= 1:
        return list(range(groups))
    order = [(z, 0) for z in range(4)]
    for z in range(3, -1, -1):
        ys = range(1, wide) if z % 2 else range(wide - 1, 0, -1)
        order += [(z, y) for y in ys]
    return [z * wide + y for z, y in order]


def split_steps(steps, most):
    calls = -(-steps // most)
    base, extra = divmod(steps, calls)
    return [base + (1 if i < extra else 0) for i in range(calls)]


def nesterov(param, grad, mom, avg, steps_done, rate):
    mom_new = MU * mom + grad
    param_new = param - rate * (grad + MU * mom_new)
    avg_new = avg + (param_new - avg) / (steps_done + 1.0)
    return [mom_new, avg_new, param_new, param_new.astype(BF16)]


def logistic(v):
    return 0.5 * jnp.tanh(0.5 * v) + 0.5


def dot_nt(a, b):
    return lax.dot_general(a, b, (((1,), (1,)), ((), ())), preferred_element_type=F32)


def dot_tn(a, b):
    return lax.dot_general(a, b, (((0,), (0,)), ((), ())), preferred_element_type=F32)


def cut(total, pieces):
    base, extra = divmod(total, pieces)
    spans, at = [], 0
    for i in range(pieces):
        size = base + (1 if i < extra else 0)
        spans.append((at, size))
        at += size
    return spans


def cut_by_four(total, pieces):
    spans, at = [], 0
    for i in range(pieces):
        left = pieces - i
        size = total - at if left == 1 else (total - at) // left // 4 * 4
        if size:
            spans.append((at, size))
        at += size
    return spans


class Geometry:
    def __init__(self, groups, pixels):
        self.rows = pixels // COLS
        self.own = COLS // groups
        self.halo = min(5, self.own // 2)
        self.calls = [(0, n) for n in split_steps(EIN, self.halo)] + [(1, n) for n in split_steps(EOUT, self.halo)]
        self.front = self.own + 4 * self.halo
        self.back = self.own + 2 * self.halo
        self.union = self.front + (len(self.calls) - 1) * self.halo
        self.window = -(-(self.union + 2) * self.rows // 256) * 256


TAPS = [(dr, dc) for dr in (-1, 0, 1) for dc in (-1, 0, 1)]
CELL_COLS = 16


def window_kernel(geo, start, frames, valid, regions, win, meta, mrm, mrp, mcm, mcp, count, lhs, pick):
    rows, own, halo, union, width = geo.rows, geo.own, geo.halo, geo.union, geo.window
    nf = frames.shape[0]
    nv = valid.shape[0]
    lhs[:nf, :] = frames[...]
    lhs[nf : nf + nv, :] = valid[...].astype(F32).astype(BF16)
    lhs[nf + nv : nf + nv + 1, :] = regions[...].astype(F32).astype(BF16)
    per = 256 // rows
    source = lax.broadcasted_iota(jnp.int32, (COLS, 256), 0)
    lane = lax.broadcasted_iota(jnp.int32, (COLS, 256), 1)
    lane_row = lax.broadcasted_iota(jnp.int32, (1, 256), 1) % rows

    def one(n, carry):
        column = (start[0] + n * per + lane // rows) % COLS
        hit = (source == column).astype(F32).astype(BF16)
        for r in range(rows):
            keep = (lane_row == r).astype(F32).astype(BF16)
            pick[r * COLS : (r + 1) * COLS, :] = hit * keep
        got = jnp.dot(lhs[...], pick[...], preferred_element_type=F32)
        at = pl.multiple_of(n * 256, 256)
        win[:, pl.ds(at, 256)] = got[:nf].astype(BF16)
        meta[:, pl.ds(at, 256)] = got[nf:]
        return carry

    lax.fori_loop(0, width // 256, one, 0)
    px = union * rows
    ids = meta[nv : nv + 1, :]
    bands = jnp.floor(ids * 0.5)
    here = ids[:, rows : rows + px]
    band_here = bands[:, rows : rows + px]
    picked = [
        ids[:, rows - 1 : rows - 1 + px] == here,
        ids[:, rows + 1 : rows + 1 + px] == here,
        bands[:, :px] == band_here,
        bands[:, 2 * rows : 2 * rows + px] == band_here,
    ]
    row_at = lax.broadcasted_iota(jnp.int32, (8, px), 0)
    stack = jnp.zeros((8, px), F32)
    for k, m in enumerate(picked):
        stack = jnp.where(row_at == k, jnp.broadcast_to(m.astype(F32), (8, px)), stack)
    stack = stack.astype(BF16)
    sel = lax.broadcasted_iota(jnp.int32, (8, 128), 0)
    for k, out in enumerate((mrm, mrp, mcm, mcp)):
        out[...] = dot_tn(stack, (sel == k).astype(F32).astype(BF16)).astype(BF16)
    a = (2 * halo + 1) * rows
    count[...] = jnp.broadcast_to(jnp.sum(meta[:nv, a : a + own * rows]), count.shape)


def window_call(geo, start, frames, valid, regions):
    nf, nv = frames.shape[0], valid.shape[0]
    pixels = frames.shape[1]
    px = geo.union * geo.rows
    smem = pl.BlockSpec(memory_space=pltpu.SMEM)
    vmem = pl.BlockSpec(memory_space=pltpu.VMEM)
    total = nf + nv + 1
    return pl.pallas_call(
        functools.partial(window_kernel, geo),
        in_specs=[smem, vmem, vmem, vmem],
        out_specs=[vmem] * 7,
        out_shape=[
            jax.ShapeDtypeStruct((nf, geo.window), BF16),
            jax.ShapeDtypeStruct((nv + 1, geo.window), F32),
        ]
        + [jax.ShapeDtypeStruct((px, 128), BF16)] * 4
        + [jax.ShapeDtypeStruct((8, 128), F32)],
        scratch_shapes=[pltpu.VMEM((total, pixels), BF16), pltpu.VMEM((pixels, 256), BF16)],
        compiler_params=pltpu.CompilerParams(vmem_limit_bytes=VMEM_LIMIT),
        cost_estimate=pl.CostEstimate(
            flops=2 * total * pixels * geo.window, bytes_accessed=10 << 20, transcendentals=0
        ),
        name="window",
    )(start, frames, valid, regions)


def pack_kernel(groups, rank, conv, cells, out0, out1):
    share, depth9 = conv.shape[2:]
    chans9 = out0.shape[-1] - CELL_COLS - 9 * 128
    chans = chans9 // 9
    depth = chans + 128
    row = lax.broadcasted_iota(jnp.int32, (7, CELL_COLS), 0)
    col = lax.broadcasted_iota(jnp.int32, (7, CELL_COLS), 1)
    half = (rank[0] & 1) * 2
    for l, at, gate, out in ((0, 0, rank[0], out0), (1, 0, half, out1), (1, share, half + 1, out1)):
        w = conv[l, gate].astype(BF16)
        parts = [w[:, k * depth + chans : (k + 1) * depth] for k in range(9)]
        parts += [w[:, k * depth : k * depth + chans] for k in range(9)]
        rest = cells[:, l, :]
        cols = jnp.zeros((share, CELL_COLS), F32)
        for k in range(3):
            low = rest.astype(BF16)
            rest = rest - low.astype(F32)
            sel = ((row == gate) & (col == k)) | ((row == gate + 4) & (col == 3 + k))
            cols = cols + dot_tn(low, sel.astype(F32).astype(BF16))
        parts.append(cols.astype(BF16))
        line = jnp.concatenate(parts, 1)
        for g in range(groups):
            out[g, at : at + share, :] = line


def pack_call(groups, rank, conv_w, cells, sent_w):
    share = conv_w.shape[2]
    return plain_call(
        functools.partial(pack_kernel, groups),
        "pack",
        [jax.ShapeDtypeStruct((groups, k * share, sent_w), BF16) for k in (1, 2)],
        rank,
        conv_w,
        cells,
        smem=1,
    )


def peephole_rows(wf):
    tail = wf[:, 9 * 128 :]
    depth = tail.shape[1]
    col = lax.broadcasted_iota(jnp.int32, (8, depth), 1)
    at = depth - CELL_COLS + 3
    sel = ((col >= at) & (col < at + 3)).astype(F32).astype(BF16)
    got = dot_nt(sel, tail)
    return [got[0:1, k * 128 : (k + 1) * 128] for k in range(3)]


def make_variants(geo, hn, hb, mrm, mrp, base):
    rows = geo.rows
    for c0, cw in cut(geo.front, 4):
        r0, m = c0 * rows, cw * rows
        h = hn[r0 : r0 + m, :]
        up = pltpu.roll(h, 1, 0)
        down = pltpu.roll(h, m - 1, 0)
        g0 = base * rows + r0
        hb[0, r0 : r0 + m, :] = up.astype(BF16) * mrm[g0 : g0 + m, :]
        hb[1, r0 : r0 + m, :] = h.astype(BF16)
        hb[2, r0 : r0 + m, :] = down.astype(BF16) * mrp[g0 : g0 + m, :]


def forward_kernel(geo, layer, base, steps, first, gather, *refs):
    refs = list(refs)
    if gather:
        rank, pieces, refs = refs[0], refs[1 : 1 + gather], refs[1 + gather :]
    if not first:
        near, far = refs[:2]
        refs = refs[2:]
    if gather:
        win, meta, mrm, mrp, mcm, mcp = refs[:6]
        wf = refs[13]
        refs = refs[6:13] + refs[14:]
    else:
        win, meta, wf, mrm, mrp, mcm, mcp = refs[:7]
        refs = refs[7:]
    gates_out, cprev_out, hvar_out, hnew_out, xown_out, state_out, send_out = refs[:7]
    hb, hn, cb, xs, keeps, peeps = refs[7:]
    rows, halo, own, front, back = geo.rows, geo.halo, geo.own, geo.front, geo.back
    chans = win.shape[0]
    chans9 = 9 * chans
    lanes = (front - 2) * rows
    x0 = (base + 2) * rows
    step = pl.program_id(0)

    @pl.when(step == 0)
    def _():
        if first:
            hn[...] = jnp.zeros_like(hn)
            cb[...] = jnp.zeros_like(cb)
        else:
            nb = back * rows
            hn[:nb, :] = near[:, :128].astype(F32)
            hn[nb:, :] = far[:, :128].astype(F32)
            cb[:nb, :] = near[:, 128:].astype(F32)
            cb[nb:, :] = far[:, 128:].astype(F32)
        make_variants(geo, hn, hb, mrm, mrp, base)
        if gather:
            for k, piece in enumerate(pieces):
                if gather == 4:
                    wf[pl.ds(pl.multiple_of((rank[0] ^ k) * 128, 128), 128), :] = piece[...]
                    continue
                peers, span = piece.shape[0], piece.shape[1] // 2
                half = pl.multiple_of(((rank[0] ^ k) & 1) * 256, 256)
                for g in range(peers):
                    for j in range(2):
                        at = pl.multiple_of(half + j * 128 + g * span, span)
                        wf[pl.ds(at, span), :] = piece[g, j * span : (j + 1) * span, :]
        ids = meta[meta.shape[0] - 1 :, :]
        here = ids[:, x0 : x0 + lanes]
        for tap, (dr, dc) in enumerate(TAPS):
            off = x0 + dc * rows + dr
            same = (ids[:, off : off + lanes] == here).astype(F32)
            keeps[tap * chans : (tap + 1) * chans, :] = jnp.broadcast_to(same, (chans, lanes)).astype(BF16)
        ones = lax.broadcasted_iota(jnp.int32, (CELL_COLS, lanes), 0) < 3
        xs[chans9:, :] = ones.astype(F32).astype(BF16)
        for k, row in enumerate(peephole_rows(wf)):
            peeps[k : k + 1, :] = row

    s0, sn = (2 * halo - 1) * rows, (own + 2) * rows
    for v in range(3):
        hvar_out[0, v, :, :] = hb[v, s0 : s0 + sn, :]
    cprev_out[0, :, :] = cb[halo * rows : (halo + back) * rows, :].astype(BF16)
    for tap, (dr, dc) in enumerate(TAPS):
        off = x0 + dc * rows + dr
        part = slice(tap * chans, (tap + 1) * chans)
        xs[part, :] = win[:, off : off + lanes] * keeps[part, :]
    q0 = (2 * halo - 1) * rows
    xown_out[0, :, :] = xs[:, q0 : q0 + own * rows]

    for c0, cw in cut_by_four(front - 2, 4):
        r0, m = (c0 + 1) * rows, cw * rows
        g0 = base * rows + r0
        parts = []
        for dr in range(3):
            left = hb[dr, r0 - rows : r0 - rows + m, :] * mcm[g0 : g0 + m, :]
            mid = hb[dr, r0 : r0 + m, :]
            right = hb[dr, r0 + rows : r0 + rows + m, :] * mcp[g0 : g0 + m, :]
            parts += [left, mid, right]
        z = dot_nt(jnp.concatenate(parts, 1), wf[:, : 9 * 128]) + lax.dot_general(
            xs[:, r0 - rows : r0 - rows + m], wf[:, 9 * 128 :], (((0,), (1,)), ((), ())), preferred_element_type=F32
        )
        c = cb[r0 : r0 + m, :]
        gi = logistic(z[:, 0:128] + peeps[0:1, :] * c)
        gf = logistic(z[:, 128:256] + peeps[1:2, :] * c)
        gg = jnp.tanh(z[:, 384:512])
        cn = gf * c + gi * gg
        go = logistic(z[:, 256:384] + peeps[2:3, :] * cn)
        h = go * jnp.tanh(cn)
        cb[r0 : r0 + m, :] = cn
        hn[r0 : r0 + m, :] = h.astype(BF16).astype(F32)
        lo, hi = max(c0 + 1, halo), min(c0 + 1 + cw, halo + back)
        a, b = (lo - c0 - 1) * rows, (hi - c0 - 1) * rows
        o = (lo - halo) * rows
        n = b - a
        if n > 0:
            gates_out[0, o : o + n, 0:128] = gi[a:b].astype(BF16)
            gates_out[0, o : o + n, 128:256] = gf[a:b].astype(BF16)
            gates_out[0, o : o + n, 256:384] = go[a:b].astype(BF16)
            gates_out[0, o : o + n, 384:512] = gg[a:b].astype(BF16)
            hnew_out[0, o : o + n, :] = h[a:b].astype(BF16)

    make_variants(geo, hn, hb, mrm, mrp, base)

    @pl.when(step == steps - 1)
    def _():
        a, b = halo * rows, (halo + back) * rows
        state_out[:, :128] = hn[a:b, :].astype(BF16)
        state_out[:, 128:] = cb[a:b, :].astype(BF16)
        a, b = 3 * halo * rows, 5 * halo * rows
        send_out[:, :128] = hn[a:b, :].astype(BF16)
        send_out[:, 128:] = cb[a:b, :].astype(BF16)


def whole(shape):
    return pl.BlockSpec(shape, lambda *_: (0,) * len(shape))


def forward_call(geo, layer, base, first_frame, steps, state, win, meta, weights, masks):
    rows, own, front, back = geo.rows, geo.own, geo.front, geo.back
    chans = win.shape[0] // (EIN + EOUT)
    gather = len(weights) - 1 if isinstance(weights, tuple) else 0
    sent_w = weights[1].shape[-1] if gather else weights.shape[1]
    depth = sent_w - 9 * 128
    by_step = lambda *dims: pl.BlockSpec((1,) + dims, lambda t: (t,) + (0,) * len(dims))
    lead = list(weights) if gather else []
    operands = lead + list(state) + [win, meta] + ([] if gather else [weights]) + list(masks)
    in_specs = [pl.BlockSpec(memory_space=pltpu.SMEM)] if gather else []
    in_specs += [whole(v.shape) for v in lead[1:]]
    in_specs += [whole(s.shape) for s in state]
    in_specs += [pl.BlockSpec((chans, win.shape[1]), lambda t: (first_frame + t, 0))]
    in_specs += [whole(v.shape) for v in operands[len(lead) + len(state) + 1 :]]
    shapes = [
        (steps, back * rows, 512),
        (steps, back * rows, 128),
        (steps, 3, (own + 2) * rows, 128),
        (steps, back * rows, 128),
        (steps, depth, own * rows),
    ]
    flat = [(back * rows, 256), (2 * geo.halo * rows, 256)] + ([(512, sent_w)] if gather else [])
    outs = [jax.ShapeDtypeStruct(s, BF16) for s in shapes + flat]
    out_specs = [by_step(*s[1:]) for s in shapes] + [whole(s) for s in flat]
    px = front * rows
    return pl.pallas_call(
        functools.partial(forward_kernel, geo, layer, base, steps, not state, gather),
        grid=(steps,),
        in_specs=in_specs,
        out_specs=out_specs,
        out_shape=outs,
        scratch_shapes=[
            pltpu.VMEM((3, px, 128), BF16),
            pltpu.VMEM((px, 128), F32),
            pltpu.VMEM((px, 128), F32),
            pltpu.VMEM((depth, px - 2 * rows), BF16),
            pltpu.VMEM((9 * chans, px - 2 * rows), BF16),
            pltpu.VMEM((8, 128), F32),
        ],
        compiler_params=pltpu.CompilerParams(vmem_limit_bytes=VMEM_LIMIT),
        cost_estimate=pl.CostEstimate(
            flops=steps * px * 512 * 1296 * 2, bytes_accessed=8 << 20, transcendentals=steps * px * 640
        ),
        name=f"forward_{base}",
    )(*operands)


def backward_kernel(geo, layer, base, steps, first_live, first, last, carried, *refs):
    refs = list(refs)
    if carried:
        sums_in, head_in = refs[:2]
        refs = refs[2:]
    if not first:
        local, far = refs[:2]
        refs = refs[2:]
    gates, cprev, wf, mrm, mrp, mcm, mcp = refs[:7]
    refs = refs[7:]
    if layer == 1:
        hnew, target, meta, head, head_b = refs[:5]
        refs = refs[5:]
    dz_out, sums_out, head_out, carry_out, send_out = refs[:5]
    dh, dc, dzs, peeps, wb = refs[5:]
    rows, halo, own, back = geo.rows, geo.halo, geo.own, geo.back
    o0, on = halo * rows, own * rows
    step = pl.program_id(0)

    @pl.when(step == 0)
    def _():
        sums_out[...] = sums_in[...] if carried else jnp.zeros_like(sums_out)
        head_out[...] = head_in[...] if carried else jnp.zeros_like(head_out)
        for tap in range(9):
            across, along = tap % 3 * 512, tap // 3 * 128
            wb[across : across + 512, along : along + 128] = wf[:, tap * 128 : (tap + 1) * 128]
        edge = jnp.zeros((rows, 512), BF16)
        for k in range(3):
            dzs[k, :rows, :] = edge
            dzs[k, rows + back * rows :, :] = edge
        for k, row in enumerate(peephole_rows(wf)):
            peeps[k : k + 1, :] = row
        if first:
            dh[...] = jnp.zeros_like(dh)
            dc[...] = jnp.zeros_like(dc)
        else:
            nf = 2 * halo * rows
            dh[:nf, :] = far[:, :128].astype(F32)
            dc[:nf, :] = far[:, 128:].astype(F32)
            dh[nf:, :] = local[:, :128]
            dc[nf:, :] = local[:, 128:]

    if layer == 1:
        guess = dot_nt(head[...], hnew[0]) + head_b[...]
        a0 = (base + halo + 1) * rows
        err = guess - target[:, a0 : a0 + back * rows].astype(F32)
        dy = meta[pl.ds(first_live + steps - 1 - step, 1), a0 : a0 + back * rows] * err
        low = dy.astype(BF16)
        head_out[:, 0:128] += jnp.dot(low[:, o0 : o0 + on], hnew[0, o0 : o0 + on, :], preferred_element_type=F32)
        own_dy = low[:, o0 : o0 + on].astype(F32)
        head_out[:, 128:129] += jnp.sum(own_dy, 1, keepdims=True)
        head_out[:, 129:130] += jnp.sum((dy * err)[:, o0 : o0 + on], 1, keepdims=True)
        dh[...] += dot_tn(low, head[...])

    def gates_chunk(c0, cw):
        r0, m = c0 * rows, cw * rows
        span = slice(r0, r0 + m)
        gi = gates[0, span, 0:128].astype(F32)
        gf = gates[0, span, 128:256].astype(F32)
        go = gates[0, span, 256:384].astype(F32)
        gg = gates[0, span, 384:512].astype(F32)
        c = cprev[0, span, :].astype(F32)
        cn = gf * c + gi * gg
        tc = jnp.tanh(cn)
        g = dh[span, :]
        d_o = g * tc * go * (1.0 - go)
        d_c = dc[span, :] + g * go * (1.0 - tc * tc) + d_o * peeps[2:3, :]
        d_i = d_c * gg * gi * (1.0 - gi)
        d_f = d_c * c * gf * (1.0 - gf)
        d_g = d_c * gi * (1.0 - gg * gg)
        dc[span, :] = d_c * gf + d_i * peeps[0:1, :] + d_f * peeps[1:2, :]
        p0 = rows + r0
        g0 = (base + halo) * rows + r0
        left, right = mcm[g0 : g0 + m, :], mcp[g0 : g0 + m, :]
        for n, d in enumerate((d_i, d_f, d_o, d_g)):
            low = d.astype(BF16)
            lanes = slice(n * 128, (n + 1) * 128)
            dzs[0, p0 : p0 + m, lanes] = low * left
            dzs[1, p0 : p0 + m, lanes] = low
            dzs[2, p0 : p0 + m, lanes] = low * right
        a = max(r0, o0) - r0
        b = min(r0 + m, o0 + on) - r0
        if b > a:
            for n, d in enumerate((d_i * c, d_f * c, d_o * cn)):
                part = d[a:b].reshape((b - a) // 8, 8, 128)
                sums_out[n * 8 : (n + 1) * 8, :] += jnp.sum(part, 0)

    def hidden_chunk(c0, cw):
        r0, m = c0 * rows, cw * rows
        g0 = (base + halo) * rows + r0
        parts = [dzs[k, 2 * rows + r0 - k * rows : 2 * rows + r0 - k * rows + m, :] for k in range(3)]
        acc = jnp.dot(jnp.concatenate(parts, 1), wb[...], preferred_element_type=F32)
        above = pltpu.roll(acc[:, :128] * mrm[g0 : g0 + m, :].astype(F32), m - 1, 0)
        below = pltpu.roll(acc[:, 256:] * mrp[g0 : g0 + m, :].astype(F32), 1, 0)
        dh[r0 : r0 + m, :] = acc[:, 128:256] + above + below

    half = back // 2
    pending = [(0, half), (half, back - half)]
    for c0, cw in cut(back, 4):
        gates_chunk(c0, cw)
        if pending and c0 + cw > pending[0][0] + pending[0][1]:
            hidden_chunk(*pending.pop(0))
    for chunk in pending:
        hidden_chunk(*chunk)
    dz_out[0, :, :] = dzs[1, rows + o0 : rows + o0 + on, :]

    @pl.when(step == steps - 1)
    def _():
        carry_out[:, :128] = dh[o0 : o0 + on, :]
        carry_out[:, 128:] = dc[o0 : o0 + on, :]
        ns = 2 * halo * rows
        s0 = o0 + on - ns
        send_out[:, :128] = dh[s0 : s0 + ns, :].astype(BF16)
        send_out[:, 128:] = dc[s0 : s0 + ns, :].astype(BF16)


def backward_call(geo, layer, base, steps, last, carried, state, saved, wf, masks, extra):
    rows, own, back, halo = geo.rows, geo.own, geo.back, geo.halo
    by_step = lambda *dims: pl.BlockSpec((1,) + dims, lambda t: (steps - 1 - t,) + (0,) * len(dims))
    first_live = saved["t"] - EIN
    lead = list(carried) + list(state)
    operands = lead + [saved["gates"], saved["cprev"], wf] + list(masks)
    in_specs = [whole(s.shape) for s in lead]
    in_specs += [by_step(back * rows, 512), by_step(back * rows, 128)]
    in_specs += [whole(v.shape) for v in operands[len(lead) + 2 :]]
    if layer == 1:
        win, meta, head, head_b = extra
        operands += [saved["hnew"], win, meta, head, head_b]
        t0 = saved["t"]
        in_specs += [
            by_step(back * rows, 128),
            pl.BlockSpec((head.shape[0], win.shape[1]), lambda t: (t0 + steps - 1 - t, 0)),
            whole(meta.shape),
            whole(head.shape),
            whole(head_b.shape),
        ]
    outs = [
        jax.ShapeDtypeStruct((steps, own * rows, 512), BF16),
        jax.ShapeDtypeStruct((24, 128), F32),
        jax.ShapeDtypeStruct((16, 256), F32),
        jax.ShapeDtypeStruct((own * rows, 256), F32),
        jax.ShapeDtypeStruct((2 * halo * rows, 256), BF16),
    ]
    out_specs = [by_step(own * rows, 512)] + [whole(o.shape) for o in outs[1:]]
    px = back * rows
    return pl.pallas_call(
        functools.partial(backward_kernel, geo, layer, base, steps, first_live, not state, last, bool(carried)),
        grid=(steps,),
        in_specs=in_specs,
        out_specs=out_specs,
        out_shape=outs,
        scratch_shapes=[
            pltpu.VMEM((px, 128), F32),
            pltpu.VMEM((px, 128), F32),
            pltpu.VMEM((3, px + 2 * rows, 512), BF16),
            pltpu.VMEM((8, 128), F32),
            pltpu.VMEM((3 * 512, 3 * 128), BF16),
        ],
        compiler_params=pltpu.CompilerParams(vmem_limit_bytes=VMEM_LIMIT),
        cost_estimate=pl.CostEstimate(
            flops=steps * px * 512 * 1536 * 2, bytes_accessed=8 << 20, transcendentals=steps * px * 128
        ),
        name=f"backward_{base}",
    )(*operands)


def split_low(v, axis=0):
    hi = v.astype(BF16)
    return jnp.concatenate([hi, (v - hi.astype(F32)).astype(BF16)], axis)


def joined(v):
    half = v.shape[0] // 2
    return v[:half].astype(F32) + v[half:].astype(F32)


def weight_kernel(geo, base, steps, add, final, small, *refs):
    refs = list(refs)
    if final:
        rank, refs = refs[0], refs[1:]
    if add:
        acc, refs = refs[0], refs[1:]
    if small:
        sums0, sums1, bias1, head, count = refs[:5]
        refs = refs[5:]
    dz, hvar, xown, mcm, mcp = refs[:5]
    outs, rhs = refs[5:-1], refs[-1]
    rows, own, halo = geo.rows, geo.own, geo.halo
    on = own * rows
    g0 = (base + 2 * halo) * rows
    wide = hvar.shape[-1]
    if final:
        odd = (rank[0] & 1) == 1

    def put(lo, g):
        at = slice(lo, lo + g.shape[0])
        if add:
            g = g + acc[at, :]
        if not final:
            outs[0][at, :] = g
            return g
        keep, send = outs[:2]
        for j in range(2):
            even_gate = g[:, 2 * j * wide : (2 * j + 1) * wide]
            odd_gate = g[:, (2 * j + 1) * wide : (2 * j + 2) * wide]
            keep[j, at, :] = jnp.where(odd, odd_gate, even_gate)
            to = slice(j * keep.shape[1] + lo, j * keep.shape[1] + lo + g.shape[0])
            send[to, :] = jnp.where(odd, even_gate, odd_gate).astype(BF16)
        return g

    chans9 = xown.shape[1] - CELL_COLS
    for dr in range(3):
        for dc in range(3):
            for j in range(steps):
                v = hvar[j, dr, dc * rows : dc * rows + on, :]
                if dc == 0:
                    v = v * mcm[g0 : g0 + on, :]
                elif dc == 2:
                    v = v * mcp[g0 : g0 + on, :]
                rhs[dr % 2, j * on : (j + 1) * on, dc * wide : (dc + 1) * wide] = v
        put(3 * dr * wide, dot_tn(rhs[dr % 2], dz[...]))
    inputs = None
    for j in range(steps):
        part = jnp.dot(xown[j], dz[j * on : (j + 1) * on, :], preferred_element_type=F32)
        inputs = part if inputs is None else inputs + part
    bias = put(9 * wide, inputs)[chans9 : chans9 + 8]
    if final and not small:
        outs[2][...] = bias
    if small:
        few = []
        for row, sums in ((bias, sums0), (bias1[...], sums1)):
            few += [row[0:1, k * wide : (k + 1) * wide] for k in range(4)]
            few.append(jnp.sum(sums[...].reshape(3, 8, wide), 1))
        few = jnp.concatenate(few + [jnp.zeros((2, wide), F32)], 0)
        col = lax.broadcasted_iota(jnp.int32, (16, wide), 1)
        extra = jnp.where(col == 2, jnp.broadcast_to(count[0:1, :], (16, wide)), head[:, wide:])
        few = jnp.concatenate([few, head[:, :wide], extra], 0)
        outs[2][...] = few
        outs[1][2 * outs[0].shape[1] :, :] = split_low(few)


def weight_call(geo, base, steps, acc, dz, hvar, xown, mcm, mcp, rank=None, small=()):
    on = geo.own * geo.rows
    dz = dz.reshape(steps * on, 512)
    depth = 1152 + xown.shape[1]
    final = rank is not None
    operands = ([rank] if final else []) + ([] if acc is None else [acc]) + list(small) + [dz, hvar, xown, mcm, mcp]
    in_specs = [pl.BlockSpec(memory_space=pltpu.VMEM)] * len(operands)
    out_shape = jax.ShapeDtypeStruct((depth, 512), F32)
    if final:
        in_specs[0] = pl.BlockSpec(memory_space=pltpu.SMEM)
        out_shape = [
            jax.ShapeDtypeStruct((2, depth, 128), F32),
            jax.ShapeDtypeStruct((2 * depth + (96 if small else 0), 128), BF16),
            jax.ShapeDtypeStruct((48, 128) if small else (8, 512), F32),
        ]
    return pl.pallas_call(
        functools.partial(weight_kernel, geo, base, steps, acc is not None, final, bool(small)),
        in_specs=in_specs,
        out_shape=out_shape,
        scratch_shapes=[pltpu.VMEM((2, steps * on, 384), BF16)],
        compiler_params=pltpu.CompilerParams(vmem_limit_bytes=VMEM_LIMIT),
        cost_estimate=pl.CostEstimate(
            flops=steps * on * 512 * 1296 * 2, bytes_accessed=16 << 20, transcendentals=0
        ),
        name=f"weights_{base}",
    )(*operands)


SMALL_AT = 1408


def core_stage_kernel(rank, keep, got, *refs):
    depth = keep.shape[1]
    high = (rank[0] & 2) == 2
    small = len(refs) > 2
    if small:
        few, keep_out, send_out, few_out = refs
    else:
        keep_out, send_out = refs
    a = keep[0] + got[:depth, :].astype(F32)
    b = keep[1] + got[depth : 2 * depth, :].astype(F32)
    keep_out[...] = jnp.where(high, b, a)
    send_out[:depth, :] = jnp.where(high, a, b).astype(BF16)
    if small:
        total = few[...] + joined(got[2 * depth :, :])
        few_out[...] = total
        send_out[depth:, :] = split_low(total)


def chip_stage_kernel(groups, keep, got, *refs):
    depth, wide = keep.shape
    small = len(refs) > 1
    if small:
        few, out = refs
    else:
        (out,) = refs
    width = depth - CELL_COLS
    share = wide // groups
    total = (keep[...] + got[:depth, :].astype(F32)).T[:, :width].astype(BF16)
    if small:
        sums = few[...] + joined(got[depth:, :])
        head = split_low(sums[16:32], 1)
        extra = split_low(sums[32:, :16], 1)
        fill = jnp.zeros((16, SMALL_AT - width - 2 * share - 32), BF16)
    for g in range(groups):
        part = total[g * share : (g + 1) * share, :]
        if not small:
            out[g, :, :] = part
        else:
            cells = split_low(sums[:16, g * share : (g + 1) * share], 1)
            out[g, :, :] = jnp.concatenate([part, cells, extra, fill, head], 1)


def sum_stage_kernel(got, out):
    total = got[0].astype(F32)
    for g in range(1, got.shape[0]):
        total = total + got[g].astype(F32)
    out[...] = total


def finish_kernel(rate, chans, got, steps_done, *refs):
    (cell_refs, head_refs, bias_refs), refs = (refs[:3], refs[3:6], refs[6:9]), refs[9:]
    shard, scalars, loss, cell_outs, head_outs, bias_outs = refs[0], refs[1], refs[2], refs[3:7], refs[7:11], refs[11:]
    total = got[0].astype(F32)
    for g in range(1, got.shape[0]):
        total = total + got[g].astype(F32)
    width = shard.shape[1]
    share = total.shape[0]
    shard[...] = total[:, :width]
    cells = total[:, width : width + share] + total[:, width + share : width + 2 * share]
    at = width + 2 * share
    extra = total[:, at : at + 16] + total[:, at + 16 : at + 32]
    head = total[:, SMALL_AT : SMALL_AT + 128] + total[:, SMALL_AT + 128 :]
    count = chans * extra[0:1, 2:3]
    scale = 2.0 / count
    fresh = [1.0 / (jnp.full((1, 1), steps_done[k].astype(F32)) + 1.0) for k in range(4)]
    loss[...] = jnp.sum(extra[:, 1:2], 0, keepdims=True) / count
    lane = lax.broadcasted_iota(jnp.int32, (8, 128), 1)
    scalars[...] = jnp.where(lane == 0, scale, jnp.where(lane == 1, rate, fresh[0]))

    def update(refs, outs, at, grad, fresh):
        param, mom, avg = (v[at] for v in refs)
        grad = grad * scale
        m = MU * mom + grad
        p = param - rate * (grad + MU * m)
        outs[0][at] = m
        outs[1][at] = avg + (p - avg) * fresh
        outs[2][at] = p
        outs[3][at] = p.astype(BF16)

    for l in range(2):
        update(cell_refs, cell_outs, (slice(None), l, slice(None)), cells[l * 7 : (l + 1) * 7, :], fresh[1])
    update(head_refs, head_outs, (slice(None), slice(None)), head, fresh[2])
    row = lax.broadcasted_iota(jnp.int32, (16, 16), 0)
    col = lax.broadcasted_iota(jnp.int32, (16, 16), 1)
    bias = jnp.sum(jnp.where(row == col, jnp.broadcast_to(extra[:, 0:1], (16, 16)), 0.0), 0, keepdims=True)
    update(bias_refs, bias_outs, (slice(None), slice(None)), bias, fresh[3])


def plain_call(kernel, name, out_shape, *operands, smem=0, moved=4 << 20, smem_at=()):
    where = [pltpu.SMEM if i < smem or i in smem_at else pltpu.VMEM for i in range(len(operands))]
    specs = [pl.BlockSpec(memory_space=m) for m in where]
    return pl.pallas_call(
        kernel,
        in_specs=specs,
        out_shape=out_shape,
        compiler_params=pltpu.CompilerParams(vmem_limit_bytes=VMEM_LIMIT),
        cost_estimate=pl.CostEstimate(flops=1 << 20, bytes_accessed=moved, transcendentals=0),
        name=name,
    )(*operands)


def core_stage(name, rank, keep, got, small):
    depth, wide = keep.shape[1:]
    more = 96 if small else 0
    shapes = [jax.ShapeDtypeStruct((depth, wide), F32), jax.ShapeDtypeStruct((depth + more, wide), BF16)]
    shapes += [jax.ShapeDtypeStruct(v.shape, F32) for v in small]
    return plain_call(core_stage_kernel, "core_stage_" + name, shapes, rank, keep, got, *small, smem=1)


def chip_stage(name, groups, keep, got, small):
    depth, wide = keep.shape
    lanes = SMALL_AT + 256 if small else depth - CELL_COLS
    shape = jax.ShapeDtypeStruct((groups, wide // groups, lanes), BF16)
    kernel = functools.partial(chip_stage_kernel, groups)
    return plain_call(kernel, "chip_stage_" + name, shape, keep, got, *small, moved=2 << 20)


def sum_stage(name, got):
    shape = jax.ShapeDtypeStruct(got.shape[1:], F32)
    return plain_call(sum_stage_kernel, "sum_stage_" + name, shape, got, moved=1 << 20)


def finish_stage(rate, chans, width, got, step_count, small_args):
    shapes = [
        jax.ShapeDtypeStruct((got.shape[1], width), F32),
        jax.ShapeDtypeStruct((8, 128), F32),
        jax.ShapeDtypeStruct((1, 1), F32),
    ]
    for v in small_args[::3]:
        shapes += [jax.ShapeDtypeStruct(v.shape, F32)] * 3 + [jax.ShapeDtypeStruct(v.shape, BF16)]
    kernel = functools.partial(finish_kernel, rate, chans)
    return plain_call(kernel, "finish", shapes, got, step_count, *small_args, moved=1 << 20, smem_at=(1,))


def update_kernel(rank, scalars, *refs):
    pieces = (refs[:4], refs[4:8])
    param, mom, avg, mom_out, avg_out, new_out, low_out, grad = refs[8:]
    layer = pl.program_id(0)
    chans = (grad.shape[-1] - 9 * 128) // 9
    scale, rate, fresh = (scalars[0:1, k : k + 1] for k in range(3))
    for l in range(2):

        @pl.when(layer == l)
        def _():
            for k, piece in enumerate(pieces[l]):
                v = piece[...]
                parts = []
                for tap in range(9):
                    parts.append(v[:, 9 * 128 + tap * chans : 9 * 128 + (tap + 1) * chans])
                    parts.append(v[:, tap * 128 : (tap + 1) * 128])
                grad[rank[0] ^ k] = jnp.concatenate(parts, 1) * scale

    g = grad[...]
    m = MU * mom[0] + g
    p = param[0] - rate * (g + MU * m)
    mom_out[0] = m
    new_out[0] = p
    low_out[0] = p.astype(BF16)
    avg_out[0] = avg[0] + (p - avg[0]) * fresh


def update_call(rank, scalars, pieces, param, mom, avg):
    layers, gates, share, width = param.shape
    block = pl.BlockSpec((1, gates, share, width), lambda l: (l, 0, 0, 0))
    smem = pl.BlockSpec(memory_space=pltpu.SMEM)
    shape = jax.ShapeDtypeStruct(param.shape, F32)
    return pl.pallas_call(
        update_kernel,
        grid=(layers,),
        in_specs=[smem, whole(scalars.shape)] + [whole(v.shape) for v in pieces] + [block] * 3,
        out_specs=[block] * 4,
        out_shape=[shape] * 3 + [jax.ShapeDtypeStruct(param.shape, BF16)],
        scratch_shapes=[pltpu.VMEM((gates, share, width), F32)],
        compiler_params=pltpu.CompilerParams(vmem_limit_bytes=VMEM_LIMIT),
        cost_estimate=pl.CostEstimate(flops=1 << 20, bytes_accessed=6 << 20, transcendentals=0),
        name="update",
    )(rank, scalars, *pieces, param, mom, avg)


def swap_pairs(size, bit):
    return [(i, i ^ bit) for i in range(size)]


def butterfly_bits(size):
    bits, bit = [], 1
    while bit < size:
        bits.append(bit)
        bit *= 2
    return bits


def gather_dp(piece, ranks):
    me = lax.axis_index("dp")
    for bit in butterfly_bits(ranks)[1:] + [1]:
        other = lax.ppermute(piece, "dp", swap_pairs(ranks, bit))
        high = (me & bit) != 0
        pair = jnp.stack([jnp.where(high, other, piece), jnp.where(high, piece, other)])
        if bit == 1:
            piece = jnp.swapaxes(pair, 0, 1).reshape((-1,) + piece.shape[1:])
        else:
            piece = pair.reshape((-1,) + piece.shape[1:])
    return piece


def scatter_sum_dp(whole_sum, ranks, small):
    me = lax.axis_index("dp")
    value = whole_sum
    bits = butterfly_bits(ranks)
    for n, bit in enumerate([1] + bits[:0:-1]):
        if bit == 1:
            halves = value.reshape((ranks // 2, 2) + value.shape[1:])
            low, high = halves[:, 0], halves[:, 1]
        else:
            half = value.shape[0] // 2
            low, high = value[:half], value[half:]
        mine_high = (me & bit) != 0
        send = jnp.where(mine_high, low, high).astype(BF16)
        keep = jnp.where(mine_high, high, low)
        pairs = swap_pairs(ranks, bit)
        value = keep + lax.ppermute(send, "dp", pairs).astype(F32)
        hi = lax.reduce_precision(small, 8, 7)
        got = lax.ppermute(jnp.stack([hi, small - hi]).astype(BF16), "dp", pairs).astype(F32)
        small = small + (got[0] + got[1])
    return value[0], small


def gathered_weights(conv_w, cell_params, dp_at, groups, ranks, chans):
    share = conv_w.shape[2]
    wide = share * groups
    taps = conv_w.reshape(2, 4 * share, 9, chans + wide).astype(BF16)
    parts = [
        taps[..., chans:].reshape(2, 4 * share, 9 * wide),
        taps[..., :chans].reshape(2, 4 * share, 9 * chans),
    ]
    cells = jnp.stack([cell_params[:, :4], jnp.pad(cell_params[:, 4:], ((0, 0), (0, 1), (0, 0)))], -1)
    cell_hi = lax.reduce_precision(cells, 8, 7)
    cell_mid = lax.reduce_precision(cells - cell_hi, 8, 7)
    cell_lo = cells - cell_hi - cell_mid
    cell_parts = jnp.stack([cell_hi, cell_mid, cell_lo], -1).astype(BF16).reshape(2, 4 * share, 6)
    parts.append(jnp.pad(cell_parts, ((0, 0), (0, 0), (0, CELL_COLS - 6))))
    packed = jnp.concatenate(parts, -1)
    slab = 4 * share // ranks
    sent_w = packed.shape[-1]
    mine = lax.dynamic_slice_in_dim(packed.reshape(2, ranks, slab, sent_w), dp_at, 1, 1)[:, 0]
    everyone = lax.all_to_all(
        jnp.broadcast_to(mine[None], (groups, 2, slab, sent_w)), "gate", 0, 0, tiled=True
    )
    gathered = gather_dp(everyone[None], ranks)
    full = gathered.transpose(2, 1, 0, 3, 4).reshape(2, groups, 4, share, sent_w)
    full = full.transpose(0, 2, 1, 3, 4).reshape(2, 4 * wide, sent_w)
    return [full[0], full[1]]


def on_device(
    frames,
    regions,
    valid,
    step_count,
    conv_w,
    cell_params,
    head_w,
    head_b,
    conv_mom,
    cell_mom,
    head_mom,
    bias_mom,
    conv_avg,
    cell_avg,
    head_avg,
    bias_avg,
):
    share = conv_w.shape[2]
    chans = frames.shape[1]
    pixels = frames.shape[2]
    wide = head_w.shape[1]
    groups = lax.axis_size("gate")
    ranks = lax.axis_size("dp")
    geo = Geometry(groups, pixels)
    rows, own, halo, front, back, union = geo.rows, geo.own, geo.halo, geo.front, geo.back, geo.union
    gate_at = lax.axis_index("gate")
    dp_at = lax.axis_index("dp")

    order = ring_order(groups)
    place = [order.index(g) for g in range(groups)]
    spot = jnp.asarray(place, jnp.int32)[gate_at]
    from_right = [(order[(i + 1) % groups], order[i]) for i in range(groups)]
    from_left = [(order[i], order[(i + 1) % groups]) for i in range(groups)]

    slab = 4 * share // ranks
    packed_w = 9 * (wide + chans)
    sent_w = packed_w + CELL_COLS
    direct = ranks == 4 and slab == share and share % 16 == 0
    rank = dp_at.astype(jnp.int32).reshape(1)

    start = jnp.mod(spot * own - 2 * halo - 1, COLS).astype(jnp.int32).reshape(1)
    win, meta, mrm, mrp, mcm, mcp, counted = window_call(
        geo, start, frames.reshape(-1, pixels), valid, regions.reshape(1, pixels)
    )
    masks = (mrm, mrp, mcm, mcp)

    head_low = head_w.astype(BF16)
    head_bias = head_b[:, None]
    if direct:
        by_core, by_chip = swap_pairs(ranks, 1), swap_pairs(ranks, 2)
        cells_first = jnp.swapaxes(cell_params, 0, 1)
        mine0, mine1 = pack_call(groups, rank, conv_w, cells_first, sent_w)
        mixed0 = lax.all_to_all(mine0, "gate", 0, 0, tiled=True).reshape(groups * share, sent_w)
        mixed0, win, mine1 = lax.optimization_barrier((mixed0, win, mine1))
        over_x = lax.ppermute(mixed0, "dp", by_chip)
        over_core = lax.ppermute(mixed0, "dp", by_core)
        weights = [(rank, mixed0, over_core, over_x, lax.ppermute(over_x, "dp", by_core))]
        mixed1 = lax.all_to_all(mine1, "gate", 0, 0, tiled=True)
        weights.append((rank, mixed1))
    else:
        weights = gathered_weights(conv_w, cell_params, dp_at, groups, ranks, chans)

    state = ()
    kept = []
    t = 0
    for n, (layer, steps) in enumerate(geo.calls):
        base = n * halo
        first_frame = t if layer == 0 else t - 1
        got = forward_call(geo, layer, base, first_frame, steps, state, win, meta, weights[layer], masks)
        if len(got) > 7:
            weights[layer] = got[7]
        if direct and n == 0:
            mixed1, sent = lax.optimization_barrier((weights[1][1], got[6]))
            weights[1] = (rank, mixed1, lax.ppermute(mixed1, "dp", swap_pairs(ranks, 1)))
            got = [*got[:6], sent, *got[7:]]
        kept.append(dict(gates=got[0], cprev=got[1], hvar=got[2], hnew=got[3], xown=got[4], t=t))
        out = got[5]
        t += steps
        if n + 1 < len(geo.calls):
            far = lax.ppermute(got[6], "gate", from_right)
            state = (out, far)

    state = ()
    grads = [None, None]
    cell_sums = [None, None]
    head_sums = None
    for n in range(len(geo.calls) - 1, -1, -1):
        layer, steps = geo.calls[n]
        base = n * halo
        saved = kept[n]
        extra = (win, meta, head_low, head_bias) if layer == 1 else None
        carried = () if cell_sums[layer] is None else (cell_sums[layer], head_sums)
        got = backward_call(
            geo, layer, base, steps, n == 0, carried, state, saved, weights[layer], masks, extra
        )
        if n > 0:
            far = lax.ppermute(got[4], "gate", from_left)
            state = (got[3], far)
        cell_sums[layer] = got[1]
        if layer == 1:
            head_sums = got[2]
        done = direct and (n == 0 or geo.calls[n - 1][0] != layer)
        dz = got[0]
        if done and layer == 0:
            keep1, send1, dz = lax.optimization_barrier((*core_stage("1", rank, grads[1][0], crossed1, ()), dz))
            crossed1 = lax.ppermute(send1, "dp", swap_pairs(ranks, 2))
        grads[layer] = weight_call(
            geo,
            base,
            steps,
            grads[layer],
            dz,
            saved["hvar"],
            saved["xown"],
            masks[2],
            masks[3],
            rank if done else None,
            (cell_sums[0], cell_sums[1], grads[1][2], head_sums, counted) if done and layer == 0 else (),
        )
        if done and layer == 1:
            crossed1 = lax.ppermute(grads[1][1], "dp", swap_pairs(ranks, 1))
    if direct:
        pairs = swap_pairs(ranks, 1)
        across = swap_pairs(ranks, 2)
        keep0, send0, few = grads[0]
        send0, crossed1 = lax.optimization_barrier((send0, crossed1))
        crossed0 = lax.ppermute(send0, "dp", pairs)
        message1, crossed0 = lax.optimization_barrier((chip_stage("1", groups, keep1, crossed1, ()), crossed0))
        mixed1 = lax.all_to_all(message1, "gate", 0, 0, tiled=True)
        keep0, send0, few = core_stage("0", rank, keep0, crossed0, (few,))
        crossed0 = lax.ppermute(send0, "dp", across)
        shard1, crossed0 = lax.optimization_barrier((sum_stage("1", mixed1), crossed0))
        from_dp1 = [lax.ppermute(shard1, "dp", swap_pairs(ranks, k)) for k in (1, 2, 3)]
        message0 = chip_stage("0", groups, keep0, crossed0, (few,))
        mixed0 = lax.all_to_all(message0, "gate", 0, 0, tiled=True)
        *from_dp1, mixed0 = lax.optimization_barrier((*from_dp1, mixed0))
        total_pixels = EOUT * pixels * ranks
        flip = lambda v: jnp.swapaxes(v, 0, 1)
        small_args = [cells_first, flip(cell_mom), flip(cell_avg), head_w, head_mom, head_avg]
        small_args += [v[None] for v in (head_b, bias_mom, bias_avg)]
        rate = float(RATE_SCALE * chans * total_pixels**0.5)
        done = finish_stage(rate, chans, packed_w, mixed0, step_count, small_args)
        shard0, scalars, loss = done[:3]
        pieces = [shard0] + [lax.ppermute(shard0, "dp", swap_pairs(ranks, k)) for k in (1, 2, 3)]
        pieces += [shard1] + from_dp1
        outs = [loss[0, 0]]
        outs += update_call(rank, scalars, pieces, conv_w, conv_mom, conv_avg)
        outs += [flip(v) for v in done[3:7]] + list(done[7:11]) + [v[0] for v in done[11:15]]
        return tuple(outs)

    rate = RATE_SCALE * chans * jnp.sqrt(jnp.float32(EOUT * pixels * ranks))
    counts_done = step_count.astype(F32)
    biases = jnp.stack([g[packed_w].reshape(4, wide) for g in grads])
    cells = jnp.concatenate([biases, jnp.stack(cell_sums).reshape(2, 3, 8, wide).sum(2)], 1)
    grads = [g[:packed_w].T for g in grads]
    loss_sum = jnp.sum(head_sums[:, 129])
    shared_small = jnp.concatenate(
        [head_sums[:, :128].reshape(-1), head_sums[:, 128], loss_sum[None], counted[0, :1]]
    )
    small = jnp.concatenate([cells.reshape(-1), shared_small])
    big = jnp.stack(grads).reshape(2, 4, groups, share, packed_w).transpose(2, 1, 3, 0, 4)
    big = big.reshape(groups, ranks, slab, 2, packed_w).transpose(1, 0, 2, 3, 4)
    part, small = scatter_sum_dp(big, ranks, small)
    ncell = 14 * wide
    for_gate = small[:ncell].reshape(14, groups, share).transpose(1, 0, 2).reshape(groups, 14 * share)
    to_gate = jnp.concatenate(
        [for_gate, jnp.broadcast_to(small[None, ncell:], (groups, small.shape[0] - ncell))], 1
    )
    hi = lax.reduce_precision(to_gate, 8, 7)
    lo = (to_gate - hi).astype(BF16)
    hi = hi.astype(BF16)
    width = slab * 2 * packed_w
    message = jnp.concatenate([part.reshape(groups, width).astype(BF16), hi, lo], 1)
    got = lax.all_to_all(message, "gate", 0, 0, tiled=True).astype(F32)
    got = jnp.sum(got.reshape(groups, -1), 0)
    nsmall = to_gate.shape[1]
    small_sum = got[width : width + nsmall] + got[width + nsmall :]
    piece = got[:width].reshape(1, slab, 2, packed_w)
    rows_all = gather_dp(piece, ranks).reshape(4 * share, 2, packed_w).transpose(1, 0, 2)
    count = chans * small_sum[-1]
    scale = 2.0 / count
    rows_all = rows_all * scale
    grad_conv = jnp.concatenate(
        [
            rows_all[..., 9 * wide :].reshape(2, 4 * share, 9, chans),
            rows_all[..., : 9 * wide].reshape(2, 4 * share, 9, wide),
        ],
        -1,
    ).reshape(conv_w.shape)
    grad_cell = small_sum[: 14 * share].reshape(2, 7, share) * scale
    rest = small_sum[14 * share :]
    grad_head = rest[: chans * wide].reshape(chans, wide) * scale
    grad_bias = rest[chans * wide : chans * wide + chans] * scale
    loss = rest[chans * wide + chans] / count

    outs = [loss]
    outs += nesterov(conv_w, grad_conv, conv_mom, conv_avg, counts_done[0], rate)
    outs += nesterov(cell_params, grad_cell, cell_mom, cell_avg, counts_done[1], rate)
    outs += nesterov(head_w, grad_head, head_mom, head_avg, counts_done[2], rate)
    outs += nesterov(head_b, grad_bias, bias_mom, bias_avg, counts_done[3], rate)
    return tuple(outs)


def solution(mesh):
    in_specs = (
        P(None, None, "dp"),
        P("dp"),
        P(None, "dp"),
        P(),
        P(None, None, "gate", None),
        P(None, None, "gate"),
        P(),
        P(),
        P(None, None, "gate", None),
        P(None, None, "gate"),
        P(),
        P(),
        P(None, None, "gate", None),
        P(None, None, "gate"),
        P(),
        P(),
    )
    out_specs = (
        P(),
        P(None, None, "gate", None),
        P(None, None, "gate", None),
        P(None, None, "gate", None),
        P(None, None, "gate", None),
        P(None, None, "gate"),
        P(None, None, "gate"),
        P(None, None, "gate"),
        P(None, None, "gate"),
        P(),
        P(),
        P(),
        P(),
        P(),
        P(),
        P(),
        P(),
    )
    return jax.shard_map(
        on_device, mesh=mesh, in_specs=in_specs, out_specs=out_specs, check_vma=False
    )
```

```python
import functools

import jax
import jax.numpy as jnp
from jax import lax
from jax.experimental import pallas as pl
from jax.experimental.pallas import tpu as pltpu
from jax.sharding import PartitionSpec as P

EIN = 5
EOUT = 15
COLS = 128

MU = 0.9
RATE_SCALE = 0.05
F32 = jnp.float32
BF16 = jnp.bfloat16
VMEM_LIMIT = 60 * 1024 * 1024


def ring_order(groups):
    wide = groups // 4
    if wide <= 1:
        return list(range(groups))
    order = [(z, 0) for z in range(4)]
    for z in range(3, -1, -1):
        ys = range(1, wide) if z % 2 else range(wide - 1, 0, -1)
        order += [(z, y) for y in ys]
    return [z * wide + y for z, y in order]


def split_steps(steps, most):
    calls = -(-steps // most)
    base, extra = divmod(steps, calls)
    return [base + (1 if i < extra else 0) for i in range(calls)]


def nesterov(param, grad, mom, avg, steps_done, rate):
    mom_new = MU * mom + grad
    param_new = param - rate * (grad + MU * mom_new)
    avg_new = avg + (param_new - avg) / (steps_done + 1.0)
    return [mom_new, avg_new, param_new, param_new.astype(BF16)]


def logistic(v):
    return 0.5 * jnp.tanh(0.5 * v) + 0.5


def dot_nt(a, b):
    return lax.dot_general(a, b, (((1,), (1,)), ((), ())), preferred_element_type=F32)


def dot_tn(a, b):
    return lax.dot_general(a, b, (((0,), (0,)), ((), ())), preferred_element_type=F32)


def cut(total, pieces):
    base, extra = divmod(total, pieces)
    spans, at = [], 0
    for i in range(pieces):
        size = base + (1 if i < extra else 0)
        spans.append((at, size))
        at += size
    return spans


def cut_by_four(total, pieces):
    spans, at = [], 0
    for i in range(pieces):
        left = pieces - i
        size = total - at if left == 1 else (total - at) // left // 4 * 4
        if size:
            spans.append((at, size))
        at += size
    return spans


class Geometry:
    def __init__(self, groups, pixels):
        self.rows = pixels // COLS
        self.own = COLS // groups
        self.halo = min(5, self.own // 2)
        self.calls = [(0, n) for n in split_steps(EIN, self.halo)] + [(1, n) for n in split_steps(EOUT, self.halo)]
        self.front = self.own + 4 * self.halo
        self.back = self.own + 2 * self.halo
        self.union = self.front + (len(self.calls) - 1) * self.halo
        self.window = -(-(self.union + 2) * self.rows // 256) * 256


TAPS = [(dr, dc) for dr in (-1, 0, 1) for dc in (-1, 0, 1)]
CELL_COLS = 16


def window_kernel(geo, start, frames, valid, regions, win, meta, mrm, mrp, mcm, mcp, count, lhs, pick):
    rows, own, halo, union, width = geo.rows, geo.own, geo.halo, geo.union, geo.window
    nf = frames.shape[0]
    nv = valid.shape[0]
    lhs[:nf, :] = frames[...]
    lhs[nf : nf + nv, :] = valid[...].astype(F32).astype(BF16)
    lhs[nf + nv : nf + nv + 1, :] = regions[...].astype(F32).astype(BF16)
    per = 256 // rows
    source = lax.broadcasted_iota(jnp.int32, (COLS, 256), 0)
    lane = lax.broadcasted_iota(jnp.int32, (COLS, 256), 1)
    lane_row = lax.broadcasted_iota(jnp.int32, (1, 256), 1) % rows

    def one(n, carry):
        column = (start[0] + n * per + lane // rows) % COLS
        hit = (source == column).astype(F32).astype(BF16)
        for r in range(rows):
            keep = (lane_row == r).astype(F32).astype(BF16)
            pick[r * COLS : (r + 1) * COLS, :] = hit * keep
        got = jnp.dot(lhs[...], pick[...], preferred_element_type=F32)
        at = pl.multiple_of(n * 256, 256)
        win[:, pl.ds(at, 256)] = got[:nf].astype(BF16)
        meta[:, pl.ds(at, 256)] = got[nf:]
        return carry

    lax.fori_loop(0, width // 256, one, 0)
    px = union * rows
    ids = meta[nv : nv + 1, :]
    bands = jnp.floor(ids * 0.5)
    here = ids[:, rows : rows + px]
    band_here = bands[:, rows : rows + px]
    picked = [
        ids[:, rows - 1 : rows - 1 + px] == here,
        ids[:, rows + 1 : rows + 1 + px] == here,
        bands[:, :px] == band_here,
        bands[:, 2 * rows : 2 * rows + px] == band_here,
    ]
    row_at = lax.broadcasted_iota(jnp.int32, (8, px), 0)
    stack = jnp.zeros((8, px), F32)
    for k, m in enumerate(picked):
        stack = jnp.where(row_at == k, jnp.broadcast_to(m.astype(F32), (8, px)), stack)
    stack = stack.astype(BF16)
    sel = lax.broadcasted_iota(jnp.int32, (8, 128), 0)
    for k, out in enumerate((mrm, mrp, mcm, mcp)):
        out[...] = dot_tn(stack, (sel == k).astype(F32).astype(BF16)).astype(BF16)
    a = (2 * halo + 1) * rows
    count[...] = jnp.broadcast_to(jnp.sum(meta[:nv, a : a + own * rows]), count.shape)


def window_call(geo, start, frames, valid, regions):
    nf, nv = frames.shape[0], valid.shape[0]
    pixels = frames.shape[1]
    px = geo.union * geo.rows
    smem = pl.BlockSpec(memory_space=pltpu.SMEM)
    vmem = pl.BlockSpec(memory_space=pltpu.VMEM)
    total = nf + nv + 1
    return pl.pallas_call(
        functools.partial(window_kernel, geo),
        in_specs=[smem, vmem, vmem, vmem],
        out_specs=[vmem] * 7,
        out_shape=[
            jax.ShapeDtypeStruct((nf, geo.window), BF16),
            jax.ShapeDtypeStruct((nv + 1, geo.window), F32),
        ]
        + [jax.ShapeDtypeStruct((px, 128), BF16)] * 4
        + [jax.ShapeDtypeStruct((8, 128), F32)],
        scratch_shapes=[pltpu.VMEM((total, pixels), BF16), pltpu.VMEM((pixels, 256), BF16)],
        compiler_params=pltpu.CompilerParams(vmem_limit_bytes=VMEM_LIMIT),
        cost_estimate=pl.CostEstimate(
            flops=2 * total * pixels * geo.window, bytes_accessed=10 << 20, transcendentals=0
        ),
        name="window",
    )(start, frames, valid, regions)


def pack_kernel(groups, rank, conv, cells, out0, out1):
    share, depth9 = conv.shape[2:]
    chans9 = out0.shape[-1] - CELL_COLS - 9 * 128
    chans = chans9 // 9
    depth = chans + 128
    row = lax.broadcasted_iota(jnp.int32, (7, CELL_COLS), 0)
    col = lax.broadcasted_iota(jnp.int32, (7, CELL_COLS), 1)
    half = (rank[0] & 1) * 2
    for l, at, gate, out in ((0, 0, rank[0], out0), (1, 0, half, out1), (1, share, half + 1, out1)):
        w = conv[l, gate].astype(BF16)
        parts = [w[:, k * depth + chans : (k + 1) * depth] for k in range(9)]
        parts += [w[:, k * depth : k * depth + chans] for k in range(9)]
        rest = cells[:, l, :]
        cols = jnp.zeros((share, CELL_COLS), F32)
        for k in range(3):
            low = rest.astype(BF16)
            rest = rest - low.astype(F32)
            sel = ((row == gate) & (col == k)) | ((row == gate + 4) & (col == 3 + k))
            cols = cols + dot_tn(low, sel.astype(F32).astype(BF16))
        parts.append(cols.astype(BF16))
        line = jnp.concatenate(parts, 1)
        for g in range(groups):
            out[g, at : at + share, :] = line


def pack_call(groups, rank, conv_w, cells, sent_w):
    share = conv_w.shape[2]
    return plain_call(
        functools.partial(pack_kernel, groups),
        "pack",
        [jax.ShapeDtypeStruct((groups, k * share, sent_w), BF16) for k in (1, 2)],
        rank,
        conv_w,
        cells,
        smem=1,
    )


def peephole_rows(wf):
    tail = wf[:, 9 * 128 :]
    depth = tail.shape[1]
    col = lax.broadcasted_iota(jnp.int32, (8, depth), 1)
    at = depth - CELL_COLS + 3
    sel = ((col >= at) & (col < at + 3)).astype(F32).astype(BF16)
    got = dot_nt(sel, tail)
    return [got[0:1, k * 128 : (k + 1) * 128] for k in range(3)]


def make_variants(geo, h, r0, hb, mrm, mrp, base):
    m = h.shape[0]
    g0 = base * geo.rows + r0
    hb[0, r0 : r0 + m, :] = pltpu.roll(h, 1, 0).astype(BF16) * mrm[g0 : g0 + m, :]
    hb[1, r0 : r0 + m, :] = h.astype(BF16)
    hb[2, r0 : r0 + m, :] = pltpu.roll(h, m - 1, 0).astype(BF16) * mrp[g0 : g0 + m, :]


def forward_kernel(geo, layer, base, steps, first, gather, *refs):
    refs = list(refs)
    if gather:
        rank, pieces, refs = refs[0], refs[1 : 1 + gather], refs[1 + gather :]
    if not first:
        near, far = refs[:2]
        refs = refs[2:]
    if gather:
        cols, win, meta, mrm, mrp = refs[:5]
        wf = refs[12]
        refs = refs[5:12] + refs[13:]
    else:
        cols, win, meta, wf, mrm, mrp = refs[:6]
        refs = refs[6:]
    gates_out, cprev_out, hvar_out, hnew_out, xown_out, state_out, send_out = refs[:7]
    hb, hnext, cb, xs, keeps, peeps = refs[7:]
    rows, halo, own, front, back = geo.rows, geo.halo, geo.own, geo.front, geo.back
    chans = win.shape[0]
    chans9 = 9 * chans
    lanes = (front - 2) * rows
    x0 = (base + 2) * rows
    step = pl.program_id(0)

    @pl.when(step == 0)
    def _():
        hb[:, front * rows :, :] = jnp.zeros((3, rows, 128), BF16)
        if first:
            hb[:, : front * rows, :] = jnp.zeros((3, front * rows, 128), BF16)
            hnext[...] = jnp.zeros_like(hnext)
            cb[...] = jnp.zeros_like(cb)
        else:
            nb = back * rows
            make_variants(geo, near[:, :128].astype(F32), 0, hb, mrm, mrp, base)
            make_variants(geo, far[:, :128].astype(F32), nb, hb, mrm, mrp, base)
            for c in (0, front - 1):
                hnext[:, c * rows : (c + 1) * rows, :] = jnp.zeros((3, rows, 128), BF16)
            cb[:nb, :] = near[:, 128:].astype(F32)
            cb[nb:, :] = far[:, 128:].astype(F32)
        if gather:
            for k, piece in enumerate(pieces):
                if gather == 4:
                    wf[pl.ds(pl.multiple_of((rank[0] ^ k) * 128, 128), 128), :] = piece[...]
                    continue
                peers, span = piece.shape[0], piece.shape[1] // 2
                half = pl.multiple_of(((rank[0] ^ k) & 1) * 256, 256)
                for g in range(peers):
                    for j in range(2):
                        at = pl.multiple_of(half + j * 128 + g * span, span)
                        wf[pl.ds(at, span), :] = piece[g, j * span : (j + 1) * span, :]
        ids = meta[meta.shape[0] - 1 :, :]
        here = ids[:, x0 : x0 + lanes]
        for tap, (dr, dc) in enumerate(TAPS):
            off = x0 + dc * rows + dr
            same = (ids[:, off : off + lanes] == here).astype(F32)
            keeps[tap * chans : (tap + 1) * chans, :] = jnp.broadcast_to(same, (chans, lanes)).astype(BF16)
        ones = lax.broadcasted_iota(jnp.int32, (CELL_COLS, lanes), 0) < 3
        xs[chans9:, :] = ones.astype(F32).astype(BF16)
        for k, row in enumerate(peephole_rows(wf)):
            peeps[k : k + 1, :] = row

    s0, sn = (2 * halo - 1) * rows, (own + 2) * rows
    for v in range(3):
        hvar_out[0, v, :, :] = hb[v, s0 : s0 + sn, :]
    cprev_out[0, :, :] = cb[halo * rows : (halo + back) * rows, :].astype(BF16)
    for tap, (dr, dc) in enumerate(TAPS):
        off = x0 + dc * rows + dr
        part = slice(tap * chans, (tap + 1) * chans)
        xs[part, :] = win[:, off : off + lanes] * keeps[part, :]
    q0 = (2 * halo - 1) * rows
    xown_out[0, :, :] = xs[:, q0 : q0 + own * rows]

    for c0, cw in cut_by_four(front - 2, 4):
        r0, m = (c0 + 1) * rows, cw * rows
        zero = front * rows
        lefts, rights = [], []
        for c in range(c0 + 1, c0 + 1 + cw):
            for at, side, starts in ((c - 1, 0, lefts), (c + 1, 1, rights)):
                starts.append(pl.multiple_of(zero + cols[side * geo.union + base + c] * (at * rows - zero), rows))
        parts = []
        for dr in range(3):
            parts.append(jnp.concatenate([hb[dr, pl.ds(at, rows), :] for at in lefts], 0))
            parts.append(hb[dr, r0 : r0 + m, :])
            parts.append(jnp.concatenate([hb[dr, pl.ds(at, rows), :] for at in rights], 0))
        z = dot_nt(jnp.concatenate(parts, 1), wf[:, : 9 * 128]) + lax.dot_general(
            xs[:, r0 - rows : r0 - rows + m], wf[:, 9 * 128 :], (((0,), (1,)), ((), ())), preferred_element_type=F32
        )
        c = cb[r0 : r0 + m, :]
        gi = logistic(z[:, 0:128] + peeps[0:1, :] * c)
        gf = logistic(z[:, 128:256] + peeps[1:2, :] * c)
        gg = jnp.tanh(z[:, 384:512])
        cn = gf * c + gi * gg
        go = logistic(z[:, 256:384] + peeps[2:3, :] * cn)
        h = go * jnp.tanh(cn)
        cb[r0 : r0 + m, :] = cn
        make_variants(geo, h, r0, hnext, mrm, mrp, base)
        lo, hi = max(c0 + 1, halo), min(c0 + 1 + cw, halo + back)
        a, b = (lo - c0 - 1) * rows, (hi - c0 - 1) * rows
        o = (lo - halo) * rows
        n = b - a
        if n > 0:
            gates_out[0, 0, o : o + n, :] = gi[a:b].astype(BF16)
            gates_out[0, 1, o : o + n, :] = gf[a:b].astype(BF16)
            gates_out[0, 2, o : o + n, :] = go[a:b].astype(BF16)
            gates_out[0, 3, o : o + n, :] = gg[a:b].astype(BF16)
            hnew_out[0, o : o + n, :] = h[a:b].astype(BF16)

    hb[:, : front * rows, :] = hnext[...]

    @pl.when(step == steps - 1)
    def _():
        a, b = halo * rows, (halo + back) * rows
        state_out[:, :128] = hb[1, a:b, :]
        state_out[:, 128:] = cb[a:b, :].astype(BF16)
        a, b = 3 * halo * rows, 5 * halo * rows
        send_out[:, :128] = hb[1, a:b, :]
        send_out[:, 128:] = cb[a:b, :].astype(BF16)


def whole(shape):
    return pl.BlockSpec(shape, lambda *_: (0,) * len(shape))


def forward_call(geo, layer, base, first_frame, steps, state, win, meta, weights, masks):
    rows, own, front, back = geo.rows, geo.own, geo.front, geo.back
    chans = win.shape[0] // (EIN + EOUT)
    gather = len(weights) - 1 if isinstance(weights, tuple) else 0
    sent_w = weights[1].shape[-1] if gather else weights.shape[1]
    depth = sent_w - 9 * 128
    by_step = lambda *dims: pl.BlockSpec((1,) + dims, lambda t: (t,) + (0,) * len(dims))
    lead = list(weights) if gather else []
    cols, masks = masks[4], masks[:2]
    smem = pl.BlockSpec(memory_space=pltpu.SMEM)
    operands = lead + list(state) + [cols, win, meta] + ([] if gather else [weights]) + list(masks)
    in_specs = [smem] if gather else []
    in_specs += [whole(v.shape) for v in lead[1:]]
    in_specs += [whole(s.shape) for s in state]
    in_specs += [smem, pl.BlockSpec((chans, win.shape[1]), lambda t: (first_frame + t, 0))]
    in_specs += [whole(v.shape) for v in operands[len(lead) + len(state) + 2 :]]
    shapes = [
        (steps, 4, back * rows, 128),
        (steps, back * rows, 128),
        (steps, 3, (own + 2) * rows, 128),
        (steps, back * rows, 128),
        (steps, depth, own * rows),
    ]
    flat = [(back * rows, 256), (2 * geo.halo * rows, 256)] + ([(512, sent_w)] if gather else [])
    outs = [jax.ShapeDtypeStruct(s, BF16) for s in shapes + flat]
    out_specs = [by_step(*s[1:]) for s in shapes] + [whole(s) for s in flat]
    px = front * rows
    return pl.pallas_call(
        functools.partial(forward_kernel, geo, layer, base, steps, not state, gather),
        grid=(steps,),
        in_specs=in_specs,
        out_specs=out_specs,
        out_shape=outs,
        scratch_shapes=[
            pltpu.VMEM((3, px + rows, 128), BF16),
            pltpu.VMEM((3, px, 128), BF16),
            pltpu.VMEM((px, 128), F32),
            pltpu.VMEM((depth, px - 2 * rows), BF16),
            pltpu.VMEM((9 * chans, px - 2 * rows), BF16),
            pltpu.VMEM((8, 128), F32),
        ],
        compiler_params=pltpu.CompilerParams(vmem_limit_bytes=VMEM_LIMIT),
        cost_estimate=pl.CostEstimate(
            flops=steps * px * 512 * 1296 * 2, bytes_accessed=8 << 20, transcendentals=steps * px * 640
        ),
        name=f"forward_{base}",
    )(*operands)


def backward_kernel(geo, layer, base, steps, first_live, first, last, carried, *refs):
    refs = list(refs)
    if carried:
        sums_in, head_in = refs[:2]
        refs = refs[2:]
    if not first:
        local, far = refs[:2]
        refs = refs[2:]
    cols, gates, cprev, wf, mrm, mrp = refs[:6]
    refs = refs[6:]
    if layer == 1:
        hnew, target, meta, head, head_b = refs[:5]
        refs = refs[5:]
    dz_out, sums_out, head_out, carry_out, send_out = refs[:5]
    dh, dc, dz_near, dz_far, peeps, wb = refs[5:]
    rows, halo, own, back = geo.rows, geo.halo, geo.own, geo.back
    o0, on = halo * rows, own * rows
    half = back // 2
    step = pl.program_id(0)

    @pl.when(step == 0)
    def _():
        sums_out[...] = sums_in[...] if carried else jnp.zeros_like(sums_out)
        head_out[...] = head_in[...] if carried else jnp.zeros_like(head_out)
        for tap in range(9):
            across, along = tap % 3 * 512, tap // 3 * 128
            wb[across : across + 512, along : along + 128] = wf[:, tap * 128 : (tap + 1) * 128]
        edge = jnp.zeros((4, rows, 128), BF16)
        dz_near[:, :rows, :] = edge
        dz_far[:, :rows, :] = edge
        dz_far[:, (back - half) * rows :, :] = edge
        for k, row in enumerate(peephole_rows(wf)):
            peeps[k : k + 1, :] = row
        if first:
            dh[...] = jnp.zeros_like(dh)
            dc[...] = jnp.zeros_like(dc)
        else:
            nf = 2 * halo * rows
            dh[:nf, :] = far[:, :128]
            dc[:nf, :] = far[:, 128:]
            dh[nf:, :] = local[:, :128]
            dc[nf:, :] = local[:, 128:]

    if layer == 1:
        guess = dot_nt(head[...], hnew[0]) + head_b[...]
        a0 = (base + halo + 1) * rows
        err = guess - target[:, a0 : a0 + back * rows].astype(F32)
        dy = meta[pl.ds(first_live + steps - 1 - step, 1), a0 : a0 + back * rows] * err
        low = dy.astype(BF16)
        head_out[:, 0:128] += jnp.dot(low[:, o0 : o0 + on], hnew[0, o0 : o0 + on, :], preferred_element_type=F32)
        own_dy = low[:, o0 : o0 + on].astype(F32)
        head_out[:, 128:129] += jnp.sum(own_dy, 1, keepdims=True)
        head_out[:, 129:130] += jnp.sum((dy * err)[:, o0 : o0 + on], 1, keepdims=True)
        dh[...] = (dh[...].astype(F32) + dot_tn(low, head[...])).astype(BF16)

    def gates_chunk(c0, cw):
        r0, m = c0 * rows, cw * rows
        span = slice(r0, r0 + m)
        gi, gf, go, gg = (gates[0, n, span, :] for n in range(4))
        pi, pf, po = (peeps[n : n + 1, :].astype(BF16) for n in range(3))
        c = cprev[0, span, :]
        cn = gf * c + gi * gg
        tc = jnp.tanh(cn)
        u = dh[span, :] * go
        w = u * tc
        d_o = w * (1 - go)
        d_c = dc[span, :] + u * ((1 - tc) * (1 + tc)) + d_o * po
        a_i = d_c * gi
        d_i = a_i * gg * (1 - gi)
        d_g = a_i * ((1 - gg) * (1 + gg))
        a_f = d_c * gf
        d_f = a_f * c * (1 - gf)
        dc[span, :] = a_f + d_i * pi + d_f * pf
        store, p0 = (dz_near, rows + r0) if c0 <= half else (dz_far, r0 - half * rows)
        for n, d in enumerate((d_i, d_f, d_o, d_g)):
            store[n, p0 : p0 + m, :] = d
        a = max(r0, o0) - r0
        b = min(r0 + m, o0 + on) - r0
        if b > a:
            for n, d in enumerate((d_i * c, d_f * c, d_o * cn)):
                part = d[a:b].astype(F32).reshape((b - a) // 8, 8, 128)
                sums_out[n * 8 : (n + 1) * 8, :] += jnp.sum(part, 0)

    def hidden_chunk(c0, cw):
        r0, m = c0 * rows, cw * rows
        g0 = (base + halo) * rows + r0
        parts = []
        for side, shift in ((0, 1), (None, 0), (1, -1)):
            pieces = []
            for c in range(c0 + shift, c0 + cw + shift):
                ref, at = (dz_near, (c + 1) * rows) if c <= half else (dz_far, (c - half) * rows)
                if side is not None:
                    at = pl.multiple_of(cols[side * geo.union + base + halo + c] * at, rows)
                pieces.append((ref, at))
            for n in range(4):
                parts.append(jnp.concatenate([ref[n, pl.ds(at, rows), :] for ref, at in pieces], 0))
        acc = jnp.dot(jnp.concatenate(parts, 1), wb[...], preferred_element_type=F32)
        above = pltpu.roll(acc[:, :128] * mrm[g0 : g0 + m, :].astype(F32), m - 1, 0)
        below = pltpu.roll(acc[:, 256:] * mrp[g0 : g0 + m, :].astype(F32), 1, 0)
        dh[r0 : r0 + m, :] = (acc[:, 128:256] + above + below).astype(BF16)

    for c0, cw in cut(half + 1, 2):
        gates_chunk(c0, cw)
    hidden_chunk(0, half)
    for c0, cw in cut(back - half - 1, 2):
        gates_chunk(half + 1 + c0, cw)
    hidden_chunk(half, back - half)
    lo = (half + 1 - halo) * rows
    for n in range(4):
        dz_out[0, :lo, n * 128 : (n + 1) * 128] = dz_near[n, rows + o0 : rows + o0 + lo, :]
        dz_out[0, lo:, n * 128 : (n + 1) * 128] = dz_far[n, rows : rows + on - lo, :]

    @pl.when(step == steps - 1)
    def _():
        carry_out[:, :128] = dh[o0 : o0 + on, :]
        carry_out[:, 128:] = dc[o0 : o0 + on, :]
        ns = 2 * halo * rows
        s0 = o0 + on - ns
        send_out[:, :128] = dh[s0 : s0 + ns, :]
        send_out[:, 128:] = dc[s0 : s0 + ns, :]


def backward_call(geo, layer, base, steps, last, carried, state, saved, wf, masks, extra):
    rows, own, back, halo = geo.rows, geo.own, geo.back, geo.halo
    by_step = lambda *dims: pl.BlockSpec((1,) + dims, lambda t: (steps - 1 - t,) + (0,) * len(dims))
    first_live = saved["t"] - EIN
    lead = list(carried) + list(state)
    cols, masks = masks[4], masks[:2]
    operands = lead + [cols, saved["gates"], saved["cprev"], wf] + list(masks)
    in_specs = [whole(s.shape) for s in lead] + [pl.BlockSpec(memory_space=pltpu.SMEM)]
    in_specs += [by_step(4, back * rows, 128), by_step(back * rows, 128)]
    in_specs += [whole(v.shape) for v in operands[len(lead) + 3 :]]
    if layer == 1:
        win, meta, head, head_b = extra
        operands += [saved["hnew"], win, meta, head, head_b]
        t0 = saved["t"]
        in_specs += [
            by_step(back * rows, 128),
            pl.BlockSpec((head.shape[0], win.shape[1]), lambda t: (t0 + steps - 1 - t, 0)),
            whole(meta.shape),
            whole(head.shape),
            whole(head_b.shape),
        ]
    outs = [
        jax.ShapeDtypeStruct((steps, own * rows, 512), BF16),
        jax.ShapeDtypeStruct((24, 128), F32),
        jax.ShapeDtypeStruct((16, 256), F32),
        jax.ShapeDtypeStruct((own * rows, 256), BF16),
        jax.ShapeDtypeStruct((2 * halo * rows, 256), BF16),
    ]
    out_specs = [by_step(own * rows, 512)] + [whole(o.shape) for o in outs[1:]]
    px = back * rows
    return pl.pallas_call(
        functools.partial(backward_kernel, geo, layer, base, steps, first_live, not state, last, bool(carried)),
        grid=(steps,),
        in_specs=in_specs,
        out_specs=out_specs,
        out_shape=outs,
        scratch_shapes=[
            pltpu.VMEM((px, 128), BF16),
            pltpu.VMEM((px, 128), BF16),
            pltpu.VMEM((4, (back // 2 + 2) * rows, 128), BF16),
            pltpu.VMEM((4, (back - back // 2 + 1) * rows, 128), BF16),
            pltpu.VMEM((8, 128), F32),
            pltpu.VMEM((3 * 512, 3 * 128), BF16),
        ],
        compiler_params=pltpu.CompilerParams(vmem_limit_bytes=VMEM_LIMIT),
        cost_estimate=pl.CostEstimate(
            flops=steps * px * 512 * 1536 * 2, bytes_accessed=8 << 20, transcendentals=steps * px * 128
        ),
        name=f"backward_{base}",
    )(*operands)


def split_low(v, axis=0):
    hi = v.astype(BF16)
    return jnp.concatenate([hi, (v - hi.astype(F32)).astype(BF16)], axis)


def joined(v):
    half = v.shape[0] // 2
    return v[:half].astype(F32) + v[half:].astype(F32)


def weight_kernel(geo, base, steps, add, final, small, *refs):
    refs = list(refs)
    if final:
        rank, refs = refs[0], refs[1:]
    if add:
        acc, refs = refs[0], refs[1:]
    if small:
        sums0, sums1, bias1, head, count = refs[:5]
        refs = refs[5:]
    dz, hvar, xown, mcm, mcp = refs[:5]
    outs, rhs = refs[5:-1], refs[-1]
    rows, own, halo = geo.rows, geo.own, geo.halo
    on = own * rows
    g0 = (base + 2 * halo) * rows
    wide = hvar.shape[-1]
    part = pl.program_id(0)
    if final:
        odd = (rank[0] & 1) == 1

    def put(g):
        at = slice(0, g.shape[0])
        if add:
            g = g + acc[at, :]
        if not final:
            outs[0][at, :] = g
            return g
        keep, send = outs[:2]
        for j in range(2):
            even_gate = g[:, 2 * j * wide : (2 * j + 1) * wide]
            odd_gate = g[:, (2 * j + 1) * wide : (2 * j + 2) * wide]
            keep[j, at, :] = jnp.where(odd, odd_gate, even_gate)
            send[j, at, :] = jnp.where(odd, even_gate, odd_gate).astype(BF16)
        return g

    @pl.when(part < 3)
    def _():
        for dc in range(3):
            for j in range(steps):
                v = hvar[j, 0, dc * rows : dc * rows + on, :]
                if dc == 0:
                    v = v * mcm[g0 : g0 + on, :]
                elif dc == 2:
                    v = v * mcp[g0 : g0 + on, :]
                rhs[j * on : (j + 1) * on, dc * wide : (dc + 1) * wide] = v
        put(dot_tn(rhs[...], dz[...]))

    @pl.when(part == 3)
    def _():
        depth = xown.shape[1]
        inputs = None
        for j in range(steps):
            got = jnp.dot(xown[j], dz[j * on : (j + 1) * on, :], preferred_element_type=F32)
            inputs = got if inputs is None else inputs + got
        bias = put(inputs)[depth - CELL_COLS : depth - CELL_COLS + 8]
        if final and not small:
            outs[2][...] = bias
        if small:
            few = []
            for row, sums in ((bias, sums0), (bias1[...], sums1)):
                few += [row[0:1, k * wide : (k + 1) * wide] for k in range(4)]
                few.append(jnp.sum(sums[...].reshape(3, 8, wide), 1))
            few = jnp.concatenate(few + [jnp.zeros((2, wide), F32)], 0)
            col = lax.broadcasted_iota(jnp.int32, (16, wide), 1)
            extra = jnp.where(col == 2, jnp.broadcast_to(count[0:1, :], (16, wide)), head[:, wide:])
            few = jnp.concatenate([few, head[:, :wide], extra], 0)
            outs[2][...] = few
            outs[1][0, depth : depth + 96, :] = split_low(few)


def weight_call(geo, base, steps, acc, dz, hvar, xown, mcm, mcp, rank=None, small=()):
    on = geo.own * geo.rows
    dz = dz.reshape(steps * on, 512)
    final = rank is not None
    band = 3 * hvar.shape[-1]
    operands = ([rank] if final else []) + ([] if acc is None else [acc]) + list(small) + [dz, hvar, xown, mcm, mcp]
    specs = [pl.BlockSpec(memory_space=pltpu.SMEM)] if final else []
    specs += [] if acc is None else [pl.BlockSpec((band, 512), lambda i: (i, 0))]
    specs += [whole(v.shape) for v in small] + [whole(dz.shape)]
    specs += [pl.BlockSpec((steps, 1) + hvar.shape[2:], lambda i: (0, jnp.minimum(i, 2), 0, 0))]
    specs += [whole(v.shape) for v in (xown, mcm, mcp)]
    out_shape = jax.ShapeDtypeStruct((4 * band, 512), F32)
    out_specs = pl.BlockSpec((band, 512), lambda i: (i, 0))
    if final:
        out_shape = [
            jax.ShapeDtypeStruct((2, 4 * band, 128), F32),
            jax.ShapeDtypeStruct((2, 4 * band, 128), BF16),
            jax.ShapeDtypeStruct((48, 128) if small else (8, 512), F32),
        ]
        out_specs = [pl.BlockSpec((2, band, 128), lambda i: (0, i, 0))] * 2 + [whole(out_shape[2].shape)]
    return pl.pallas_call(
        functools.partial(weight_kernel, geo, base, steps, acc is not None, final, bool(small)),
        grid=(4,),
        in_specs=specs,
        out_specs=out_specs,
        out_shape=out_shape,
        scratch_shapes=[pltpu.VMEM((steps * on, band), BF16)],
        compiler_params=pltpu.CompilerParams(vmem_limit_bytes=VMEM_LIMIT),
        cost_estimate=pl.CostEstimate(
            flops=steps * on * 512 * 1296 * 2, bytes_accessed=16 << 20, transcendentals=0
        ),
        name=f"weights_{base}",
    )(*operands)


SMALL_AT = 1408


def core_stage_kernel(rank, keep, got, *refs):
    depth = refs[1].shape[0] if len(refs) > 2 else refs[0].shape[0]
    high = (rank[0] & 2) == 2
    small = len(refs) > 2
    if small:
        few, keep_out, send_out, few_out = refs
    else:
        keep_out, send_out = refs
    a = keep[0, :depth, :] + got[0, :depth, :].astype(F32)
    b = keep[1, :depth, :] + got[1, :depth, :].astype(F32)
    keep_out[...] = jnp.where(high, b, a)
    send_out[:depth, :] = jnp.where(high, a, b).astype(BF16)
    if small:
        total = few[...] + joined(got[0, depth : depth + 96, :])
        few_out[...] = total
        send_out[depth:, :] = split_low(total)


def chip_stage_kernel(groups, keep, got, *refs):
    depth, wide = keep.shape
    small = len(refs) > 1
    if small:
        few, out = refs
    else:
        (out,) = refs
    width = depth - CELL_COLS
    share = wide // groups
    total = (keep[...] + got[:depth, :].astype(F32)).T[:, :width].astype(BF16)
    if small:
        sums = few[...] + joined(got[depth:, :])
        head = split_low(sums[16:32], 1)
        extra = split_low(sums[32:, :16], 1)
        fill = jnp.zeros((16, SMALL_AT - width - 2 * share - 32), BF16)
    for g in range(groups):
        part = total[g * share : (g + 1) * share, :]
        if not small:
            out[g, :, :] = part
        else:
            cells = split_low(sums[:16, g * share : (g + 1) * share], 1)
            out[g, :, :] = jnp.concatenate([part, cells, extra, fill, head], 1)


def sum_stage_kernel(got, out):
    total = got[0].astype(F32)
    for g in range(1, got.shape[0]):
        total = total + got[g].astype(F32)
    out[...] = total


def finish_kernel(rate, chans, got, steps_done, *refs):
    (cell_refs, head_refs, bias_refs), refs = (refs[:3], refs[3:6], refs[6:9]), refs[9:]
    shard, scalars, loss, cell_outs, head_outs, bias_outs = refs[0], refs[1], refs[2], refs[3:7], refs[7:11], refs[11:]
    total = got[0].astype(F32)
    for g in range(1, got.shape[0]):
        total = total + got[g].astype(F32)
    width = shard.shape[1]
    share = total.shape[0]
    shard[...] = total[:, :width]
    cells = total[:, width : width + share] + total[:, width + share : width + 2 * share]
    at = width + 2 * share
    extra = total[:, at : at + 16] + total[:, at + 16 : at + 32]
    head = total[:, SMALL_AT : SMALL_AT + 128] + total[:, SMALL_AT + 128 :]
    count = chans * extra[0:1, 2:3]
    scale = 2.0 / count
    fresh = [1.0 / (jnp.full((1, 1), steps_done[k].astype(F32)) + 1.0) for k in range(4)]
    loss[...] = jnp.sum(extra[:, 1:2], 0, keepdims=True) / count
    lane = lax.broadcasted_iota(jnp.int32, (8, 128), 1)
    scalars[...] = jnp.where(lane == 0, scale, jnp.where(lane == 1, rate, fresh[0]))

    def update(refs, outs, at, grad, fresh):
        param, mom, avg = (v[at] for v in refs)
        grad = grad * scale
        m = MU * mom + grad
        p = param - rate * (grad + MU * m)
        outs[0][at] = m
        outs[1][at] = avg + (p - avg) * fresh
        outs[2][at] = p
        outs[3][at] = p.astype(BF16)

    for l in range(2):
        update(cell_refs, cell_outs, (slice(None), l, slice(None)), cells[l * 7 : (l + 1) * 7, :], fresh[1])
    update(head_refs, head_outs, (slice(None), slice(None)), head, fresh[2])
    row = lax.broadcasted_iota(jnp.int32, (16, 16), 0)
    col = lax.broadcasted_iota(jnp.int32, (16, 16), 1)
    bias = jnp.sum(jnp.where(row == col, jnp.broadcast_to(extra[:, 0:1], (16, 16)), 0.0), 0, keepdims=True)
    update(bias_refs, bias_outs, (slice(None), slice(None)), bias, fresh[3])


def plain_call(kernel, name, out_shape, *operands, smem=0, moved=4 << 20, smem_at=()):
    where = [pltpu.SMEM if i < smem or i in smem_at else pltpu.VMEM for i in range(len(operands))]
    specs = [pl.BlockSpec(memory_space=m) for m in where]
    return pl.pallas_call(
        kernel,
        in_specs=specs,
        out_shape=out_shape,
        compiler_params=pltpu.CompilerParams(vmem_limit_bytes=VMEM_LIMIT),
        cost_estimate=pl.CostEstimate(flops=1 << 20, bytes_accessed=moved, transcendentals=0),
        name=name,
    )(*operands)


def core_stage(name, rank, depth, keep, got, small):
    wide = keep.shape[2]
    more = 96 if small else 0
    shapes = [jax.ShapeDtypeStruct((depth, wide), F32), jax.ShapeDtypeStruct((depth + more, wide), BF16)]
    shapes += [jax.ShapeDtypeStruct(v.shape, F32) for v in small]
    return plain_call(core_stage_kernel, "core_stage_" + name, shapes, rank, keep, got, *small, smem=1)


def chip_stage(name, groups, keep, got, small):
    depth, wide = keep.shape
    lanes = SMALL_AT + 256 if small else depth - CELL_COLS
    shape = jax.ShapeDtypeStruct((groups, wide // groups, lanes), BF16)
    kernel = functools.partial(chip_stage_kernel, groups)
    return plain_call(kernel, "chip_stage_" + name, shape, keep, got, *small, moved=2 << 20)


def sum_stage(name, got):
    shape = jax.ShapeDtypeStruct(got.shape[1:], F32)
    return plain_call(sum_stage_kernel, "sum_stage_" + name, shape, got, moved=1 << 20)


def finish_stage(rate, chans, width, got, step_count, small_args):
    shapes = [
        jax.ShapeDtypeStruct((got.shape[1], width), F32),
        jax.ShapeDtypeStruct((8, 128), F32),
        jax.ShapeDtypeStruct((1, 1), F32),
    ]
    for v in small_args[::3]:
        shapes += [jax.ShapeDtypeStruct(v.shape, F32)] * 3 + [jax.ShapeDtypeStruct(v.shape, BF16)]
    kernel = functools.partial(finish_kernel, rate, chans)
    return plain_call(kernel, "finish", shapes, got, step_count, *small_args, moved=1 << 20, smem_at=(1,))


def update_kernel(rank, scalars, *refs):
    pieces = (refs[:4], refs[4:8])
    param, mom, avg, mom_out, avg_out, new_out, low_out, grad = refs[8:]
    layer = pl.program_id(0)
    chans = (grad.shape[-1] - 9 * 128) // 9
    scale, rate, fresh = (scalars[0:1, k : k + 1] for k in range(3))
    for l in range(2):

        @pl.when(layer == l)
        def _():
            for k, piece in enumerate(pieces[l]):
                v = piece[...]
                parts = []
                for tap in range(9):
                    parts.append(v[:, 9 * 128 + tap * chans : 9 * 128 + (tap + 1) * chans])
                    parts.append(v[:, tap * 128 : (tap + 1) * 128])
                grad[rank[0] ^ k] = jnp.concatenate(parts, 1) * scale

    g = grad[...]
    m = MU * mom[0] + g
    p = param[0] - rate * (g + MU * m)
    mom_out[0] = m
    new_out[0] = p
    low_out[0] = p.astype(BF16)
    avg_out[0] = avg[0] + (p - avg[0]) * fresh


def update_call(rank, scalars, pieces, param, mom, avg):
    layers, gates, share, width = param.shape
    block = pl.BlockSpec((1, gates, share, width), lambda l: (l, 0, 0, 0))
    smem = pl.BlockSpec(memory_space=pltpu.SMEM)
    shape = jax.ShapeDtypeStruct(param.shape, F32)
    return pl.pallas_call(
        update_kernel,
        grid=(layers,),
        in_specs=[smem, whole(scalars.shape)] + [whole(v.shape) for v in pieces] + [block] * 3,
        out_specs=[block] * 4,
        out_shape=[shape] * 3 + [jax.ShapeDtypeStruct(param.shape, BF16)],
        scratch_shapes=[pltpu.VMEM((gates, share, width), F32)],
        compiler_params=pltpu.CompilerParams(vmem_limit_bytes=VMEM_LIMIT),
        cost_estimate=pl.CostEstimate(flops=1 << 20, bytes_accessed=6 << 20, transcendentals=0),
        name="update",
    )(rank, scalars, *pieces, param, mom, avg)


def swap_pairs(size, bit):
    return [(i, i ^ bit) for i in range(size)]


def butterfly_bits(size):
    bits, bit = [], 1
    while bit < size:
        bits.append(bit)
        bit *= 2
    return bits


def gather_dp(piece, ranks):
    me = lax.axis_index("dp")
    for bit in butterfly_bits(ranks)[1:] + [1]:
        other = lax.ppermute(piece, "dp", swap_pairs(ranks, bit))
        high = (me & bit) != 0
        pair = jnp.stack([jnp.where(high, other, piece), jnp.where(high, piece, other)])
        if bit == 1:
            piece = jnp.swapaxes(pair, 0, 1).reshape((-1,) + piece.shape[1:])
        else:
            piece = pair.reshape((-1,) + piece.shape[1:])
    return piece


def scatter_sum_dp(whole_sum, ranks, small):
    me = lax.axis_index("dp")
    value = whole_sum
    bits = butterfly_bits(ranks)
    for n, bit in enumerate([1] + bits[:0:-1]):
        if bit == 1:
            halves = value.reshape((ranks // 2, 2) + value.shape[1:])
            low, high = halves[:, 0], halves[:, 1]
        else:
            half = value.shape[0] // 2
            low, high = value[:half], value[half:]
        mine_high = (me & bit) != 0
        send = jnp.where(mine_high, low, high).astype(BF16)
        keep = jnp.where(mine_high, high, low)
        pairs = swap_pairs(ranks, bit)
        value = keep + lax.ppermute(send, "dp", pairs).astype(F32)
        hi = lax.reduce_precision(small, 8, 7)
        got = lax.ppermute(jnp.stack([hi, small - hi]).astype(BF16), "dp", pairs).astype(F32)
        small = small + (got[0] + got[1])
    return value[0], small


def gathered_weights(conv_w, cell_params, dp_at, groups, ranks, chans):
    share = conv_w.shape[2]
    wide = share * groups
    taps = conv_w.reshape(2, 4 * share, 9, chans + wide).astype(BF16)
    parts = [
        taps[..., chans:].reshape(2, 4 * share, 9 * wide),
        taps[..., :chans].reshape(2, 4 * share, 9 * chans),
    ]
    cells = jnp.stack([cell_params[:, :4], jnp.pad(cell_params[:, 4:], ((0, 0), (0, 1), (0, 0)))], -1)
    cell_hi = lax.reduce_precision(cells, 8, 7)
    cell_mid = lax.reduce_precision(cells - cell_hi, 8, 7)
    cell_lo = cells - cell_hi - cell_mid
    cell_parts = jnp.stack([cell_hi, cell_mid, cell_lo], -1).astype(BF16).reshape(2, 4 * share, 6)
    parts.append(jnp.pad(cell_parts, ((0, 0), (0, 0), (0, CELL_COLS - 6))))
    packed = jnp.concatenate(parts, -1)
    slab = 4 * share // ranks
    sent_w = packed.shape[-1]
    mine = lax.dynamic_slice_in_dim(packed.reshape(2, ranks, slab, sent_w), dp_at, 1, 1)[:, 0]
    everyone = lax.all_to_all(
        jnp.broadcast_to(mine[None], (groups, 2, slab, sent_w)), "gate", 0, 0, tiled=True
    )
    gathered = gather_dp(everyone[None], ranks)
    full = gathered.transpose(2, 1, 0, 3, 4).reshape(2, groups, 4, share, sent_w)
    full = full.transpose(0, 2, 1, 3, 4).reshape(2, 4 * wide, sent_w)
    return [full[0], full[1]]


def on_device(
    frames,
    regions,
    valid,
    step_count,
    conv_w,
    cell_params,
    head_w,
    head_b,
    conv_mom,
    cell_mom,
    head_mom,
    bias_mom,
    conv_avg,
    cell_avg,
    head_avg,
    bias_avg,
):
    share = conv_w.shape[2]
    chans = frames.shape[1]
    pixels = frames.shape[2]
    wide = head_w.shape[1]
    groups = lax.axis_size("gate")
    ranks = lax.axis_size("dp")
    geo = Geometry(groups, pixels)
    rows, own, halo, front, back, union = geo.rows, geo.own, geo.halo, geo.front, geo.back, geo.union
    gate_at = lax.axis_index("gate")
    dp_at = lax.axis_index("dp")

    order = ring_order(groups)
    place = [order.index(g) for g in range(groups)]
    spot = jnp.asarray(place, jnp.int32)[gate_at]
    from_right = [(order[(i + 1) % groups], order[i]) for i in range(groups)]
    from_left = [(order[i], order[(i + 1) % groups]) for i in range(groups)]

    slab = 4 * share // ranks
    packed_w = 9 * (wide + chans)
    sent_w = packed_w + CELL_COLS
    direct = ranks == 4 and slab == share and share % 16 == 0
    rank = dp_at.astype(jnp.int32).reshape(1)

    start = jnp.mod(spot * own - 2 * halo - 1, COLS).astype(jnp.int32).reshape(1)
    win, meta, mrm, mrp, mcm, mcp, counted = window_call(
        geo, start, frames.reshape(-1, pixels), valid, regions.reshape(1, pixels)
    )
    first_row = lax.slice_in_dim(regions, 0, COLS) // 2
    bands = lax.dynamic_slice_in_dim(jnp.concatenate([first_row, first_row]), start[0], union + 2)
    same = (bands[1:] == bands[:-1]).astype(jnp.int32)
    cols = jnp.concatenate([same[:-1], same[1:]])
    masks = (mrm, mrp, mcm, mcp, cols)

    head_low = head_w.astype(BF16)
    head_bias = head_b[:, None]
    if direct:
        by_core, by_chip = swap_pairs(ranks, 1), swap_pairs(ranks, 2)
        cells_first = jnp.swapaxes(cell_params, 0, 1)
        mine0, mine1 = pack_call(groups, rank, conv_w, cells_first, sent_w)
        mixed0 = lax.all_to_all(mine0, "gate", 0, 0, tiled=True).reshape(groups * share, sent_w)
        mixed0, win, mine1 = lax.optimization_barrier((mixed0, win, mine1))
        over_x = lax.ppermute(mixed0, "dp", by_chip)
        over_core = lax.ppermute(mixed0, "dp", by_core)
        weights = [(rank, mixed0, over_core, over_x, lax.ppermute(over_x, "dp", by_core))]
        mixed1 = lax.all_to_all(mine1, "gate", 0, 0, tiled=True)
        weights.append((rank, mixed1))
    else:
        weights = gathered_weights(conv_w, cell_params, dp_at, groups, ranks, chans)

    state = ()
    kept = []
    t = 0
    for n, (layer, steps) in enumerate(geo.calls):
        base = n * halo
        first_frame = t if layer == 0 else t - 1
        got = forward_call(geo, layer, base, first_frame, steps, state, win, meta, weights[layer], masks)
        if len(got) > 7:
            weights[layer] = got[7]
        if direct and n == 0:
            mixed1, sent = lax.optimization_barrier((weights[1][1], got[6]))
            weights[1] = (rank, mixed1, lax.ppermute(mixed1, "dp", swap_pairs(ranks, 1)))
            got = [*got[:6], sent, *got[7:]]
        kept.append(dict(gates=got[0], cprev=got[1], hvar=got[2], hnew=got[3], xown=got[4], t=t))
        out = got[5]
        t += steps
        if n + 1 < len(geo.calls):
            far = lax.ppermute(got[6], "gate", from_right)
            state = (out, far)

    state = ()
    grads = [None, None]
    cell_sums = [None, None]
    head_sums = None
    for n in range(len(geo.calls) - 1, -1, -1):
        layer, steps = geo.calls[n]
        base = n * halo
        saved = kept[n]
        extra = (win, meta, head_low, head_bias) if layer == 1 else None
        carried = () if cell_sums[layer] is None else (cell_sums[layer], head_sums)
        got = backward_call(
            geo, layer, base, steps, n == 0, carried, state, saved, weights[layer], masks, extra
        )
        if n > 0:
            far = lax.ppermute(got[4], "gate", from_left)
            state = (got[3], far)
        cell_sums[layer] = got[1]
        if layer == 1:
            head_sums = got[2]
        done = direct and (n == 0 or geo.calls[n - 1][0] != layer)
        dz = got[0]
        if done and layer == 0:
            keep1, send1, dz = lax.optimization_barrier((*core_stage("1", rank, sent_w, grads[1][0], crossed1, ()), dz))
            crossed1 = lax.ppermute(send1, "dp", swap_pairs(ranks, 2))
        grads[layer] = weight_call(
            geo,
            base,
            steps,
            grads[layer],
            dz,
            saved["hvar"],
            saved["xown"],
            masks[2],
            masks[3],
            rank if done else None,
            (cell_sums[0], cell_sums[1], grads[1][2], head_sums, counted) if done and layer == 0 else (),
        )
        if done and layer == 1:
            send1, far = lax.optimization_barrier((grads[1][1], far))
            state = (got[3], far)
            crossed1 = lax.ppermute(send1, "dp", swap_pairs(ranks, 1))
    if direct:
        pairs = swap_pairs(ranks, 1)
        across = swap_pairs(ranks, 2)
        keep0, send0, few = grads[0]
        send0, crossed1 = lax.optimization_barrier((send0, crossed1))
        crossed0 = lax.ppermute(send0, "dp", pairs)
        message1, crossed0 = lax.optimization_barrier((chip_stage("1", groups, keep1, crossed1, ()), crossed0))
        mixed1 = lax.all_to_all(message1, "gate", 0, 0, tiled=True)
        keep0, send0, few = core_stage("0", rank, sent_w, keep0, crossed0, (few,))
        crossed0 = lax.ppermute(send0, "dp", across)
        shard1, crossed0 = lax.optimization_barrier((sum_stage("1", mixed1), crossed0))
        from_dp1 = [lax.ppermute(shard1, "dp", swap_pairs(ranks, k)) for k in (1, 2, 3)]
        message0 = chip_stage("0", groups, keep0, crossed0, (few,))
        mixed0 = lax.all_to_all(message0, "gate", 0, 0, tiled=True)
        *from_dp1, mixed0 = lax.optimization_barrier((*from_dp1, mixed0))
        total_pixels = EOUT * pixels * ranks
        flip = lambda v: jnp.swapaxes(v, 0, 1)
        small_args = [cells_first, flip(cell_mom), flip(cell_avg), head_w, head_mom, head_avg]
        small_args += [v[None] for v in (head_b, bias_mom, bias_avg)]
        rate = float(RATE_SCALE * chans * total_pixels**0.5)
        done = finish_stage(rate, chans, packed_w, mixed0, step_count, small_args)
        shard0, scalars, loss = done[:3]
        pieces = [shard0] + [lax.ppermute(shard0, "dp", swap_pairs(ranks, k)) for k in (1, 2, 3)]
        pieces += [shard1] + from_dp1
        outs = [loss[0, 0]]
        outs += update_call(rank, scalars, pieces, conv_w, conv_mom, conv_avg)
        outs += [flip(v) for v in done[3:7]] + list(done[7:11]) + [v[0] for v in done[11:15]]
        return tuple(outs)

    rate = RATE_SCALE * chans * jnp.sqrt(jnp.float32(EOUT * pixels * ranks))
    counts_done = step_count.astype(F32)
    biases = jnp.stack([g[packed_w].reshape(4, wide) for g in grads])
    cells = jnp.concatenate([biases, jnp.stack(cell_sums).reshape(2, 3, 8, wide).sum(2)], 1)
    grads = [g[:packed_w].T for g in grads]
    loss_sum = jnp.sum(head_sums[:, 129])
    shared_small = jnp.concatenate(
        [head_sums[:, :128].reshape(-1), head_sums[:, 128], loss_sum[None], counted[0, :1]]
    )
    small = jnp.concatenate([cells.reshape(-1), shared_small])
    big = jnp.stack(grads).reshape(2, 4, groups, share, packed_w).transpose(2, 1, 3, 0, 4)
    big = big.reshape(groups, ranks, slab, 2, packed_w).transpose(1, 0, 2, 3, 4)
    part, small = scatter_sum_dp(big, ranks, small)
    ncell = 14 * wide
    for_gate = small[:ncell].reshape(14, groups, share).transpose(1, 0, 2).reshape(groups, 14 * share)
    to_gate = jnp.concatenate(
        [for_gate, jnp.broadcast_to(small[None, ncell:], (groups, small.shape[0] - ncell))], 1
    )
    hi = lax.reduce_precision(to_gate, 8, 7)
    lo = (to_gate - hi).astype(BF16)
    hi = hi.astype(BF16)
    width = slab * 2 * packed_w
    message = jnp.concatenate([part.reshape(groups, width).astype(BF16), hi, lo], 1)
    got = lax.all_to_all(message, "gate", 0, 0, tiled=True).astype(F32)
    got = jnp.sum(got.reshape(groups, -1), 0)
    nsmall = to_gate.shape[1]
    small_sum = got[width : width + nsmall] + got[width + nsmall :]
    piece = got[:width].reshape(1, slab, 2, packed_w)
    rows_all = gather_dp(piece, ranks).reshape(4 * share, 2, packed_w).transpose(1, 0, 2)
    count = chans * small_sum[-1]
    scale = 2.0 / count
    rows_all = rows_all * scale
    grad_conv = jnp.concatenate(
        [
            rows_all[..., 9 * wide :].reshape(2, 4 * share, 9, chans),
            rows_all[..., : 9 * wide].reshape(2, 4 * share, 9, wide),
        ],
        -1,
    ).reshape(conv_w.shape)
    grad_cell = small_sum[: 14 * share].reshape(2, 7, share) * scale
    rest = small_sum[14 * share :]
    grad_head = rest[: chans * wide].reshape(chans, wide) * scale
    grad_bias = rest[chans * wide : chans * wide + chans] * scale
    loss = rest[chans * wide + chans] / count

    outs = [loss]
    outs += nesterov(conv_w, grad_conv, conv_mom, conv_avg, counts_done[0], rate)
    outs += nesterov(cell_params, grad_cell, cell_mom, cell_avg, counts_done[1], rate)
    outs += nesterov(head_w, grad_head, head_mom, head_avg, counts_done[2], rate)
    outs += nesterov(head_b, grad_bias, bias_mom, bias_avg, counts_done[3], rate)
    return tuple(outs)


def solution(mesh):
    in_specs = (
        P(None, None, "dp"),
        P("dp"),
        P(None, "dp"),
        P(),
        P(None, None, "gate", None),
        P(None, None, "gate"),
        P(),
        P(),
        P(None, None, "gate", None),
        P(None, None, "gate"),
        P(),
        P(),
        P(None, None, "gate", None),
        P(None, None, "gate"),
        P(),
        P(),
    )
    out_specs = (
        P(),
        P(None, None, "gate", None),
        P(None, None, "gate", None),
        P(None, None, "gate", None),
        P(None, None, "gate", None),
        P(None, None, "gate"),
        P(None, None, "gate"),
        P(None, None, "gate"),
        P(None, None, "gate"),
        P(),
        P(),
        P(),
        P(),
        P(),
        P(),
        P(),
        P(),
    )
    return jax.shard_map(
        on_device, mesh=mesh, in_specs=in_specs, out_specs=out_specs, check_vma=False
    )
```

```python
import functools

import jax
import jax.numpy as jnp
from jax import lax
from jax.experimental import pallas as pl
from jax.experimental.pallas import tpu as pltpu
from jax.sharding import PartitionSpec as P

EIN = 5
EOUT = 15
COLS = 128

MU = 0.9
RATE_SCALE = 0.05
F32 = jnp.float32
BF16 = jnp.bfloat16
VMEM_LIMIT = 60 * 1024 * 1024


def ring_order(groups):
    wide = groups // 4
    if wide <= 1:
        return list(range(groups))
    order = [(z, 0) for z in range(4)]
    for z in range(3, -1, -1):
        ys = range(1, wide) if z % 2 else range(wide - 1, 0, -1)
        order += [(z, y) for y in ys]
    return [z * wide + y for z, y in order]


def split_steps(steps, most):
    calls = -(-steps // most)
    base, extra = divmod(steps, calls)
    return [base + (1 if i < extra else 0) for i in range(calls)]


def nesterov(param, grad, mom, avg, steps_done, rate):
    mom_new = MU * mom + grad
    param_new = param - rate * (grad + MU * mom_new)
    avg_new = avg + (param_new - avg) / (steps_done + 1.0)
    return [mom_new, avg_new, param_new, param_new.astype(BF16)]


def logistic(v):
    return 0.5 * jnp.tanh(0.5 * v) + 0.5


def dot_nt(a, b):
    return lax.dot_general(a, b, (((1,), (1,)), ((), ())), preferred_element_type=F32)


def dot_tn(a, b):
    return lax.dot_general(a, b, (((0,), (0,)), ((), ())), preferred_element_type=F32)


def cut(total, pieces):
    base, extra = divmod(total, pieces)
    spans, at = [], 0
    for i in range(pieces):
        size = base + (1 if i < extra else 0)
        spans.append((at, size))
        at += size
    return spans


def cut_by_four(total, pieces):
    spans, at = [], 0
    for i in range(pieces):
        left = pieces - i
        size = total - at if left == 1 else (total - at) // left // 4 * 4
        if size:
            spans.append((at, size))
        at += size
    return spans


class Geometry:
    def __init__(self, groups, pixels):
        self.rows = pixels // COLS
        self.own = COLS // groups
        self.halo = min(5, self.own // 2)
        self.calls = [(0, n) for n in split_steps(EIN, self.halo)] + [(1, n) for n in split_steps(EOUT, self.halo)]
        self.front = self.own + 4 * self.halo
        self.back = self.own + 2 * self.halo
        self.union = self.front + (len(self.calls) - 1) * self.halo
        self.window = -(-(self.union + 2) * self.rows // 256) * 256


TAPS = [(dr, dc) for dr in (-1, 0, 1) for dc in (-1, 0, 1)]
CELL_COLS = 16


def window_kernel(geo, start, frames, valid, regions, win, meta, mrm, mrp, mcm, mcp, count, lhs, pick):
    rows, own, halo, union, width = geo.rows, geo.own, geo.halo, geo.union, geo.window
    nf = frames.shape[0]
    nv = valid.shape[0]
    lhs[:nf, :] = frames[...]
    lhs[nf : nf + nv, :] = valid[...].astype(F32).astype(BF16)
    lhs[nf + nv : nf + nv + 1, :] = regions[...].astype(F32).astype(BF16)
    per = 256 // rows
    source = lax.broadcasted_iota(jnp.int32, (COLS, 256), 0)
    lane = lax.broadcasted_iota(jnp.int32, (COLS, 256), 1)
    lane_row = lax.broadcasted_iota(jnp.int32, (1, 256), 1) % rows

    def one(n, carry):
        column = (start[0] + n * per + lane // rows) % COLS
        hit = (source == column).astype(F32).astype(BF16)
        for r in range(rows):
            keep = (lane_row == r).astype(F32).astype(BF16)
            pick[r * COLS : (r + 1) * COLS, :] = hit * keep
        got = jnp.dot(lhs[...], pick[...], preferred_element_type=F32)
        at = pl.multiple_of(n * 256, 256)
        win[:, pl.ds(at, 256)] = got[:nf].astype(BF16)
        meta[:, pl.ds(at, 256)] = got[nf:]
        return carry

    lax.fori_loop(0, width // 256, one, 0)
    px = union * rows
    ids = meta[nv : nv + 1, :]
    bands = jnp.floor(ids * 0.5)
    here = ids[:, rows : rows + px]
    band_here = bands[:, rows : rows + px]
    picked = [
        ids[:, rows - 1 : rows - 1 + px] == here,
        ids[:, rows + 1 : rows + 1 + px] == here,
        bands[:, :px] == band_here,
        bands[:, 2 * rows : 2 * rows + px] == band_here,
    ]
    row_at = lax.broadcasted_iota(jnp.int32, (8, px), 0)
    stack = jnp.zeros((8, px), F32)
    for k, m in enumerate(picked):
        stack = jnp.where(row_at == k, jnp.broadcast_to(m.astype(F32), (8, px)), stack)
    stack = stack.astype(BF16)
    sel = lax.broadcasted_iota(jnp.int32, (8, 128), 0)
    for k, out in enumerate((mrm, mrp, mcm, mcp)):
        out[...] = dot_tn(stack, (sel == k).astype(F32).astype(BF16)).astype(BF16)
    a = (2 * halo + 1) * rows
    count[...] = jnp.broadcast_to(jnp.sum(meta[:nv, a : a + own * rows]), count.shape)


def window_call(geo, start, frames, valid, regions):
    nf, nv = frames.shape[0], valid.shape[0]
    pixels = frames.shape[1]
    px = geo.union * geo.rows
    smem = pl.BlockSpec(memory_space=pltpu.SMEM)
    vmem = pl.BlockSpec(memory_space=pltpu.VMEM)
    total = nf + nv + 1
    return pl.pallas_call(
        functools.partial(window_kernel, geo),
        in_specs=[smem, vmem, vmem, vmem],
        out_specs=[vmem] * 7,
        out_shape=[
            jax.ShapeDtypeStruct((nf, geo.window), BF16),
            jax.ShapeDtypeStruct((nv + 1, geo.window), F32),
        ]
        + [jax.ShapeDtypeStruct((px, 128), BF16)] * 4
        + [jax.ShapeDtypeStruct((8, 128), F32)],
        scratch_shapes=[pltpu.VMEM((total, pixels), BF16), pltpu.VMEM((pixels, 256), BF16)],
        compiler_params=pltpu.CompilerParams(vmem_limit_bytes=VMEM_LIMIT),
        cost_estimate=pl.CostEstimate(
            flops=2 * total * pixels * geo.window, bytes_accessed=10 << 20, transcendentals=0
        ),
        name="window",
    )(start, frames, valid, regions)


def pack_kernel(groups, rank, conv, cells, out0, out1):
    share, depth9 = conv.shape[2:]
    chans9 = out0.shape[-1] - CELL_COLS - 9 * 128
    chans = chans9 // 9
    depth = chans + 128
    row = lax.broadcasted_iota(jnp.int32, (7, CELL_COLS), 0)
    col = lax.broadcasted_iota(jnp.int32, (7, CELL_COLS), 1)
    half = (rank[0] & 1) * 2
    for l, at, gate, out in ((0, 0, rank[0], out0), (1, 0, half, out1), (1, share, half + 1, out1)):
        w = conv[l, gate].astype(BF16)
        parts = [w[:, k * depth + chans : (k + 1) * depth] for k in range(9)]
        parts += [w[:, k * depth : k * depth + chans] for k in range(9)]
        rest = cells[:, l, :]
        cols = jnp.zeros((share, CELL_COLS), F32)
        for k in range(3):
            low = rest.astype(BF16)
            rest = rest - low.astype(F32)
            sel = ((row == gate) & (col == k)) | ((row == gate + 4) & (col == 3 + k))
            cols = cols + dot_tn(low, sel.astype(F32).astype(BF16))
        parts.append(cols.astype(BF16))
        line = jnp.concatenate(parts, 1)
        for g in range(groups):
            out[g, at : at + share, :] = line


def pack_call(groups, rank, conv_w, cells, sent_w):
    share = conv_w.shape[2]
    return plain_call(
        functools.partial(pack_kernel, groups),
        "pack",
        [jax.ShapeDtypeStruct((groups, k * share, sent_w), BF16) for k in (1, 2)],
        rank,
        conv_w,
        cells,
        smem=1,
    )


def peephole_rows(wf):
    tail = wf[:, 9 * 128 :]
    depth = tail.shape[1]
    col = lax.broadcasted_iota(jnp.int32, (8, depth), 1)
    at = depth - CELL_COLS + 3
    sel = ((col >= at) & (col < at + 3)).astype(F32).astype(BF16)
    got = dot_nt(sel, tail)
    return [got[0:1, k * 128 : (k + 1) * 128] for k in range(3)]


def make_variants(geo, h, r0, hb, mrm, mrp, base):
    m = h.shape[0]
    g0 = base * geo.rows + r0
    hb[0, r0 : r0 + m, :] = pltpu.roll(h, 1, 0).astype(BF16) * mrm[g0 : g0 + m, :]
    hb[1, r0 : r0 + m, :] = h.astype(BF16)
    hb[2, r0 : r0 + m, :] = pltpu.roll(h, m - 1, 0).astype(BF16) * mrp[g0 : g0 + m, :]


def forward_kernel(geo, layer, base, steps, first, gather, *refs):
    refs = list(refs)
    if gather:
        rank, pieces, refs = refs[0], refs[1 : 1 + gather], refs[1 + gather :]
    if not first:
        near, far = refs[:2]
        refs = refs[2:]
    if gather:
        cols, win, meta, mrm, mrp = refs[:5]
        wf = refs[12]
        refs = refs[5:12] + refs[13:]
    else:
        cols, win, meta, wf, mrm, mrp = refs[:6]
        refs = refs[6:]
    gates_out, cprev_out, hvar_out, hnew_out, xown_out, state_out, send_out = refs[:7]
    hb, hnext, cb, xs, keeps, peeps = refs[7:]
    rows, halo, own, front, back = geo.rows, geo.halo, geo.own, geo.front, geo.back
    chans = win.shape[0]
    chans9 = 9 * chans
    lanes = (front - 2) * rows
    x0 = (base + 2) * rows
    step = pl.program_id(0)

    @pl.when(step == 0)
    def _():
        hb[:, front * rows :, :] = jnp.zeros((3, rows, 128), BF16)
        if first:
            hb[:, : front * rows, :] = jnp.zeros((3, front * rows, 128), BF16)
            cb[...] = jnp.zeros_like(cb)
        else:
            nb = back * rows
            make_variants(geo, near[:, :128].astype(F32), 0, hb, mrm, mrp, base)
            make_variants(geo, far[:, :128].astype(F32), nb, hb, mrm, mrp, base)
            cb[:nb, :] = near[:, 128:].astype(F32)
            cb[nb:, :] = far[:, 128:].astype(F32)
        if gather:
            for k, piece in enumerate(pieces):
                if gather == 4:
                    wf[pl.ds(pl.multiple_of((rank[0] ^ k) * 128, 128), 128), :] = piece[...]
                    continue
                peers, span = piece.shape[0], piece.shape[1] // 2
                half = pl.multiple_of(((rank[0] ^ k) & 1) * 256, 256)
                for g in range(peers):
                    for j in range(2):
                        at = pl.multiple_of(half + j * 128 + g * span, span)
                        wf[pl.ds(at, span), :] = piece[g, j * span : (j + 1) * span, :]
        ids = meta[meta.shape[0] - 1 :, :]
        here = ids[:, x0 : x0 + lanes]
        for tap, (dr, dc) in enumerate(TAPS):
            off = x0 + dc * rows + dr
            same = (ids[:, off : off + lanes] == here).astype(F32)
            keeps[tap * chans : (tap + 1) * chans, :] = jnp.broadcast_to(same, (chans, lanes)).astype(BF16)
        ones = lax.broadcasted_iota(jnp.int32, (CELL_COLS, lanes), 0) < 3
        xs[chans9:, :] = ones.astype(F32).astype(BF16)
        for k, row in enumerate(peephole_rows(wf)):
            peeps[k : k + 1, :] = row

    def input_taps(a, m):
        for tap, (dr, dc) in enumerate(TAPS):
            off = x0 + a + dc * rows + dr
            part = slice(tap * chans, (tap + 1) * chans)
            xs[part, a : a + m] = win[:, off : off + m] * keeps[part, a : a + m]

    chunks = cut_by_four(front - 2, 2)
    for c0, cw in chunks:
        r0, m = (c0 + 1) * rows, cw * rows
        final = c0 == chunks[-1][0]
        input_taps(c0 * rows, m)
        zero = front * rows
        lefts, rights = [], []
        for c in range(c0 + 1, c0 + 1 + cw):
            for at, side, starts in ((c - 1, 0, lefts), (c + 1, 1, rights)):
                starts.append(pl.multiple_of(zero + cols[side * geo.union + base + c] * (at * rows - zero), rows))
        parts = []
        for dr in range(3):
            parts.append(jnp.concatenate([hb[dr, pl.ds(at, rows), :] for at in lefts], 0))
            parts.append(hb[dr, r0 : r0 + m, :])
            parts.append(jnp.concatenate([hb[dr, pl.ds(at, rows), :] for at in rights], 0))
        z = dot_nt(jnp.concatenate(parts, 1), wf[:, : 9 * 128]) + lax.dot_general(
            xs[:, r0 - rows : r0 - rows + m], wf[:, 9 * 128 :], (((0,), (1,)), ((), ())), preferred_element_type=F32
        )
        if final:
            s0, sn = (2 * halo - 1) * rows, (own + 2) * rows
            hvar_out[0, :, :, :] = hb[:, s0 : s0 + sn, :]
            hb[:, rows:r0, :] = hnext[:, rows:r0, :]
        for c in range(c0 + 1, c0 + 1 + cw):
            at = slice(c * rows, (c + 1) * rows)
            zi, zf, zo, zg = (z[(c - c0 - 1) * rows : (c - c0) * rows, n * 128 : (n + 1) * 128] for n in range(4))
            cell = cb[at, :]
            if halo <= c < halo + back:
                cprev_out[0, (c - halo) * rows : (c - halo + 1) * rows, :] = cell.astype(BF16)
            gi = logistic(zi + peeps[0:1, :] * cell)
            gf = logistic(zf + peeps[1:2, :] * cell)
            gg = jnp.tanh(zg)
            cell = gf * cell + gi * gg
            go = logistic(zo + peeps[2:3, :] * cell)
            h = go * jnp.tanh(cell)
            cb[at, :] = cell
            make_variants(geo, h, c * rows, hb if final else hnext, mrm, mrp, base)
            if halo <= c < halo + back:
                out = slice((c - halo) * rows, (c - halo + 1) * rows)
                for n, gate in enumerate((gi, gf, go, gg)):
                    gates_out[0, n, out, :] = gate.astype(BF16)
                hnew_out[0, out, :] = h.astype(BF16)

    q0 = (2 * halo - 1) * rows
    xown_out[0, :, :] = xs[:, q0 : q0 + own * rows]

    @pl.when(step == steps - 1)
    def _():
        a, b = halo * rows, (halo + back) * rows
        state_out[:, :128] = hb[1, a:b, :]
        state_out[:, 128:] = cb[a:b, :].astype(BF16)
        a, b = 3 * halo * rows, 5 * halo * rows
        send_out[:, :128] = hb[1, a:b, :]
        send_out[:, 128:] = cb[a:b, :].astype(BF16)


def whole(shape):
    return pl.BlockSpec(shape, lambda *_: (0,) * len(shape))


def forward_call(geo, layer, base, first_frame, steps, state, win, meta, weights, masks):
    rows, own, front, back = geo.rows, geo.own, geo.front, geo.back
    chans = win.shape[0] // (EIN + EOUT)
    gather = len(weights) - 1 if isinstance(weights, tuple) else 0
    sent_w = weights[1].shape[-1] if gather else weights.shape[1]
    depth = sent_w - 9 * 128
    by_step = lambda *dims: pl.BlockSpec((1,) + dims, lambda t: (t,) + (0,) * len(dims))
    lead = list(weights) if gather else []
    cols, masks = masks[4], masks[:2]
    smem = pl.BlockSpec(memory_space=pltpu.SMEM)
    operands = lead + list(state) + [cols, win, meta] + ([] if gather else [weights]) + list(masks)
    in_specs = [smem] if gather else []
    in_specs += [whole(v.shape) for v in lead[1:]]
    in_specs += [whole(s.shape) for s in state]
    in_specs += [smem, pl.BlockSpec((chans, win.shape[1]), lambda t: (first_frame + t, 0))]
    in_specs += [whole(v.shape) for v in operands[len(lead) + len(state) + 2 :]]
    shapes = [
        (steps, 4, back * rows, 128),
        (steps, back * rows, 128),
        (steps, 3, (own + 2) * rows, 128),
        (steps, back * rows, 128),
        (steps, depth, own * rows),
    ]
    flat = [(back * rows, 256), (2 * geo.halo * rows, 256)] + ([(512, sent_w)] if gather else [])
    outs = [jax.ShapeDtypeStruct(s, BF16) for s in shapes + flat]
    out_specs = [by_step(*s[1:]) for s in shapes] + [whole(s) for s in flat]
    px = front * rows
    return pl.pallas_call(
        functools.partial(forward_kernel, geo, layer, base, steps, not state, gather),
        grid=(steps,),
        in_specs=in_specs,
        out_specs=out_specs,
        out_shape=outs,
        scratch_shapes=[
            pltpu.VMEM((3, px + rows, 128), BF16),
            pltpu.VMEM((3, px, 128), BF16),
            pltpu.VMEM((px, 128), F32),
            pltpu.VMEM((depth, px - 2 * rows), BF16),
            pltpu.VMEM((9 * chans, px - 2 * rows), BF16),
            pltpu.VMEM((8, 128), F32),
        ],
        compiler_params=pltpu.CompilerParams(vmem_limit_bytes=VMEM_LIMIT),
        cost_estimate=pl.CostEstimate(
            flops=steps * px * 512 * 1296 * 2, bytes_accessed=8 << 20, transcendentals=steps * px * 640
        ),
        name=f"forward_{base}",
    )(*operands)


def backward_kernel(geo, layer, base, steps, first_live, first, last, carried, *refs):
    refs = list(refs)
    if carried:
        sums_in, head_in = refs[:2]
        refs = refs[2:]
    if not first:
        local, far = refs[:2]
        refs = refs[2:]
    cols, gates, cprev, wf, mrm, mrp = refs[:6]
    refs = refs[6:]
    if layer == 1:
        hnew, target, meta, head, head_b = refs[:5]
        refs = refs[5:]
    dz_out, sums_out, head_out, carry_out, send_out = refs[:5]
    dh, dc, dz_near, dz_far, peeps, wb = refs[5:]
    rows, halo, own, back = geo.rows, geo.halo, geo.own, geo.back
    o0, on = halo * rows, own * rows
    half = back // 2
    step = pl.program_id(0)

    @pl.when(step == 0)
    def _():
        sums_out[...] = sums_in[...] if carried else jnp.zeros_like(sums_out)
        head_out[...] = head_in[...] if carried else jnp.zeros_like(head_out)
        for tap in range(9):
            across, along = tap % 3 * 512, tap // 3 * 128
            wb[across : across + 512, along : along + 128] = wf[:, tap * 128 : (tap + 1) * 128]
        edge = jnp.zeros((4, rows, 128), BF16)
        dz_near[:, :rows, :] = edge
        dz_far[:, :rows, :] = edge
        dz_far[:, (back - half) * rows :, :] = edge
        for k, row in enumerate(peephole_rows(wf)):
            peeps[k : k + 1, :] = row
        if first:
            dh[...] = jnp.zeros_like(dh)
            dc[...] = jnp.zeros_like(dc)
        else:
            nf = 2 * halo * rows
            dh[:nf, :] = far[:, :128]
            dc[:nf, :] = far[:, 128:]
            dh[nf:, :] = local[:, :128]
            dc[nf:, :] = local[:, 128:]

    if layer == 1:
        guess = dot_nt(head[...], hnew[0]) + head_b[...]
        a0 = (base + halo + 1) * rows
        err = guess - target[:, a0 : a0 + back * rows].astype(F32)
        dy = meta[pl.ds(first_live + steps - 1 - step, 1), a0 : a0 + back * rows] * err
        low = dy.astype(BF16)
        head_out[:, 0:128] += jnp.dot(low[:, o0 : o0 + on], hnew[0, o0 : o0 + on, :], preferred_element_type=F32)
        own_dy = low[:, o0 : o0 + on].astype(F32)
        head_out[:, 128:129] += jnp.sum(own_dy, 1, keepdims=True)
        head_out[:, 129:130] += jnp.sum((dy * err)[:, o0 : o0 + on], 1, keepdims=True)
        dh[...] = (dh[...].astype(F32) + dot_tn(low, head[...])).astype(BF16)

    def gates_chunk(c0, cw):
        r0, m = c0 * rows, cw * rows
        span = slice(r0, r0 + m)
        gi, gf, go, gg = (gates[0, n, span, :] for n in range(4))
        pi, pf, po = (peeps[n : n + 1, :].astype(BF16) for n in range(3))
        c = cprev[0, span, :]
        cn = gf * c + gi * gg
        tc = jnp.tanh(cn)
        u = dh[span, :] * go
        w = u * tc
        d_o = w * (1 - go)
        d_c = dc[span, :] + u * ((1 - tc) * (1 + tc)) + d_o * po
        a_i = d_c * gi
        d_i = a_i * gg * (1 - gi)
        d_g = a_i * ((1 - gg) * (1 + gg))
        a_f = d_c * gf
        d_f = a_f * c * (1 - gf)
        dc[span, :] = a_f + d_i * pi + d_f * pf
        store, p0 = (dz_near, rows + r0) if c0 <= half else (dz_far, r0 - half * rows)
        for n, d in enumerate((d_i, d_f, d_o, d_g)):
            store[n, p0 : p0 + m, :] = d
        a = max(r0, o0) - r0
        b = min(r0 + m, o0 + on) - r0
        if b > a:
            for n, d in enumerate((d_i * c, d_f * c, d_o * cn)):
                part = d[a:b].astype(F32).reshape((b - a) // 8, 8, 128)
                sums_out[n * 8 : (n + 1) * 8, :] += jnp.sum(part, 0)

    def hidden_chunk(c0, cw):
        r0, m = c0 * rows, cw * rows
        g0 = (base + halo) * rows + r0
        parts = []
        for side, shift in ((0, 1), (None, 0), (1, -1)):
            pieces = []
            for c in range(c0 + shift, c0 + cw + shift):
                ref, at = (dz_near, (c + 1) * rows) if c <= half else (dz_far, (c - half) * rows)
                if side is not None:
                    at = pl.multiple_of(cols[side * geo.union + base + halo + c] * at, rows)
                pieces.append((ref, at))
            for n in range(4):
                parts.append(jnp.concatenate([ref[n, pl.ds(at, rows), :] for ref, at in pieces], 0))
        acc = jnp.dot(jnp.concatenate(parts, 1), wb[...], preferred_element_type=F32)
        above = pltpu.roll(acc[:, :128] * mrm[g0 : g0 + m, :].astype(F32), m - 1, 0)
        below = pltpu.roll(acc[:, 256:] * mrp[g0 : g0 + m, :].astype(F32), 1, 0)
        dh[r0 : r0 + m, :] = (acc[:, 128:256] + above + below).astype(BF16)

    for c0, cw in cut(half + 1, max(1, (half + 1) // 1)):
        gates_chunk(c0, cw)
    hidden_chunk(0, half)
    for c0, cw in cut(back - half - 1, max(1, (back - half - 1) // 1)):
        gates_chunk(half + 1 + c0, cw)
    hidden_chunk(half, back - half)
    lo = (half + 1 - halo) * rows
    for n in range(4):
        dz_out[0, :lo, n * 128 : (n + 1) * 128] = dz_near[n, rows + o0 : rows + o0 + lo, :]
        dz_out[0, lo:, n * 128 : (n + 1) * 128] = dz_far[n, rows : rows + on - lo, :]

    @pl.when(step == steps - 1)
    def _():
        carry_out[:, :128] = dh[o0 : o0 + on, :]
        carry_out[:, 128:] = dc[o0 : o0 + on, :]
        ns = 2 * halo * rows
        s0 = o0 + on - ns
        send_out[:, :128] = dh[s0 : s0 + ns, :]
        send_out[:, 128:] = dc[s0 : s0 + ns, :]


def backward_call(geo, layer, base, steps, last, carried, state, saved, wf, masks, extra):
    rows, own, back, halo = geo.rows, geo.own, geo.back, geo.halo
    by_step = lambda *dims: pl.BlockSpec((1,) + dims, lambda t: (steps - 1 - t,) + (0,) * len(dims))
    first_live = saved["t"] - EIN
    lead = list(carried) + list(state)
    cols, masks = masks[4], masks[:2]
    operands = lead + [cols, saved["gates"], saved["cprev"], wf] + list(masks)
    in_specs = [whole(s.shape) for s in lead] + [pl.BlockSpec(memory_space=pltpu.SMEM)]
    in_specs += [by_step(4, back * rows, 128), by_step(back * rows, 128)]
    in_specs += [whole(v.shape) for v in operands[len(lead) + 3 :]]
    if layer == 1:
        win, meta, head, head_b = extra
        operands += [saved["hnew"], win, meta, head, head_b]
        t0 = saved["t"]
        in_specs += [
            by_step(back * rows, 128),
            pl.BlockSpec((head.shape[0], win.shape[1]), lambda t: (t0 + steps - 1 - t, 0)),
            whole(meta.shape),
            whole(head.shape),
            whole(head_b.shape),
        ]
    outs = [
        jax.ShapeDtypeStruct((steps, own * rows, 512), BF16),
        jax.ShapeDtypeStruct((24, 128), F32),
        jax.ShapeDtypeStruct((16, 256), F32),
        jax.ShapeDtypeStruct((own * rows, 256), BF16),
        jax.ShapeDtypeStruct((2 * halo * rows, 256), BF16),
    ]
    out_specs = [by_step(own * rows, 512)] + [whole(o.shape) for o in outs[1:]]
    px = back * rows
    return pl.pallas_call(
        functools.partial(backward_kernel, geo, layer, base, steps, first_live, not state, last, bool(carried)),
        grid=(steps,),
        in_specs=in_specs,
        out_specs=out_specs,
        out_shape=outs,
        scratch_shapes=[
            pltpu.VMEM((px, 128), BF16),
            pltpu.VMEM((px, 128), BF16),
            pltpu.VMEM((4, (back // 2 + 2) * rows, 128), BF16),
            pltpu.VMEM((4, (back - back // 2 + 1) * rows, 128), BF16),
            pltpu.VMEM((8, 128), F32),
            pltpu.VMEM((3 * 512, 3 * 128), BF16),
        ],
        compiler_params=pltpu.CompilerParams(vmem_limit_bytes=VMEM_LIMIT),
        cost_estimate=pl.CostEstimate(
            flops=steps * px * 512 * 1536 * 2, bytes_accessed=8 << 20, transcendentals=steps * px * 128
        ),
        name=f"backward_{base}",
    )(*operands)


def split_low(v, axis=0):
    hi = v.astype(BF16)
    return jnp.concatenate([hi, (v - hi.astype(F32)).astype(BF16)], axis)


def joined(v):
    half = v.shape[0] // 2
    return v[:half].astype(F32) + v[half:].astype(F32)


def weight_kernel(geo, base, steps, add, final, small, *refs):
    refs = list(refs)
    if final:
        rank, refs = refs[0], refs[1:]
    if add:
        acc, refs = refs[0], refs[1:]
    if small:
        sums0, sums1, bias1, head, count = refs[:5]
        refs = refs[5:]
    dz, hvar, xown, mcm, mcp = refs[:5]
    outs, rhs = refs[5:-1], refs[-1]
    rows, own, halo = geo.rows, geo.own, geo.halo
    on = own * rows
    g0 = (base + 2 * halo) * rows
    wide = hvar.shape[-1]
    part = pl.program_id(0)
    if final:
        odd = (rank[0] & 1) == 1

    def put(g):
        at = slice(0, g.shape[0])
        if add:
            g = g + acc[at, :]
        if not final:
            outs[0][at, :] = g
            return g
        keep, send = outs[:2]
        for j in range(2):
            even_gate = g[:, 2 * j * wide : (2 * j + 1) * wide]
            odd_gate = g[:, (2 * j + 1) * wide : (2 * j + 2) * wide]
            keep[j, at, :] = jnp.where(odd, odd_gate, even_gate)
            send[j, at, :] = jnp.where(odd, even_gate, odd_gate).astype(BF16)
        return g

    @pl.when(part < 3)
    def _():
        for dc in range(3):
            for j in range(steps):
                v = hvar[j, 0, dc * rows : dc * rows + on, :]
                if dc == 0:
                    v = v * mcm[g0 : g0 + on, :]
                elif dc == 2:
                    v = v * mcp[g0 : g0 + on, :]
                rhs[j * on : (j + 1) * on, dc * wide : (dc + 1) * wide] = v
        put(dot_tn(rhs[...], dz[...]))

    @pl.when(part == 3)
    def _():
        depth = xown.shape[1]
        inputs = None
        for j in range(steps):
            got = jnp.dot(xown[j], dz[j * on : (j + 1) * on, :], preferred_element_type=F32)
            inputs = got if inputs is None else inputs + got
        bias = put(inputs)[depth - CELL_COLS : depth - CELL_COLS + 8]
        if final and not small:
            outs[2][...] = bias
        if small:
            few = []
            for row, sums in ((bias, sums0), (bias1[...], sums1)):
                few += [row[0:1, k * wide : (k + 1) * wide] for k in range(4)]
                few.append(jnp.sum(sums[...].reshape(3, 8, wide), 1))
            few = jnp.concatenate(few + [jnp.zeros((2, wide), F32)], 0)
            col = lax.broadcasted_iota(jnp.int32, (16, wide), 1)
            extra = jnp.where(col == 2, jnp.broadcast_to(count[0:1, :], (16, wide)), head[:, wide:])
            few = jnp.concatenate([few, head[:, :wide], extra], 0)
            outs[2][...] = few
            outs[1][0, depth : depth + 96, :] = split_low(few)


def weight_call(geo, base, steps, acc, dz, hvar, xown, mcm, mcp, rank=None, small=()):
    on = geo.own * geo.rows
    dz = dz.reshape(steps * on, 512)
    final = rank is not None
    band = 3 * hvar.shape[-1]
    operands = ([rank] if final else []) + ([] if acc is None else [acc]) + list(small) + [dz, hvar, xown, mcm, mcp]
    specs = [pl.BlockSpec(memory_space=pltpu.SMEM)] if final else []
    specs += [] if acc is None else [pl.BlockSpec((band, 512), lambda i: (i, 0))]
    specs += [whole(v.shape) for v in small] + [whole(dz.shape)]
    specs += [pl.BlockSpec((steps, 1) + hvar.shape[2:], lambda i: (0, jnp.minimum(i, 2), 0, 0))]
    specs += [whole(v.shape) for v in (xown, mcm, mcp)]
    out_shape = jax.ShapeDtypeStruct((4 * band, 512), F32)
    out_specs = pl.BlockSpec((band, 512), lambda i: (i, 0))
    if final:
        out_shape = [
            jax.ShapeDtypeStruct((2, 4 * band, 128), F32),
            jax.ShapeDtypeStruct((2, 4 * band, 128), BF16),
            jax.ShapeDtypeStruct((48, 128) if small else (8, 512), F32),
        ]
        out_specs = [pl.BlockSpec((2, band, 128), lambda i: (0, i, 0))] * 2 + [whole(out_shape[2].shape)]
    return pl.pallas_call(
        functools.partial(weight_kernel, geo, base, steps, acc is not None, final, bool(small)),
        grid=(4,),
        in_specs=specs,
        out_specs=out_specs,
        out_shape=out_shape,
        scratch_shapes=[pltpu.VMEM((steps * on, band), BF16)],
        compiler_params=pltpu.CompilerParams(vmem_limit_bytes=VMEM_LIMIT),
        cost_estimate=pl.CostEstimate(
            flops=steps * on * 512 * 1296 * 2, bytes_accessed=16 << 20, transcendentals=0
        ),
        name=f"weights_{base}",
    )(*operands)


SMALL_AT = 1408


def core_stage_kernel(rank, keep, got, *refs):
    depth = refs[1].shape[0] if len(refs) > 2 else refs[0].shape[0]
    high = (rank[0] & 2) == 2
    small = len(refs) > 2
    if small:
        few, keep_out, send_out, few_out = refs
    else:
        keep_out, send_out = refs
    a = keep[0, :depth, :] + got[0, :depth, :].astype(F32)
    b = keep[1, :depth, :] + got[1, :depth, :].astype(F32)
    keep_out[...] = jnp.where(high, b, a)
    send_out[:depth, :] = jnp.where(high, a, b).astype(BF16)
    if small:
        total = few[...] + joined(got[0, depth : depth + 96, :])
        few_out[...] = total
        send_out[depth:, :] = split_low(total)


def chip_stage_kernel(groups, keep, got, *refs):
    depth, wide = keep.shape
    small = len(refs) > 1
    if small:
        few, out = refs
    else:
        (out,) = refs
    width = depth - CELL_COLS
    share = wide // groups
    total = (keep[...] + got[:depth, :].astype(F32)).T[:, :width].astype(BF16)
    if small:
        sums = few[...] + joined(got[depth:, :])
        head = split_low(sums[16:32], 1)
        extra = split_low(sums[32:, :16], 1)
        fill = jnp.zeros((16, SMALL_AT - width - 2 * share - 32), BF16)
    for g in range(groups):
        part = total[g * share : (g + 1) * share, :]
        if not small:
            out[g, :, :] = part
        else:
            cells = split_low(sums[:16, g * share : (g + 1) * share], 1)
            out[g, :, :] = jnp.concatenate([part, cells, extra, fill, head], 1)


def sum_stage_kernel(got, out):
    total = got[0].astype(F32)
    for g in range(1, got.shape[0]):
        total = total + got[g].astype(F32)
    out[...] = total


def finish_kernel(rate, chans, got, steps_done, *refs):
    (cell_refs, head_refs, bias_refs), refs = (refs[:3], refs[3:6], refs[6:9]), refs[9:]
    shard, scalars, loss, cell_outs, head_outs, bias_outs = refs[0], refs[1], refs[2], refs[3:7], refs[7:11], refs[11:]
    total = got[0].astype(F32)
    for g in range(1, got.shape[0]):
        total = total + got[g].astype(F32)
    width = shard.shape[1]
    share = total.shape[0]
    shard[...] = total[:, :width]
    cells = total[:, width : width + share] + total[:, width + share : width + 2 * share]
    at = width + 2 * share
    extra = total[:, at : at + 16] + total[:, at + 16 : at + 32]
    head = total[:, SMALL_AT : SMALL_AT + 128] + total[:, SMALL_AT + 128 :]
    count = chans * extra[0:1, 2:3]
    scale = 2.0 / count
    fresh = [1.0 / (jnp.full((1, 1), steps_done[k].astype(F32)) + 1.0) for k in range(4)]
    loss[...] = jnp.sum(extra[:, 1:2], 0, keepdims=True) / count
    lane = lax.broadcasted_iota(jnp.int32, (8, 128), 1)
    scalars[...] = jnp.where(lane == 0, scale, jnp.where(lane == 1, rate, fresh[0]))

    def update(refs, outs, at, grad, fresh):
        param, mom, avg = (v[at] for v in refs)
        grad = grad * scale
        m = MU * mom + grad
        p = param - rate * (grad + MU * m)
        outs[0][at] = m
        outs[1][at] = avg + (p - avg) * fresh
        outs[2][at] = p
        outs[3][at] = p.astype(BF16)

    for l in range(2):
        update(cell_refs, cell_outs, (slice(None), l, slice(None)), cells[l * 7 : (l + 1) * 7, :], fresh[1])
    update(head_refs, head_outs, (slice(None), slice(None)), head, fresh[2])
    row = lax.broadcasted_iota(jnp.int32, (16, 16), 0)
    col = lax.broadcasted_iota(jnp.int32, (16, 16), 1)
    bias = jnp.sum(jnp.where(row == col, jnp.broadcast_to(extra[:, 0:1], (16, 16)), 0.0), 0, keepdims=True)
    update(bias_refs, bias_outs, (slice(None), slice(None)), bias, fresh[3])


def plain_call(kernel, name, out_shape, *operands, smem=0, moved=4 << 20, smem_at=()):
    where = [pltpu.SMEM if i < smem or i in smem_at else pltpu.VMEM for i in range(len(operands))]
    specs = [pl.BlockSpec(memory_space=m) for m in where]
    return pl.pallas_call(
        kernel,
        in_specs=specs,
        out_shape=out_shape,
        compiler_params=pltpu.CompilerParams(vmem_limit_bytes=VMEM_LIMIT),
        cost_estimate=pl.CostEstimate(flops=1 << 20, bytes_accessed=moved, transcendentals=0),
        name=name,
    )(*operands)


def core_stage(name, rank, depth, keep, got, small):
    wide = keep.shape[2]
    more = 96 if small else 0
    shapes = [jax.ShapeDtypeStruct((depth, wide), F32), jax.ShapeDtypeStruct((depth + more, wide), BF16)]
    shapes += [jax.ShapeDtypeStruct(v.shape, F32) for v in small]
    return plain_call(core_stage_kernel, "core_stage_" + name, shapes, rank, keep, got, *small, smem=1)


def chip_stage(name, groups, keep, got, small):
    depth, wide = keep.shape
    lanes = SMALL_AT + 256 if small else depth - CELL_COLS
    shape = jax.ShapeDtypeStruct((groups, wide // groups, lanes), BF16)
    kernel = functools.partial(chip_stage_kernel, groups)
    return plain_call(kernel, "chip_stage_" + name, shape, keep, got, *small, moved=2 << 20)


def sum_stage(name, got):
    shape = jax.ShapeDtypeStruct(got.shape[1:], F32)
    return plain_call(sum_stage_kernel, "sum_stage_" + name, shape, got, moved=1 << 20)


def finish_stage(rate, chans, width, got, step_count, small_args):
    shapes = [
        jax.ShapeDtypeStruct((got.shape[1], width), F32),
        jax.ShapeDtypeStruct((8, 128), F32),
        jax.ShapeDtypeStruct((1, 1), F32),
    ]
    for v in small_args[::3]:
        shapes += [jax.ShapeDtypeStruct(v.shape, F32)] * 3 + [jax.ShapeDtypeStruct(v.shape, BF16)]
    kernel = functools.partial(finish_kernel, rate, chans)
    return plain_call(kernel, "finish", shapes, got, step_count, *small_args, moved=1 << 20, smem_at=(1,))


def update_kernel(rank, scalars, *refs):
    pieces = (refs[:4], refs[4:8])
    param, mom, avg, mom_out, avg_out, new_out, low_out, grad = refs[8:]
    layer = pl.program_id(0)
    chans = (grad.shape[-1] - 9 * 128) // 9
    scale, rate, fresh = (scalars[0:1, k : k + 1] for k in range(3))
    for l in range(2):

        @pl.when(layer == l)
        def _():
            for k, piece in enumerate(pieces[l]):
                v = piece[...]
                parts = []
                for tap in range(9):
                    parts.append(v[:, 9 * 128 + tap * chans : 9 * 128 + (tap + 1) * chans])
                    parts.append(v[:, tap * 128 : (tap + 1) * 128])
                grad[rank[0] ^ k] = jnp.concatenate(parts, 1) * scale

    g = grad[...]
    m = MU * mom[0] + g
    p = param[0] - rate * (g + MU * m)
    mom_out[0] = m
    new_out[0] = p
    low_out[0] = p.astype(BF16)
    avg_out[0] = avg[0] + (p - avg[0]) * fresh


def update_call(rank, scalars, pieces, param, mom, avg):
    layers, gates, share, width = param.shape
    block = pl.BlockSpec((1, gates, share, width), lambda l: (l, 0, 0, 0))
    smem = pl.BlockSpec(memory_space=pltpu.SMEM)
    shape = jax.ShapeDtypeStruct(param.shape, F32)
    return pl.pallas_call(
        update_kernel,
        grid=(layers,),
        in_specs=[smem, whole(scalars.shape)] + [whole(v.shape) for v in pieces] + [block] * 3,
        out_specs=[block] * 4,
        out_shape=[shape] * 3 + [jax.ShapeDtypeStruct(param.shape, BF16)],
        scratch_shapes=[pltpu.VMEM((gates, share, width), F32)],
        compiler_params=pltpu.CompilerParams(vmem_limit_bytes=VMEM_LIMIT),
        cost_estimate=pl.CostEstimate(flops=1 << 20, bytes_accessed=6 << 20, transcendentals=0),
        name="update",
    )(rank, scalars, *pieces, param, mom, avg)


def swap_pairs(size, bit):
    return [(i, i ^ bit) for i in range(size)]


def butterfly_bits(size):
    bits, bit = [], 1
    while bit < size:
        bits.append(bit)
        bit *= 2
    return bits


def gather_dp(piece, ranks):
    me = lax.axis_index("dp")
    for bit in butterfly_bits(ranks)[1:] + [1]:
        other = lax.ppermute(piece, "dp", swap_pairs(ranks, bit))
        high = (me & bit) != 0
        pair = jnp.stack([jnp.where(high, other, piece), jnp.where(high, piece, other)])
        if bit == 1:
            piece = jnp.swapaxes(pair, 0, 1).reshape((-1,) + piece.shape[1:])
        else:
            piece = pair.reshape((-1,) + piece.shape[1:])
    return piece


def scatter_sum_dp(whole_sum, ranks, small):
    me = lax.axis_index("dp")
    value = whole_sum
    bits = butterfly_bits(ranks)
    for n, bit in enumerate([1] + bits[:0:-1]):
        if bit == 1:
            halves = value.reshape((ranks // 2, 2) + value.shape[1:])
            low, high = halves[:, 0], halves[:, 1]
        else:
            half = value.shape[0] // 2
            low, high = value[:half], value[half:]
        mine_high = (me & bit) != 0
        send = jnp.where(mine_high, low, high).astype(BF16)
        keep = jnp.where(mine_high, high, low)
        pairs = swap_pairs(ranks, bit)
        value = keep + lax.ppermute(send, "dp", pairs).astype(F32)
        hi = lax.reduce_precision(small, 8, 7)
        got = lax.ppermute(jnp.stack([hi, small - hi]).astype(BF16), "dp", pairs).astype(F32)
        small = small + (got[0] + got[1])
    return value[0], small


def gathered_weights(conv_w, cell_params, dp_at, groups, ranks, chans):
    share = conv_w.shape[2]
    wide = share * groups
    taps = conv_w.reshape(2, 4 * share, 9, chans + wide).astype(BF16)
    parts = [
        taps[..., chans:].reshape(2, 4 * share, 9 * wide),
        taps[..., :chans].reshape(2, 4 * share, 9 * chans),
    ]
    cells = jnp.stack([cell_params[:, :4], jnp.pad(cell_params[:, 4:], ((0, 0), (0, 1), (0, 0)))], -1)
    cell_hi = lax.reduce_precision(cells, 8, 7)
    cell_mid = lax.reduce_precision(cells - cell_hi, 8, 7)
    cell_lo = cells - cell_hi - cell_mid
    cell_parts = jnp.stack([cell_hi, cell_mid, cell_lo], -1).astype(BF16).reshape(2, 4 * share, 6)
    parts.append(jnp.pad(cell_parts, ((0, 0), (0, 0), (0, CELL_COLS - 6))))
    packed = jnp.concatenate(parts, -1)
    slab = 4 * share // ranks
    sent_w = packed.shape[-1]
    mine = lax.dynamic_slice_in_dim(packed.reshape(2, ranks, slab, sent_w), dp_at, 1, 1)[:, 0]
    everyone = lax.all_to_all(
        jnp.broadcast_to(mine[None], (groups, 2, slab, sent_w)), "gate", 0, 0, tiled=True
    )
    gathered = gather_dp(everyone[None], ranks)
    full = gathered.transpose(2, 1, 0, 3, 4).reshape(2, groups, 4, share, sent_w)
    full = full.transpose(0, 2, 1, 3, 4).reshape(2, 4 * wide, sent_w)
    return [full[0], full[1]]


def on_device(
    frames,
    regions,
    valid,
    step_count,
    conv_w,
    cell_params,
    head_w,
    head_b,
    conv_mom,
    cell_mom,
    head_mom,
    bias_mom,
    conv_avg,
    cell_avg,
    head_avg,
    bias_avg,
):
    share = conv_w.shape[2]
    chans = frames.shape[1]
    pixels = frames.shape[2]
    wide = head_w.shape[1]
    groups = lax.axis_size("gate")
    ranks = lax.axis_size("dp")
    geo = Geometry(groups, pixels)
    rows, own, halo, front, back, union = geo.rows, geo.own, geo.halo, geo.front, geo.back, geo.union
    gate_at = lax.axis_index("gate")
    dp_at = lax.axis_index("dp")

    order = ring_order(groups)
    place = [order.index(g) for g in range(groups)]
    spot = jnp.asarray(place, jnp.int32)[gate_at]
    from_right = [(order[(i + 1) % groups], order[i]) for i in range(groups)]
    from_left = [(order[i], order[(i + 1) % groups]) for i in range(groups)]

    slab = 4 * share // ranks
    packed_w = 9 * (wide + chans)
    sent_w = packed_w + CELL_COLS
    direct = ranks == 4 and slab == share and share % 16 == 0
    rank = dp_at.astype(jnp.int32).reshape(1)

    start = jnp.mod(spot * own - 2 * halo - 1, COLS).astype(jnp.int32).reshape(1)
    win, meta, mrm, mrp, mcm, mcp, counted = window_call(
        geo, start, frames.reshape(-1, pixels), valid, regions.reshape(1, pixels)
    )
    first_row = lax.slice_in_dim(regions, 0, COLS) // 2
    bands = lax.dynamic_slice_in_dim(jnp.concatenate([first_row, first_row]), start[0], union + 2)
    same = (bands[1:] == bands[:-1]).astype(jnp.int32)
    cols = jnp.concatenate([same[:-1], same[1:]])
    masks = (mrm, mrp, mcm, mcp, cols)

    head_low = head_w.astype(BF16)
    head_bias = head_b[:, None]
    if direct:
        by_core, by_chip = swap_pairs(ranks, 1), swap_pairs(ranks, 2)
        cells_first = jnp.swapaxes(cell_params, 0, 1)
        mine0, mine1 = pack_call(groups, rank, conv_w, cells_first, sent_w)
        mixed0 = lax.all_to_all(mine0, "gate", 0, 0, tiled=True).reshape(groups * share, sent_w)
        mixed0, win, mine1 = lax.optimization_barrier((mixed0, win, mine1))
        over_x = lax.ppermute(mixed0, "dp", by_chip)
        over_core = lax.ppermute(mixed0, "dp", by_core)
        weights = [(rank, mixed0, over_core, over_x, lax.ppermute(over_x, "dp", by_core))]
        mixed1 = lax.all_to_all(mine1, "gate", 0, 0, tiled=True)
        weights.append((rank, mixed1))
    else:
        weights = gathered_weights(conv_w, cell_params, dp_at, groups, ranks, chans)

    state = ()
    kept = []
    t = 0
    for n, (layer, steps) in enumerate(geo.calls):
        base = n * halo
        first_frame = t if layer == 0 else t - 1
        got = forward_call(geo, layer, base, first_frame, steps, state, win, meta, weights[layer], masks)
        if len(got) > 7:
            weights[layer] = got[7]
        if direct and n == 0:
            mixed1, sent = lax.optimization_barrier((weights[1][1], got[6]))
            weights[1] = (rank, mixed1, lax.ppermute(mixed1, "dp", swap_pairs(ranks, 1)))
            got = [*got[:6], sent, *got[7:]]
        kept.append(dict(gates=got[0], cprev=got[1], hvar=got[2], hnew=got[3], xown=got[4], t=t))
        out = got[5]
        t += steps
        if n + 1 < len(geo.calls):
            far = lax.ppermute(got[6], "gate", from_right)
            state = (out, far)

    state = ()
    grads = [None, None]
    cell_sums = [None, None]
    head_sums = None
    for n in range(len(geo.calls) - 1, -1, -1):
        layer, steps = geo.calls[n]
        base = n * halo
        saved = kept[n]
        extra = (win, meta, head_low, head_bias) if layer == 1 else None
        carried = () if cell_sums[layer] is None else (cell_sums[layer], head_sums)
        got = backward_call(
            geo, layer, base, steps, n == 0, carried, state, saved, weights[layer], masks, extra
        )
        if n > 0:
            far = lax.ppermute(got[4], "gate", from_left)
            state = (got[3], far)
        cell_sums[layer] = got[1]
        if layer == 1:
            head_sums = got[2]
        done = direct and (n == 0 or geo.calls[n - 1][0] != layer)
        dz = got[0]
        if done and layer == 0:
            keep1, send1, dz = lax.optimization_barrier((*core_stage("1", rank, sent_w, grads[1][0], crossed1, ()), dz))
            crossed1 = lax.ppermute(send1, "dp", swap_pairs(ranks, 2))
        grads[layer] = weight_call(
            geo,
            base,
            steps,
            grads[layer],
            dz,
            saved["hvar"],
            saved["xown"],
            masks[2],
            masks[3],
            rank if done else None,
            (cell_sums[0], cell_sums[1], grads[1][2], head_sums, counted) if done and layer == 0 else (),
        )
        if done and layer == 1:
            send1, far = lax.optimization_barrier((grads[1][1], far))
            state = (got[3], far)
            crossed1 = lax.ppermute(send1, "dp", swap_pairs(ranks, 1))
    if direct:
        pairs = swap_pairs(ranks, 1)
        across = swap_pairs(ranks, 2)
        keep0, send0, few = grads[0]
        send0, crossed1 = lax.optimization_barrier((send0, crossed1))
        crossed0 = lax.ppermute(send0, "dp", pairs)
        message1, crossed0 = lax.optimization_barrier((chip_stage("1", groups, keep1, crossed1, ()), crossed0))
        mixed1 = lax.all_to_all(message1, "gate", 0, 0, tiled=True)
        keep0, send0, few = core_stage("0", rank, sent_w, keep0, crossed0, (few,))
        crossed0 = lax.ppermute(send0, "dp", across)
        shard1, crossed0 = lax.optimization_barrier((sum_stage("1", mixed1), crossed0))
        from_dp1 = [lax.ppermute(shard1, "dp", swap_pairs(ranks, k)) for k in (1, 2, 3)]
        message0 = chip_stage("0", groups, keep0, crossed0, (few,))
        mixed0 = lax.all_to_all(message0, "gate", 0, 0, tiled=True)
        *from_dp1, mixed0 = lax.optimization_barrier((*from_dp1, mixed0))
        total_pixels = EOUT * pixels * ranks
        flip = lambda v: jnp.swapaxes(v, 0, 1)
        small_args = [cells_first, flip(cell_mom), flip(cell_avg), head_w, head_mom, head_avg]
        small_args += [v[None] for v in (head_b, bias_mom, bias_avg)]
        rate = float(RATE_SCALE * chans * total_pixels**0.5)
        done = finish_stage(rate, chans, packed_w, mixed0, step_count, small_args)
        shard0, scalars, loss = done[:3]
        pieces = [shard0] + [lax.ppermute(shard0, "dp", swap_pairs(ranks, k)) for k in (1, 2, 3)]
        pieces += [shard1] + from_dp1
        outs = [loss[0, 0]]
        outs += update_call(rank, scalars, pieces, conv_w, conv_mom, conv_avg)
        outs += [flip(v) for v in done[3:7]] + list(done[7:11]) + [v[0] for v in done[11:15]]
        return tuple(outs)

    rate = RATE_SCALE * chans * jnp.sqrt(jnp.float32(EOUT * pixels * ranks))
    counts_done = step_count.astype(F32)
    biases = jnp.stack([g[packed_w].reshape(4, wide) for g in grads])
    cells = jnp.concatenate([biases, jnp.stack(cell_sums).reshape(2, 3, 8, wide).sum(2)], 1)
    grads = [g[:packed_w].T for g in grads]
    loss_sum = jnp.sum(head_sums[:, 129])
    shared_small = jnp.concatenate(
        [head_sums[:, :128].reshape(-1), head_sums[:, 128], loss_sum[None], counted[0, :1]]
    )
    small = jnp.concatenate([cells.reshape(-1), shared_small])
    big = jnp.stack(grads).reshape(2, 4, groups, share, packed_w).transpose(2, 1, 3, 0, 4)
    big = big.reshape(groups, ranks, slab, 2, packed_w).transpose(1, 0, 2, 3, 4)
    part, small = scatter_sum_dp(big, ranks, small)
    ncell = 14 * wide
    for_gate = small[:ncell].reshape(14, groups, share).transpose(1, 0, 2).reshape(groups, 14 * share)
    to_gate = jnp.concatenate(
        [for_gate, jnp.broadcast_to(small[None, ncell:], (groups, small.shape[0] - ncell))], 1
    )
    hi = lax.reduce_precision(to_gate, 8, 7)
    lo = (to_gate - hi).astype(BF16)
    hi = hi.astype(BF16)
    width = slab * 2 * packed_w
    message = jnp.concatenate([part.reshape(groups, width).astype(BF16), hi, lo], 1)
    got = lax.all_to_all(message, "gate", 0, 0, tiled=True).astype(F32)
    got = jnp.sum(got.reshape(groups, -1), 0)
    nsmall = to_gate.shape[1]
    small_sum = got[width : width + nsmall] + got[width + nsmall :]
    piece = got[:width].reshape(1, slab, 2, packed_w)
    rows_all = gather_dp(piece, ranks).reshape(4 * share, 2, packed_w).transpose(1, 0, 2)
    count = chans * small_sum[-1]
    scale = 2.0 / count
    rows_all = rows_all * scale
    grad_conv = jnp.concatenate(
        [
            rows_all[..., 9 * wide :].reshape(2, 4 * share, 9, chans),
            rows_all[..., : 9 * wide].reshape(2, 4 * share, 9, wide),
        ],
        -1,
    ).reshape(conv_w.shape)
    grad_cell = small_sum[: 14 * share].reshape(2, 7, share) * scale
    rest = small_sum[14 * share :]
    grad_head = rest[: chans * wide].reshape(chans, wide) * scale
    grad_bias = rest[chans * wide : chans * wide + chans] * scale
    loss = rest[chans * wide + chans] / count

    outs = [loss]
    outs += nesterov(conv_w, grad_conv, conv_mom, conv_avg, counts_done[0], rate)
    outs += nesterov(cell_params, grad_cell, cell_mom, cell_avg, counts_done[1], rate)
    outs += nesterov(head_w, grad_head, head_mom, head_avg, counts_done[2], rate)
    outs += nesterov(head_b, grad_bias, bias_mom, bias_avg, counts_done[3], rate)
    return tuple(outs)


def solution(mesh):
    in_specs = (
        P(None, None, "dp"),
        P("dp"),
        P(None, "dp"),
        P(),
        P(None, None, "gate", None),
        P(None, None, "gate"),
        P(),
        P(),
        P(None, None, "gate", None),
        P(None, None, "gate"),
        P(),
        P(),
        P(None, None, "gate", None),
        P(None, None, "gate"),
        P(),
        P(),
    )
    out_specs = (
        P(),
        P(None, None, "gate", None),
        P(None, None, "gate", None),
        P(None, None, "gate", None),
        P(None, None, "gate", None),
        P(None, None, "gate"),
        P(None, None, "gate"),
        P(None, None, "gate"),
        P(None, None, "gate"),
        P(),
        P(),
        P(),
        P(),
        P(),
        P(),
        P(),
        P(),
    )
    return jax.shard_map(
        on_device, mesh=mesh, in_specs=in_specs, out_specs=out_specs, check_vma=False
    )
```

```python
import functools

import jax
import jax.numpy as jnp
from jax import lax
from jax.experimental import pallas as pl
from jax.experimental.pallas import tpu as pltpu
from jax.sharding import PartitionSpec as P

EIN = 5
EOUT = 15
COLS = 128

MU = 0.9
RATE_SCALE = 0.05
F32 = jnp.float32
BF16 = jnp.bfloat16
VMEM_LIMIT = 60 * 1024 * 1024


def ring_order(groups):
    wide = groups // 4
    if wide <= 1:
        return list(range(groups))
    order = [(z, 0) for z in range(4)]
    for z in range(3, -1, -1):
        ys = range(1, wide) if z % 2 else range(wide - 1, 0, -1)
        order += [(z, y) for y in ys]
    return [z * wide + y for z, y in order]


def split_steps(steps, most):
    calls = -(-steps // most)
    base, extra = divmod(steps, calls)
    return [base + (1 if i < extra else 0) for i in range(calls)]


def nesterov(param, grad, mom, avg, steps_done, rate):
    mom_new = MU * mom + grad
    param_new = param - rate * (grad + MU * mom_new)
    avg_new = avg + (param_new - avg) / (steps_done + 1.0)
    return [mom_new, avg_new, param_new, param_new.astype(BF16)]


def logistic_of_twice(v):
    return 0.5 * jnp.tanh(v) + 0.5


def halving(gate, lanes):
    return jnp.full((1, lanes), jnp.where(gate == 3, 1.0, 0.5), F32).astype(BF16)


def dot_nt(a, b):
    return lax.dot_general(a, b, (((1,), (1,)), ((), ())), preferred_element_type=F32)


def dot_tn(a, b):
    return lax.dot_general(a, b, (((0,), (0,)), ((), ())), preferred_element_type=F32)


def cut(total, pieces):
    base, extra = divmod(total, pieces)
    spans, at = [], 0
    for i in range(pieces):
        size = base + (1 if i < extra else 0)
        spans.append((at, size))
        at += size
    return spans


def cut_by_four(total, pieces):
    spans, at = [], 0
    for i in range(pieces):
        left = pieces - i
        size = total - at if left == 1 else (total - at) // left // 4 * 4
        if size:
            spans.append((at, size))
        at += size
    return spans


class Geometry:
    def __init__(self, groups, pixels):
        self.rows = pixels // COLS
        self.own = COLS // groups
        self.halo = min(5, self.own // 2)
        self.calls = [(0, n) for n in split_steps(EIN, self.halo)] + [(1, n) for n in split_steps(EOUT, self.halo)]
        self.front = self.own + 4 * self.halo
        self.back = self.own + 2 * self.halo
        self.union = self.front + (len(self.calls) - 1) * self.halo
        self.window = -(-(self.union + 2) * self.rows // 256) * 256


TAPS = [(dr, dc) for dr in (-1, 0, 1) for dc in (-1, 0, 1)]
CELL_COLS = 16


def window_kernel(geo, start, frames, valid, regions, win, meta, mrm, mrp, mcm, mcp, count, lhs, pick):
    rows, own, halo, union, width = geo.rows, geo.own, geo.halo, geo.union, geo.window
    nf = frames.shape[0]
    nv = valid.shape[0]
    lhs[:nf, :] = frames[...]
    lhs[nf : nf + nv, :] = valid[...].astype(F32).astype(BF16)
    lhs[nf + nv : nf + nv + 1, :] = regions[...].astype(F32).astype(BF16)
    per = 256 // rows
    source = lax.broadcasted_iota(jnp.int32, (COLS, 256), 0)
    lane = lax.broadcasted_iota(jnp.int32, (COLS, 256), 1)
    lane_row = lax.broadcasted_iota(jnp.int32, (1, 256), 1) % rows

    def one(n, carry):
        column = (start[0] + n * per + lane // rows) % COLS
        hit = (source == column).astype(F32).astype(BF16)
        for r in range(rows):
            keep = (lane_row == r).astype(F32).astype(BF16)
            pick[r * COLS : (r + 1) * COLS, :] = hit * keep
        got = jnp.dot(lhs[...], pick[...], preferred_element_type=F32)
        at = pl.multiple_of(n * 256, 256)
        win[:, pl.ds(at, 256)] = got[:nf].astype(BF16)
        meta[:, pl.ds(at, 256)] = got[nf:]
        return carry

    lax.fori_loop(0, width // 256, one, 0)
    px = union * rows
    ids = meta[nv : nv + 1, :]
    bands = jnp.floor(ids * 0.5)
    here = ids[:, rows : rows + px]
    band_here = bands[:, rows : rows + px]
    picked = [
        ids[:, rows - 1 : rows - 1 + px] == here,
        ids[:, rows + 1 : rows + 1 + px] == here,
        bands[:, :px] == band_here,
        bands[:, 2 * rows : 2 * rows + px] == band_here,
    ]
    row_at = lax.broadcasted_iota(jnp.int32, (8, px), 0)
    stack = jnp.zeros((8, px), F32)
    for k, m in enumerate(picked):
        stack = jnp.where(row_at == k, jnp.broadcast_to(m.astype(F32), (8, px)), stack)
    stack = stack.astype(BF16)
    sel = lax.broadcasted_iota(jnp.int32, (8, 128), 0)
    for k, out in enumerate((mrm, mrp, mcm, mcp)):
        out[...] = dot_tn(stack, (sel == k).astype(F32).astype(BF16)).astype(BF16)
    a = (2 * halo + 1) * rows
    count[...] = jnp.broadcast_to(jnp.sum(meta[:nv, a : a + own * rows]), count.shape)


def window_call(geo, start, frames, valid, regions):
    nf, nv = frames.shape[0], valid.shape[0]
    pixels = frames.shape[1]
    px = geo.union * geo.rows
    smem = pl.BlockSpec(memory_space=pltpu.SMEM)
    vmem = pl.BlockSpec(memory_space=pltpu.VMEM)
    total = nf + nv + 1
    return pl.pallas_call(
        functools.partial(window_kernel, geo),
        in_specs=[smem, vmem, vmem, vmem],
        out_specs=[vmem] * 7,
        out_shape=[
            jax.ShapeDtypeStruct((nf, geo.window), BF16),
            jax.ShapeDtypeStruct((nv + 1, geo.window), F32),
        ]
        + [jax.ShapeDtypeStruct((px, 128), BF16)] * 4
        + [jax.ShapeDtypeStruct((8, 128), F32)],
        scratch_shapes=[pltpu.VMEM((total, pixels), BF16), pltpu.VMEM((pixels, 256), BF16)],
        compiler_params=pltpu.CompilerParams(vmem_limit_bytes=VMEM_LIMIT),
        cost_estimate=pl.CostEstimate(
            flops=2 * total * pixels * geo.window, bytes_accessed=10 << 20, transcendentals=0
        ),
        name="window",
    )(start, frames, valid, regions)


def pack_kernel(groups, rank, conv, cells, out0, out1):
    share, depth9 = conv.shape[2:]
    chans9 = out0.shape[-1] - CELL_COLS - 9 * 128
    chans = chans9 // 9
    depth = chans + 128
    row = lax.broadcasted_iota(jnp.int32, (7, CELL_COLS), 0)
    col = lax.broadcasted_iota(jnp.int32, (7, CELL_COLS), 1)
    half = (rank[0] & 1) * 2
    for l, at, gate, out in ((0, 0, rank[0], out0), (1, 0, half, out1), (1, share, half + 1, out1)):
        w = conv[l, gate].astype(BF16)
        parts = [w[:, k * depth + chans : (k + 1) * depth] for k in range(9)]
        parts += [w[:, k * depth : k * depth + chans] for k in range(9)]
        rest = cells[:, l, :]
        cols = jnp.zeros((share, CELL_COLS), F32)
        for k in range(3):
            low = rest.astype(BF16)
            rest = rest - low.astype(F32)
            sel = ((row == gate) & (col == k)) | ((row == gate + 4) & (col == 3 + k))
            cols = cols + dot_tn(low, sel.astype(F32).astype(BF16))
        parts.append(cols.astype(BF16))
        line = jnp.concatenate(parts, 1)
        for g in range(groups):
            out[g, at : at + share, :] = line


def pack_call(groups, rank, conv_w, cells, sent_w):
    share = conv_w.shape[2]
    return plain_call(
        functools.partial(pack_kernel, groups),
        "pack",
        [jax.ShapeDtypeStruct((groups, k * share, sent_w), BF16) for k in (1, 2)],
        rank,
        conv_w,
        cells,
        smem=1,
    )


def peephole_rows(wf):
    tail = wf[:, 9 * 128 :]
    depth = tail.shape[1]
    col = lax.broadcasted_iota(jnp.int32, (8, depth), 1)
    at = depth - CELL_COLS + 3
    sel = ((col >= at) & (col < at + 3)).astype(F32).astype(BF16)
    got = dot_nt(sel, tail)
    return [got[0:1, k * 128 : (k + 1) * 128] for k in range(3)]


def make_variants(geo, h, r0, hb, mrm, mrp, base):
    m = h.shape[0]
    g0 = base * geo.rows + r0
    hb[0, r0 : r0 + m, :] = pltpu.roll(h, 1, 0).astype(BF16) * mrm[g0 : g0 + m, :]
    hb[1, r0 : r0 + m, :] = h.astype(BF16)
    hb[2, r0 : r0 + m, :] = pltpu.roll(h, m - 1, 0).astype(BF16) * mrp[g0 : g0 + m, :]


def forward_kernel(geo, layer, base, steps, first, gather, *refs):
    refs = list(refs)
    if gather:
        rank, pieces, refs = refs[0], refs[1 : 1 + gather], refs[1 + gather :]
    if not first:
        near, far = refs[:2]
        refs = refs[2:]
    if gather:
        cols, win, meta, mrm, mrp = refs[:5]
        wf = refs[12]
        refs = refs[5:12] + refs[13:]
    else:
        cols, win, meta, wf, mrm, mrp = refs[:6]
        refs = refs[6:]
    gates_out, cprev_out, hvar_out, hnew_out, xown_out, state_out, send_out = refs[:7]
    hb, hnext, cb, xs, keeps, peeps = refs[7:]
    rows, halo, own, front, back = geo.rows, geo.halo, geo.own, geo.front, geo.back
    chans = win.shape[0]
    chans9 = 9 * chans
    lanes = (front - 2) * rows
    x0 = (base + 2) * rows
    step = pl.program_id(0)

    @pl.when(step == 0)
    def _():
        hb[:, front * rows :, :] = jnp.zeros((3, rows, 128), BF16)
        if first:
            hb[:, : front * rows, :] = jnp.zeros((3, front * rows, 128), BF16)
            cb[...] = jnp.zeros_like(cb)
        else:
            nb = back * rows
            make_variants(geo, near[:, :128].astype(F32), 0, hb, mrm, mrp, base)
            make_variants(geo, far[:, :128].astype(F32), nb, hb, mrm, mrp, base)
            cb[:nb, :] = near[:, 128:].astype(F32)
            cb[nb:, :] = far[:, 128:].astype(F32)
        if gather:
            for k, piece in enumerate(pieces):
                if gather == 4:
                    gate = rank[0] ^ k
                    wf[pl.ds(pl.multiple_of(gate * 128, 128), 128), :] = piece[...] * halving(gate, piece.shape[1])
                    continue
                peers, span = piece.shape[0], piece.shape[1] // 2
                for j in range(2):
                    gate = ((rank[0] ^ k) & 1) * 2 + j
                    factor = halving(gate, piece.shape[2])
                    for g in range(peers):
                        at = pl.multiple_of(gate * 128 + g * span, span)
                        wf[pl.ds(at, span), :] = piece[g, j * span : (j + 1) * span, :] * factor
        ids = meta[meta.shape[0] - 1 :, :]
        here = ids[:, x0 : x0 + lanes]
        for tap, (dr, dc) in enumerate(TAPS):
            off = x0 + dc * rows + dr
            same = (ids[:, off : off + lanes] == here).astype(F32)
            keeps[tap * chans : (tap + 1) * chans, :] = jnp.broadcast_to(same, (chans, lanes)).astype(BF16)
        ones = lax.broadcasted_iota(jnp.int32, (CELL_COLS, lanes), 0) < 3
        xs[chans9:, :] = ones.astype(F32).astype(BF16)
        for k, row in enumerate(peephole_rows(wf)):
            peeps[k : k + 1, :] = row

    def input_taps(a, m):
        for tap, (dr, dc) in enumerate(TAPS):
            off = x0 + a + dc * rows + dr
            part = slice(tap * chans, (tap + 1) * chans)
            xs[part, a : a + m] = win[:, off : off + m] * keeps[part, a : a + m]

    chunks = cut_by_four(front - 2, 2)
    for c0, cw in chunks:
        r0, m = (c0 + 1) * rows, cw * rows
        final = c0 == chunks[-1][0]
        input_taps(c0 * rows, m)
        zero = front * rows
        lefts, rights = [], []
        for c in range(c0 + 1, c0 + 1 + cw):
            for at, side, starts in ((c - 1, 0, lefts), (c + 1, 1, rights)):
                starts.append(pl.multiple_of(zero + cols[side * geo.union + base + c] * (at * rows - zero), rows))
        parts = []
        for dr in range(3):
            parts.append(jnp.concatenate([hb[dr, pl.ds(at, rows), :] for at in lefts], 0))
            parts.append(hb[dr, r0 : r0 + m, :])
            parts.append(jnp.concatenate([hb[dr, pl.ds(at, rows), :] for at in rights], 0))
        z = dot_nt(jnp.concatenate(parts, 1), wf[:, : 9 * 128]) + lax.dot_general(
            xs[:, r0 - rows : r0 - rows + m], wf[:, 9 * 128 :], (((0,), (1,)), ((), ())), preferred_element_type=F32
        )
        if final:
            s0, sn = (2 * halo - 1) * rows, (own + 2) * rows
            hvar_out[0, :, :, :] = hb[:, s0 : s0 + sn, :]
            hb[:, rows:r0, :] = hnext[:, rows:r0, :]
        for c in range(c0 + 1, c0 + 1 + cw):
            at = slice(c * rows, (c + 1) * rows)
            zi, zf, zo, zg = (z[(c - c0 - 1) * rows : (c - c0) * rows, n * 128 : (n + 1) * 128] for n in range(4))
            cell = cb[at, :]
            if halo <= c < halo + back:
                cprev_out[0, (c - halo) * rows : (c - halo + 1) * rows, :] = cell.astype(BF16)
            gi = logistic_of_twice(zi + peeps[0:1, :] * cell)
            gf = logistic_of_twice(zf + peeps[1:2, :] * cell)
            gg = jnp.tanh(zg)
            cell = gf * cell + gi * gg
            go = logistic_of_twice(zo + peeps[2:3, :] * cell)
            h = go * jnp.tanh(cell)
            cb[at, :] = cell
            make_variants(geo, h, c * rows, hb if final else hnext, mrm, mrp, base)
            if halo <= c < halo + back:
                out = slice((c - halo) * rows, (c - halo + 1) * rows)
                for n, gate in enumerate((gi, gf, go, gg)):
                    gates_out[0, n, out, :] = gate.astype(BF16)
                hnew_out[0, out, :] = h.astype(BF16)

    q0 = (2 * halo - 1) * rows
    xown_out[0, :, :] = xs[:, q0 : q0 + own * rows]

    @pl.when(step == steps - 1)
    def _():
        a, b = halo * rows, (halo + back) * rows
        state_out[:, :128] = hb[1, a:b, :]
        state_out[:, 128:] = cb[a:b, :].astype(BF16)
        a, b = 3 * halo * rows, 5 * halo * rows
        send_out[:, :128] = hb[1, a:b, :]
        send_out[:, 128:] = cb[a:b, :].astype(BF16)


def whole(shape):
    return pl.BlockSpec(shape, lambda *_: (0,) * len(shape))


def forward_call(geo, layer, base, first_frame, steps, state, win, meta, weights, masks):
    rows, own, front, back = geo.rows, geo.own, geo.front, geo.back
    chans = win.shape[0] // (EIN + EOUT)
    gather = len(weights) - 1 if isinstance(weights, tuple) else 0
    sent_w = weights[1].shape[-1] if gather else weights.shape[1]
    depth = sent_w - 9 * 128
    by_step = lambda *dims: pl.BlockSpec((1,) + dims, lambda t: (t,) + (0,) * len(dims))
    lead = list(weights) if gather else []
    cols, masks = masks[4], masks[:2]
    smem = pl.BlockSpec(memory_space=pltpu.SMEM)
    operands = lead + list(state) + [cols, win, meta] + ([] if gather else [weights]) + list(masks)
    in_specs = [smem] if gather else []
    in_specs += [whole(v.shape) for v in lead[1:]]
    in_specs += [whole(s.shape) for s in state]
    in_specs += [smem, pl.BlockSpec((chans, win.shape[1]), lambda t: (first_frame + t, 0))]
    in_specs += [whole(v.shape) for v in operands[len(lead) + len(state) + 2 :]]
    shapes = [
        (steps, 4, back * rows, 128),
        (steps, back * rows, 128),
        (steps, 3, (own + 2) * rows, 128),
        (steps, back * rows, 128),
        (steps, depth, own * rows),
    ]
    flat = [(back * rows, 256), (2 * geo.halo * rows, 256)] + ([(512, sent_w)] if gather else [])
    outs = [jax.ShapeDtypeStruct(s, BF16) for s in shapes + flat]
    out_specs = [by_step(*s[1:]) for s in shapes] + [whole(s) for s in flat]
    px = front * rows
    return pl.pallas_call(
        functools.partial(forward_kernel, geo, layer, base, steps, not state, gather),
        grid=(steps,),
        in_specs=in_specs,
        out_specs=out_specs,
        out_shape=outs,
        scratch_shapes=[
            pltpu.VMEM((3, px + rows, 128), BF16),
            pltpu.VMEM((3, px, 128), BF16),
            pltpu.VMEM((px, 128), F32),
            pltpu.VMEM((depth, px - 2 * rows), BF16),
            pltpu.VMEM((9 * chans, px - 2 * rows), BF16),
            pltpu.VMEM((8, 128), F32),
        ],
        compiler_params=pltpu.CompilerParams(vmem_limit_bytes=VMEM_LIMIT),
        cost_estimate=pl.CostEstimate(
            flops=steps * px * 512 * 1296 * 2, bytes_accessed=8 << 20, transcendentals=steps * px * 640
        ),
        name=f"forward_{base}",
    )(*operands)


def backward_kernel(geo, layer, base, steps, first_live, first, last, carried, *refs):
    refs = list(refs)
    if carried:
        sums_in, head_in = refs[:2]
        refs = refs[2:]
    if not first:
        local, far = refs[:2]
        refs = refs[2:]
    cols, gates, cprev, wf, mrm, mrp = refs[:6]
    refs = refs[6:]
    if layer == 1:
        hnew, target, meta, head, head_b = refs[:5]
        refs = refs[5:]
    dz_out, sums_out, head_out, carry_out, send_out = refs[:5]
    dh, dc, dz_near, dz_far, peeps, wb = refs[5:]
    rows, halo, own, back = geo.rows, geo.halo, geo.own, geo.back
    o0, on = halo * rows, own * rows
    half = back // 2
    step = pl.program_id(0)

    @pl.when(step == 0)
    def _():
        sums_out[...] = sums_in[...] if carried else jnp.zeros_like(sums_out)
        head_out[...] = head_in[...] if carried else jnp.zeros_like(head_out)
        for tap in range(9):
            across, along = tap % 3 * 512, tap // 3 * 128
            wb[across : across + 384, along : along + 128] = wf[:384, tap * 128 : (tap + 1) * 128] * 2
            wb[across + 384 : across + 512, along : along + 128] = wf[384:, tap * 128 : (tap + 1) * 128]
        edge = jnp.zeros((4, rows, 128), BF16)
        dz_near[:, :rows, :] = edge
        dz_far[:, :rows, :] = edge
        dz_far[:, (back - half) * rows :, :] = edge
        for k, row in enumerate(peephole_rows(wf)):
            peeps[k : k + 1, :] = row * 2.0
        if first:
            dh[...] = jnp.zeros_like(dh)
            dc[...] = jnp.zeros_like(dc)
        else:
            nf = 2 * halo * rows
            dh[:nf, :] = far[:, :128]
            dc[:nf, :] = far[:, 128:]
            dh[nf:, :] = local[:, :128]
            dc[nf:, :] = local[:, 128:]

    if layer == 1:
        guess = dot_nt(head[...], hnew[0]) + head_b[...]
        a0 = (base + halo + 1) * rows
        err = guess - target[:, a0 : a0 + back * rows].astype(F32)
        dy = meta[pl.ds(first_live + steps - 1 - step, 1), a0 : a0 + back * rows] * err
        low = dy.astype(BF16)
        head_out[:, 0:128] += jnp.dot(low[:, o0 : o0 + on], hnew[0, o0 : o0 + on, :], preferred_element_type=F32)
        own_dy = low[:, o0 : o0 + on].astype(F32)
        head_out[:, 128:129] += jnp.sum(own_dy, 1, keepdims=True)
        head_out[:, 129:130] += jnp.sum((dy * err)[:, o0 : o0 + on], 1, keepdims=True)
        dh[...] = (dh[...].astype(F32) + dot_tn(low, head[...])).astype(BF16)

    def gates_chunk(c0, cw):
        r0, m = c0 * rows, cw * rows
        span = slice(r0, r0 + m)
        gi, gf, go, gg = (gates[0, n, span, :] for n in range(4))
        pi, pf, po = (peeps[n : n + 1, :].astype(BF16) for n in range(3))
        c = cprev[0, span, :]
        cn = gf * c + gi * gg
        tc = jnp.tanh(cn)
        u = dh[span, :] * go
        w = u * tc
        d_o = w * (1 - go)
        d_c = dc[span, :] + u * ((1 - tc) * (1 + tc)) + d_o * po
        a_i = d_c * gi
        d_i = a_i * gg * (1 - gi)
        d_g = a_i * ((1 - gg) * (1 + gg))
        a_f = d_c * gf
        d_f = a_f * c * (1 - gf)
        dc[span, :] = a_f + d_i * pi + d_f * pf
        store, p0 = (dz_near, rows + r0) if c0 <= half else (dz_far, r0 - half * rows)
        for n, d in enumerate((d_i, d_f, d_o, d_g)):
            store[n, p0 : p0 + m, :] = d
        a = max(r0, o0) - r0
        b = min(r0 + m, o0 + on) - r0
        if b > a:
            for n, d in enumerate((d_i * c, d_f * c, d_o * cn)):
                part = d[a:b].astype(F32).reshape((b - a) // 8, 8, 128)
                sums_out[n * 8 : (n + 1) * 8, :] += jnp.sum(part, 0)

    def hidden_chunk(c0, cw):
        r0, m = c0 * rows, cw * rows
        g0 = (base + halo) * rows + r0
        parts = []
        for side, shift in ((0, 1), (None, 0), (1, -1)):
            pieces = []
            for c in range(c0 + shift, c0 + cw + shift):
                ref, at = (dz_near, (c + 1) * rows) if c <= half else (dz_far, (c - half) * rows)
                if side is not None:
                    at = pl.multiple_of(cols[side * geo.union + base + halo + c] * at, rows)
                pieces.append((ref, at))
            for n in range(4):
                parts.append(jnp.concatenate([ref[n, pl.ds(at, rows), :] for ref, at in pieces], 0))
        acc = jnp.dot(jnp.concatenate(parts, 1), wb[...], preferred_element_type=F32)
        above = pltpu.roll(acc[:, :128] * mrm[g0 : g0 + m, :].astype(F32), m - 1, 0)
        below = pltpu.roll(acc[:, 256:] * mrp[g0 : g0 + m, :].astype(F32), 1, 0)
        dh[r0 : r0 + m, :] = (acc[:, 128:256] + above + below).astype(BF16)

    for c0, cw in cut(half + 1, max(1, (half + 1) // 1)):
        gates_chunk(c0, cw)
    hidden_chunk(0, half)
    for c0, cw in cut(back - half - 1, max(1, (back - half - 1) // 1)):
        gates_chunk(half + 1 + c0, cw)
    hidden_chunk(half, back - half)
    lo = (half + 1 - halo) * rows
    for n in range(4):
        dz_out[0, :lo, n * 128 : (n + 1) * 128] = dz_near[n, rows + o0 : rows + o0 + lo, :]
        dz_out[0, lo:, n * 128 : (n + 1) * 128] = dz_far[n, rows : rows + on - lo, :]

    @pl.when(step == steps - 1)
    def _():
        carry_out[:, :128] = dh[o0 : o0 + on, :]
        carry_out[:, 128:] = dc[o0 : o0 + on, :]
        ns = 2 * halo * rows
        s0 = o0 + on - ns
        send_out[:, :128] = dh[s0 : s0 + ns, :]
        send_out[:, 128:] = dc[s0 : s0 + ns, :]


def backward_call(geo, layer, base, steps, last, carried, state, saved, wf, masks, extra):
    rows, own, back, halo = geo.rows, geo.own, geo.back, geo.halo
    by_step = lambda *dims: pl.BlockSpec((1,) + dims, lambda t: (steps - 1 - t,) + (0,) * len(dims))
    first_live = saved["t"] - EIN
    lead = list(carried) + list(state)
    cols, masks = masks[4], masks[:2]
    operands = lead + [cols, saved["gates"], saved["cprev"], wf] + list(masks)
    in_specs = [whole(s.shape) for s in lead] + [pl.BlockSpec(memory_space=pltpu.SMEM)]
    in_specs += [by_step(4, back * rows, 128), by_step(back * rows, 128)]
    in_specs += [whole(v.shape) for v in operands[len(lead) + 3 :]]
    if layer == 1:
        win, meta, head, head_b = extra
        operands += [saved["hnew"], win, meta, head, head_b]
        t0 = saved["t"]
        in_specs += [
            by_step(back * rows, 128),
            pl.BlockSpec((head.shape[0], win.shape[1]), lambda t: (t0 + steps - 1 - t, 0)),
            whole(meta.shape),
            whole(head.shape),
            whole(head_b.shape),
        ]
    outs = [
        jax.ShapeDtypeStruct((steps, own * rows, 512), BF16),
        jax.ShapeDtypeStruct((24, 128), F32),
        jax.ShapeDtypeStruct((16, 256), F32),
        jax.ShapeDtypeStruct((own * rows, 256), BF16),
        jax.ShapeDtypeStruct((2 * halo * rows, 256), BF16),
    ]
    out_specs = [by_step(own * rows, 512)] + [whole(o.shape) for o in outs[1:]]
    px = back * rows
    return pl.pallas_call(
        functools.partial(backward_kernel, geo, layer, base, steps, first_live, not state, last, bool(carried)),
        grid=(steps,),
        in_specs=in_specs,
        out_specs=out_specs,
        out_shape=outs,
        scratch_shapes=[
            pltpu.VMEM((px, 128), BF16),
            pltpu.VMEM((px, 128), BF16),
            pltpu.VMEM((4, (back // 2 + 2) * rows, 128), BF16),
            pltpu.VMEM((4, (back - back // 2 + 1) * rows, 128), BF16),
            pltpu.VMEM((8, 128), F32),
            pltpu.VMEM((3 * 512, 3 * 128), BF16),
        ],
        compiler_params=pltpu.CompilerParams(vmem_limit_bytes=VMEM_LIMIT),
        cost_estimate=pl.CostEstimate(
            flops=steps * px * 512 * 1536 * 2, bytes_accessed=8 << 20, transcendentals=steps * px * 128
        ),
        name=f"backward_{base}",
    )(*operands)


def split_low(v, axis=0):
    hi = v.astype(BF16)
    return jnp.concatenate([hi, (v - hi.astype(F32)).astype(BF16)], axis)


def joined(v):
    half = v.shape[0] // 2
    return v[:half].astype(F32) + v[half:].astype(F32)


def weight_kernel(geo, base, steps, add, final, small, *refs):
    refs = list(refs)
    if final:
        rank, refs = refs[0], refs[1:]
    if add:
        acc, refs = refs[0], refs[1:]
    if small:
        sums0, sums1, bias1, head, count = refs[:5]
        refs = refs[5:]
    dz, hvar, xown, mcm, mcp = refs[:5]
    outs, rhs = refs[5:-1], refs[-1]
    rows, own, halo = geo.rows, geo.own, geo.halo
    on = own * rows
    g0 = (base + 2 * halo) * rows
    wide = hvar.shape[-1]
    part = pl.program_id(0)
    if final:
        odd = (rank[0] & 1) == 1

    def put(g):
        at = slice(0, g.shape[0])
        if add:
            g = g + acc[at, :]
        if not final:
            outs[0][at, :] = g
            return g
        keep, send = outs[:2]
        for j in range(2):
            even_gate = g[:, 2 * j * wide : (2 * j + 1) * wide]
            odd_gate = g[:, (2 * j + 1) * wide : (2 * j + 2) * wide]
            keep[j, at, :] = jnp.where(odd, odd_gate, even_gate)
            send[j, at, :] = jnp.where(odd, even_gate, odd_gate).astype(BF16)
        return g

    @pl.when(part < 3)
    def _():
        for dc in range(3):
            for j in range(steps):
                v = hvar[j, 0, dc * rows : dc * rows + on, :]
                if dc == 0:
                    v = v * mcm[g0 : g0 + on, :]
                elif dc == 2:
                    v = v * mcp[g0 : g0 + on, :]
                rhs[j * on : (j + 1) * on, dc * wide : (dc + 1) * wide] = v
        put(dot_tn(rhs[...], dz[...]))

    @pl.when(part == 3)
    def _():
        depth = xown.shape[1]
        inputs = None
        for j in range(steps):
            got = jnp.dot(xown[j], dz[j * on : (j + 1) * on, :], preferred_element_type=F32)
            inputs = got if inputs is None else inputs + got
        bias = put(inputs)[depth - CELL_COLS : depth - CELL_COLS + 8]
        if final and not small:
            outs[2][...] = bias
        if small:
            few = []
            for row, sums in ((bias, sums0), (bias1[...], sums1)):
                few += [row[0:1, k * wide : (k + 1) * wide] for k in range(4)]
                few.append(jnp.sum(sums[...].reshape(3, 8, wide), 1))
            few = jnp.concatenate(few + [jnp.zeros((2, wide), F32)], 0)
            col = lax.broadcasted_iota(jnp.int32, (16, wide), 1)
            extra = jnp.where(col == 2, jnp.broadcast_to(count[0:1, :], (16, wide)), head[:, wide:])
            few = jnp.concatenate([few, head[:, :wide], extra], 0)
            outs[2][...] = few
            outs[1][0, depth : depth + 96, :] = split_low(few)


def weight_call(geo, base, steps, acc, dz, hvar, xown, mcm, mcp, rank=None, small=()):
    on = geo.own * geo.rows
    dz = dz.reshape(steps * on, 512)
    final = rank is not None
    band = 3 * hvar.shape[-1]
    operands = ([rank] if final else []) + ([] if acc is None else [acc]) + list(small) + [dz, hvar, xown, mcm, mcp]
    specs = [pl.BlockSpec(memory_space=pltpu.SMEM)] if final else []
    specs += [] if acc is None else [pl.BlockSpec((band, 512), lambda i: (i, 0))]
    specs += [whole(v.shape) for v in small] + [whole(dz.shape)]
    specs += [pl.BlockSpec((steps, 1) + hvar.shape[2:], lambda i: (0, jnp.minimum(i, 2), 0, 0))]
    specs += [whole(v.shape) for v in (xown, mcm, mcp)]
    out_shape = jax.ShapeDtypeStruct((4 * band, 512), F32)
    out_specs = pl.BlockSpec((band, 512), lambda i: (i, 0))
    if final:
        out_shape = [
            jax.ShapeDtypeStruct((2, 4 * band, 128), F32),
            jax.ShapeDtypeStruct((2, 4 * band, 128), BF16),
            jax.ShapeDtypeStruct((48, 128) if small else (8, 512), F32),
        ]
        out_specs = [pl.BlockSpec((2, band, 128), lambda i: (0, i, 0))] * 2 + [whole(out_shape[2].shape)]
    return pl.pallas_call(
        functools.partial(weight_kernel, geo, base, steps, acc is not None, final, bool(small)),
        grid=(4,),
        in_specs=specs,
        out_specs=out_specs,
        out_shape=out_shape,
        scratch_shapes=[pltpu.VMEM((steps * on, band), BF16)],
        compiler_params=pltpu.CompilerParams(vmem_limit_bytes=VMEM_LIMIT),
        cost_estimate=pl.CostEstimate(
            flops=steps * on * 512 * 1296 * 2, bytes_accessed=16 << 20, transcendentals=0
        ),
        name=f"weights_{base}",
    )(*operands)


SMALL_AT = 1408


def core_stage_kernel(rank, keep, got, *refs):
    depth = refs[1].shape[0] if len(refs) > 2 else refs[0].shape[0]
    high = (rank[0] & 2) == 2
    small = len(refs) > 2
    if small:
        few, keep_out, send_out, few_out = refs
    else:
        keep_out, send_out = refs
    a = keep[0, :depth, :] + got[0, :depth, :].astype(F32)
    b = keep[1, :depth, :] + got[1, :depth, :].astype(F32)
    keep_out[...] = jnp.where(high, b, a)
    send_out[:depth, :] = jnp.where(high, a, b).astype(BF16)
    if small:
        total = few[...] + joined(got[0, depth : depth + 96, :])
        few_out[...] = total
        send_out[depth:, :] = split_low(total)


def chip_stage_kernel(groups, keep, got, *refs):
    depth, wide = keep.shape
    small = len(refs) > 1
    if small:
        few, out = refs
    else:
        (out,) = refs
    width = depth - CELL_COLS
    share = wide // groups
    total = (keep[...] + got[:depth, :].astype(F32)).T[:, :width].astype(BF16)
    if small:
        sums = few[...] + joined(got[depth:, :])
        head = split_low(sums[16:32], 1)
        extra = split_low(sums[32:, :16], 1)
        fill = jnp.zeros((16, SMALL_AT - width - 2 * share - 32), BF16)
    for g in range(groups):
        part = total[g * share : (g + 1) * share, :]
        if not small:
            out[g, :, :] = part
        else:
            cells = split_low(sums[:16, g * share : (g + 1) * share], 1)
            out[g, :, :] = jnp.concatenate([part, cells, extra, fill, head], 1)


def sum_stage_kernel(got, out):
    total = got[0].astype(F32)
    for g in range(1, got.shape[0]):
        total = total + got[g].astype(F32)
    out[...] = total.astype(BF16)


def finish_kernel(rate, chans, got, steps_done, *refs):
    (cell_refs, head_refs, bias_refs), refs = (refs[:3], refs[3:6], refs[6:9]), refs[9:]
    shard, scalars, loss, cell_outs, head_outs, bias_outs = refs[0], refs[1], refs[2], refs[3:7], refs[7:11], refs[11:]
    total = got[0].astype(F32)
    for g in range(1, got.shape[0]):
        total = total + got[g].astype(F32)
    width = shard.shape[1]
    share = total.shape[0]
    shard[...] = total[:, :width].astype(BF16)
    cells = total[:, width : width + share] + total[:, width + share : width + 2 * share]
    at = width + 2 * share
    extra = total[:, at : at + 16] + total[:, at + 16 : at + 32]
    head = total[:, SMALL_AT : SMALL_AT + 128] + total[:, SMALL_AT + 128 :]
    count = chans * extra[0:1, 2:3]
    scale = 2.0 / count
    fresh = [1.0 / (jnp.full((1, 1), steps_done[k].astype(F32)) + 1.0) for k in range(4)]
    loss[...] = jnp.sum(extra[:, 1:2], 0, keepdims=True) / count
    lane = lax.broadcasted_iota(jnp.int32, (8, 128), 1)
    scalars[...] = jnp.where(lane == 0, scale, jnp.where(lane == 1, rate, fresh[0]))

    def update(refs, outs, at, grad, fresh):
        param, mom, avg = (v[at] for v in refs)
        grad = grad * scale
        m = MU * mom + grad
        p = param - rate * (grad + MU * m)
        outs[0][at] = m
        outs[1][at] = avg + (p - avg) * fresh
        outs[2][at] = p
        outs[3][at] = p.astype(BF16)

    for l in range(2):
        update(cell_refs, cell_outs, (slice(None), l, slice(None)), cells[l * 7 : (l + 1) * 7, :], fresh[1])
    update(head_refs, head_outs, (slice(None), slice(None)), head, fresh[2])
    row = lax.broadcasted_iota(jnp.int32, (16, 16), 0)
    col = lax.broadcasted_iota(jnp.int32, (16, 16), 1)
    bias = jnp.sum(jnp.where(row == col, jnp.broadcast_to(extra[:, 0:1], (16, 16)), 0.0), 0, keepdims=True)
    update(bias_refs, bias_outs, (slice(None), slice(None)), bias, fresh[3])


def plain_call(kernel, name, out_shape, *operands, smem=0, moved=4 << 20, smem_at=()):
    where = [pltpu.SMEM if i < smem or i in smem_at else pltpu.VMEM for i in range(len(operands))]
    specs = [pl.BlockSpec(memory_space=m) for m in where]
    return pl.pallas_call(
        kernel,
        in_specs=specs,
        out_shape=out_shape,
        compiler_params=pltpu.CompilerParams(vmem_limit_bytes=VMEM_LIMIT),
        cost_estimate=pl.CostEstimate(flops=1 << 20, bytes_accessed=moved, transcendentals=0),
        name=name,
    )(*operands)


def core_stage(name, rank, depth, keep, got, small):
    wide = keep.shape[2]
    more = 96 if small else 0
    shapes = [jax.ShapeDtypeStruct((depth, wide), F32), jax.ShapeDtypeStruct((depth + more, wide), BF16)]
    shapes += [jax.ShapeDtypeStruct(v.shape, F32) for v in small]
    return plain_call(core_stage_kernel, "core_stage_" + name, shapes, rank, keep, got, *small, smem=1)


def chip_stage(name, groups, keep, got, small):
    depth, wide = keep.shape
    lanes = SMALL_AT + 256 if small else depth - CELL_COLS
    shape = jax.ShapeDtypeStruct((groups, wide // groups, lanes), BF16)
    kernel = functools.partial(chip_stage_kernel, groups)
    return plain_call(kernel, "chip_stage_" + name, shape, keep, got, *small, moved=2 << 20)


def sum_stage(name, got):
    shape = jax.ShapeDtypeStruct(got.shape[1:], BF16)
    return plain_call(sum_stage_kernel, "sum_stage_" + name, shape, got, moved=1 << 20)


def finish_stage(rate, chans, width, got, step_count, small_args):
    shapes = [
        jax.ShapeDtypeStruct((got.shape[1], width), BF16),
        jax.ShapeDtypeStruct((8, 128), F32),
        jax.ShapeDtypeStruct((1, 1), F32),
    ]
    for v in small_args[::3]:
        shapes += [jax.ShapeDtypeStruct(v.shape, F32)] * 3 + [jax.ShapeDtypeStruct(v.shape, BF16)]
    kernel = functools.partial(finish_kernel, rate, chans)
    return plain_call(kernel, "finish", shapes, got, step_count, *small_args, moved=1 << 20, smem_at=(1,))


def update_kernel(rank, scalars, *refs):
    pieces = (refs[:4], refs[4:8])
    param, mom, avg, mom_out, avg_out, new_out, low_out, grad = refs[8:]
    layer = pl.program_id(0)
    chans = (grad.shape[-1] - 9 * 128) // 9
    scale, rate, fresh = (scalars[0:1, k : k + 1] for k in range(3))
    for l in range(2):

        @pl.when(layer == l)
        def _():
            for k, piece in enumerate(pieces[l]):
                v = piece[...].astype(F32)
                parts = []
                for tap in range(9):
                    parts.append(v[:, 9 * 128 + tap * chans : 9 * 128 + (tap + 1) * chans])
                    parts.append(v[:, tap * 128 : (tap + 1) * 128])
                grad[rank[0] ^ k] = jnp.concatenate(parts, 1) * scale

    g = grad[...]
    m = MU * mom[0] + g
    p = param[0] - rate * (g + MU * m)
    mom_out[0] = m
    new_out[0] = p
    low_out[0] = p.astype(BF16)
    avg_out[0] = avg[0] + (p - avg[0]) * fresh


def update_call(rank, scalars, pieces, param, mom, avg):
    layers, gates, share, width = param.shape
    block = pl.BlockSpec((1, gates, share, width), lambda l: (l, 0, 0, 0))
    smem = pl.BlockSpec(memory_space=pltpu.SMEM)
    shape = jax.ShapeDtypeStruct(param.shape, F32)
    return pl.pallas_call(
        update_kernel,
        grid=(layers,),
        in_specs=[smem, whole(scalars.shape)] + [whole(v.shape) for v in pieces] + [block] * 3,
        out_specs=[block] * 4,
        out_shape=[shape] * 3 + [jax.ShapeDtypeStruct(param.shape, BF16)],
        scratch_shapes=[pltpu.VMEM((gates, share, width), F32)],
        compiler_params=pltpu.CompilerParams(vmem_limit_bytes=VMEM_LIMIT),
        cost_estimate=pl.CostEstimate(flops=1 << 20, bytes_accessed=6 << 20, transcendentals=0),
        name="update",
    )(rank, scalars, *pieces, param, mom, avg)


def swap_pairs(size, bit):
    return [(i, i ^ bit) for i in range(size)]


def butterfly_bits(size):
    bits, bit = [], 1
    while bit < size:
        bits.append(bit)
        bit *= 2
    return bits


def gather_dp(piece, ranks):
    me = lax.axis_index("dp")
    for bit in butterfly_bits(ranks)[1:] + [1]:
        other = lax.ppermute(piece, "dp", swap_pairs(ranks, bit))
        high = (me & bit) != 0
        pair = jnp.stack([jnp.where(high, other, piece), jnp.where(high, piece, other)])
        if bit == 1:
            piece = jnp.swapaxes(pair, 0, 1).reshape((-1,) + piece.shape[1:])
        else:
            piece = pair.reshape((-1,) + piece.shape[1:])
    return piece


def scatter_sum_dp(whole_sum, ranks, small):
    me = lax.axis_index("dp")
    value = whole_sum
    bits = butterfly_bits(ranks)
    for n, bit in enumerate([1] + bits[:0:-1]):
        if bit == 1:
            halves = value.reshape((ranks // 2, 2) + value.shape[1:])
            low, high = halves[:, 0], halves[:, 1]
        else:
            half = value.shape[0] // 2
            low, high = value[:half], value[half:]
        mine_high = (me & bit) != 0
        send = jnp.where(mine_high, low, high).astype(BF16)
        keep = jnp.where(mine_high, high, low)
        pairs = swap_pairs(ranks, bit)
        value = keep + lax.ppermute(send, "dp", pairs).astype(F32)
        hi = lax.reduce_precision(small, 8, 7)
        got = lax.ppermute(jnp.stack([hi, small - hi]).astype(BF16), "dp", pairs).astype(F32)
        small = small + (got[0] + got[1])
    return value[0], small


def gathered_weights(conv_w, cell_params, dp_at, groups, ranks, chans):
    share = conv_w.shape[2]
    wide = share * groups
    taps = conv_w.reshape(2, 4 * share, 9, chans + wide).astype(BF16)
    parts = [
        taps[..., chans:].reshape(2, 4 * share, 9 * wide),
        taps[..., :chans].reshape(2, 4 * share, 9 * chans),
    ]
    cells = jnp.stack([cell_params[:, :4], jnp.pad(cell_params[:, 4:], ((0, 0), (0, 1), (0, 0)))], -1)
    cell_hi = lax.reduce_precision(cells, 8, 7)
    cell_mid = lax.reduce_precision(cells - cell_hi, 8, 7)
    cell_lo = cells - cell_hi - cell_mid
    cell_parts = jnp.stack([cell_hi, cell_mid, cell_lo], -1).astype(BF16).reshape(2, 4 * share, 6)
    parts.append(jnp.pad(cell_parts, ((0, 0), (0, 0), (0, CELL_COLS - 6))))
    packed = jnp.concatenate(parts, -1)
    slab = 4 * share // ranks
    sent_w = packed.shape[-1]
    mine = lax.dynamic_slice_in_dim(packed.reshape(2, ranks, slab, sent_w), dp_at, 1, 1)[:, 0]
    everyone = lax.all_to_all(
        jnp.broadcast_to(mine[None], (groups, 2, slab, sent_w)), "gate", 0, 0, tiled=True
    )
    gathered = gather_dp(everyone[None], ranks)
    full = gathered.transpose(2, 1, 0, 3, 4).reshape(2, groups, 4, share, sent_w)
    full = full.transpose(0, 2, 1, 3, 4).reshape(2, 4 * wide, sent_w)
    gate = jnp.arange(4 * wide)[:, None] // wide
    full = full * jnp.where(gate == 3, 1.0, 0.5).astype(BF16)
    return [full[0], full[1]]


def on_device(
    frames,
    regions,
    valid,
    step_count,
    conv_w,
    cell_params,
    head_w,
    head_b,
    conv_mom,
    cell_mom,
    head_mom,
    bias_mom,
    conv_avg,
    cell_avg,
    head_avg,
    bias_avg,
):
    share = conv_w.shape[2]
    chans = frames.shape[1]
    pixels = frames.shape[2]
    wide = head_w.shape[1]
    groups = lax.axis_size("gate")
    ranks = lax.axis_size("dp")
    geo = Geometry(groups, pixels)
    rows, own, halo, front, back, union = geo.rows, geo.own, geo.halo, geo.front, geo.back, geo.union
    gate_at = lax.axis_index("gate")
    dp_at = lax.axis_index("dp")

    order = ring_order(groups)
    place = [order.index(g) for g in range(groups)]
    spot = jnp.asarray(place, jnp.int32)[gate_at]
    spot = jnp.where(dp_at % 2 == 1, groups - 1 - spot, spot)
    ring = ("dp", "gate")
    from_right = []
    for r in range(ranks):
        walk = order[::-1] if r % 2 else order
        from_right += [(r * groups + walk[(i + 1) % groups], r * groups + walk[i]) for i in range(groups)]
    from_left = [(b, a) for a, b in from_right]

    slab = 4 * share // ranks
    packed_w = 9 * (wide + chans)
    sent_w = packed_w + CELL_COLS
    direct = ranks == 4 and slab == share and share % 16 == 0
    rank = dp_at.astype(jnp.int32).reshape(1)

    start = jnp.mod(spot * own - 2 * halo - 1, COLS).astype(jnp.int32).reshape(1)
    win, meta, mrm, mrp, mcm, mcp, counted = window_call(
        geo, start, frames.reshape(-1, pixels), valid, regions.reshape(1, pixels)
    )
    first_row = lax.slice_in_dim(regions, 0, COLS) // 2
    bands = lax.dynamic_slice_in_dim(jnp.concatenate([first_row, first_row]), start[0], union + 2)
    same = (bands[1:] == bands[:-1]).astype(jnp.int32)
    cols = jnp.concatenate([same[:-1], same[1:]])
    masks = (mrm, mrp, mcm, mcp, cols)

    head_low = head_w.astype(BF16)
    head_bias = head_b[:, None]
    if direct:
        by_core, by_chip = swap_pairs(ranks, 1), swap_pairs(ranks, 2)
        cells_first = jnp.swapaxes(cell_params, 0, 1)
        mine0, mine1 = pack_call(groups, rank, conv_w, cells_first, sent_w)
        mixed0 = lax.all_to_all(mine0, "gate", 0, 0, tiled=True).reshape(groups * share, sent_w)
        mixed0, win, mine1 = lax.optimization_barrier((mixed0, win, mine1))
        over_x = lax.ppermute(mixed0, "dp", by_chip)
        over_core = lax.ppermute(mixed0, "dp", by_core)
        weights = [(rank, mixed0, over_core, over_x, lax.ppermute(over_x, "dp", by_core))]
        mixed1 = lax.all_to_all(mine1, "gate", 0, 0, tiled=True)
        weights.append((rank, mixed1))
    else:
        weights = gathered_weights(conv_w, cell_params, dp_at, groups, ranks, chans)

    state = ()
    kept = []
    t = 0
    for n, (layer, steps) in enumerate(geo.calls):
        base = n * halo
        first_frame = t if layer == 0 else t - 1
        got = forward_call(geo, layer, base, first_frame, steps, state, win, meta, weights[layer], masks)
        if len(got) > 7:
            weights[layer] = got[7]
        if direct and n == 0:
            mixed1, sent = lax.optimization_barrier((weights[1][1], got[6]))
            weights[1] = (rank, mixed1, lax.ppermute(mixed1, "dp", swap_pairs(ranks, 1)))
            got = [*got[:6], sent, *got[7:]]
        kept.append(dict(gates=got[0], cprev=got[1], hvar=got[2], hnew=got[3], xown=got[4], t=t))
        out = got[5]
        t += steps
        if n + 1 < len(geo.calls):
            far = lax.ppermute(got[6], ring, from_right)
            state = (out, far)

    state = ()
    grads = [None, None]
    cell_sums = [None, None]
    head_sums = None
    for n in range(len(geo.calls) - 1, -1, -1):
        layer, steps = geo.calls[n]
        base = n * halo
        saved = kept[n]
        extra = (win, meta, head_low, head_bias) if layer == 1 else None
        carried = () if cell_sums[layer] is None else (cell_sums[layer], head_sums)
        got = backward_call(
            geo, layer, base, steps, n == 0, carried, state, saved, weights[layer], masks, extra
        )
        if n > 0:
            far = lax.ppermute(got[4], ring, from_left)
            state = (got[3], far)
        cell_sums[layer] = got[1]
        if layer == 1:
            head_sums = got[2]
        done = direct and (n == 0 or geo.calls[n - 1][0] != layer)
        dz = got[0]
        if done and layer == 0:
            keep1, send1, dz = lax.optimization_barrier((*core_stage("1", rank, sent_w, grads[1][0], crossed1, ()), dz))
            crossed1 = lax.ppermute(send1, "dp", swap_pairs(ranks, 2))
        grads[layer] = weight_call(
            geo,
            base,
            steps,
            grads[layer],
            dz,
            saved["hvar"],
            saved["xown"],
            masks[2],
            masks[3],
            rank if done else None,
            (cell_sums[0], cell_sums[1], grads[1][2], head_sums, counted) if done and layer == 0 else (),
        )
        if done and layer == 1:
            send1, far = lax.optimization_barrier((grads[1][1], far))
            state = (got[3], far)
            crossed1 = lax.ppermute(send1, "dp", swap_pairs(ranks, 1))
    if direct:
        pairs = swap_pairs(ranks, 1)
        across = swap_pairs(ranks, 2)
        keep0, send0, few = grads[0]
        send0, crossed1 = lax.optimization_barrier((send0, crossed1))
        crossed0 = lax.ppermute(send0, "dp", pairs)
        message1, crossed0 = lax.optimization_barrier((chip_stage("1", groups, keep1, crossed1, ()), crossed0))
        mixed1 = lax.all_to_all(message1, "gate", 0, 0, tiled=True)
        keep0, send0, few = core_stage("0", rank, sent_w, keep0, crossed0, (few,))
        crossed0 = lax.ppermute(send0, "dp", across)
        shard1, crossed0 = lax.optimization_barrier((sum_stage("1", mixed1), crossed0))
        from_dp1 = [lax.ppermute(shard1, "dp", swap_pairs(ranks, k)) for k in (1, 2, 3)]
        message0 = chip_stage("0", groups, keep0, crossed0, (few,))
        mixed0 = lax.all_to_all(message0, "gate", 0, 0, tiled=True)
        *from_dp1, mixed0 = lax.optimization_barrier((*from_dp1, mixed0))
        total_pixels = EOUT * pixels * ranks
        flip = lambda v: jnp.swapaxes(v, 0, 1)
        small_args = [cells_first, flip(cell_mom), flip(cell_avg), head_w, head_mom, head_avg]
        small_args += [v[None] for v in (head_b, bias_mom, bias_avg)]
        rate = float(RATE_SCALE * chans * total_pixels**0.5)
        done = finish_stage(rate, chans, packed_w, mixed0, step_count, small_args)
        shard0, scalars, loss = done[:3]
        pieces = [shard0] + [lax.ppermute(shard0, "dp", swap_pairs(ranks, k)) for k in (1, 2, 3)]
        pieces += [shard1] + from_dp1
        outs = [loss[0, 0]]
        outs += update_call(rank, scalars, pieces, conv_w, conv_mom, conv_avg)
        outs += [flip(v) for v in done[3:7]] + list(done[7:11]) + [v[0] for v in done[11:15]]
        return tuple(outs)

    rate = RATE_SCALE * chans * jnp.sqrt(jnp.float32(EOUT * pixels * ranks))
    counts_done = step_count.astype(F32)
    biases = jnp.stack([g[packed_w].reshape(4, wide) for g in grads])
    cells = jnp.concatenate([biases, jnp.stack(cell_sums).reshape(2, 3, 8, wide).sum(2)], 1)
    grads = [g[:packed_w].T for g in grads]
    loss_sum = jnp.sum(head_sums[:, 129])
    shared_small = jnp.concatenate(
        [head_sums[:, :128].reshape(-1), head_sums[:, 128], loss_sum[None], counted[0, :1]]
    )
    small = jnp.concatenate([cells.reshape(-1), shared_small])
    big = jnp.stack(grads).reshape(2, 4, groups, share, packed_w).transpose(2, 1, 3, 0, 4)
    big = big.reshape(groups, ranks, slab, 2, packed_w).transpose(1, 0, 2, 3, 4)
    part, small = scatter_sum_dp(big, ranks, small)
    ncell = 14 * wide
    for_gate = small[:ncell].reshape(14, groups, share).transpose(1, 0, 2).reshape(groups, 14 * share)
    to_gate = jnp.concatenate(
        [for_gate, jnp.broadcast_to(small[None, ncell:], (groups, small.shape[0] - ncell))], 1
    )
    hi = lax.reduce_precision(to_gate, 8, 7)
    lo = (to_gate - hi).astype(BF16)
    hi = hi.astype(BF16)
    width = slab * 2 * packed_w
    message = jnp.concatenate([part.reshape(groups, width).astype(BF16), hi, lo], 1)
    got = lax.all_to_all(message, "gate", 0, 0, tiled=True).astype(F32)
    got = jnp.sum(got.reshape(groups, -1), 0)
    nsmall = to_gate.shape[1]
    small_sum = got[width : width + nsmall] + got[width + nsmall :]
    piece = got[:width].reshape(1, slab, 2, packed_w)
    rows_all = gather_dp(piece, ranks).reshape(4 * share, 2, packed_w).transpose(1, 0, 2)
    count = chans * small_sum[-1]
    scale = 2.0 / count
    rows_all = rows_all * scale
    grad_conv = jnp.concatenate(
        [
            rows_all[..., 9 * wide :].reshape(2, 4 * share, 9, chans),
            rows_all[..., : 9 * wide].reshape(2, 4 * share, 9, wide),
        ],
        -1,
    ).reshape(conv_w.shape)
    grad_cell = small_sum[: 14 * share].reshape(2, 7, share) * scale
    rest = small_sum[14 * share :]
    grad_head = rest[: chans * wide].reshape(chans, wide) * scale
    grad_bias = rest[chans * wide : chans * wide + chans] * scale
    loss = rest[chans * wide + chans] / count

    outs = [loss]
    outs += nesterov(conv_w, grad_conv, conv_mom, conv_avg, counts_done[0], rate)
    outs += nesterov(cell_params, grad_cell, cell_mom, cell_avg, counts_done[1], rate)
    outs += nesterov(head_w, grad_head, head_mom, head_avg, counts_done[2], rate)
    outs += nesterov(head_b, grad_bias, bias_mom, bias_avg, counts_done[3], rate)
    return tuple(outs)


def solution(mesh):
    in_specs = (
        P(None, None, "dp"),
        P("dp"),
        P(None, "dp"),
        P(),
        P(None, None, "gate", None),
        P(None, None, "gate"),
        P(),
        P(),
        P(None, None, "gate", None),
        P(None, None, "gate"),
        P(),
        P(),
        P(None, None, "gate", None),
        P(None, None, "gate"),
        P(),
        P(),
    )
    out_specs = (
        P(),
        P(None, None, "gate", None),
        P(None, None, "gate", None),
        P(None, None, "gate", None),
        P(None, None, "gate", None),
        P(None, None, "gate"),
        P(None, None, "gate"),
        P(None, None, "gate"),
        P(None, None, "gate"),
        P(),
        P(),
        P(),
        P(),
        P(),
        P(),
        P(),
        P(),
    )
    return jax.shard_map(
        on_device, mesh=mesh, in_specs=in_specs, out_specs=out_specs, check_vma=False
    )
```

```python
import functools

import jax
import jax.numpy as jnp
from jax import lax
from jax.experimental import pallas as pl
from jax.experimental.pallas import tpu as pltpu
from jax.sharding import PartitionSpec as P

EIN = 5
EOUT = 15
COLS = 128

MU = 0.9
RATE_SCALE = 0.05
F32 = jnp.float32
BF16 = jnp.bfloat16
VMEM_LIMIT = 60 * 1024 * 1024


def ring_order(groups):
    wide = groups // 4
    if wide <= 1:
        return list(range(groups))
    order = [(z, 0) for z in range(4)]
    for z in range(3, -1, -1):
        ys = range(1, wide) if z % 2 else range(wide - 1, 0, -1)
        order += [(z, y) for y in ys]
    return [z * wide + y for z, y in order]


def split_steps(steps, most):
    calls = -(-steps // most)
    base, extra = divmod(steps, calls)
    return [base + (1 if i < extra else 0) for i in range(calls)]


def nesterov(param, grad, mom, avg, steps_done, rate):
    mom_new = MU * mom + grad
    param_new = param - rate * (grad + MU * mom_new)
    avg_new = avg + (param_new - avg) / (steps_done + 1.0)
    return [mom_new, avg_new, param_new, param_new.astype(BF16)]


def logistic_of_twice(v):
    return 0.5 * jnp.tanh(v) + 0.5


def halving(gate, lanes):
    return jnp.full((1, lanes), jnp.where(gate == 3, 1.0, 0.5), F32).astype(BF16)


def dot_nt(a, b):
    return lax.dot_general(a, b, (((1,), (1,)), ((), ())), preferred_element_type=F32)


def dot_tn(a, b):
    return lax.dot_general(a, b, (((0,), (0,)), ((), ())), preferred_element_type=F32)


def cut(total, pieces):
    base, extra = divmod(total, pieces)
    spans, at = [], 0
    for i in range(pieces):
        size = base + (1 if i < extra else 0)
        spans.append((at, size))
        at += size
    return spans


def cut_by_four(total, pieces):
    spans, at = [], 0
    for i in range(pieces):
        left = pieces - i
        size = total - at if left == 1 else (total - at) // left // 4 * 4
        if size:
            spans.append((at, size))
        at += size
    return spans


class Geometry:
    def __init__(self, groups, pixels):
        self.rows = pixels // COLS
        self.own = COLS // groups
        self.halo = min(5, self.own // 2)
        self.calls = [(0, n) for n in split_steps(EIN, self.halo)] + [(1, n) for n in split_steps(EOUT, self.halo)]
        self.front = self.own + 4 * self.halo
        self.back = self.own + 2 * self.halo
        self.union = self.front + (len(self.calls) - 1) * self.halo
        self.window = -(-(self.union + 2) * self.rows // 256) * 256


TAPS = [(dr, dc) for dr in (-1, 0, 1) for dc in (-1, 0, 1)]
CELL_COLS = 16


def window_kernel(geo, start, frames, valid, regions, win, meta, mrm, mrp, count, lhs, pick):
    rows, own, halo, union, width = geo.rows, geo.own, geo.halo, geo.union, geo.window
    nf = frames.shape[0]
    nv = valid.shape[0]
    lhs[:nf, :] = frames[...]
    lhs[nf : nf + nv, :] = valid[...].astype(F32).astype(BF16)
    lhs[nf + nv : nf + nv + 1, :] = regions[...].astype(F32).astype(BF16)
    per = 256 // rows
    source = lax.broadcasted_iota(jnp.int32, (COLS, 256), 0)
    lane = lax.broadcasted_iota(jnp.int32, (COLS, 256), 1)
    lane_row = lax.broadcasted_iota(jnp.int32, (1, 256), 1) % rows

    def one(n, carry):
        column = (start[0] + n * per + lane // rows) % COLS
        hit = (source == column).astype(F32).astype(BF16)
        for r in range(rows):
            keep = (lane_row == r).astype(F32).astype(BF16)
            pick[r * COLS : (r + 1) * COLS, :] = hit * keep
        got = jnp.dot(lhs[...], pick[...], preferred_element_type=F32)
        at = pl.multiple_of(n * 256, 256)
        win[:, pl.ds(at, 256)] = got[:nf].astype(BF16)
        meta[:, pl.ds(at, 256)] = got[nf:]
        return carry

    lax.fori_loop(0, width // 256, one, 0)
    px = union * rows
    ids = meta[nv : nv + 1, :]
    here = ids[:, rows : rows + px]
    picked = [
        ids[:, rows - 1 : rows - 1 + px] == here,
        ids[:, rows + 1 : rows + 1 + px] == here,
    ]
    row_at = lax.broadcasted_iota(jnp.int32, (8, px), 0)
    stack = jnp.zeros((8, px), F32)
    for k, m in enumerate(picked):
        stack = jnp.where(row_at == k, jnp.broadcast_to(m.astype(F32), (8, px)), stack)
    stack = stack.astype(BF16)
    sel = lax.broadcasted_iota(jnp.int32, (8, 128), 0)
    for k, out in enumerate((mrm, mrp)):
        out[...] = dot_tn(stack, (sel == k).astype(F32).astype(BF16)).astype(BF16)
    a = (2 * halo + 1) * rows
    count[...] = jnp.broadcast_to(jnp.sum(meta[:nv, a : a + own * rows]), count.shape)


def window_call(geo, start, frames, valid, regions):
    nf, nv = frames.shape[0], valid.shape[0]
    pixels = frames.shape[1]
    px = geo.union * geo.rows
    smem = pl.BlockSpec(memory_space=pltpu.SMEM)
    vmem = pl.BlockSpec(memory_space=pltpu.VMEM)
    total = nf + nv + 1
    return pl.pallas_call(
        functools.partial(window_kernel, geo),
        in_specs=[smem, vmem, vmem, vmem],
        out_specs=[vmem] * 5,
        out_shape=[
            jax.ShapeDtypeStruct((nf, geo.window), BF16),
            jax.ShapeDtypeStruct((nv + 1, geo.window), F32),
        ]
        + [jax.ShapeDtypeStruct((px, 128), BF16)] * 2
        + [jax.ShapeDtypeStruct((8, 128), F32)],
        scratch_shapes=[pltpu.VMEM((total, pixels), BF16), pltpu.VMEM((pixels, 256), BF16)],
        compiler_params=pltpu.CompilerParams(vmem_limit_bytes=VMEM_LIMIT),
        cost_estimate=pl.CostEstimate(
            flops=2 * total * pixels * geo.window, bytes_accessed=10 << 20, transcendentals=0
        ),
        name="window",
    )(start, frames, valid, regions)


def pack_kernel(groups, rank, conv, cells, out0, out1):
    share, depth9 = conv.shape[2:]
    chans9 = out0.shape[-1] - CELL_COLS - 9 * 128
    chans = chans9 // 9
    depth = chans + 128
    row = lax.broadcasted_iota(jnp.int32, (7, CELL_COLS), 0)
    col = lax.broadcasted_iota(jnp.int32, (7, CELL_COLS), 1)
    half = (rank[0] & 1) * 2
    for l, at, gate, out in ((0, 0, rank[0], out0), (1, 0, half, out1), (1, share, half + 1, out1)):
        w = conv[l, gate].astype(BF16)
        parts = [w[:, k * depth + chans : (k + 1) * depth] for k in range(9)]
        parts += [w[:, k * depth : k * depth + chans] for k in range(9)]
        rest = cells[:, l, :]
        cols = jnp.zeros((share, CELL_COLS), F32)
        for k in range(3):
            low = rest.astype(BF16)
            rest = rest - low.astype(F32)
            sel = ((row == gate) & (col == k)) | ((row == gate + 4) & (col == 3 + k))
            cols = cols + dot_tn(low, sel.astype(F32).astype(BF16))
        parts.append(cols.astype(BF16))
        line = jnp.concatenate(parts, 1)
        for g in range(groups):
            out[g, at : at + share, :] = line


def pack_call(groups, rank, conv_w, cells, sent_w):
    share = conv_w.shape[2]
    return plain_call(
        functools.partial(pack_kernel, groups),
        "pack",
        [jax.ShapeDtypeStruct((groups, k * share, sent_w), BF16) for k in (1, 2)],
        rank,
        conv_w,
        cells,
        smem=1,
    )


def peephole_rows(wf):
    tail = wf[:, 9 * 128 :]
    depth = tail.shape[1]
    col = lax.broadcasted_iota(jnp.int32, (8, depth), 1)
    at = depth - CELL_COLS + 3
    sel = ((col >= at) & (col < at + 3)).astype(F32).astype(BF16)
    got = dot_nt(sel, tail)
    return [got[0:1, k * 128 : (k + 1) * 128] for k in range(3)]


def make_variants(geo, h, r0, hb, mrm, mrp, base):
    m = h.shape[0]
    g0 = base * geo.rows + r0
    hb[0, r0 : r0 + m, :] = pltpu.roll(h, 1, 0).astype(BF16) * mrm[g0 : g0 + m, :]
    hb[1, r0 : r0 + m, :] = h.astype(BF16)
    hb[2, r0 : r0 + m, :] = pltpu.roll(h, m - 1, 0).astype(BF16) * mrp[g0 : g0 + m, :]


def forward_kernel(geo, layer, base, steps, first, gather, *refs):
    refs = list(refs)
    if gather:
        rank, pieces, refs = refs[0], refs[1 : 1 + gather], refs[1 + gather :]
    if not first:
        near, far = refs[:2]
        refs = refs[2:]
    if gather:
        cols, win, meta, mrm, mrp = refs[:5]
        wf = refs[12]
        refs = refs[5:12] + refs[13:]
    else:
        cols, win, meta, wf, mrm, mrp = refs[:6]
        refs = refs[6:]
    gates_out, cprev_out, hvar_out, hnew_out, xown_out, state_out, send_out = refs[:7]
    hb, hnext, cb, xs, keeps, peeps = refs[7:]
    rows, halo, own, front, back = geo.rows, geo.halo, geo.own, geo.front, geo.back
    chans = win.shape[0]
    chans9 = 9 * chans
    lanes = (front - 2) * rows
    x0 = (base + 2) * rows
    step = pl.program_id(0)

    @pl.when(step == 0)
    def _():
        hb[:, front * rows :, :] = jnp.zeros((3, rows, 128), BF16)
        if first:
            hb[:, : front * rows, :] = jnp.zeros((3, front * rows, 128), BF16)
            cb[...] = jnp.zeros_like(cb)
        else:
            nb = back * rows
            make_variants(geo, near[:, :128].astype(F32), 0, hb, mrm, mrp, base)
            make_variants(geo, far[:, :128].astype(F32), nb, hb, mrm, mrp, base)
            cb[:nb, :] = near[:, 128:].astype(F32)
            cb[nb:, :] = far[:, 128:].astype(F32)
        if gather:
            for k, piece in enumerate(pieces):
                if gather == 4:
                    gate = rank[0] ^ k
                    wf[pl.ds(pl.multiple_of(gate * 128, 128), 128), :] = piece[...] * halving(gate, piece.shape[1])
                    continue
                peers, span = piece.shape[0], piece.shape[1] // 2
                for j in range(2):
                    gate = ((rank[0] ^ k) & 1) * 2 + j
                    factor = halving(gate, piece.shape[2])
                    for g in range(peers):
                        at = pl.multiple_of(gate * 128 + g * span, span)
                        wf[pl.ds(at, span), :] = piece[g, j * span : (j + 1) * span, :] * factor
        ids = meta[meta.shape[0] - 1 :, :]
        here = ids[:, x0 : x0 + lanes]
        for tap, (dr, dc) in enumerate(TAPS):
            off = x0 + dc * rows + dr
            same = (ids[:, off : off + lanes] == here).astype(F32)
            keeps[tap * chans : (tap + 1) * chans, :] = jnp.broadcast_to(same, (chans, lanes)).astype(BF16)
        ones = lax.broadcasted_iota(jnp.int32, (CELL_COLS, lanes), 0) < 3
        xs[chans9:, :] = ones.astype(F32).astype(BF16)
        for k, row in enumerate(peephole_rows(wf)):
            peeps[k : k + 1, :] = row

    def input_taps(a, m):
        for tap, (dr, dc) in enumerate(TAPS):
            off = x0 + a + dc * rows + dr
            part = slice(tap * chans, (tap + 1) * chans)
            xs[part, a : a + m] = win[:, off : off + m] * keeps[part, a : a + m]

    chunks = cut_by_four(front - 2, 2)
    for c0, cw in chunks:
        r0, m = (c0 + 1) * rows, cw * rows
        final = c0 == chunks[-1][0]
        input_taps(c0 * rows, m)
        zero = front * rows
        lefts, rights = [], []
        for c in range(c0 + 1, c0 + 1 + cw):
            for at, side, starts in ((c - 1, 0, lefts), (c + 1, 1, rights)):
                starts.append(pl.multiple_of(zero + cols[side * geo.union + base + c] * (at * rows - zero), rows))
        parts = []
        for dr in range(3):
            parts.append(jnp.concatenate([hb[dr, pl.ds(at, rows), :] for at in lefts], 0))
            parts.append(hb[dr, r0 : r0 + m, :])
            parts.append(jnp.concatenate([hb[dr, pl.ds(at, rows), :] for at in rights], 0))
        z = dot_nt(jnp.concatenate(parts, 1), wf[:, : 9 * 128]) + lax.dot_general(
            xs[:, r0 - rows : r0 - rows + m], wf[:, 9 * 128 :], (((0,), (1,)), ((), ())), preferred_element_type=F32
        )
        if final:
            s0, sn = (2 * halo - 1) * rows, (own + 2) * rows
            hvar_out[0, :, :, :] = hb[:, s0 : s0 + sn, :]
            hb[:, rows:r0, :] = hnext[:, rows:r0, :]
        for c in range(c0 + 1, c0 + 1 + cw):
            at = slice(c * rows, (c + 1) * rows)
            zi, zf, zo, zg = (z[(c - c0 - 1) * rows : (c - c0) * rows, n * 128 : (n + 1) * 128] for n in range(4))
            cell = cb[at, :]
            if halo <= c < halo + back:
                cprev_out[0, (c - halo) * rows : (c - halo + 1) * rows, :] = cell.astype(BF16)
            gi = logistic_of_twice(zi + peeps[0:1, :] * cell)
            gf = logistic_of_twice(zf + peeps[1:2, :] * cell)
            gg = jnp.tanh(zg)
            cell = gf * cell + gi * gg
            go = logistic_of_twice(zo + peeps[2:3, :] * cell)
            h = go * jnp.tanh(cell)
            cb[at, :] = cell
            make_variants(geo, h, c * rows, hb if final else hnext, mrm, mrp, base)
            if halo <= c < halo + back:
                out = slice((c - halo) * rows, (c - halo + 1) * rows)
                for n, gate in enumerate((gi, gf, go, gg)):
                    gates_out[0, n, out, :] = gate.astype(BF16)
                hnew_out[0, out, :] = h.astype(BF16)

    q0 = (2 * halo - 1) * rows
    xown_out[0, :, :] = xs[:, q0 : q0 + own * rows]

    @pl.when(step == steps - 1)
    def _():
        a, b = halo * rows, (halo + back) * rows
        state_out[:, :128] = hb[1, a:b, :]
        state_out[:, 128:] = cb[a:b, :].astype(BF16)
        a, b = 3 * halo * rows, 5 * halo * rows
        send_out[:, :128] = hb[1, a:b, :]
        send_out[:, 128:] = cb[a:b, :].astype(BF16)


def whole(shape):
    return pl.BlockSpec(shape, lambda *_: (0,) * len(shape))


def forward_call(geo, layer, base, first_frame, steps, state, win, meta, weights, masks):
    rows, own, front, back = geo.rows, geo.own, geo.front, geo.back
    chans = win.shape[0] // (EIN + EOUT)
    gather = len(weights) - 1 if isinstance(weights, tuple) else 0
    sent_w = weights[1].shape[-1] if gather else weights.shape[1]
    depth = sent_w - 9 * 128
    by_step = lambda *dims: pl.BlockSpec((1,) + dims, lambda t: (t,) + (0,) * len(dims))
    lead = list(weights) if gather else []
    cols, masks = masks[2], masks[:2]
    smem = pl.BlockSpec(memory_space=pltpu.SMEM)
    operands = lead + list(state) + [cols, win, meta] + ([] if gather else [weights]) + list(masks)
    in_specs = [smem] if gather else []
    in_specs += [whole(v.shape) for v in lead[1:]]
    in_specs += [whole(s.shape) for s in state]
    in_specs += [smem, pl.BlockSpec((chans, win.shape[1]), lambda t: (first_frame + t, 0))]
    in_specs += [whole(v.shape) for v in operands[len(lead) + len(state) + 2 :]]
    shapes = [
        (steps, 4, back * rows, 128),
        (steps, back * rows, 128),
        (steps, 3, (own + 2) * rows, 128),
        (steps, back * rows, 128),
        (steps, depth, own * rows),
    ]
    flat = [(back * rows, 256), (2 * geo.halo * rows, 256)] + ([(512, sent_w)] if gather else [])
    outs = [jax.ShapeDtypeStruct(s, BF16) for s in shapes + flat]
    out_specs = [by_step(*s[1:]) for s in shapes] + [whole(s) for s in flat]
    px = front * rows
    return pl.pallas_call(
        functools.partial(forward_kernel, geo, layer, base, steps, not state, gather),
        grid=(steps,),
        in_specs=in_specs,
        out_specs=out_specs,
        out_shape=outs,
        scratch_shapes=[
            pltpu.VMEM((3, px + rows, 128), BF16),
            pltpu.VMEM((3, px, 128), BF16),
            pltpu.VMEM((px, 128), F32),
            pltpu.VMEM((depth, px - 2 * rows), BF16),
            pltpu.VMEM((9 * chans, px - 2 * rows), BF16),
            pltpu.VMEM((8, 128), F32),
        ],
        compiler_params=pltpu.CompilerParams(vmem_limit_bytes=VMEM_LIMIT),
        cost_estimate=pl.CostEstimate(
            flops=steps * px * 512 * 1296 * 2, bytes_accessed=8 << 20, transcendentals=steps * px * 640
        ),
        name=f"forward_{base}",
    )(*operands)


def backward_kernel(geo, layer, base, steps, first_live, first, last, carried, *refs):
    refs = list(refs)
    if carried:
        sums_in, head_in = refs[:2]
        refs = refs[2:]
    if not first:
        local, far = refs[:2]
        refs = refs[2:]
    cols, gates, cprev, wf, mrm, mrp = refs[:6]
    refs = refs[6:]
    if layer == 1:
        hnew, target, meta, head, head_b = refs[:5]
        refs = refs[5:]
    dz_out, sums_out, head_out, carry_out, send_out = refs[:5]
    dh, dc, dz_near, dz_far, peeps, wb = refs[5:]
    rows, halo, own, back = geo.rows, geo.halo, geo.own, geo.back
    o0, on = halo * rows, own * rows
    half = back // 2
    step = pl.program_id(0)

    @pl.when(step == 0)
    def _():
        sums_out[...] = sums_in[...] if carried else jnp.zeros_like(sums_out)
        head_out[...] = head_in[...] if carried else jnp.zeros_like(head_out)
        for tap in range(9):
            across, along = tap % 3 * 512, tap // 3 * 128
            wb[across : across + 384, along : along + 128] = wf[:384, tap * 128 : (tap + 1) * 128] * 2
            wb[across + 384 : across + 512, along : along + 128] = wf[384:, tap * 128 : (tap + 1) * 128]
        edge = jnp.zeros((4, rows, 128), BF16)
        dz_near[:, :rows, :] = edge
        dz_far[:, :rows, :] = edge
        dz_far[:, (back - half) * rows :, :] = edge
        for k, row in enumerate(peephole_rows(wf)):
            peeps[k : k + 1, :] = row * 2.0
        if first:
            dh[...] = jnp.zeros_like(dh)
            dc[...] = jnp.zeros_like(dc)
        else:
            nf = 2 * halo * rows
            dh[:nf, :] = far[:, :128]
            dc[:nf, :] = far[:, 128:]
            dh[nf:, :] = local[:, :128]
            dc[nf:, :] = local[:, 128:]

    if layer == 1:
        guess = dot_nt(head[...], hnew[0]) + head_b[...]
        a0 = (base + halo + 1) * rows
        err = guess - target[:, a0 : a0 + back * rows].astype(F32)
        dy = meta[pl.ds(first_live + steps - 1 - step, 1), a0 : a0 + back * rows] * err
        low = dy.astype(BF16)
        head_out[:, 0:128] += jnp.dot(low[:, o0 : o0 + on], hnew[0, o0 : o0 + on, :], preferred_element_type=F32)
        own_dy = low[:, o0 : o0 + on].astype(F32)
        head_out[:, 128:129] += jnp.sum(own_dy, 1, keepdims=True)
        head_out[:, 129:130] += jnp.sum((dy * err)[:, o0 : o0 + on], 1, keepdims=True)
        dh[...] = (dh[...].astype(F32) + dot_tn(low, head[...])).astype(BF16)

    def gates_chunk(c0, cw):
        r0, m = c0 * rows, cw * rows
        span = slice(r0, r0 + m)
        gi, gf, go, gg = (gates[0, n, span, :] for n in range(4))
        pi, pf, po = (peeps[n : n + 1, :].astype(BF16) for n in range(3))
        c = cprev[0, span, :]
        cn = gf * c + gi * gg
        tc = jnp.tanh(cn)
        u = dh[span, :] * go
        w = u * tc
        d_o = w * (1 - go)
        d_c = dc[span, :] + u * ((1 - tc) * (1 + tc)) + d_o * po
        a_i = d_c * gi
        d_i = a_i * gg * (1 - gi)
        d_g = a_i * ((1 - gg) * (1 + gg))
        a_f = d_c * gf
        d_f = a_f * c * (1 - gf)
        dc[span, :] = a_f + d_i * pi + d_f * pf
        store, p0 = (dz_near, rows + r0) if c0 <= half else (dz_far, r0 - half * rows)
        for n, d in enumerate((d_i, d_f, d_o, d_g)):
            store[n, p0 : p0 + m, :] = d
        a = max(r0, o0) - r0
        b = min(r0 + m, o0 + on) - r0
        if b > a:
            for n, d in enumerate((d_i * c, d_f * c, d_o * cn)):
                part = d[a:b].astype(F32).reshape((b - a) // 8, 8, 128)
                sums_out[n * 8 : (n + 1) * 8, :] += jnp.sum(part, 0)

    def hidden_chunk(c0, cw):
        r0, m = c0 * rows, cw * rows
        g0 = (base + halo) * rows + r0
        parts = []
        for side, shift in ((0, 1), (None, 0), (1, -1)):
            pieces = []
            for c in range(c0 + shift, c0 + cw + shift):
                ref, at = (dz_near, (c + 1) * rows) if c <= half else (dz_far, (c - half) * rows)
                if side is not None:
                    at = pl.multiple_of(cols[side * geo.union + base + halo + c] * at, rows)
                pieces.append((ref, at))
            for n in range(4):
                parts.append(jnp.concatenate([ref[n, pl.ds(at, rows), :] for ref, at in pieces], 0))
        acc = jnp.dot(jnp.concatenate(parts, 1), wb[...], preferred_element_type=F32)
        above = pltpu.roll(acc[:, :128] * mrm[g0 : g0 + m, :].astype(F32), m - 1, 0)
        below = pltpu.roll(acc[:, 256:] * mrp[g0 : g0 + m, :].astype(F32), 1, 0)
        dh[r0 : r0 + m, :] = (acc[:, 128:256] + above + below).astype(BF16)

    for c0, cw in cut(half + 1, max(1, (half + 1) // 1)):
        gates_chunk(c0, cw)
    hidden_chunk(0, half)
    for c0, cw in cut(back - half - 1, max(1, (back - half - 1) // 1)):
        gates_chunk(half + 1 + c0, cw)
    hidden_chunk(half, back - half)
    lo = (half + 1 - halo) * rows
    for n in range(4):
        dz_out[0, :lo, n * 128 : (n + 1) * 128] = dz_near[n, rows + o0 : rows + o0 + lo, :]
        dz_out[0, lo:, n * 128 : (n + 1) * 128] = dz_far[n, rows : rows + on - lo, :]

    @pl.when(step == steps - 1)
    def _():
        carry_out[:, :128] = dh[o0 : o0 + on, :]
        carry_out[:, 128:] = dc[o0 : o0 + on, :]
        ns = 2 * halo * rows
        s0 = o0 + on - ns
        send_out[:, :128] = dh[s0 : s0 + ns, :]
        send_out[:, 128:] = dc[s0 : s0 + ns, :]


def backward_call(geo, layer, base, steps, last, carried, state, saved, wf, masks, extra):
    rows, own, back, halo = geo.rows, geo.own, geo.back, geo.halo
    by_step = lambda *dims: pl.BlockSpec((1,) + dims, lambda t: (steps - 1 - t,) + (0,) * len(dims))
    first_live = saved["t"] - EIN
    lead = list(carried) + list(state)
    cols, masks = masks[2], masks[:2]
    operands = lead + [cols, saved["gates"], saved["cprev"], wf] + list(masks)
    in_specs = [whole(s.shape) for s in lead] + [pl.BlockSpec(memory_space=pltpu.SMEM)]
    in_specs += [by_step(4, back * rows, 128), by_step(back * rows, 128)]
    in_specs += [whole(v.shape) for v in operands[len(lead) + 3 :]]
    if layer == 1:
        win, meta, head, head_b = extra
        operands += [saved["hnew"], win, meta, head, head_b]
        t0 = saved["t"]
        in_specs += [
            by_step(back * rows, 128),
            pl.BlockSpec((head.shape[0], win.shape[1]), lambda t: (t0 + steps - 1 - t, 0)),
            whole(meta.shape),
            whole(head.shape),
            whole(head_b.shape),
        ]
    outs = [
        jax.ShapeDtypeStruct((steps, own * rows, 512), BF16),
        jax.ShapeDtypeStruct((24, 128), F32),
        jax.ShapeDtypeStruct((16, 256), F32),
        jax.ShapeDtypeStruct((own * rows, 256), BF16),
        jax.ShapeDtypeStruct((2 * halo * rows, 256), BF16),
    ]
    out_specs = [by_step(own * rows, 512)] + [whole(o.shape) for o in outs[1:]]
    px = back * rows
    return pl.pallas_call(
        functools.partial(backward_kernel, geo, layer, base, steps, first_live, not state, last, bool(carried)),
        grid=(steps,),
        in_specs=in_specs,
        out_specs=out_specs,
        out_shape=outs,
        scratch_shapes=[
            pltpu.VMEM((px, 128), BF16),
            pltpu.VMEM((px, 128), BF16),
            pltpu.VMEM((4, (back // 2 + 2) * rows, 128), BF16),
            pltpu.VMEM((4, (back - back // 2 + 1) * rows, 128), BF16),
            pltpu.VMEM((8, 128), F32),
            pltpu.VMEM((3 * 512, 3 * 128), BF16),
        ],
        compiler_params=pltpu.CompilerParams(vmem_limit_bytes=VMEM_LIMIT),
        cost_estimate=pl.CostEstimate(
            flops=steps * px * 512 * 1536 * 2, bytes_accessed=8 << 20, transcendentals=steps * px * 128
        ),
        name=f"backward_{base}",
    )(*operands)


def split_low(v, axis=0):
    hi = v.astype(BF16)
    return jnp.concatenate([hi, (v - hi.astype(F32)).astype(BF16)], axis)


def joined(v):
    half = v.shape[0] // 2
    return v[:half].astype(F32) + v[half:].astype(F32)


def weight_kernel(geo, base, steps, add, final, small, *refs):
    refs = list(refs)
    if final:
        rank, refs = refs[0], refs[1:]
    if add:
        acc, refs = refs[0], refs[1:]
    if small:
        sums0, sums1, bias1, head, count = refs[:5]
        refs = refs[5:]
    cols, dz, hvar, xown = refs[:4]
    outs, rhs = refs[4:-1], refs[-1]
    rows, own, halo = geo.rows, geo.own, geo.halo
    on = own * rows
    wide = hvar.shape[-1]
    part = pl.program_id(0)
    if final:
        odd = (rank[0] & 1) == 1

    def put(g):
        at = slice(0, g.shape[0])
        if add:
            g = g + acc[at, :]
        if not final:
            outs[0][at, :] = g
            return g
        keep, send = outs[:2]
        for j in range(2):
            even_gate = g[:, 2 * j * wide : (2 * j + 1) * wide]
            odd_gate = g[:, (2 * j + 1) * wide : (2 * j + 2) * wide]
            keep[j, at, :] = jnp.where(odd, odd_gate, even_gate)
            send[j, at, :] = jnp.where(odd, even_gate, odd_gate).astype(BF16)
        return g

    @pl.when(part < 3)
    def _():
        for dc in range(3):
            lanes = slice(dc * wide, (dc + 1) * wide)
            if dc == 1:
                for j in range(steps):
                    rhs[j * on : (j + 1) * on, lanes] = hvar[j, 0, rows : rows + on, :]
                continue
            for c in range(own):
                keep = cols[dc // 2 * geo.union + base + 2 * halo + c].astype(F32)
                keep = jnp.full((1, wide), keep, F32).astype(BF16)
                for j in range(steps):
                    at = j * on + c * rows
                    rhs[at : at + rows, lanes] = hvar[j, 0, (dc + c) * rows : (dc + c + 1) * rows, :] * keep
        put(dot_tn(rhs[...], dz[...]))

    @pl.when(part == 3)
    def _():
        depth = xown.shape[1]
        inputs = None
        for j in range(steps):
            got = jnp.dot(xown[j], dz[j * on : (j + 1) * on, :], preferred_element_type=F32)
            inputs = got if inputs is None else inputs + got
        bias = put(inputs)[depth - CELL_COLS : depth - CELL_COLS + 8]
        if final and not small:
            outs[2][...] = bias
        if small:
            few = []
            for row, sums in ((bias, sums0), (bias1[...], sums1)):
                few += [row[0:1, k * wide : (k + 1) * wide] for k in range(4)]
                few.append(jnp.sum(sums[...].reshape(3, 8, wide), 1))
            few = jnp.concatenate(few + [jnp.zeros((2, wide), F32)], 0)
            col = lax.broadcasted_iota(jnp.int32, (16, wide), 1)
            extra = jnp.where(col == 2, jnp.broadcast_to(count[0:1, :], (16, wide)), head[:, wide:])
            few = jnp.concatenate([few, head[:, :wide], extra], 0)
            outs[2][...] = few
            outs[1][0, depth : depth + 96, :] = split_low(few)


def weight_call(geo, base, steps, acc, dz, hvar, xown, cols, rank=None, small=()):
    on = geo.own * geo.rows
    dz = dz.reshape(steps * on, 512)
    final = rank is not None
    band = 3 * hvar.shape[-1]
    operands = ([rank] if final else []) + ([] if acc is None else [acc]) + list(small) + [cols, dz, hvar, xown]
    specs = [pl.BlockSpec(memory_space=pltpu.SMEM)] if final else []
    specs += [] if acc is None else [pl.BlockSpec((band, 512), lambda i: (i, 0))]
    specs += [whole(v.shape) for v in small] + [pl.BlockSpec(memory_space=pltpu.SMEM), whole(dz.shape)]
    specs += [pl.BlockSpec((steps, 1) + hvar.shape[2:], lambda i: (0, jnp.minimum(i, 2), 0, 0))]
    specs += [whole(xown.shape)]
    out_shape = jax.ShapeDtypeStruct((4 * band, 512), F32)
    out_specs = pl.BlockSpec((band, 512), lambda i: (i, 0))
    if final:
        out_shape = [
            jax.ShapeDtypeStruct((2, 4 * band, 128), F32),
            jax.ShapeDtypeStruct((2, 4 * band, 128), BF16),
            jax.ShapeDtypeStruct((48, 128) if small else (8, 512), F32),
        ]
        out_specs = [pl.BlockSpec((2, band, 128), lambda i: (0, i, 0))] * 2 + [whole(out_shape[2].shape)]
    return pl.pallas_call(
        functools.partial(weight_kernel, geo, base, steps, acc is not None, final, bool(small)),
        grid=(4,),
        in_specs=specs,
        out_specs=out_specs,
        out_shape=out_shape,
        scratch_shapes=[pltpu.VMEM((steps * on, band), BF16)],
        compiler_params=pltpu.CompilerParams(vmem_limit_bytes=VMEM_LIMIT),
        cost_estimate=pl.CostEstimate(
            flops=steps * on * 512 * 1296 * 2, bytes_accessed=16 << 20, transcendentals=0
        ),
        name=f"weights_{base}",
    )(*operands)


SMALL_AT = 1408


def core_stage_kernel(rank, keep, got, *refs):
    depth = refs[1].shape[0] if len(refs) > 2 else refs[0].shape[0]
    high = (rank[0] & 2) == 2
    small = len(refs) > 2
    if small:
        few, keep_out, send_out, few_out = refs
    else:
        keep_out, send_out = refs
    a = keep[0, :depth, :] + got[0, :depth, :].astype(F32)
    b = keep[1, :depth, :] + got[1, :depth, :].astype(F32)
    keep_out[...] = jnp.where(high, b, a)
    send_out[:depth, :] = jnp.where(high, a, b).astype(BF16)
    if small:
        total = few[...] + joined(got[0, depth : depth + 96, :])
        few_out[...] = total
        send_out[depth:, :] = split_low(total)


def chip_stage_kernel(groups, keep, got, *refs):
    depth, wide = keep.shape
    small = len(refs) > 1
    if small:
        few, out = refs
    else:
        (out,) = refs
    width = depth - CELL_COLS
    share = wide // groups
    total = (keep[...] + got[:depth, :].astype(F32)).T[:, :width].astype(BF16)
    if small:
        sums = few[...] + joined(got[depth:, :])
        head = split_low(sums[16:32], 1)
        extra = split_low(sums[32:, :16], 1)
        fill = jnp.zeros((16, SMALL_AT - width - 2 * share - 32), BF16)
    for g in range(groups):
        part = total[g * share : (g + 1) * share, :]
        if not small:
            out[g, :, :] = part
        else:
            cells = split_low(sums[:16, g * share : (g + 1) * share], 1)
            out[g, :, :] = jnp.concatenate([part, cells, extra, fill, head], 1)


def sum_stage_kernel(got, out):
    total = got[0].astype(F32)
    for g in range(1, got.shape[0]):
        total = total + got[g].astype(F32)
    out[...] = total.astype(BF16)


def finish_kernel(rate, chans, got, steps_done, *refs):
    (cell_refs, head_refs, bias_refs), refs = (refs[:3], refs[3:6], refs[6:9]), refs[9:]
    shard, scalars, loss, cell_outs, head_outs, bias_outs = refs[0], refs[1], refs[2], refs[3:7], refs[7:11], refs[11:]
    total = got[0].astype(F32)
    for g in range(1, got.shape[0]):
        total = total + got[g].astype(F32)
    width = shard.shape[1]
    share = total.shape[0]
    shard[...] = total[:, :width].astype(BF16)
    cells = total[:, width : width + share] + total[:, width + share : width + 2 * share]
    at = width + 2 * share
    extra = total[:, at : at + 16] + total[:, at + 16 : at + 32]
    head = total[:, SMALL_AT : SMALL_AT + 128] + total[:, SMALL_AT + 128 :]
    count = chans * extra[0:1, 2:3]
    scale = 2.0 / count
    fresh = [1.0 / (jnp.full((1, 1), steps_done[k].astype(F32)) + 1.0) for k in range(4)]
    loss[...] = jnp.sum(extra[:, 1:2], 0, keepdims=True) / count
    lane = lax.broadcasted_iota(jnp.int32, (8, 128), 1)
    scalars[...] = jnp.where(lane == 0, scale, jnp.where(lane == 1, rate, fresh[0]))

    def update(refs, outs, at, grad, fresh):
        param, mom, avg = (v[at] for v in refs)
        grad = grad * scale
        m = MU * mom + grad
        p = param - rate * (grad + MU * m)
        outs[0][at] = m
        outs[1][at] = avg + (p - avg) * fresh
        outs[2][at] = p
        outs[3][at] = p.astype(BF16)

    for l in range(2):
        update(cell_refs, cell_outs, (slice(None), l, slice(None)), cells[l * 7 : (l + 1) * 7, :], fresh[1])
    update(head_refs, head_outs, (slice(None), slice(None)), head, fresh[2])
    row = lax.broadcasted_iota(jnp.int32, (16, 16), 0)
    col = lax.broadcasted_iota(jnp.int32, (16, 16), 1)
    bias = jnp.sum(jnp.where(row == col, jnp.broadcast_to(extra[:, 0:1], (16, 16)), 0.0), 0, keepdims=True)
    update(bias_refs, bias_outs, (slice(None), slice(None)), bias, fresh[3])


def plain_call(kernel, name, out_shape, *operands, smem=0, moved=4 << 20, smem_at=()):
    where = [pltpu.SMEM if i < smem or i in smem_at else pltpu.VMEM for i in range(len(operands))]
    specs = [pl.BlockSpec(memory_space=m) for m in where]
    return pl.pallas_call(
        kernel,
        in_specs=specs,
        out_shape=out_shape,
        compiler_params=pltpu.CompilerParams(vmem_limit_bytes=VMEM_LIMIT),
        cost_estimate=pl.CostEstimate(flops=1 << 20, bytes_accessed=moved, transcendentals=0),
        name=name,
    )(*operands)


def core_stage(name, rank, depth, keep, got, small):
    wide = keep.shape[2]
    more = 96 if small else 0
    shapes = [jax.ShapeDtypeStruct((depth, wide), F32), jax.ShapeDtypeStruct((depth + more, wide), BF16)]
    shapes += [jax.ShapeDtypeStruct(v.shape, F32) for v in small]
    return plain_call(core_stage_kernel, "core_stage_" + name, shapes, rank, keep, got, *small, smem=1)


def chip_stage(name, groups, keep, got, small):
    depth, wide = keep.shape
    lanes = SMALL_AT + 256 if small else depth - CELL_COLS
    shape = jax.ShapeDtypeStruct((groups, wide // groups, lanes), BF16)
    kernel = functools.partial(chip_stage_kernel, groups)
    return plain_call(kernel, "chip_stage_" + name, shape, keep, got, *small, moved=2 << 20)


def sum_stage(name, got):
    shape = jax.ShapeDtypeStruct(got.shape[1:], BF16)
    return plain_call(sum_stage_kernel, "sum_stage_" + name, shape, got, moved=1 << 20)


def finish_stage(rate, chans, width, got, step_count, small_args):
    shapes = [
        jax.ShapeDtypeStruct((got.shape[1], width), BF16),
        jax.ShapeDtypeStruct((8, 128), F32),
        jax.ShapeDtypeStruct((1, 1), F32),
    ]
    for v in small_args[::3]:
        shapes += [jax.ShapeDtypeStruct(v.shape, F32)] * 3 + [jax.ShapeDtypeStruct(v.shape, BF16)]
    kernel = functools.partial(finish_kernel, rate, chans)
    return plain_call(kernel, "finish", shapes, got, step_count, *small_args, moved=1 << 20, smem_at=(1,))


def update_kernel(rank, scalars, *refs):
    pieces = (refs[:4], refs[4:8])
    param, mom, avg, mom_out, avg_out, new_out, low_out, grad = refs[8:]
    layer = pl.program_id(0)
    chans = (grad.shape[-1] - 9 * 128) // 9
    scale, rate, fresh = (scalars[0:1, k : k + 1] for k in range(3))
    for l in range(2):

        @pl.when(layer == l)
        def _():
            for k, piece in enumerate(pieces[l]):
                v = piece[...].astype(F32)
                parts = []
                for tap in range(9):
                    parts.append(v[:, 9 * 128 + tap * chans : 9 * 128 + (tap + 1) * chans])
                    parts.append(v[:, tap * 128 : (tap + 1) * 128])
                grad[rank[0] ^ k] = jnp.concatenate(parts, 1) * scale

    g = grad[...]
    m = MU * mom[0] + g
    p = param[0] - rate * (g + MU * m)
    mom_out[0] = m
    new_out[0] = p
    low_out[0] = p.astype(BF16)
    avg_out[0] = avg[0] + (p - avg[0]) * fresh


def update_call(rank, scalars, pieces, param, mom, avg):
    layers, gates, share, width = param.shape
    block = pl.BlockSpec((1, gates, share, width), lambda l: (l, 0, 0, 0))
    smem = pl.BlockSpec(memory_space=pltpu.SMEM)
    shape = jax.ShapeDtypeStruct(param.shape, F32)
    return pl.pallas_call(
        update_kernel,
        grid=(layers,),
        in_specs=[smem, whole(scalars.shape)] + [whole(v.shape) for v in pieces] + [block] * 3,
        out_specs=[block] * 4,
        out_shape=[shape] * 3 + [jax.ShapeDtypeStruct(param.shape, BF16)],
        scratch_shapes=[pltpu.VMEM((gates, share, width), F32)],
        compiler_params=pltpu.CompilerParams(vmem_limit_bytes=VMEM_LIMIT),
        cost_estimate=pl.CostEstimate(flops=1 << 20, bytes_accessed=6 << 20, transcendentals=0),
        name="update",
    )(rank, scalars, *pieces, param, mom, avg)


def swap_pairs(size, bit):
    return [(i, i ^ bit) for i in range(size)]


def butterfly_bits(size):
    bits, bit = [], 1
    while bit < size:
        bits.append(bit)
        bit *= 2
    return bits


def gather_dp(piece, ranks):
    me = lax.axis_index("dp")
    for bit in butterfly_bits(ranks)[1:] + [1]:
        other = lax.ppermute(piece, "dp", swap_pairs(ranks, bit))
        high = (me & bit) != 0
        pair = jnp.stack([jnp.where(high, other, piece), jnp.where(high, piece, other)])
        if bit == 1:
            piece = jnp.swapaxes(pair, 0, 1).reshape((-1,) + piece.shape[1:])
        else:
            piece = pair.reshape((-1,) + piece.shape[1:])
    return piece


def scatter_sum_dp(whole_sum, ranks, small):
    me = lax.axis_index("dp")
    value = whole_sum
    bits = butterfly_bits(ranks)
    for n, bit in enumerate([1] + bits[:0:-1]):
        if bit == 1:
            halves = value.reshape((ranks // 2, 2) + value.shape[1:])
            low, high = halves[:, 0], halves[:, 1]
        else:
            half = value.shape[0] // 2
            low, high = value[:half], value[half:]
        mine_high = (me & bit) != 0
        send = jnp.where(mine_high, low, high).astype(BF16)
        keep = jnp.where(mine_high, high, low)
        pairs = swap_pairs(ranks, bit)
        value = keep + lax.ppermute(send, "dp", pairs).astype(F32)
        hi = lax.reduce_precision(small, 8, 7)
        got = lax.ppermute(jnp.stack([hi, small - hi]).astype(BF16), "dp", pairs).astype(F32)
        small = small + (got[0] + got[1])
    return value[0], small


def gathered_weights(conv_w, cell_params, dp_at, groups, ranks, chans):
    share = conv_w.shape[2]
    wide = share * groups
    taps = conv_w.reshape(2, 4 * share, 9, chans + wide).astype(BF16)
    parts = [
        taps[..., chans:].reshape(2, 4 * share, 9 * wide),
        taps[..., :chans].reshape(2, 4 * share, 9 * chans),
    ]
    cells = jnp.stack([cell_params[:, :4], jnp.pad(cell_params[:, 4:], ((0, 0), (0, 1), (0, 0)))], -1)
    cell_hi = lax.reduce_precision(cells, 8, 7)
    cell_mid = lax.reduce_precision(cells - cell_hi, 8, 7)
    cell_lo = cells - cell_hi - cell_mid
    cell_parts = jnp.stack([cell_hi, cell_mid, cell_lo], -1).astype(BF16).reshape(2, 4 * share, 6)
    parts.append(jnp.pad(cell_parts, ((0, 0), (0, 0), (0, CELL_COLS - 6))))
    packed = jnp.concatenate(parts, -1)
    slab = 4 * share // ranks
    sent_w = packed.shape[-1]
    mine = lax.dynamic_slice_in_dim(packed.reshape(2, ranks, slab, sent_w), dp_at, 1, 1)[:, 0]
    everyone = lax.all_to_all(
        jnp.broadcast_to(mine[None], (groups, 2, slab, sent_w)), "gate", 0, 0, tiled=True
    )
    gathered = gather_dp(everyone[None], ranks)
    full = gathered.transpose(2, 1, 0, 3, 4).reshape(2, groups, 4, share, sent_w)
    full = full.transpose(0, 2, 1, 3, 4).reshape(2, 4 * wide, sent_w)
    gate = jnp.arange(4 * wide)[:, None] // wide
    full = full * jnp.where(gate == 3, 1.0, 0.5).astype(BF16)
    return [full[0], full[1]]


def on_device(
    frames,
    regions,
    valid,
    step_count,
    conv_w,
    cell_params,
    head_w,
    head_b,
    conv_mom,
    cell_mom,
    head_mom,
    bias_mom,
    conv_avg,
    cell_avg,
    head_avg,
    bias_avg,
):
    share = conv_w.shape[2]
    chans = frames.shape[1]
    pixels = frames.shape[2]
    wide = head_w.shape[1]
    groups = lax.axis_size("gate")
    ranks = lax.axis_size("dp")
    geo = Geometry(groups, pixels)
    rows, own, halo, front, back, union = geo.rows, geo.own, geo.halo, geo.front, geo.back, geo.union
    gate_at = lax.axis_index("gate")
    dp_at = lax.axis_index("dp")

    order = ring_order(groups)
    place = [order.index(g) for g in range(groups)]
    spot = jnp.asarray(place, jnp.int32)[gate_at]
    spot = jnp.where(dp_at % 2 == 1, groups - 1 - spot, spot)
    ring = ("dp", "gate")
    from_right = []
    for r in range(ranks):
        walk = order[::-1] if r % 2 else order
        from_right += [(r * groups + walk[(i + 1) % groups], r * groups + walk[i]) for i in range(groups)]
    from_left = [(b, a) for a, b in from_right]

    slab = 4 * share // ranks
    packed_w = 9 * (wide + chans)
    sent_w = packed_w + CELL_COLS
    direct = ranks == 4 and slab == share and share % 16 == 0
    rank = dp_at.astype(jnp.int32).reshape(1)

    start = jnp.mod(spot * own - 2 * halo - 1, COLS).astype(jnp.int32).reshape(1)
    win, meta, mrm, mrp, counted = window_call(
        geo, start, frames.reshape(-1, pixels), valid, regions.reshape(1, pixels)
    )
    first_row = lax.slice_in_dim(regions, 0, COLS) // 2
    bands = lax.dynamic_slice_in_dim(jnp.concatenate([first_row, first_row]), start[0], union + 2)
    same = (bands[1:] == bands[:-1]).astype(jnp.int32)
    cols = jnp.concatenate([same[:-1], same[1:]])
    masks = (mrm, mrp, cols)

    head_low = head_w.astype(BF16)
    head_bias = head_b[:, None]
    if direct:
        by_core, by_chip = swap_pairs(ranks, 1), swap_pairs(ranks, 2)
        cells_first = jnp.swapaxes(cell_params, 0, 1)
        mine0, mine1 = pack_call(groups, rank, conv_w, cells_first, sent_w)
        mixed0 = lax.all_to_all(mine0, "gate", 0, 0, tiled=True).reshape(groups * share, sent_w)
        mixed0, win, mine1 = lax.optimization_barrier((mixed0, win, mine1))
        over_x = lax.ppermute(mixed0, "dp", by_chip)
        over_core = lax.ppermute(mixed0, "dp", by_core)
        weights = [(rank, mixed0, over_core, over_x, lax.ppermute(over_x, "dp", by_core))]
        mixed1 = lax.all_to_all(mine1, "gate", 0, 0, tiled=True)
        weights.append((rank, mixed1))
    else:
        weights = gathered_weights(conv_w, cell_params, dp_at, groups, ranks, chans)

    state = ()
    kept = []
    t = 0
    for n, (layer, steps) in enumerate(geo.calls):
        base = n * halo
        first_frame = t if layer == 0 else t - 1
        got = forward_call(geo, layer, base, first_frame, steps, state, win, meta, weights[layer], masks)
        if len(got) > 7:
            weights[layer] = got[7]
        if direct and n == 0:
            mixed1, sent = lax.optimization_barrier((weights[1][1], got[6]))
            weights[1] = (rank, mixed1, lax.ppermute(mixed1, "dp", swap_pairs(ranks, 1)))
            got = [*got[:6], sent, *got[7:]]
        kept.append(dict(gates=got[0], cprev=got[1], hvar=got[2], hnew=got[3], xown=got[4], t=t))
        out = got[5]
        t += steps
        if n + 1 < len(geo.calls):
            far = lax.ppermute(got[6], ring, from_right)
            state = (out, far)

    state = ()
    grads = [None, None]
    cell_sums = [None, None]
    head_sums = None
    for n in range(len(geo.calls) - 1, -1, -1):
        layer, steps = geo.calls[n]
        base = n * halo
        saved = kept[n]
        extra = (win, meta, head_low, head_bias) if layer == 1 else None
        carried = () if cell_sums[layer] is None else (cell_sums[layer], head_sums)
        got = backward_call(
            geo, layer, base, steps, n == 0, carried, state, saved, weights[layer], masks, extra
        )
        if n > 0:
            far = lax.ppermute(got[4], ring, from_left)
            state = (got[3], far)
        cell_sums[layer] = got[1]
        if layer == 1:
            head_sums = got[2]
        done = direct and (n == 0 or geo.calls[n - 1][0] != layer)
        dz = got[0]
        if done and layer == 0:
            keep1, send1, dz = lax.optimization_barrier((*core_stage("1", rank, sent_w, grads[1][0], crossed1, ()), dz))
            crossed1 = lax.ppermute(send1, "dp", swap_pairs(ranks, 2))
        grads[layer] = weight_call(
            geo,
            base,
            steps,
            grads[layer],
            dz,
            saved["hvar"],
            saved["xown"],
            cols,
            rank if done else None,
            (cell_sums[0], cell_sums[1], grads[1][2], head_sums, counted) if done and layer == 0 else (),
        )
        if done and layer == 1:
            send1, far = lax.optimization_barrier((grads[1][1], far))
            state = (got[3], far)
            crossed1 = lax.ppermute(send1, "dp", swap_pairs(ranks, 1))
    if direct:
        pairs = swap_pairs(ranks, 1)
        across = swap_pairs(ranks, 2)
        keep0, send0, few = grads[0]
        send0, crossed1 = lax.optimization_barrier((send0, crossed1))
        crossed0 = lax.ppermute(send0, "dp", pairs)
        message1, crossed0 = lax.optimization_barrier((chip_stage("1", groups, keep1, crossed1, ()), crossed0))
        mixed1 = lax.all_to_all(message1, "gate", 0, 0, tiled=True)
        keep0, send0, few = core_stage("0", rank, sent_w, keep0, crossed0, (few,))
        crossed0 = lax.ppermute(send0, "dp", across)
        shard1, crossed0 = lax.optimization_barrier((sum_stage("1", mixed1), crossed0))
        from_dp1 = [lax.ppermute(shard1, "dp", swap_pairs(ranks, k)) for k in (1, 2, 3)]
        message0 = chip_stage("0", groups, keep0, crossed0, (few,))
        mixed0 = lax.all_to_all(message0, "gate", 0, 0, tiled=True)
        *from_dp1, mixed0 = lax.optimization_barrier((*from_dp1, mixed0))
        total_pixels = EOUT * pixels * ranks
        flip = lambda v: jnp.swapaxes(v, 0, 1)
        small_args = [cells_first, flip(cell_mom), flip(cell_avg), head_w, head_mom, head_avg]
        small_args += [v[None] for v in (head_b, bias_mom, bias_avg)]
        rate = float(RATE_SCALE * chans * total_pixels**0.5)
        done = finish_stage(rate, chans, packed_w, mixed0, step_count, small_args)
        shard0, scalars, loss = done[:3]
        pieces = [shard0] + [lax.ppermute(shard0, "dp", swap_pairs(ranks, k)) for k in (1, 2, 3)]
        pieces += [shard1] + from_dp1
        outs = [loss[0, 0]]
        outs += update_call(rank, scalars, pieces, conv_w, conv_mom, conv_avg)
        outs += [flip(v) for v in done[3:7]] + list(done[7:11]) + [v[0] for v in done[11:15]]
        return tuple(outs)

    rate = RATE_SCALE * chans * jnp.sqrt(jnp.float32(EOUT * pixels * ranks))
    counts_done = step_count.astype(F32)
    biases = jnp.stack([g[packed_w].reshape(4, wide) for g in grads])
    cells = jnp.concatenate([biases, jnp.stack(cell_sums).reshape(2, 3, 8, wide).sum(2)], 1)
    grads = [g[:packed_w].T for g in grads]
    loss_sum = jnp.sum(head_sums[:, 129])
    shared_small = jnp.concatenate(
        [head_sums[:, :128].reshape(-1), head_sums[:, 128], loss_sum[None], counted[0, :1]]
    )
    small = jnp.concatenate([cells.reshape(-1), shared_small])
    big = jnp.stack(grads).reshape(2, 4, groups, share, packed_w).transpose(2, 1, 3, 0, 4)
    big = big.reshape(groups, ranks, slab, 2, packed_w).transpose(1, 0, 2, 3, 4)
    part, small = scatter_sum_dp(big, ranks, small)
    ncell = 14 * wide
    for_gate = small[:ncell].reshape(14, groups, share).transpose(1, 0, 2).reshape(groups, 14 * share)
    to_gate = jnp.concatenate(
        [for_gate, jnp.broadcast_to(small[None, ncell:], (groups, small.shape[0] - ncell))], 1
    )
    hi = lax.reduce_precision(to_gate, 8, 7)
    lo = (to_gate - hi).astype(BF16)
    hi = hi.astype(BF16)
    width = slab * 2 * packed_w
    message = jnp.concatenate([part.reshape(groups, width).astype(BF16), hi, lo], 1)
    got = lax.all_to_all(message, "gate", 0, 0, tiled=True).astype(F32)
    got = jnp.sum(got.reshape(groups, -1), 0)
    nsmall = to_gate.shape[1]
    small_sum = got[width : width + nsmall] + got[width + nsmall :]
    piece = got[:width].reshape(1, slab, 2, packed_w)
    rows_all = gather_dp(piece, ranks).reshape(4 * share, 2, packed_w).transpose(1, 0, 2)
    count = chans * small_sum[-1]
    scale = 2.0 / count
    rows_all = rows_all * scale
    grad_conv = jnp.concatenate(
        [
            rows_all[..., 9 * wide :].reshape(2, 4 * share, 9, chans),
            rows_all[..., : 9 * wide].reshape(2, 4 * share, 9, wide),
        ],
        -1,
    ).reshape(conv_w.shape)
    grad_cell = small_sum[: 14 * share].reshape(2, 7, share) * scale
    rest = small_sum[14 * share :]
    grad_head = rest[: chans * wide].reshape(chans, wide) * scale
    grad_bias = rest[chans * wide : chans * wide + chans] * scale
    loss = rest[chans * wide + chans] / count

    outs = [loss]
    outs += nesterov(conv_w, grad_conv, conv_mom, conv_avg, counts_done[0], rate)
    outs += nesterov(cell_params, grad_cell, cell_mom, cell_avg, counts_done[1], rate)
    outs += nesterov(head_w, grad_head, head_mom, head_avg, counts_done[2], rate)
    outs += nesterov(head_b, grad_bias, bias_mom, bias_avg, counts_done[3], rate)
    return tuple(outs)


def solution(mesh):
    in_specs = (
        P(None, None, "dp"),
        P("dp"),
        P(None, "dp"),
        P(),
        P(None, None, "gate", None),
        P(None, None, "gate"),
        P(),
        P(),
        P(None, None, "gate", None),
        P(None, None, "gate"),
        P(),
        P(),
        P(None, None, "gate", None),
        P(None, None, "gate"),
        P(),
        P(),
    )
    out_specs = (
        P(),
        P(None, None, "gate", None),
        P(None, None, "gate", None),
        P(None, None, "gate", None),
        P(None, None, "gate", None),
        P(None, None, "gate"),
        P(None, None, "gate"),
        P(None, None, "gate"),
        P(None, None, "gate"),
        P(),
        P(),
        P(),
        P(),
        P(),
        P(),
        P(),
        P(),
    )
    return jax.shard_map(
        on_device, mesh=mesh, in_specs=in_specs, out_specs=out_specs, check_vma=False
    )
```
